32 devices in a mesh: sp: 4 (over y, core), ep: 8 (over z, x).
Axes of the slice: x: 2, y: 2, z: 4, core: 2. Of those that a mesh axis runs over, the one named last changes fastest.
Arguments:
- tokens: bfloat16 [8, 1024, 2048], P('ep', 'sp'), may hold values from -6 to 6
- doc_lengths: int32 [8, 8], P('ep'), may hold values from 1 to 512, 1024 in all within a row
- routes: int32 [8, 1024, 8], P('ep', 'sp'), may hold values from 0 to 15, all different within a row
- attn_gain: bfloat16 [2048], P('ep'), may hold values from 0.25 to 1.75
- w_query: bfloat16 [2048, 2048], P('ep'), may hold values from -0.125 to 0.125
- w_key: bfloat16 [2048, 2048], P('ep'), may hold values from -0.125 to 0.125
- w_value: bfloat16 [2048, 2048], P('ep'), may hold values from -0.125 to 0.125
- q_gain: bfloat16 [2048], P('ep'), may hold values from 0.25 to 1.75
- k_gain: bfloat16 [2048], P('ep'), may hold values from 0.25 to 1.75
- w_out: bfloat16 [2048, 2048], P('ep'), may hold values from -1 to 1
- ffn_gain: bfloat16 [2048], P('ep'), may hold values from 0.25 to 1.75
- w_router: bfloat16 [2048, 16], P('ep'), may hold values from -0.0625 to 0.0625
- w_gate: bfloat16 [16, 2048, 1024], P('ep'), may hold values from -0.125 to 0.125
- w_up: bfloat16 [16, 2048, 1024], P('ep'), may hold values from -0.125 to 0.125
- w_down: bfloat16 [16, 1024, 2048], P('ep'), may hold values from -0.5 to 0.5
- cotangent: bfloat16 [8, 1024, 2048], P('ep', 'sp'), may hold values from -6 to 6
Outputs:
- output: bfloat16 [8, 1024, 2048], P('ep', 'sp')
- input_grad: float32 [8, 1024, 2048], P('ep', 'sp')
- grad_attn_gain: float32 [2048], P('ep')
- grad_query: float32 [2048, 2048], P('ep')
- grad_key: float32 [2048, 2048], P('ep')
- grad_value: float32 [2048, 2048], P('ep')
- grad_q_gain: float32 [2048], P('ep')
- grad_k_gain: float32 [2048], P('ep')
- grad_out: float32 [2048, 2048], P('ep')
- grad_ffn_gain: float32 [2048], P('ep')
- grad_router: float32 [2048, 16], P('ep')
- grad_gate: float32 [16, 2048, 1024], P('ep', 'sp')
- grad_up: float32 [16, 2048, 1024], P('ep', 'sp')
- grad_down: float32 [16, 1024, 2048], P('ep', 'sp')
The draws below stay inside these ranges and needn't reach their ends.
Inputs may be any that keep to these rules, and one draw needn't show every extreme that they name: `doc_lengths`: in each sequence the 8 lengths sum to 1024, and the longest is exactly 512. `routes`: each token names 8 different experts; every expert is named by some token.
All inputs are finite; a program needn't handle non-finite values.
Results may differ from the reference program's by a relative error of at most 0.02.
Values may be sent and summed in bfloat16 or wider, within the bound.
No kernel may reach another device: no remote copies, remote signals or barrier semaphores. Data moves between devices by JAX's collectives and lax.ppermute only.
A program may use at most 384 MiB of HBM per device.

```python
import math
import jax
import jax.numpy as jnp
import numpy as np
from jax import lax

D = 2048
HEAD_DIM = 128
FF = 1024
TOP = 8
TOK_DEV = 256
DOCS = 8
EXPERTS = 16
SEQ = 1024
SEQS = 8
DOC_MOST = 512
CAP = 144


def level_of(rng, extent, cuts, smallest, top_value):
    def one(axis_at, blocks):
        draws = jax.random.uniform(jax.random.fold_in(jax.random.fold_in(rng, 6), axis_at), (blocks,), jnp.float32, smallest / len(cuts), top_value / len(cuts))
        return jnp.repeat(jnp.exp(draws), extent[axis_at] // blocks).reshape((-1,) + (1,) * (len(extent) - axis_at - 1))

    factor_of = one(*cuts[0])
    for cut in cuts[1:]:
        factor_of = factor_of * one(*cut)
    return factor_of


def distinct(own_key, rows, count, top, lift):
    ranking = jax.random.permutation(jax.random.fold_in(own_key, 1), count)
    favour = ranking
    for power in range(3):
        favour = favour * favour // count
    favour = favour * lift // count
    lots = jax.random.randint(jax.random.fold_in(own_key, 2), (rows, count), 0, 4096) + favour
    fixed_rows = jax.random.permutation(jax.random.fold_in(own_key, 3), rows)[jnp.arange(count) % rows]
    lots = jnp.where(jnp.arange(rows)[:, None] == fixed_rows[None, :], 1 << 14, lots)
    merit = lots * count + jnp.arange(count)
    return lax.top_k(merit.astype(jnp.int32), top)[1].astype(jnp.int32)


def split_up(amount, total, most, slope):
    weights = [(1 << 20) // math.isqrt(rank ** slope) + 1 for rank in range(2, amount + 1)]
    surplus, holding = total - most - (amount - 1), [1] * (amount - 1)
    while surplus > 0:
        movable = [i for i in range(amount - 1) if holding[i] < most]
        mass, budget = sum([weights[i] for i in movable]), surplus
        for i in movable:
            more = min(most - holding[i], max(1, budget * weights[i] // mass), surplus)
            holding[i] = holding[i] + more
            surplus = surplus - more
    return np.array([most] + holding)


def uneven(own_key, number_of, total, limit, skew):
    if number_of == 2:
        one = jax.random.randint(own_key, (), max(1, total - limit), min(limit, total - 1) + 1)
        return jnp.stack([one, total - one])
    tallies = jnp.asarray(split_up(number_of, total, limit, skew), jnp.int32)
    pairs = (number_of - 1) // 2
    source_of, sink = tallies[1:1 + 2 * pairs:2], tallies[2:2 + 2 * pairs:2]
    room = jnp.minimum(source_of - 1, limit - sink)
    passed = jax.random.randint(jax.random.fold_in(own_key, 1), (pairs,), 0, 1 << 20) % (room + 1)
    tallies = tallies.at[1:1 + 2 * pairs:2].set(source_of - passed).at[2:2 + 2 * pairs:2].set(sink + passed)
    return tallies[jax.random.permutation(jax.random.fold_in(own_key, 2), number_of)]


def bell_draw(key, shape, scale, bound, shards=(), held_as=jnp.bfloat16):
    array = scale * jax.random.normal(key, shape, jnp.float32)
    if shards:
        array = array * level_of(key, shape, shards, -0.22, 0.18)
    return jnp.clip(array, -bound, bound).astype(held_as)


def setup_inputs(seed: int = 0) -> dict:
    key_list = jax.random.split(jax.random.key(seed), 17)
    return {
        "tokens": bell_draw(key_list[0], (SEQS, SEQ, D), 1.0, 6.0, ((0, 8), (1, 4))),
        "doc_lengths": jax.vmap(lambda own: uneven(own, DOCS, SEQ, DOC_MOST, 1))(jax.random.split(key_list[1], SEQS)).reshape((SEQS, DOCS)).astype(jnp.int32),
        "routes": distinct(key_list[2], SEQS * SEQ, EXPERTS, TOP, 0).reshape((SEQS, SEQ, TOP)),
        "attn_gain": jnp.clip(1.0 + 0.15 * jax.random.normal(key_list[3], (D,), jnp.float32), 0.25, 1.75).astype(jnp.bfloat16),
        "w_query": bell_draw(key_list[4], (D, D), D ** -0.5, 0.125, ((0, 8),)),
        "w_key": bell_draw(key_list[5], (D, D), D ** -0.5, 0.125, ((0, 8),)),
        "w_value": bell_draw(key_list[6], (D, D), D ** -0.5, 0.125, ((0, 8),)),
        "q_gain": jnp.clip(1.0 + 0.15 * jax.random.normal(key_list[7], (D,), jnp.float32), 0.25, 1.75).astype(jnp.bfloat16),
        "k_gain": jnp.clip(1.0 + 0.15 * jax.random.normal(key_list[8], (D,), jnp.float32), 0.25, 1.75).astype(jnp.bfloat16),
        "w_out": bell_draw(key_list[9], (D, D), (D // 64) ** -0.5, 1.0, ((0, 8),)),
        "ffn_gain": jnp.clip(1.0 + 0.15 * jax.random.normal(key_list[10], (D,), jnp.float32), 0.25, 1.75).astype(jnp.bfloat16),
        "w_router": bell_draw(key_list[11], (D, EXPERTS), (4 * D) ** -0.5, 0.0625, ((0, 8),)),
        "w_gate": bell_draw(key_list[12], (EXPERTS, D, FF), D ** -0.5, 0.125, ((0, 8),)),
        "w_up": bell_draw(key_list[13], (EXPERTS, D, FF), D ** -0.5, 0.125, ((0, 8),)),
        "w_down": bell_draw(key_list[14], (EXPERTS, FF, D), (FF // 8) ** -0.5, 0.5, ((0, 8),)),
        "cotangent": bell_draw(key_list[15], (SEQS, SEQ, D), 1.0, 6.0, ((0, 8), (1, 4))),
    }


EPS = 1e-05
THETA = 10000.0
NEG_FILL = -1e+30

@jax.custom_vjp
def low(v):
    return lax.optimization_barrier(v.astype(jnp.bfloat16)).astype(jnp.float32)

@jax.custom_vjp
def low_back(v):
    return v

def low_keep(v):
    return (low(v), None)

def low_pass(kept, grad):
    return (grad,)

def back_keep(v):
    return (v, None)

def back_low(kept, grad):
    return (low(grad),)
low.defvjp(low_keep, low_pass)
low_back.defvjp(back_keep, back_low)

def product_high(left, right):
    return jnp.dot(left, right, precision=lax.Precision.HIGHEST, preferred_element_type=jnp.float32)

def rms_scale(values_in, gain_vec):
    return values_in * lax.rsqrt(lax.optimization_barrier(jnp.mean(values_in * values_in, axis=-1, keepdims=True)) + EPS) * gain_vec

def rotate_table(positions):
    half_dim = HEAD_DIM // 2
    frequency = THETA ** (-(2.0 * jnp.arange(half_dim, dtype=jnp.float32)) / HEAD_DIM)
    angles = positions.astype(jnp.float32)[:, None] * frequency[None, :]
    cosine_table = jnp.concatenate([jnp.cos(angles), jnp.cos(angles)], axis=1)
    sine_table = jnp.concatenate([jnp.sin(angles), jnp.sin(angles)], axis=1)
    return (cosine_table[:, None, :], sine_table[:, None, :])

def rotary(values_in, cosine_table, sine_table):
    row_count = values_in.shape[0]
    half_dim = HEAD_DIM // 2
    shaped = values_in.reshape(row_count, -1, HEAD_DIM)
    turned = jnp.concatenate([-shaped[..., half_dim:], shaped[..., :half_dim]], axis=-1)
    return (shaped * cosine_table + turned * sine_table).reshape(row_count, -1)

def doc_starts(lengths, row_count):
    doc_ends = jnp.cumsum(lengths).astype(jnp.int32)
    places = jnp.arange(row_count, dtype=jnp.int32)
    return lax.optimization_barrier(jnp.sum(jnp.where(doc_ends[None, :] <= places[:, None], lengths[None, :], 0), axis=1)).astype(jnp.int32)

def attend(q_rot, k_rot, values_in, starts):
    row_count = q_rot.shape[0]
    block_rows = min(512, row_count)
    block_count = row_count // block_rows
    head_count = q_rot.shape[1] // HEAD_DIM
    query_blocks = q_rot.reshape(block_count, block_rows, head_count, HEAD_DIM)
    key_rows = k_rot.reshape(row_count, head_count, HEAD_DIM)
    value_rows = values_in.reshape(row_count, head_count, HEAD_DIM)
    places = jnp.arange(row_count, dtype=jnp.int32)
    row_blocks = places.reshape(block_count, block_rows)
    start_blocks = starts.reshape(block_count, block_rows)

    def one_block(block_args):
        query_rows, row_ids, row_starts = block_args
        scores = low_back(jnp.einsum('qhd,khd->hqk', query_rows, key_rows, precision=lax.Precision.HIGHEST)) * HEAD_DIM ** (-0.5)
        allowed = (places[None, :] <= row_ids[:, None]) & (places[None, :] >= row_starts[:, None])
        scores = jnp.where(allowed[None], scores, NEG_FILL)
        probs_low = low(jax.nn.softmax(scores, axis=-1))
        mixed_rows = jnp.einsum('hqk,khd->qhd', probs_low, value_rows, precision=lax.Precision.HIGHEST)
        return mixed_rows.reshape(block_rows, -1)
    result = lax.map(jax.checkpoint(one_block), (query_blocks, row_blocks, start_blocks))
    return result.reshape(row_count, -1)

def expert_mix(h2_low, route_rows, gate_probs, w_gate, w_up, w_down):
    row_count = h2_low.shape[0]
    model_width = h2_low.shape[1]
    expert_count = w_gate.shape[0]
    top_count = route_rows.shape[1]
    block_count = row_count // TOK_DEV
    flat_routes = route_rows.reshape(block_count, TOK_DEV * top_count)
    onehot = (flat_routes[:, :, None] == jnp.arange(expert_count, dtype=jnp.int32)[None, None, :]).astype(jnp.int32)
    earlier = jnp.cumsum(onehot, axis=1) - onehot
    slot_index = lax.optimization_barrier(jnp.sum(earlier * onehot, axis=2))
    block_ids = jnp.arange(block_count, dtype=jnp.int32)[:, None]
    expert_rows = block_count * CAP
    pair_place = flat_routes * expert_rows + block_ids * CAP + slot_index
    pair_place = jnp.where(slot_index < CAP, pair_place, expert_count * expert_rows).reshape(-1).astype(jnp.int32)
    token_ids = (jnp.arange(row_count * top_count, dtype=jnp.int32) // top_count).astype(jnp.int32)
    source = jnp.full((expert_count * expert_rows,), row_count, jnp.int32).at[pair_place].set(token_ids, mode='drop')
    padded = jnp.concatenate([h2_low, jnp.zeros((1, model_width), jnp.float32)], axis=0)
    dispatched = low_back(padded[source].reshape(expert_count, expert_rows, model_width))
    gate_pre = low_back(jnp.einsum('erd,edf->erf', dispatched, w_gate, precision=lax.Precision.HIGHEST))
    up_pre = low_back(jnp.einsum('erd,edf->erf', dispatched, w_up, precision=lax.Precision.HIGHEST))
    act_low = low(jax.nn.silu(gate_pre) * up_pre)
    expert_out = low_back(low(jnp.einsum('erf,efd->erd', act_low, w_down, precision=lax.Precision.HIGHEST)))
    out_padded = jnp.concatenate([expert_out.reshape(-1, model_width), jnp.zeros((1, model_width), jnp.float32)], axis=0)
    per_pair = out_padded[pair_place].reshape(row_count, top_count, model_width)
    return lax.optimization_barrier(jnp.sum(gate_probs[:, :, None] * per_pair, axis=1))

def layer(stream, params, positions, starts, route_rows):
    attn_gain, w_query, w_key, w_value, q_gain, k_gain, w_out, ffn_gain, w_router, w_gate, w_up, w_down = params
    h_low = low(rms_scale(stream, attn_gain))
    q_raw = low_back(product_high(h_low, w_query))
    k_raw = low_back(product_high(h_low, w_key))
    v_low = low_back(low(product_high(h_low, w_value)))
    cosine_table, sine_table = rotate_table(positions)
    q_rot = low_back(low(rotary(rms_scale(q_raw, q_gain), cosine_table, sine_table)))
    k_rot = low_back(low(rotary(rms_scale(k_raw, k_gain), cosine_table, sine_table)))
    attn_low = low_back(low(attend(q_rot, k_rot, v_low, starts)))
    stream_one = stream + low_back(product_high(attn_low, w_out))
    h2_low = low(rms_scale(stream_one, ffn_gain))
    logits = low_back(product_high(h2_low, w_router))
    chosen = jnp.take_along_axis(logits, route_rows, axis=1)
    gate_probs = jax.nn.softmax(chosen, axis=-1)
    return stream_one + expert_mix(h2_low, route_rows, gate_probs, w_gate, w_up, w_down)

def reference(tokens, doc_lengths, routes, attn_gain, w_query, w_key, w_value, q_gain, k_gain, w_out, ffn_gain, w_router, w_gate, w_up, w_down, cotangent):
    params = (attn_gain.astype(jnp.float32), w_query.astype(jnp.float32), w_key.astype(jnp.float32), w_value.astype(jnp.float32), q_gain.astype(jnp.float32), k_gain.astype(jnp.float32), w_out.astype(jnp.float32), ffn_gain.astype(jnp.float32), w_router.astype(jnp.float32), w_gate.astype(jnp.float32), w_up.astype(jnp.float32), w_down.astype(jnp.float32))

    def one_sequence(totals, seq_items):
        seq_tokens, seq_cot, lengths, seq_routes = seq_items
        row_count = seq_tokens.shape[0]
        starts = doc_starts(lengths, row_count)
        positions = (jnp.arange(row_count, dtype=jnp.int32) - starts).astype(jnp.int32)

        def forward(stream, weights):
            return layer(stream, weights, positions, starts, seq_routes)
        layer_out, pull_back = jax.vjp(forward, seq_tokens.astype(jnp.float32), params)
        d_stream, d_params = pull_back(seq_cot.astype(jnp.float32))
        totals = jax.tree.map(lambda left, right: left + right, totals, d_params)
        return (totals, (layer_out.astype(jnp.bfloat16), d_stream))
    zero_grads = jax.tree.map(jnp.zeros_like, params)
    totals, outputs = lax.scan(one_sequence, zero_grads, (tokens, cotangent, doc_lengths, routes))
    output, input_grad = outputs
    return (output, input_grad, totals[0], totals[1], totals[2], totals[3], totals[4], totals[5], totals[6], totals[7], totals[8], totals[9], totals[10], totals[11])
```

```python
import functools

import jax
import jax.numpy as jnp
from jax import lax
from jax.experimental import pallas as pl
from jax.experimental.pallas import tpu as pltpu
from jax.sharding import PartitionSpec as P

HEAD_DIM = 128
EPS = 1e-05
THETA = 10000.0
NEG_FILL = -1e30
F32 = jnp.float32
BF16 = jnp.bfloat16
MIB = 1 << 20


def product(left, right):
    return jnp.dot(left, right, preferred_element_type=F32)


def product_left(left, right):
    return lax.dot_general(left, right, (((0,), (0,)), ((), ())), preferred_element_type=F32)


def product_right(left, right):
    return lax.dot_general(left, right, (((1,), (1,)), ((), ())), preferred_element_type=F32)


def row_sums(values_in):
    ones = jnp.ones((8, values_in.shape[1]), F32)
    return lax.dot_general(
        ones, values_in, (((1,), (1,)), ((), ())),
        preferred_element_type=F32, precision=lax.Precision.HIGHEST,
    )


def call(kernel, out_shape, args, flops, name, scratch=(), scalars=(), grid=(1,), in_specs=None,
         out_specs=None, aliases=None, vmem=60):
    single = not isinstance(out_shape, (list, tuple))
    shapes = [out_shape] if single else list(out_shape)
    count = len(grid)

    def fixed(shape):
        rank = len(shape)
        return pl.BlockSpec(tuple(shape), lambda *ids: (0,) * rank)

    in_specs = in_specs or [None] * len(args)
    out_specs = out_specs or [None] * len(shapes)
    in_specs = [s if s is not None else fixed(a.shape) for s, a in zip(in_specs, args)]
    out_specs = [s if s is not None else fixed(o.shape) for s, o in zip(out_specs, shapes)]
    moved = sum(a.size * a.dtype.itemsize for a in args)
    moved += sum(o.size * o.dtype.itemsize for o in shapes)
    result = pl.pallas_call(
        kernel,
        grid_spec=pltpu.PrefetchScalarGridSpec(
            num_scalar_prefetch=len(scalars), grid=grid, in_specs=in_specs, out_specs=out_specs,
            scratch_shapes=list(scratch),
        ),
        out_shape=shapes,
        input_output_aliases={k + len(scalars): v for k, v in (aliases or {}).items()},
        compiler_params=pltpu.CompilerParams(
            vmem_limit_bytes=vmem * MIB, dimension_semantics=("arbitrary",) * count
        ),
        cost_estimate=pl.CostEstimate(flops=int(flops), bytes_accessed=int(moved), transcendentals=0),
        name=name,
    )(*scalars, *args)
    return result[0] if single else result


def like(shape, dtype):
    return jax.ShapeDtypeStruct(tuple(shape), dtype)


MIDDLE = [(2, 4), (3, 5), (4, 2), (5, 3)]
OUTWARD = [(2, 0), (3, 1), (4, 6), (5, 7)]
INWARD = [(0, 2), (1, 3), (6, 4), (7, 5)]


def shift(value, pairs):
    return lax.ppermute(value, "ep", pairs)


def swap(value, bits):
    return shift(value, [(i, i ^ bits) for i in range(8)])


def swap_sp(value, bits):
    return lax.ppermute(value, "sp", [(i, i ^ bits) for i in range(4)])


def piece_blocks(n_ep, ep_index):
    ids = jnp.arange(n_ep, dtype=jnp.int32)
    return jnp.bitwise_xor(ids, ep_index) if n_ep == 8 else ids


def gather_line(value, n_ep):
    if n_ep != 8:
        return gather_turn(value, n_ep)
    near = swap(value, 2)
    inner_a = shift(value, MIDDLE)
    inner_b = shift(near, MIDDLE)
    third = inner_b + shift(inner_a, OUTWARD)
    fourth = inner_a + shift(inner_b, OUTWARD)
    pieces = []
    for own in (value, near, third, fourth):
        pieces += [own, swap(own, 1)]
    return pieces


def gather_turn(value, n_ep):
    if n_ep != 8:
        whole = lax.all_gather(value, "ep", axis=0, tiled=False)
        return [whole[i] for i in range(n_ep)]
    pieces = []
    for own in (value, swap(value, 2), swap(value, 4), swap(value, 6)):
        pieces += [own, swap(own, 1)]
    return pieces


def plus(left, right):
    return (left.astype(F32) + right.astype(F32)).astype(left.dtype)


def scatter_line(pieces, n_ep):
    if n_ep != 8:
        return scatter_turn(pieces, n_ep)
    own, near, third, fourth = (plus(pieces[2 * i], swap(pieces[2 * i + 1], 1)) for i in range(4))
    third_in, fourth_in = shift(fourth, INWARD), shift(third, INWARD)
    third, fourth = plus(third, third_in), plus(fourth, fourth_in)
    near = plus(near, shift(third, MIDDLE))
    return own.astype(F32) + shift(fourth, MIDDLE).astype(F32) + swap(near, 2).astype(F32)


def scatter_turn(pieces, n_ep):
    if n_ep != 8:
        stacked = jnp.stack(pieces)
        return lax.psum_scatter(stacked, "ep", scatter_dimension=0, tiled=False).astype(F32)
    sums = [plus(pieces[2 * i], swap(pieces[2 * i + 1], 1)) for i in range(4)]
    total = sums[0].astype(F32)
    for i in range(1, 4):
        total = total + swap(sums[i], 2 * i).astype(F32)
    return total


def gather_sp(value):
    over = swap_sp(value, 2)
    return [value, swap_sp(value, 1), over, swap_sp(over, 1)]


def sum_sp(value):
    value = value + swap_sp(value, 1)
    return value + swap_sp(value, 2)


def block_at(ids, position, size):
    if size % HEAD_DIM:
        return pl.ds(position * size, size)
    return pl.ds(pl.multiple_of(ids[position] * size, size), size)


def qk_kernel(count, ids, h_ref, *refs):
    pieces, (q_ref, k_ref, squares_ref, w_ref) = refs[:count], refs[count:]
    shard = pieces[0].shape[0]

    @pl.when(pl.program_id(0) == 0)
    def _():
        for k in range(count):
            w_ref[block_at(ids, k, shard), :] = pieces[k][...]

    width = q_ref.shape[1]
    for at, ref in enumerate((q_ref, k_ref)):
        part = product(h_ref[...], w_ref[:, at * width : (at + 1) * width])
        ref[...] = part
        squares_ref[8 * at : 8 * at + 8, :] = row_sums(part * part)


def qk_project(ids, h_all, pieces):
    total, depth = h_all.shape
    shard, both = pieces[0].shape
    width = both // 2
    rows = min(256, total)
    block = pl.BlockSpec((rows, width), lambda i, ids: (i, 0))
    return call(
        functools.partial(qk_kernel, len(pieces)),
        [like((total, width), F32)] * 2 + [like((16, total), F32), like((depth, both), BF16)],
        [h_all, *pieces],
        2 * total * depth * both,
        "qk_project",
        scalars=(ids,),
        grid=(total // rows,),
        in_specs=[pl.BlockSpec((rows, depth), lambda i, ids: (i, 0))] + [None] * len(pieces),
        out_specs=[block, block, pl.BlockSpec((16, rows), lambda i, ids: (0, i)), None],
    )


def v_kernel(count, ids, h_ref, *refs):
    pieces, (v_ref, w_ref, out_ref) = refs[:count], refs[count:]
    shard = pieces[0].shape[0]
    width = v_ref.shape[1]

    @pl.when(pl.program_id(0) == 0)
    def _():
        for k in range(count):
            rows = block_at(ids, k, shard)
            w_ref[rows, :] = pieces[k][:, :width]
            out_ref[rows, :] = pieces[k][:, width:]

    v_ref[...] = product(h_ref[...], w_ref[...]).astype(BF16)


def v_project(ids, h_all, pieces):
    total, depth = h_all.shape
    width = pieces[0].shape[1] // 2
    rows = min(256, total)
    return call(
        functools.partial(v_kernel, len(pieces)),
        [like((total, width), BF16), like((depth, width), BF16), like((depth, width), BF16)],
        [h_all, *pieces],
        2 * total * depth * width,
        "v_project",
        scalars=(ids,),
        grid=(total // rows,),
        in_specs=[pl.BlockSpec((rows, depth), lambda i, ids: (i, 0))] + [None] * len(pieces),
        out_specs=[pl.BlockSpec((rows, width), lambda i, ids: (i, 0)), None, None],
    )


def out_kernel(n_ep, ids, attn_ref, x_ref, gain_ref, *refs):
    weights, (one_ref, low_ref) = refs[:-2], refs[-2:]
    width = weights[0].shape[1]
    for j, weight in enumerate(weights):
        cols = block_at(ids, n_ep + j, width)
        one_ref[:, cols] = x_ref[:, cols].astype(F32) + product(attn_ref[...], weight[...])
    one = one_ref[...]
    scale = lax.rsqrt(jnp.mean(one * one, axis=1, keepdims=True) + EPS)
    low_ref[...] = (one * scale * gain_ref[...]).astype(BF16)


def out_project(ids, n_ep, attn_tok, tokens, gain, weights):
    return call(
        functools.partial(out_kernel, n_ep),
        [like(tokens.shape, F32), like(tokens.shape, BF16)],
        [attn_tok, tokens, gain, *weights],
        2 * tokens.size * attn_tok.shape[1],
        "out_project",
        scalars=(ids,),
    )


def out_back_kernel(n_ep, ids, d_ref, *refs):
    weights, d_attn_ref = refs[:-1], refs[-1]
    width = weights[0].shape[1]
    total = None
    for j, weight in enumerate(weights):
        part = product_right(d_ref[:, block_at(ids, n_ep + j, width)], weight[...])
        total = part if total is None else total + part
    d_attn_ref[...] = total.astype(BF16)


def out_back(ids, n_ep, d_z, weights):
    return call(
        functools.partial(out_back_kernel, n_ep),
        like((d_z.shape[0], weights[0].shape[0]), BF16),
        [d_z, *weights],
        2 * d_z.size * weights[0].shape[0],
        "out_back",
        scalars=(ids,),
    )


def grad_pieces_kernel(count, ids, left_ref, right_ref, *pieces):
    shard = pieces[0].shape[0]
    for k in range(count):
        pieces[k][...] = product_left(
            left_ref[:, block_at(ids, k, shard)], right_ref[...]
        ).astype(BF16)


def grad_pieces(ids, count, left, right, name):
    shard = left.shape[1] // count
    return call(
        functools.partial(grad_pieces_kernel, count),
        [like((shard, right.shape[1]), BF16)] * count,
        [left, right],
        2 * left.size * right.shape[1],
        name,
        scalars=(ids,),
    )


def qkv_back_kernel(
    count, width_all, ids, h_ref, dqn_ref, dkn_ref, dv_ref, qr_ref, kr_ref, scale_ref, sums_ref,
    tiny_ref, *refs
):
    pieces, d_ref = refs[:count], refs[count]
    width = dv_ref.shape[1]
    scales = jnp.transpose(scale_ref[...])
    means = jnp.transpose(sums_ref[...]) * (1.0 / width_all)
    for at, (d_normed, raw) in enumerate(((dqn_ref, qr_ref), (dkn_ref, kr_ref))):
        scale, mean = scales[:, 8 * at : 8 * at + 1], means[:, 8 * at : 8 * at + 1]
        d_ref[:, at * width : (at + 1) * width] = (
            scale * (d_normed[...] - raw[...] * scale * mean)
        ).astype(BF16)
    d_ref[:, 2 * width :] = dv_ref[...]
    shard = h_ref.shape[1] // count
    per_row = 3 * width // shard
    for k in range(count):
        block = block_at(ids, k, shard)
        pieces[k][:shard, :] = product_left(h_ref[:, block], d_ref[...]).astype(BF16)
        pieces[k][shard:, :] = jnp.zeros_like(pieces[k][shard:, :])
        for at in range(tiny_ref.shape[0]):
            row, col = shard + at // per_row, (at % per_row) * shard
            pieces[k][row : row + 1, col : col + shard] = tiny_ref[at : at + 1, block].astype(BF16)


def qkv_back(ids, count, h_all, d_qn, d_kn, d_v, q_raw, k_raw, scales, sums, tiny):
    total, depth = h_all.shape
    width = d_v.shape[1]
    shard = depth // count
    extra = -(-tiny.shape[0] // (3 * width // shard))
    extra = -(-extra // 16) * 16
    return call(
        functools.partial(qkv_back_kernel, count, depth),
        [like((shard + extra, 3 * width), BF16)] * count + [like((total, 3 * width), BF16)],
        [h_all, d_qn, d_kn, d_v, q_raw, k_raw, scales, sums, tiny],
        2 * h_all.size * 3 * width,
        "qkv_back",
        scalars=(ids,),
    )


def d_h_kernel(d_ref, qk_ref, v_ref, out_ref):
    both = qk_ref.shape[1]
    out_ref[...] = (
        product_right(d_ref[:, :both], qk_ref[...]) + product_right(d_ref[:, both:], v_ref[...])
    ).astype(BF16)


def d_h_rows(d_qkv, w_qk, w_v):
    total, wide = d_qkv.shape
    depth = w_qk.shape[0]
    rows = min(256, total)
    return call(
        d_h_kernel,
        like((total, depth), BF16),
        [d_qkv, w_qk, w_v],
        2 * d_qkv.size * depth,
        "d_h",
        grid=(total // rows,),
        in_specs=[pl.BlockSpec((rows, wide), lambda i: (i, 0)), None, None],
        out_specs=[pl.BlockSpec((rows, depth), lambda i: (i, 0))],
    )


def finish_kernel(n_ep, ids, wq_ref, wk_ref, wv_ref, gain_ref, *refs):
    parts, (gq_ref, gk_ref, gv_ref, tiny_ref, attn_ref) = refs[:-5], refs[-5:]
    shard = wq_ref.shape[0]
    width = parts[0].shape[1] // 3
    dots = jnp.zeros((shard, 1), F32)
    tiny = jnp.zeros(tiny_ref.shape, F32)
    for j, part in enumerate(parts):
        cols = block_at(ids, n_ep + j, width)
        for at, (grad, weight) in enumerate(((gq_ref, wq_ref), (gk_ref, wk_ref), (gv_ref, wv_ref))):
            value = part[:shard, at * width : (at + 1) * width].astype(F32)
            grad[:, cols] = value
            dots += jnp.sum(value * weight[:, cols].astype(F32), axis=1, keepdims=True)
        tiny += part[shard:, :].astype(F32)
    tiny_ref[...] = tiny
    attn_ref[...] = dots / gain_ref[...]


def finish(ids, n_ep, w_query, w_key, w_value, gain, parts):
    shard, depth = w_query.shape
    extra = parts[0].shape[0] - shard
    return call(
        functools.partial(finish_kernel, n_ep),
        [like((shard, depth), F32)] * 3 + [like((extra, parts[0].shape[1]), F32), like((shard, 1), F32)],
        [w_query, w_key, w_value, gain, *parts],
        shard * depth * 6,
        "finish",
        scalars=(ids,),
    )


def turn(values_in):
    return pltpu.roll(values_in, HEAD_DIM // 2, 1)


def masked_probs(q_ref, k_ref, start_ref, block, rows):
    first, last = block * rows, (block + 1) * rows
    scores = product_right(q_ref[first:last, :], k_ref[0:last, :]) * (HEAD_DIM ** (-0.5))
    row_ids = first + lax.broadcasted_iota(jnp.int32, scores.shape, 0)
    places = lax.broadcasted_iota(jnp.int32, scores.shape, 1)
    allowed = (places <= row_ids) & (places >= start_ref[first:last, :])
    scores = jnp.where(allowed, scores, NEG_FILL)
    top = jnp.max(scores, axis=1, keepdims=True)
    weights = jnp.exp(scores - top)
    return weights * (1.0 / jnp.sum(weights, axis=1, keepdims=True))


def attend_kernel(
    rows, qr_ref, kr_ref, v_ref, scale_ref, gq_ref, gk_ref, cos_ref, sin_ref, start_ref,
    q_ref, k_ref, out_ref,
):
    scales = jnp.transpose(scale_ref[...])
    for at, (raw, gain, low) in enumerate(((qr_ref, gq_ref, q_ref), (kr_ref, gk_ref, k_ref))):
        normed = raw[...] * scales[:, 8 * at : 8 * at + 1] * gain[...]
        low[...] = (normed * cos_ref[...] + turn(normed) * sin_ref[...]).astype(BF16)
    for block in range(q_ref.shape[0] // rows):
        probs = masked_probs(q_ref, k_ref, start_ref, block, rows)
        last = (block + 1) * rows
        out_ref[block * rows : last, :] = product(
            probs.astype(BF16), v_ref[0:last, :]
        ).astype(BF16)


def head_spec(rows):
    return pl.BlockSpec((rows, HEAD_DIM), lambda h: (0, h))


def attend(q_raw, k_raw, v_low, scales, q_gain, k_gain, cosine, sine, starts):
    total, width = v_low.shape
    heads = width // HEAD_DIM
    head, gain = head_spec(total), head_spec(1)
    return call(
        functools.partial(attend_kernel, min(256, total)),
        [like((total, width), BF16)] * 3,
        [q_raw, k_raw, v_low, scales, q_gain, k_gain, cosine, sine, starts],
        3 * heads * total * total * HEAD_DIM,
        "attend",
        grid=(heads,),
        in_specs=[head, head, head, None, gain, gain, None, None, None],
        out_specs=[head, head, head],
    )


def attend_back_kernel(
    rows, q_ref, k_ref, v_ref, do_ref, qr_ref, kr_ref, scale_ref, gq_ref, gk_ref,
    cos_ref, sin_ref, start_ref,
    dq_ref, dk_ref, dv_ref, sums_ref, dgq_ref, dgk_ref, q_acc, k_acc, v_acc,
):
    k_acc[...] = jnp.zeros_like(k_acc)
    v_acc[...] = jnp.zeros_like(v_acc)
    for block in range(q_ref.shape[0] // rows):
        first, last = block * rows, (block + 1) * rows
        probs = masked_probs(q_ref, k_ref, start_ref, block, rows)
        d_rows = do_ref[first:last, :]
        d_probs = product_right(d_rows, v_ref[0:last, :])
        delta = jnp.sum(probs * d_probs, axis=1, keepdims=True)
        d_scores = (probs * (d_probs - delta) * (HEAD_DIM ** (-0.5))).astype(BF16)
        q_acc[first:last, :] = product(d_scores, k_ref[0:last, :])
        k_acc[0:last, :] += product_left(d_scores, q_ref[first:last, :])
        v_acc[0:last, :] += product_left(probs.astype(BF16), d_rows)
    dv_ref[...] = v_acc[...].astype(BF16)

    @pl.when(pl.program_id(0) == 0)
    def _():
        sums_ref[...] = jnp.zeros_like(sums_ref)

    scales = jnp.transpose(scale_ref[...])
    for at, (acc, raw, gain, d_ref, dg_ref) in enumerate(
        ((q_acc, qr_ref, gq_ref, dq_ref, dgq_ref), (k_acc, kr_ref, gk_ref, dk_ref, dgk_ref))
    ):
        turned = acc[...].astype(BF16).astype(F32)
        back = turned * cos_ref[...] + turn(turned * sin_ref[...])
        normed = raw[...] * scales[:, 8 * at : 8 * at + 1]
        both = back * normed
        dg_ref[...] = jnp.sum(both, axis=0, keepdims=True)
        d_ref[...] = back * gain[...]
        sums_ref[8 * at : 8 * at + 8, :] += row_sums(both * gain[...])


def attend_back(
    q_rot, k_rot, v_low, d_heads, q_raw, k_raw, scales, q_gain, k_gain, cosine, sine, starts
):
    total, width = v_low.shape
    heads = width // HEAD_DIM
    head, gain = head_spec(total), head_spec(1)
    wide, thin = like((total, width), F32), like((1, width), F32)
    return call(
        functools.partial(attend_back_kernel, min(256, total)),
        [wide, wide, like((total, width), BF16), like((16, total), F32), thin, thin],
        [q_rot, k_rot, v_low, d_heads, q_raw, k_raw, scales, q_gain, k_gain, cosine, sine, starts],
        7 * heads * total * total * HEAD_DIM,
        "attend_back",
        scratch=[pltpu.VMEM((total, HEAD_DIM), F32)] * 3,
        grid=(heads,),
        in_specs=[head] * 6 + [None, gain, gain, None, None, None],
        out_specs=[head, head, head, None, gain, gain],
    )


def chooser(places_ref, at, cap):
    row = places_ref[at : at + 1, :]
    slots = lax.broadcasted_iota(jnp.int32, (cap, row.shape[1]), 0)
    return slots == row


def dispatch_kernel(
    pieces_here, local, cap, gated, mine, *refs
):
    pieces, refs = refs[:pieces_here], refs[pieces_here:]
    places_ref, refs = refs[0], refs[1:]
    if gated:
        (picked_ref, router_ref), refs = refs[:2], refs[2:]
        rows_ref, gate_ref, all_ref = refs[-3:]
    else:
        rows_ref = refs[-1]
    for p in range(pieces_here):
        if gated:
            logits = product_right(router_ref[...], pieces[p][...])
            experts = logits.shape[0]
            picked = picked_ref[p * experts : (p + 1) * experts, :] > 0
            logits = jnp.where(picked, logits, NEG_FILL)
            weights = jnp.exp(logits - jnp.max(logits, axis=0, keepdims=True))
            weights = jnp.where(picked, weights, 0.0)
            gates = weights / jnp.sum(weights, axis=0, keepdims=True)
            all_ref[p * experts : (p + 1) * experts, :] = gates
        for e in range(local):
            chosen = chooser(places_ref, p * local + e, cap)
            rows_ref[e, p * cap : (p + 1) * cap, :] = product(
                chosen.astype(BF16), pieces[p][...]
            ).astype(BF16)
            if gated:
                row = all_ref[pl.ds(p * experts + mine[0] * local + e, 1), :]
                gate_ref[e, p * cap : (p + 1) * cap, :] = jnp.sum(
                    jnp.where(chosen, row, 0.0), axis=1, keepdims=True
                )


def dispatch(mine, pieces, places, picked, router, local, cap, group, at, rows, gates):
    gated = router is not None
    here = len(pieces)
    width = pieces[0].shape[1]
    args = [*pieces, places]
    shapes = [like((local, group * cap, width), BF16)]
    spec = pl.BlockSpec((local, here * cap, width), lambda i, mine: (0, at, 0))
    out_specs = [spec]
    if gated:
        args += [picked, router]
        shapes += [like((local, group * cap, 1), F32), like((picked.shape[0], places.shape[1]), F32)]
        out_specs += [pl.BlockSpec((local, here * cap, 1), lambda i, mine: (0, at, 0)), None]
    in_specs = [None] * len(args)
    aliases = {}
    if rows is not None:
        aliases[len(args)] = 0
        args.append(rows)
        in_specs.append(pl.BlockSpec(memory_space=pl.ANY))
        if gated:
            aliases[len(args)] = 1
            args.append(gates)
            in_specs.append(pl.BlockSpec(memory_space=pl.ANY))
    return call(
        functools.partial(dispatch_kernel, here, local, cap, gated),
        shapes,
        args,
        2 * here * local * cap * places.shape[1] * width,
        "dispatch",
        scalars=(mine,),
        in_specs=in_specs,
        out_specs=out_specs,
        aliases=aliases,
    )


def expert_kernel(
    x_ref, d_ref, gate_ref, wg_ref, wu_ref, wd_ref,
    act_ref, dg_ref, du_ref, dots_ref, mix_ref, back_ref, mix_acc, back_acc,
):
    step = pl.program_id(1)
    last = pl.num_programs(1) - 1
    x_rows, d_rows, gate = x_ref[0], d_ref[0], gate_ref[0]
    pre = product(x_rows, wg_ref[0])
    up = product(x_rows, wu_ref[0])
    pulled = product_right(d_rows, wd_ref[0])
    sigma = jax.nn.sigmoid(pre)
    silu = pre * sigma
    act = silu * up
    dots = jnp.sum(act * pulled, axis=1, keepdims=True)
    act_low = (act * gate).astype(BF16)
    act_ref[0] = act_low
    d_act = pulled * gate
    du_low = (d_act * silu).astype(BF16)
    dg_low = (d_act * up * sigma * (1.0 + pre * (1.0 - sigma))).astype(BF16)
    dg_ref[0] = dg_low
    du_ref[0] = du_low
    mix = product(act_low, wd_ref[0])
    back = product_right(dg_low, wg_ref[0]) + product_right(du_low, wu_ref[0])

    @pl.when(step == 0)
    def _():
        dots_ref[0] = dots
        mix_acc[...] = mix
        back_acc[...] = back

    @pl.when((step > 0) & (step < last))
    def _():
        dots_ref[0] += dots
        mix_acc[...] += mix
        back_acc[...] += back

    @pl.when(step == last)
    def _():
        dots_ref[0] += dots
        mix_ref[0] = (mix_acc[...] + mix).astype(BF16)
        back_ref[0] = (back_acc[...] + back).astype(BF16)


def experts(rows, d_rows, gates, w_gate, w_up, w_down):
    local, count, width = rows.shape
    hidden = w_gate.shape[2]
    part = hidden // 2
    wide = pl.BlockSpec((1, count, width), lambda e, f: (e, 0, 0))
    column = pl.BlockSpec((1, count, 1), lambda e, f: (e, 0, 0))
    thin = pl.BlockSpec((1, count, part), lambda e, f: (e, 0, f))
    into = pl.BlockSpec((1, width, part), lambda e, f: (e, 0, f))
    outof = pl.BlockSpec((1, part, width), lambda e, f: (e, f, 0))
    return call(
        expert_kernel,
        [like((local, count, hidden), BF16)] * 3
        + [like((local, count, 1), F32)]
        + [like((local, count, width), BF16)] * 2,
        [rows, d_rows, gates, w_gate, w_up, w_down],
        12 * rows.size * hidden,
        "experts",
        scratch=[pltpu.VMEM((count, width), F32)] * 2,
        grid=(local, 2),
        in_specs=[wide, wide, column, into, into, outof],
        out_specs=[thin, thin, thin, column, wide, wide],
    )


def combine_kernel(here, local, cap, dotted, places_ref, rows_ref, *refs):
    pieces = refs[int(dotted) : int(dotted) + here]
    for p in range(here):
        chosen = [chooser(places_ref, p * local + e, cap) for e in range(local)]
        total = None
        for e in range(local):
            part = product_left(chosen[e].astype(BF16), rows_ref[e, p * cap : (p + 1) * cap, :])
            total = part if total is None else total + part
            if dotted:
                refs[-1][p * local + e : p * local + e + 1, :] = jnp.sum(
                    jnp.where(chosen[e], refs[0][e, p * cap : (p + 1) * cap, :], 0.0),
                    axis=0, keepdims=True,
                )
        pieces[p][...] = total.astype(BF16)


def combine(places, rows, here, local, cap, at, dots=None):
    width = rows.shape[2]
    tokens = places.shape[1]
    dotted = dots is not None
    args = [places, rows] + ([dots] if dotted else [])
    in_specs = [None, pl.BlockSpec((local, here * cap, width), lambda i: (0, at, 0))]
    if dotted:
        in_specs.append(pl.BlockSpec((local, here * cap, 1), lambda i: (0, at, 0)))
    shapes = [like((tokens, width), BF16)] * here
    if dotted:
        shapes.append(like(places.shape, F32))
    return call(
        functools.partial(combine_kernel, here, local, cap, dotted),
        shapes,
        args,
        2 * here * local * cap * tokens * width,
        "combine",
        in_specs=in_specs,
    )


def weight_grad_kernel(groups, *refs):
    lefts, rights = refs[:groups], refs[groups : 2 * groups]
    total = None
    for left, right in zip(lefts, rights):
        part = product_left(left[0], right[0])
        total = part if total is None else total + part
    refs[-1][0] = total.astype(BF16)


def weight_grad(lefts, rights):
    local, count, tall = lefts[0].shape
    wide = rights[0].shape[2]
    part = min(512, tall)
    left = pl.BlockSpec((1, count, part), lambda e, i: (e, 0, i))
    right = pl.BlockSpec((1, count, wide), lambda e, i: (e, 0, 0))
    return call(
        functools.partial(weight_grad_kernel, len(lefts)),
        like((local, tall, wide), BF16),
        [*lefts, *rights],
        2 * len(lefts) * lefts[0].size * wide,
        "weight_grad",
        grid=(local, tall // part),
        in_specs=[left] * len(lefts) + [right] * len(lefts),
        out_specs=[pl.BlockSpec((1, part, wide), lambda e, i: (e, i, 0))],
    )


def tie(*values):
    return lax.optimization_barrier(values)


def body(
    tokens, doc_lengths, routes, attn_gain, w_query, w_key, w_value, q_gain, k_gain, w_out,
    ffn_gain, w_router, w_gate, w_up, w_down, cotangent,
):
    n_sp = lax.axis_size("sp")
    n_ep = lax.axis_size("ep")
    sp_index = lax.axis_index("sp")
    ep_index = lax.axis_index("ep")
    tok_dev, width = tokens.shape[1:]
    total = tok_dev * n_sp
    shard = width // n_ep
    head_width = width // n_sp
    top_count = routes.shape[2]
    local = w_gate.shape[0]
    expert_count = local * n_ep
    capacity = 9 * tok_dev * top_count // (8 * expert_count)
    cap = -(-capacity // 16) * 16
    group = 4
    blocks = piece_blocks(n_ep, ep_index)
    partners = jnp.bitwise_xor(jnp.arange(n_sp, dtype=jnp.int32), sp_index)
    ids = jnp.concatenate([blocks, partners]).astype(jnp.int32)
    mine = ep_index.astype(jnp.int32).reshape(1)

    def own_columns(value):
        return lax.dynamic_slice_in_dim(value, sp_index * head_width, head_width, 1)

    def by_block(value):
        order = jnp.bitwise_xor(jnp.arange(n_ep, dtype=jnp.int32), ep_index) if n_ep == 8 else blocks
        return jnp.stack(
            [lax.dynamic_index_in_dim(value, order[i], 0, keepdims=False) for i in range(n_ep)]
        )

    qk_pieces = gather_line(
        jnp.concatenate([own_columns(w_query), own_columns(w_key)], axis=1), n_ep
    )

    expert_ids = jnp.arange(expert_count, dtype=jnp.int32)
    picked = jnp.any(routes[0][:, :, None] == expert_ids[None, None, :], axis=1)
    small = jnp.concatenate(
        [
            jnp.stack([attn_gain, q_gain, k_gain, ffn_gain]),
            jnp.zeros((12, shard), BF16),
            w_router.T,
        ],
        axis=0,
    )
    picked_low = picked.T.astype(BF16)
    if shard == tok_dev:
        both = jnp.stack(gather_turn(jnp.concatenate([small, picked_low], axis=0), n_ep))
        small_all, picked_all = both[:, : 16 + expert_count], both[:, 16 + expert_count :]
    else:
        small_all = jnp.stack(gather_turn(small, n_ep))
        picked_all = jnp.stack(gather_turn(picked_low, n_ep))
    small_rows = jnp.swapaxes(by_block(small_all), 0, 1).reshape(16 + expert_count, width)
    gains = small_rows[:4].astype(F32)
    full_router = small_rows[16:]

    x_rows = tokens[0].astype(F32)
    x_scale = lax.rsqrt(jnp.mean(x_rows * x_rows, axis=-1, keepdims=True) + EPS)
    h_low = (x_rows * x_scale * gains[0][None, :]).astype(BF16)
    h_all = lax.all_gather(h_low, "sp", axis=0, tiled=True)

    upper = (
        jnp.arange(tok_dev, dtype=jnp.int32)[:, None] < jnp.arange(tok_dev, dtype=jnp.int32)[None, :]
    ).astype(BF16)
    picked_mine = lax.dynamic_slice_in_dim(picked_all, ep_index * local, local, 1)
    picked_mine = picked_mine.reshape(n_ep * local, tok_dev)
    earlier = product(picked_mine, upper).astype(jnp.int32)
    places = jnp.where((picked_mine > 0) & (earlier < capacity), earlier, -1)
    picked_flat = picked_all.reshape(n_ep * expert_count, tok_dev).astype(F32)

    positions = jnp.arange(total, dtype=jnp.int32)
    lengths = doc_lengths[0]
    doc_ends = jnp.cumsum(lengths)
    starts = jnp.sum(
        jnp.where(doc_ends[None, :] <= positions[:, None], lengths[None, :], 0), axis=1
    )
    half = HEAD_DIM // 2
    frequency = THETA ** (-(2.0 * jnp.arange(half, dtype=F32)) / HEAD_DIM)
    angles = (positions - starts).astype(F32)[:, None] * frequency[None, :]
    cosine = jnp.concatenate([jnp.cos(angles), jnp.cos(angles)], axis=1)
    sine = jnp.concatenate([-jnp.sin(angles), jnp.sin(angles)], axis=1)
    starts = starts[:, None].astype(jnp.int32)

    vo_own = jnp.concatenate([own_columns(w_value), own_columns(w_out)], axis=1)
    *qk_pieces, vo_own = tie(*qk_pieces, vo_own)
    vo_pieces = gather_turn(vo_own, n_ep)
    *vo_pieces, cot_own = tie(*vo_pieces, cotangent[0])
    cot_pieces = gather_turn(cot_own, n_ep)

    q_raw, k_raw, squares, w_qk = qk_project(ids, h_all, qk_pieces)
    scales = lax.rsqrt(sum_sp(squares) / width + EPS)
    v_low, w_v, w_o = v_project(ids, h_all, vo_pieces)
    w_o_parts = gather_sp(w_o)
    gain_q, gain_k = own_columns(gains)[1:2], own_columns(gains)[2:3]
    q_rot, k_rot, mixed = attend(
        q_raw, k_raw, v_low, scales, gain_q, gain_k, cosine, sine, starts
    )
    attn_tok = lax.all_to_all(mixed, "sp", split_axis=0, concat_axis=1, tiled=True)
    x_one, h2_low = out_project(ids, n_ep, attn_tok, tokens[0], gains[3:4], w_o_parts)
    attn_all = lax.all_gather(attn_tok, "sp", axis=0, tiled=True)

    def pair_places(p):
        return places[p * local : (p + 2) * local]

    h2_pieces = gather_line(h2_low, n_ep)
    groups = []
    home_gates = None
    for g in range(0, n_ep, group):
        rows = gates = d_rows = None
        for at, p in enumerate(range(g, g + group, 2)):
            (d_rows,) = dispatch(
                mine, cot_pieces[p : p + 2], pair_places(p), None, None, local, cap, group, at,
                d_rows, None,
            )
        for at, p in enumerate(range(g, g + group, 2)):
            rows, gates, piece_gates = dispatch(
                mine, h2_pieces[p : p + 2], pair_places(p),
                picked_flat[p * expert_count : (p + 2) * expert_count], full_router, local, cap,
                group, at, rows, gates,
            )
            if p == 0:
                home_gates = piece_gates
        groups.append((rows, d_rows, experts(rows, d_rows, gates, w_gate, w_up, w_down)))

    d_pieces, d_gates = [], []
    for g, (_, _, made) in enumerate(groups):
        for at in range(group // 2):
            p = g * group + 2 * at
            *two, dots = combine(pair_places(p), made[5], 2, local, cap, at, made[3])
            d_pieces += two
            d_gates.append(dots)
    d_h2 = scatter_line(d_pieces, n_ep)
    d_gates = by_block(jnp.concatenate(d_gates, axis=0).reshape(n_ep, local, tok_dev))
    d_gates = lax.all_to_all(d_gates, "ep", split_axis=0, concat_axis=0, tiled=True)
    d_gates = d_gates.reshape(expert_count, tok_dev)

    acts = [made[0] for _, _, made in groups]
    d_gate_rows = [made[1] for _, _, made in groups]
    d_up_rows = [made[2] for _, _, made in groups]
    ins = [rows for rows, _, _ in groups]
    outs = [d_rows for _, d_rows, _ in groups]
    grad_down = weight_grad(acts, outs)
    grad_gate = weight_grad(ins, d_gate_rows)
    grad_up = weight_grad(ins, d_up_rows)
    d_h2, grad_down, grad_gate, grad_up = tie(d_h2, grad_down, grad_gate, grad_up)

    def over_sp(value):
        return lax.psum_scatter(value, "sp", scatter_dimension=1, tiled=True).astype(F32)

    grad_down, grad_gate, grad_up = over_sp(grad_down), over_sp(grad_gate), over_sp(grad_up)

    if n_ep == 8:
        gates_here = home_gates[:expert_count]
    else:
        logits = product_right(full_router, h2_low)
        logits = jnp.where(picked.T, logits, NEG_FILL)
        gates_here = jax.nn.softmax(logits, axis=0)
    d_logits = gates_here * (d_gates - jnp.sum(gates_here * d_gates, axis=0, keepdims=True))
    d_logits = jnp.where(picked.T, d_logits, 0.0).astype(BF16)
    grad_router = product(d_logits, h2_low)
    d_h2 = d_h2 + product_left(d_logits, full_router)
    one_scale = lax.rsqrt(jnp.mean(x_one * x_one, axis=-1, keepdims=True) + EPS)
    one_normed = x_one * one_scale
    grad_ffn = jnp.sum(d_h2 * one_normed, axis=0)
    d_normed = d_h2 * gains[3][None, :]
    d_one = cotangent[0].astype(F32) + one_scale * (
        d_normed - one_normed * jnp.mean(d_normed * one_normed, axis=-1, keepdims=True)
    )
    d_z = d_one.astype(BF16)
    d_attn = out_back(ids, n_ep, d_z, w_o_parts)
    d_heads = lax.all_to_all(d_attn, "sp", split_axis=1, concat_axis=0, tiled=True)
    d_z_cols = lax.all_to_all(d_z, "sp", split_axis=1, concat_axis=0, tiled=True)
    out_grads = grad_pieces(ids, n_ep, attn_all, d_z_cols, "out_grads")

    mix_pieces = []
    for g, (_, _, made) in enumerate(groups):
        for at in range(group // 2):
            mix_pieces += combine(pair_places(g * group + 2 * at), made[4], 2, local, cap, at)
    if shard == tok_dev:
        sent = [jnp.concatenate(two, axis=1) for two in zip(mix_pieces, out_grads)]
        got = scatter_turn(sent, n_ep)
        mix, grad_out = got[:, :width], got[:, width:].astype(BF16)
    else:
        mix = scatter_turn(mix_pieces, n_ep)
        grad_out = scatter_turn(out_grads, n_ep).astype(BF16)
    output = (x_one + mix).astype(BF16)

    d_qn, d_kn, d_v, sums, grad_qg, grad_kg = attend_back(
        q_rot, k_rot, v_low, d_heads, q_raw, k_raw, scales, gain_q, gain_k, cosine, sine, starts
    )

    def placed(value):
        return lax.dynamic_update_slice_in_dim(
            jnp.zeros((1, width), F32), value, sp_index * head_width, 1
        )

    tiny = jnp.concatenate(
        [placed(grad_qg), placed(grad_kg), grad_ffn[None], grad_router], axis=0
    )
    *qkv_pieces, d_qkv = qkv_back(
        ids, n_ep, h_all, d_qn, d_kn, d_v, q_raw, k_raw, scales, sum_sp(sums), tiny
    )
    grad_qkv = scatter_line(qkv_pieces, n_ep).astype(BF16)

    d_h = d_h_rows(d_qkv, w_qk, w_v).reshape(n_sp, tok_dev, width)
    parts = [
        lax.dynamic_index_in_dim(d_h, partners[j], 0, keepdims=False) for j in range(4)
    ]
    kept = plus(parts[0], swap_sp(parts[1], 1))
    sent = plus(parts[2], swap_sp(parts[3], 1))
    d_h = kept.astype(F32) + swap_sp(sent, 2).astype(F32)
    x_normed = x_rows * x_scale
    d_normed = d_h * gains[0][None, :]
    input_grad = d_one + x_scale * (
        d_normed - x_normed * jnp.mean(d_normed * x_normed, axis=-1, keepdims=True)
    )

    g_query, g_key, g_value, tiny, g_attn = finish(
        ids, n_ep, w_query, w_key, w_value, attn_gain.astype(F32)[:, None], gather_sp(grad_qkv)
    )
    out_parts = gather_sp(grad_out)
    g_out = jnp.concatenate(
        [
            lax.dynamic_index_in_dim(jnp.stack(out_parts), partners[j], 0, keepdims=False)
            for j in range(4)
        ],
        axis=1,
    ).astype(F32)
    per_row = 3 * head_width // shard

    def vector(at):
        col = (at % per_row) * shard
        return tiny[at // per_row, col : col + shard]

    g_router = jnp.stack([vector(3 + i) for i in range(expert_count)], axis=1)
    return (
        output[None], input_grad[None], g_attn[:, 0], g_query, g_key, g_value, vector(0), vector(1),
        g_out, vector(2), g_router, grad_gate, grad_up, grad_down,
    )


def solution(mesh):
    seq = P("ep", "sp", None)
    vec = P("ep")
    mat = P("ep", None)
    expert = P("ep", None, None)
    in_specs = (
        seq, mat, seq, vec, mat, mat, mat, vec, vec, mat, vec, mat, expert, expert, expert, seq,
    )
    out_specs = (
        seq, seq, vec, mat, mat, mat, vec, vec, mat, vec, mat, seq, seq, seq,
    )
    return jax.shard_map(body, mesh=mesh, in_specs=in_specs, out_specs=out_specs, check_vma=False)
```

```python
import functools

import jax
import jax.numpy as jnp
from jax import lax
from jax.experimental import pallas as pl
from jax.experimental.pallas import tpu as pltpu
from jax.sharding import PartitionSpec as P

HEAD_DIM = 128
EPS = 1e-05
THETA = 10000.0
NEG_FILL = -1e30
F32 = jnp.float32
BF16 = jnp.bfloat16
MIB = 1 << 20
COVER = 20


def product(left, right):
    return jnp.dot(left, right, preferred_element_type=F32)


def product_left(left, right):
    return lax.dot_general(left, right, (((0,), (0,)), ((), ())), preferred_element_type=F32)


def product_right(left, right):
    return lax.dot_general(left, right, (((1,), (1,)), ((), ())), preferred_element_type=F32)


def row_sums(values_in):
    sums = jnp.sum(values_in, axis=1, keepdims=True)
    return jnp.transpose(jnp.broadcast_to(sums, (sums.shape[0], HEAD_DIM)))[:8]


def call(kernel, out_shape, args, flops, name, scratch=(), scalars=(), grid=(1,), in_specs=None,
         out_specs=None, aliases=None, vmem=60, after=()):
    single = not isinstance(out_shape, (list, tuple))
    shapes = [out_shape] if single else list(out_shape)
    count = len(grid)

    def fixed(shape):
        rank = len(shape)
        return pl.BlockSpec(tuple(shape), lambda *ids: (0,) * rank)

    in_specs = in_specs or [None] * len(args)
    out_specs = out_specs or [None] * len(shapes)
    in_specs = [s if s is not None else fixed(a.shape) for s, a in zip(in_specs, args)]
    out_specs = [s if s is not None else fixed(o.shape) for s, o in zip(out_specs, shapes)]
    waited = len(after)
    args = [*args, *after]
    in_specs = in_specs + [pl.BlockSpec(memory_space=pl.ANY)] * waited
    if waited:
        inner, first = kernel, len(scalars) + len(args) - waited

        def kernel(*refs):
            inner(*refs[:first], *refs[first + waited :])

    moved = sum(a.size * a.dtype.itemsize for a in args[: len(args) - waited])
    moved += sum(o.size * o.dtype.itemsize for o in shapes)
    result = pl.pallas_call(
        kernel,
        grid_spec=pltpu.PrefetchScalarGridSpec(
            num_scalar_prefetch=len(scalars), grid=grid, in_specs=in_specs, out_specs=out_specs,
            scratch_shapes=list(scratch),
        ),
        out_shape=shapes,
        input_output_aliases={k + len(scalars): v for k, v in (aliases or {}).items()},
        compiler_params=pltpu.CompilerParams(
            vmem_limit_bytes=vmem * MIB, dimension_semantics=("arbitrary",) * count
        ),
        cost_estimate=pl.CostEstimate(flops=int(COVER * flops), bytes_accessed=int(moved), transcendentals=0),
        name=name,
    )(*scalars, *args)
    return result[0] if single else result


def like(shape, dtype):
    return jax.ShapeDtypeStruct(tuple(shape), dtype)


MIDDLE = [(2, 4), (3, 5), (4, 2), (5, 3)]
OUTWARD = [(2, 0), (3, 1), (4, 6), (5, 7)]
INWARD = [(0, 2), (1, 3), (6, 4), (7, 5)]


def tie(*values):
    return lax.optimization_barrier(values)


def shift(value, pairs):
    return lax.ppermute(value, "ep", pairs)


def swap(value, bits):
    return shift(value, [(i, i ^ bits) for i in range(8)])


def swap_sp(value, bits):
    return lax.ppermute(value, "sp", [(i, i ^ bits) for i in range(4)])


def piece_blocks(n_ep, ep_index):
    ids = jnp.arange(n_ep, dtype=jnp.int32)
    return jnp.bitwise_xor(ids, ep_index) if n_ep == 8 else ids


def gather_line(value, n_ep, gate=()):
    if n_ep != 8:
        return gather_turn(value, n_ep)
    near = swap(value, 2)
    inner_a = shift(value, MIDDLE)
    inner_b = shift(near, MIDDLE)
    third = inner_b + shift(inner_a, OUTWARD)
    fourth = inner_a + shift(inner_b, OUTWARD)
    crossed = value
    if gate:
        crossed = tie(value, *gate)[0]
    pieces = [value, swap(crossed, 1)]
    for own in (near, third, fourth):
        pieces += [own, swap(own, 1)]
    return pieces


def gather_turn(value, n_ep):
    if n_ep != 8:
        whole = lax.all_gather(value, "ep", axis=0, tiled=False)
        return [whole[i] for i in range(n_ep)]
    pieces = []
    for own in (value, swap(value, 2), swap(value, 4), swap(value, 6)):
        pieces += [own, swap(own, 1)]
    return pieces


def plus(left, right):
    return (left.astype(F32) + right.astype(F32)).astype(left.dtype)


def crossed_sums(pieces):
    return [plus(pieces[i], swap(pieces[i + 1], 1)) for i in range(0, len(pieces), 2)]


def scatter_line(own, near, third, fourth):
    third_in, fourth_in = shift(fourth, INWARD), shift(third, INWARD)
    third, fourth = plus(third, third_in), plus(fourth, fourth_in)
    near = plus(near, shift(third, MIDDLE))
    total = own.astype(F32) + shift(fourth, MIDDLE).astype(F32) + swap(near, 2).astype(F32)
    return total, [third, fourth]


def turned_sum(sums):
    total = sums[0].astype(F32)
    for i in range(1, 4):
        total = total + swap(sums[i], 2 * i).astype(F32)
    return total


def scatter_turn(pieces, n_ep):
    if n_ep != 8:
        stacked = jnp.stack(pieces)
        return lax.psum_scatter(stacked, "ep", scatter_dimension=0, tiled=False).astype(F32)
    return turned_sum(crossed_sums(pieces))


def gather_sp(value):
    over = swap_sp(value, 2)
    return [value, swap_sp(value, 1), over, swap_sp(over, 1)]


def sum_sp(value):
    value = value + swap_sp(value, 1)
    return value + swap_sp(value, 2)


def block_at(ids, position, size):
    if size % HEAD_DIM:
        return pl.ds(position * size, size)
    return pl.ds(pl.multiple_of(ids[position] * size, size), size)


def qk_kernel(count, ids, h_ref, *refs):
    pieces, (q_ref, k_ref, squares_ref, w_ref) = refs[:count], refs[count:]
    shard = pieces[0].shape[0]

    @pl.when(pl.program_id(0) == 0)
    def _():
        for k in range(count):
            w_ref[block_at(ids, k, shard), :] = pieces[k][...]

    width = q_ref.shape[1]
    for at, ref in enumerate((q_ref, k_ref)):
        part = product(h_ref[...], w_ref[:, at * width : (at + 1) * width])
        ref[...] = part
        squares_ref[8 * at : 8 * at + 8, :] = row_sums(part * part)


def qk_project(ids, h_all, pieces):
    total, depth = h_all.shape
    shard, both = pieces[0].shape
    width = both // 2
    rows = min(256, total)
    block = pl.BlockSpec((rows, width), lambda i, ids: (i, 0))
    return call(
        functools.partial(qk_kernel, len(pieces)),
        [like((total, width), F32)] * 2 + [like((16, total), F32), like((depth, both), BF16)],
        [h_all, *pieces],
        2 * total * depth * both,
        "qk_project",
        scalars=(ids,),
        grid=(total // rows,),
        in_specs=[pl.BlockSpec((rows, depth), lambda i, ids: (i, 0))] + [None] * len(pieces),
        out_specs=[block, block, pl.BlockSpec((16, rows), lambda i, ids: (0, i)), None],
    )


def v_kernel(count, ids, h_ref, *refs):
    pieces, (v_ref, w_ref, out_ref) = refs[:count], refs[count:]
    shard = pieces[0].shape[0]
    width = v_ref.shape[1]

    @pl.when(pl.program_id(0) == 0)
    def _():
        for k in range(count):
            rows = block_at(ids, k, shard)
            w_ref[rows, :] = pieces[k][:, :width]
            out_ref[rows, :] = pieces[k][:, width:]

    v_ref[...] = product(h_ref[...], w_ref[...]).astype(BF16)


def v_project(ids, h_all, pieces, after):
    total, depth = h_all.shape
    width = pieces[0].shape[1] // 2
    rows = min(256, total)
    return call(
        functools.partial(v_kernel, len(pieces)),
        [like((total, width), BF16), like((depth, width), BF16), like((depth, width), BF16)],
        [h_all, *pieces],
        2 * total * depth * width,
        "v_project",
        after=after,
        scalars=(ids,),
        grid=(total // rows,),
        in_specs=[pl.BlockSpec((rows, depth), lambda i, ids: (i, 0))] + [None] * len(pieces),
        out_specs=[pl.BlockSpec((rows, width), lambda i, ids: (i, 0)), None, None],
    )


def out_kernel(n_ep, ids, attn_ref, x_ref, gain_ref, *refs):
    weights, (one_ref, low_ref) = refs[:-2], refs[-2:]
    width = weights[0].shape[1]
    for j, weight in enumerate(weights):
        cols = block_at(ids, n_ep + j, width)
        one_ref[:, cols] = x_ref[:, cols].astype(F32) + product(attn_ref[...], weight[...])
    one = one_ref[...]
    scale = lax.rsqrt(jnp.mean(one * one, axis=1, keepdims=True) + EPS)
    low_ref[...] = (one * scale * gain_ref[...]).astype(BF16)


def out_project(ids, n_ep, attn_tok, tokens, gain, weights, after):
    return call(
        functools.partial(out_kernel, n_ep),
        [like(tokens.shape, F32), like(tokens.shape, BF16)],
        [attn_tok, tokens, gain, *weights],
        2 * tokens.size * attn_tok.shape[1],
        "out_project",
        after=after,
        scalars=(ids,),
    )


def out_back_kernel(n_ep, ids, d_ref, *refs):
    weights, d_attn_ref = refs[:-1], refs[-1]
    width = weights[0].shape[1]
    total = None
    for j, weight in enumerate(weights):
        part = product_right(d_ref[:, block_at(ids, n_ep + j, width)], weight[...])
        total = part if total is None else total + part
    d_attn_ref[...] = total.astype(BF16)


def out_back(ids, n_ep, d_z, weights, after):
    return call(
        functools.partial(out_back_kernel, n_ep),
        like((d_z.shape[0], weights[0].shape[0]), BF16),
        [d_z, *weights],
        2 * d_z.size * weights[0].shape[0],
        "out_back",
        after=after,
        scalars=(ids,),
    )


def vo_grads_kernel(count, ids, h_ref, dv_ref, attn_ref, dz_ref, *pieces):
    shard = pieces[0].shape[0]
    width = dv_ref.shape[1]
    for k in range(count):
        block = block_at(ids, k, shard)
        pieces[k][:, :width] = product_left(h_ref[:, block], dv_ref[...]).astype(BF16)
        pieces[k][:, width:] = product_left(attn_ref[:, block], dz_ref[...]).astype(BF16)


def vo_grads(ids, count, h_all, d_v, attn_all, d_z_cols):
    shard = h_all.shape[1] // count
    width = d_v.shape[1]
    return call(
        functools.partial(vo_grads_kernel, count),
        [like((shard, 2 * width), BF16)] * count,
        [h_all, d_v, attn_all, d_z_cols],
        4 * h_all.size * width,
        "vo_grads",
        scalars=(ids,),
    )


def qk_back_kernel(
    count, width_all, ids, h_ref, dqn_ref, dkn_ref, qr_ref, kr_ref, scale_ref, sums_ref,
    tiny_ref, *refs
):
    pieces, d_ref = refs[:count], refs[count]
    width = dqn_ref.shape[1]
    scales = jnp.transpose(scale_ref[...])
    means = jnp.transpose(sums_ref[...]) * (1.0 / width_all)
    for at, (d_normed, raw) in enumerate(((dqn_ref, qr_ref), (dkn_ref, kr_ref))):
        scale, mean = scales[:, 8 * at : 8 * at + 1], means[:, 8 * at : 8 * at + 1]
        d_ref[:, at * width : (at + 1) * width] = (
            scale * (d_normed[...] - raw[...] * scale * mean)
        ).astype(BF16)
    shard = h_ref.shape[1] // count
    per_row = 2 * width // shard
    for k in range(count):
        block = block_at(ids, k, shard)
        pieces[k][:shard, :] = product_left(h_ref[:, block], d_ref[...]).astype(BF16)
        pieces[k][shard:, :] = jnp.zeros_like(pieces[k][shard:, :])
        for at in range(tiny_ref.shape[0]):
            row, col = shard + at // per_row, (at % per_row) * shard
            pieces[k][row : row + 1, col : col + shard] = tiny_ref[at : at + 1, block].astype(BF16)


def qk_back(ids, count, h_all, d_qn, d_kn, q_raw, k_raw, scales, sums, tiny, after):
    total, depth = h_all.shape
    width = d_qn.shape[1]
    shard = depth // count
    extra = -(-tiny.shape[0] // (2 * width // shard))
    extra = -(-extra // 16) * 16
    return call(
        functools.partial(qk_back_kernel, count, depth),
        [like((shard + extra, 2 * width), BF16)] * count + [like((total, 2 * width), BF16)],
        [h_all, d_qn, d_kn, q_raw, k_raw, scales, sums, tiny],
        2 * h_all.size * 2 * width,
        "qk_back",
        scalars=(ids,),
        after=after,
    )


def d_h_kernel(d_ref, dv_ref, qk_ref, v_ref, out_ref):
    out_ref[...] = (
        product_right(d_ref[...], qk_ref[...]) + product_right(dv_ref[...], v_ref[...])
    ).astype(BF16)


def d_h_rows(d_qk, d_v, w_qk, w_v):
    total, wide = d_qk.shape
    depth = w_qk.shape[0]
    rows = min(256, total)
    return call(
        d_h_kernel,
        like((total, depth), BF16),
        [d_qk, d_v, w_qk, w_v],
        3 * d_qk.size * depth,
        "d_h",
        grid=(total // rows,),
        in_specs=[
            pl.BlockSpec((rows, wide), lambda i: (i, 0)),
            pl.BlockSpec((rows, d_v.shape[1]), lambda i: (i, 0)), None, None,
        ],
        out_specs=[pl.BlockSpec((rows, depth), lambda i: (i, 0))],
    )


def finish_kernel(n_ep, n_sp, ids, wq_ref, wk_ref, wv_ref, gain_ref, *refs):
    firsts, seconds = refs[:n_sp], refs[n_sp : 2 * n_sp]
    gq_ref, gk_ref, gv_ref, go_ref, tiny_ref, attn_ref = refs[2 * n_sp :]
    shard = wq_ref.shape[0]
    width = firsts[0].shape[1] // 2
    dots = jnp.zeros((shard, 1), F32)
    tiny = jnp.zeros(tiny_ref.shape, F32)
    for j in range(n_sp):
        cols = block_at(ids, n_ep + j, width)
        for at, grad, weight in ((0, gq_ref, wq_ref), (1, gk_ref, wk_ref), (2, gv_ref, wv_ref)):
            part = firsts[j][:shard, at * width : (at + 1) * width] if at < 2 else seconds[j][:, :width]
            value = part.astype(F32)
            grad[:, cols] = value
            dots += jnp.sum(value * weight[:, cols].astype(F32), axis=1, keepdims=True)
        go_ref[:, cols] = seconds[j][:, width:].astype(F32)
        tiny += firsts[j][shard:, :].astype(F32)
    tiny_ref[...] = tiny
    attn_ref[...] = dots / gain_ref[...]


def finish(ids, n_ep, w_query, w_key, w_value, gain, firsts, seconds):
    shard, depth = w_query.shape
    extra = firsts[0].shape[0] - shard
    return call(
        functools.partial(finish_kernel, n_ep, len(firsts)),
        [like((shard, depth), F32)] * 4 + [like((extra, firsts[0].shape[1]), F32), like((shard, 1), F32)],
        [w_query, w_key, w_value, gain, *firsts, *seconds],
        shard * depth * 6,
        "finish",
        scalars=(ids,),
    )


def turn(values_in):
    return pltpu.roll(values_in, HEAD_DIM // 2, 1)


def masked_probs(q_ref, k_ref, start_ref, block, rows):
    first, last = block * rows, (block + 1) * rows
    scores = product_right(q_ref[first:last, :], k_ref[0:last, :]) * (HEAD_DIM ** (-0.5))
    row_ids = first + lax.broadcasted_iota(jnp.int32, scores.shape, 0)
    places = lax.broadcasted_iota(jnp.int32, scores.shape, 1)
    allowed = (places <= row_ids) & (places >= start_ref[first:last, :])
    scores = jnp.where(allowed, scores, NEG_FILL)
    top = jnp.max(scores, axis=1, keepdims=True)
    weights = jnp.exp(scores - top)
    return weights * (1.0 / jnp.sum(weights, axis=1, keepdims=True))


def attend_kernel(
    rows, qr_ref, kr_ref, v_ref, scale_ref, gq_ref, gk_ref, cos_ref, sin_ref, start_ref,
    q_ref, k_ref, out_ref,
):
    scales = jnp.transpose(scale_ref[...])
    for at, (raw, gain, low) in enumerate(((qr_ref, gq_ref, q_ref), (kr_ref, gk_ref, k_ref))):
        normed = raw[...] * scales[:, 8 * at : 8 * at + 1] * gain[...]
        low[...] = (normed * cos_ref[...] + turn(normed) * sin_ref[...]).astype(BF16)
    for block in range(q_ref.shape[0] // rows):
        probs = masked_probs(q_ref, k_ref, start_ref, block, rows)
        last = (block + 1) * rows
        out_ref[block * rows : last, :] = product(
            probs.astype(BF16), v_ref[0:last, :]
        ).astype(BF16)


def head_spec(rows):
    return pl.BlockSpec((rows, HEAD_DIM), lambda h: (0, h))


def attend(q_raw, k_raw, v_low, scales, q_gain, k_gain, cosine, sine, starts):
    total, width = v_low.shape
    heads = width // HEAD_DIM
    head, gain = head_spec(total), head_spec(1)
    return call(
        functools.partial(attend_kernel, min(256, total)),
        [like((total, width), BF16)] * 3,
        [q_raw, k_raw, v_low, scales, q_gain, k_gain, cosine, sine, starts],
        3 * heads * total * total * HEAD_DIM,
        "attend",
        grid=(heads,),
        in_specs=[head, head, head, None, gain, gain, None, None, None],
        out_specs=[head, head, head],
    )


def attend_back_kernel(
    rows, q_ref, k_ref, v_ref, do_ref, qr_ref, kr_ref, scale_ref, gq_ref, gk_ref,
    cos_ref, sin_ref, start_ref,
    dq_ref, dk_ref, dv_ref, sums_ref, dgq_ref, dgk_ref, q_acc, k_acc, v_acc,
):
    k_acc[...] = jnp.zeros_like(k_acc)
    v_acc[...] = jnp.zeros_like(v_acc)
    for block in range(q_ref.shape[0] // rows):
        first, last = block * rows, (block + 1) * rows
        probs = masked_probs(q_ref, k_ref, start_ref, block, rows)
        d_rows = do_ref[first:last, :]
        d_probs = product_right(d_rows, v_ref[0:last, :])
        delta = jnp.sum(probs * d_probs, axis=1, keepdims=True)
        d_scores = (probs * (d_probs - delta) * (HEAD_DIM ** (-0.5))).astype(BF16)
        q_acc[first:last, :] = product(d_scores, k_ref[0:last, :])
        k_acc[0:last, :] += product_left(d_scores, q_ref[first:last, :])
        v_acc[0:last, :] += product_left(probs.astype(BF16), d_rows)
    dv_ref[...] = v_acc[...].astype(BF16)

    @pl.when(pl.program_id(0) == 0)
    def _():
        sums_ref[...] = jnp.zeros_like(sums_ref)

    scales = jnp.transpose(scale_ref[...])
    for at, (acc, raw, gain, d_ref, dg_ref) in enumerate(
        ((q_acc, qr_ref, gq_ref, dq_ref, dgq_ref), (k_acc, kr_ref, gk_ref, dk_ref, dgk_ref))
    ):
        turned = acc[...].astype(BF16).astype(F32)
        back = turned * cos_ref[...] + turn(turned * sin_ref[...])
        normed = raw[...] * scales[:, 8 * at : 8 * at + 1]
        both = back * normed
        dg_ref[...] = jnp.sum(both, axis=0, keepdims=True)
        d_ref[...] = back * gain[...]
        sums_ref[8 * at : 8 * at + 8, :] += row_sums(both * gain[...])


def attend_back(
    q_rot, k_rot, v_low, d_heads, q_raw, k_raw, scales, q_gain, k_gain, cosine, sine, starts
):
    total, width = v_low.shape
    heads = width // HEAD_DIM
    head, gain = head_spec(total), head_spec(1)
    wide, thin = like((total, width), F32), like((1, width), F32)
    return call(
        functools.partial(attend_back_kernel, min(256, total)),
        [wide, wide, like((total, width), BF16), like((16, total), F32), thin, thin],
        [q_rot, k_rot, v_low, d_heads, q_raw, k_raw, scales, q_gain, k_gain, cosine, sine, starts],
        7 * heads * total * total * HEAD_DIM,
        "attend_back",
        scratch=[pltpu.VMEM((total, HEAD_DIM), F32)] * 3,
        grid=(heads,),
        in_specs=[head] * 6 + [None, gain, gain, None, None, None],
        out_specs=[head, head, head, None, gain, gain],
    )


def chooser(places_ref, at, cap):
    row = places_ref[at : at + 1, :]
    slots = lax.broadcasted_iota(jnp.int32, (cap, row.shape[1]), 0)
    return slots == row


def dispatch_kernel(
    pieces_here, local, cap, gated, mine, *refs
):
    pieces, refs = refs[:pieces_here], refs[pieces_here:]
    places_ref, refs = refs[0], refs[1:]
    if gated:
        (picked_ref, router_ref), refs = refs[:2], refs[2:]
        rows_ref, gate_ref, all_ref = refs[-3:]
    else:
        rows_ref = refs[-1]
    for p in range(pieces_here):
        if gated:
            logits = product_right(router_ref[...], pieces[p][...])
            experts = logits.shape[0]
            picked = picked_ref[p * experts : (p + 1) * experts, :] > 0
            logits = jnp.where(picked, logits, NEG_FILL)
            weights = jnp.exp(logits - jnp.max(logits, axis=0, keepdims=True))
            weights = jnp.where(picked, weights, 0.0)
            gates = weights / jnp.sum(weights, axis=0, keepdims=True)
            all_ref[p * experts : (p + 1) * experts, :] = gates
        for e in range(local):
            chosen = chooser(places_ref, p * local + e, cap)
            rows_ref[e, p * cap : (p + 1) * cap, :] = product(
                chosen.astype(BF16), pieces[p][...]
            ).astype(BF16)
            if gated:
                row = all_ref[pl.ds(p * experts + mine[0] * local + e, 1), :]
                gate_ref[e, p * cap : (p + 1) * cap, :] = jnp.sum(
                    jnp.where(chosen, row, 0.0), axis=1, keepdims=True
                )


def dispatch(mine, pieces, places, picked, router, local, cap, group, at, rows, gates, after=()):
    gated = router is not None
    here = len(pieces)
    width = pieces[0].shape[1]
    args = [*pieces, places]
    shapes = [like((local, group * cap, width), BF16)]
    spec = pl.BlockSpec((local, here * cap, width), lambda i, mine: (0, at, 0))
    out_specs = [spec]
    if gated:
        args += [picked, router]
        shapes += [like((local, group * cap, 1), F32), like((picked.shape[0], places.shape[1]), F32)]
        out_specs += [pl.BlockSpec((local, here * cap, 1), lambda i, mine: (0, at, 0)), None]
    in_specs = [None] * len(args)
    aliases = {}
    if rows is not None:
        aliases[len(args)] = 0
        args.append(rows)
        in_specs.append(pl.BlockSpec(memory_space=pl.ANY))
        if gated:
            aliases[len(args)] = 1
            args.append(gates)
            in_specs.append(pl.BlockSpec(memory_space=pl.ANY))
    return call(
        functools.partial(dispatch_kernel, here, local, cap, gated),
        shapes,
        args,
        2 * here * local * cap * places.shape[1] * width,
        "dispatch",
        scalars=(mine,),
        in_specs=in_specs,
        out_specs=out_specs,
        aliases=aliases,
        after=after,
    )


def expert_kernel(
    x_ref, d_ref, gate_ref, wg_ref, wu_ref, wd_ref,
    act_ref, dg_ref, du_ref, dots_ref, mix_ref, back_ref, mix_acc, back_acc,
):
    step = pl.program_id(1)
    last = pl.num_programs(1) - 1
    x_rows, d_rows, gate = x_ref[0], d_ref[0], gate_ref[0]
    pre = product(x_rows, wg_ref[0])
    up = product(x_rows, wu_ref[0])
    pulled = product_right(d_rows, wd_ref[0])
    sigma = jax.nn.sigmoid(pre)
    silu = pre * sigma
    act = silu * up
    dots = jnp.sum(act * pulled, axis=1, keepdims=True)
    act_low = (act * gate).astype(BF16)
    act_ref[0] = act_low
    d_act = pulled * gate
    du_low = (d_act * silu).astype(BF16)
    dg_low = (d_act * up * sigma * (1.0 + pre * (1.0 - sigma))).astype(BF16)
    dg_ref[0] = dg_low
    du_ref[0] = du_low
    mix = product(act_low, wd_ref[0])
    back = product_right(dg_low, wg_ref[0]) + product_right(du_low, wu_ref[0])

    @pl.when(step == 0)
    def _():
        dots_ref[0] = dots
        mix_acc[...] = mix
        back_acc[...] = back

    @pl.when((step > 0) & (step < last))
    def _():
        dots_ref[0] += dots
        mix_acc[...] += mix
        back_acc[...] += back

    @pl.when(step == last)
    def _():
        dots_ref[0] += dots
        mix_ref[0] = (mix_acc[...] + mix).astype(BF16)
        back_ref[0] = (back_acc[...] + back).astype(BF16)


def experts(rows, d_rows, gates, w_gate, w_up, w_down, after=()):
    local, count, width = rows.shape
    hidden = w_gate.shape[2]
    part = hidden // 2
    wide = pl.BlockSpec((1, count, width), lambda e, f: (e, 0, 0))
    column = pl.BlockSpec((1, count, 1), lambda e, f: (e, 0, 0))
    thin = pl.BlockSpec((1, count, part), lambda e, f: (e, 0, f))
    into = pl.BlockSpec((1, width, part), lambda e, f: (e, 0, f))
    outof = pl.BlockSpec((1, part, width), lambda e, f: (e, f, 0))
    return call(
        expert_kernel,
        [like((local, count, hidden), BF16)] * 3
        + [like((local, count, 1), F32)]
        + [like((local, count, width), BF16)] * 2,
        [rows, d_rows, gates, w_gate, w_up, w_down],
        12 * rows.size * hidden,
        "experts",
        after=after,
        scratch=[pltpu.VMEM((count, width), F32)] * 2,
        grid=(local, 2),
        in_specs=[wide, wide, column, into, into, outof],
        out_specs=[thin, thin, thin, column, wide, wide],
    )


def combine_kernel(here, local, cap, dotted, places_ref, rows_ref, *refs):
    pieces = refs[int(dotted) : int(dotted) + here]
    for p in range(here):
        chosen = [chooser(places_ref, p * local + e, cap) for e in range(local)]
        total = None
        for e in range(local):
            part = product_left(chosen[e].astype(BF16), rows_ref[e, p * cap : (p + 1) * cap, :])
            total = part if total is None else total + part
            if dotted:
                refs[-1][p * local + e : p * local + e + 1, :] = jnp.sum(
                    jnp.where(chosen[e], refs[0][e, p * cap : (p + 1) * cap, :], 0.0),
                    axis=0, keepdims=True,
                )
        pieces[p][...] = total.astype(BF16)


def combine(places, rows, here, local, cap, at, dots=None, after=()):
    width = rows.shape[2]
    tokens = places.shape[1]
    dotted = dots is not None
    args = [places, rows] + ([dots] if dotted else [])
    in_specs = [None, pl.BlockSpec((local, here * cap, width), lambda i: (0, at, 0))]
    if dotted:
        in_specs.append(pl.BlockSpec((local, here * cap, 1), lambda i: (0, at, 0)))
    shapes = [like((tokens, width), BF16)] * here
    if dotted:
        shapes.append(like(places.shape, F32))
    return call(
        functools.partial(combine_kernel, here, local, cap, dotted),
        shapes,
        args,
        2 * here * local * cap * tokens * width,
        "combine",
        after=after,
        in_specs=in_specs,
    )


def weight_grad_kernel(groups, *refs):
    lefts, rights = refs[:groups], refs[groups : 2 * groups]
    total = None
    for left, right in zip(lefts, rights):
        part = product_left(left[0], right[0])
        total = part if total is None else total + part
    refs[-1][0] = total.astype(BF16)


def weight_grad(lefts, rights, after=()):
    local, count, tall = lefts[0].shape
    wide = rights[0].shape[2]
    part = min(512, tall)
    left = pl.BlockSpec((1, count, part), lambda e, i: (e, 0, i))
    right = pl.BlockSpec((1, count, wide), lambda e, i: (e, 0, 0))
    return call(
        functools.partial(weight_grad_kernel, len(lefts)),
        like((local, tall, wide), BF16),
        [*lefts, *rights],
        2 * len(lefts) * lefts[0].size * wide,
        "weight_grad",
        after=after,
        grid=(local, tall // part),
        in_specs=[left] * len(lefts) + [right] * len(lefts),
        out_specs=[pl.BlockSpec((1, part, wide), lambda e, i: (e, i, 0))],
    )


def body(
    tokens, doc_lengths, routes, attn_gain, w_query, w_key, w_value, q_gain, k_gain, w_out,
    ffn_gain, w_router, w_gate, w_up, w_down, cotangent,
):
    n_sp = lax.axis_size("sp")
    n_ep = lax.axis_size("ep")
    sp_index = lax.axis_index("sp")
    ep_index = lax.axis_index("ep")
    tok_dev, width = tokens.shape[1:]
    total = tok_dev * n_sp
    shard = width // n_ep
    head_width = width // n_sp
    top_count = routes.shape[2]
    local = w_gate.shape[0]
    expert_count = local * n_ep
    capacity = 9 * tok_dev * top_count // (8 * expert_count)
    cap = -(-capacity // 16) * 16
    group = 4
    blocks = piece_blocks(n_ep, ep_index)
    partners = jnp.bitwise_xor(jnp.arange(n_sp, dtype=jnp.int32), sp_index)
    ids = jnp.concatenate([blocks, partners]).astype(jnp.int32)
    mine = ep_index.astype(jnp.int32).reshape(1)

    def own_columns(value):
        return lax.dynamic_slice_in_dim(value, sp_index * head_width, head_width, 1)

    def by_block(value):
        order = jnp.bitwise_xor(jnp.arange(n_ep, dtype=jnp.int32), ep_index) if n_ep == 8 else blocks
        return jnp.stack(
            [lax.dynamic_index_in_dim(value, order[i], 0, keepdims=False) for i in range(n_ep)]
        )

    qk_pieces = gather_turn(
        jnp.concatenate([own_columns(w_query), own_columns(w_key)], axis=1), n_ep
    )

    expert_ids = jnp.arange(expert_count, dtype=jnp.int32)
    picked = jnp.any(routes[0][:, :, None] == expert_ids[None, None, :], axis=1)
    small = jnp.concatenate(
        [
            jnp.stack([attn_gain, q_gain, k_gain, ffn_gain]),
            jnp.zeros((12, shard), BF16),
            w_router.T,
        ],
        axis=0,
    )
    picked_low = picked.T.astype(BF16)
    if shard == tok_dev:
        both = jnp.stack(gather_turn(jnp.concatenate([small, picked_low], axis=0), n_ep))
        small_all, picked_all = both[:, : 16 + expert_count], both[:, 16 + expert_count :]
    else:
        small_all = jnp.stack(gather_turn(small, n_ep))
        picked_all = jnp.stack(gather_turn(picked_low, n_ep))
    small_rows = jnp.swapaxes(by_block(small_all), 0, 1).reshape(16 + expert_count, width)
    gains = small_rows[:4].astype(F32)
    full_router = small_rows[16:]

    x_rows = tokens[0].astype(F32)
    x_scale = lax.rsqrt(jnp.mean(x_rows * x_rows, axis=-1, keepdims=True) + EPS)
    h_low = (x_rows * x_scale * gains[0][None, :]).astype(BF16)
    h_all = lax.all_gather(h_low, "sp", axis=0, tiled=True)

    upper = (
        jnp.arange(tok_dev, dtype=jnp.int32)[:, None] < jnp.arange(tok_dev, dtype=jnp.int32)[None, :]
    ).astype(BF16)
    picked_mine = lax.dynamic_slice_in_dim(picked_all, ep_index * local, local, 1)
    picked_mine = picked_mine.reshape(n_ep * local, tok_dev)
    earlier = product(picked_mine, upper).astype(jnp.int32)
    places = jnp.where((picked_mine > 0) & (earlier < capacity), earlier, -1)
    picked_flat = picked_all.reshape(n_ep * expert_count, tok_dev).astype(F32)

    positions = jnp.arange(total, dtype=jnp.int32)
    lengths = doc_lengths[0]
    doc_ends = jnp.cumsum(lengths)
    starts = jnp.sum(
        jnp.where(doc_ends[None, :] <= positions[:, None], lengths[None, :], 0), axis=1
    )
    half = HEAD_DIM // 2
    frequency = THETA ** (-(2.0 * jnp.arange(half, dtype=F32)) / HEAD_DIM)
    angles = (positions - starts).astype(F32)[:, None] * frequency[None, :]
    cosine = jnp.concatenate([jnp.cos(angles), jnp.cos(angles)], axis=1)
    sine = jnp.concatenate([-jnp.sin(angles), jnp.sin(angles)], axis=1)
    starts = starts[:, None].astype(jnp.int32)

    vo_own = jnp.concatenate([own_columns(w_value), own_columns(w_out)], axis=1)
    qk_pieces[-1], vo_own = tie(qk_pieces[-1], vo_own)
    vo_pieces = gather_turn(vo_own, n_ep)
    vo_pieces[-1], cot_own = tie(vo_pieces[-1], cotangent[0])
    cot_pieces = gather_turn(cot_own, n_ep)

    q_raw, k_raw, squares, w_qk = qk_project(ids, h_all, qk_pieces)
    scales = lax.rsqrt(sum_sp(squares) / width + EPS)
    v_low, w_v, w_o = v_project(ids, h_all, vo_pieces, [q_raw])
    w_o_parts = gather_sp(w_o)
    gain_q, gain_k = own_columns(gains)[1:2], own_columns(gains)[2:3]
    q_rot, k_rot, mixed = attend(
        q_raw, k_raw, v_low, scales, gain_q, gain_k, cosine, sine, starts
    )

    def pair_places(p):
        return places[p * local : (p + 2) * local]

    def cot_rows(g, after):
        d_rows = None
        for at, p in enumerate(range(g, g + group, 2)):
            (d_rows,) = dispatch(
                mine, cot_pieces[p : p + 2], pair_places(p), None, None, local, cap, group, at,
                d_rows, None, after,
            )
        return d_rows

    attn_tok = lax.all_to_all(mixed, "sp", split_axis=0, concat_axis=1, tiled=True)
    near_rows = cot_rows(0, [mixed])
    x_one, h2_low = out_project(
        ids, n_ep, attn_tok, tokens[0], gains[3:4], w_o_parts, [near_rows]
    )
    attn_all = lax.all_gather(attn_tok, "sp", axis=0, tiled=True)

    h2_pieces = gather_line(h2_low, n_ep, cot_pieces[-1:])
    cots = [near_rows] + [cot_rows(g, [x_one]) for g in range(group, n_ep, group)]
    groups, d_pieces, d_gates, d_sums = [], [], [], []
    home_gates = None

    def rows_of(g, after):
        rows = gates = first_gates = None
        for at, p in enumerate(range(g, g + group, 2)):
            rows, gates, piece_gates = dispatch(
                mine, h2_pieces[p : p + 2], pair_places(p),
                picked_flat[p * expert_count : (p + 2) * expert_count], full_router, local, cap,
                group, at, rows, gates, after,
            )
            first_gates = piece_gates if first_gates is None else first_gates
        return rows, gates, first_gates

    rows, gates, home_gates = rows_of(0, [])
    for g in range(0, n_ep, group):
        d_rows = cots[g // group]
        made = experts(rows, d_rows, gates, w_gate, w_up, w_down, d_pieces[-group:] + cots)
        groups.append((rows, d_rows, made))
        following = []
        if g + group < n_ep:
            rows, gates, _ = rows_of(g + group, [made[5]])
            following = [rows]
        sums_before = list(d_sums)
        for at in range(group // 2):
            *two, dots = combine(
                pair_places(g + 2 * at), made[5], 2, local, cap, at, made[3],
                sums_before + following,
            )
            d_pieces += two
            d_gates.append(dots)
        if n_ep == 8:
            d_sums += crossed_sums(d_pieces[-group:])

    acts = [made[0] for _, _, made in groups]
    d_gate_rows = [made[1] for _, _, made in groups]
    d_up_rows = [made[2] for _, _, made in groups]
    ins = [rows for rows, _, _ in groups]
    outs = [d_rows for _, d_rows, _ in groups]
    if n_ep == 8:
        d_h2, inside = scatter_line(*d_sums)
    else:
        d_h2, inside = scatter_turn(d_pieces, n_ep), []
    grad_down = weight_grad(acts, outs)
    grad_gate = weight_grad(ins, d_gate_rows)
    grad_up = weight_grad(ins, d_up_rows, [*d_sums, grad_down, grad_gate])

    def over_sp(value):
        return lax.psum_scatter(value, "sp", scatter_dimension=1, tiled=True).astype(F32)

    d_gates = by_block(jnp.concatenate(d_gates, axis=0).reshape(n_ep, local, tok_dev))
    d_gates = lax.all_to_all(d_gates, "ep", split_axis=0, concat_axis=0, tiled=True)
    d_gates = d_gates.reshape(expert_count, tok_dev)

    mix_pieces = []
    for g, (_, _, made) in enumerate(groups):
        for at in range(group // 2):
            mix_pieces += combine(
                pair_places(g * group + 2 * at), made[4], 2, local, cap, at, None,
                [grad_up, *inside],
            )

    if n_ep == 8:
        gates_here = home_gates[:expert_count]
    else:
        logits = product_right(full_router, h2_low)
        logits = jnp.where(picked.T, logits, NEG_FILL)
        gates_here = jax.nn.softmax(logits, axis=0)
    d_logits = gates_here * (d_gates - jnp.sum(gates_here * d_gates, axis=0, keepdims=True))
    d_logits = jnp.where(picked.T, d_logits, 0.0).astype(BF16)
    grad_router = product(d_logits, h2_low)
    d_h2 = d_h2 + product_left(d_logits, full_router)
    one_scale = lax.rsqrt(jnp.mean(x_one * x_one, axis=-1, keepdims=True) + EPS)
    one_normed = x_one * one_scale
    grad_ffn = jnp.sum(d_h2 * one_normed, axis=0)
    d_normed = d_h2 * gains[3][None, :]
    d_one = cotangent[0].astype(F32) + one_scale * (
        d_normed - one_normed * jnp.mean(d_normed * one_normed, axis=-1, keepdims=True)
    )
    d_z = d_one.astype(BF16)
    d_attn = out_back(ids, n_ep, d_z, w_o_parts, [grad_up, grad_gate, grad_down, *mix_pieces])
    d_heads = lax.all_to_all(d_attn, "sp", split_axis=1, concat_axis=0, tiled=True)
    d_z_cols = lax.all_to_all(d_z, "sp", split_axis=1, concat_axis=0, tiled=True)
    if n_ep == 8:
        mix_sums = crossed_sums(mix_pieces)
        mix_sums[0], mix_sums[1], d_heads = tie(mix_sums[0], mix_sums[1], d_heads)
    grad_down, grad_gate, grad_up = over_sp(grad_down), over_sp(grad_gate), over_sp(grad_up)

    d_qn, d_kn, d_v, sums, grad_qg, grad_kg = attend_back(
        q_rot, k_rot, v_low, d_heads, q_raw, k_raw, scales, gain_q, gain_k, cosine, sine, starts
    )
    if n_ep == 8:
        mix_sums[2], mix_sums[3], d_v = tie(mix_sums[2], mix_sums[3], d_v)
        mix = turned_sum(mix_sums)
    else:
        mix = scatter_turn(mix_pieces, n_ep)
    output = (x_one + mix).astype(BF16)
    vo_pieces = vo_grads(ids, n_ep, h_all, d_v, attn_all, d_z_cols)
    grad_vo = scatter_turn(vo_pieces, n_ep).astype(BF16)

    def placed(value):
        return lax.dynamic_update_slice_in_dim(
            jnp.zeros((1, width), F32), value, sp_index * head_width, 1
        )

    tiny = jnp.concatenate(
        [placed(grad_qg), placed(grad_kg), grad_ffn[None], grad_router], axis=0
    )
    *qk_pieces, d_qk = qk_back(
        ids, n_ep, h_all, d_qn, d_kn, q_raw, k_raw, scales, sum_sp(sums), tiny, vo_pieces[-1:]
    )
    grad_qk = scatter_turn(qk_pieces, n_ep).astype(BF16)

    d_h = d_h_rows(d_qk, d_v, w_qk, w_v).reshape(n_sp, tok_dev, width)
    parts = [
        lax.dynamic_index_in_dim(d_h, partners[j], 0, keepdims=False) for j in range(4)
    ]
    kept = plus(parts[0], swap_sp(parts[1], 1))
    sent = plus(parts[2], swap_sp(parts[3], 1))
    d_h = kept.astype(F32) + swap_sp(sent, 2).astype(F32)
    x_normed = x_rows * x_scale
    d_normed = d_h * gains[0][None, :]
    input_grad = d_one + x_scale * (
        d_normed - x_normed * jnp.mean(d_normed * x_normed, axis=-1, keepdims=True)
    )

    g_query, g_key, g_value, g_out, tiny, g_attn = finish(
        ids, n_ep, w_query, w_key, w_value, attn_gain.astype(F32)[:, None],
        gather_sp(grad_qk), gather_sp(grad_vo),
    )
    per_row = 2 * head_width // shard

    def vector(at):
        col = (at % per_row) * shard
        return tiny[at // per_row, col : col + shard]

    g_router = jnp.stack([vector(3 + i) for i in range(expert_count)], axis=1)
    return (
        output[None], input_grad[None], g_attn[:, 0], g_query, g_key, g_value, vector(0), vector(1),
        g_out, vector(2), g_router, grad_gate, grad_up, grad_down,
    )


def solution(mesh):
    seq = P("ep", "sp", None)
    vec = P("ep")
    mat = P("ep", None)
    expert = P("ep", None, None)
    in_specs = (
        seq, mat, seq, vec, mat, mat, mat, vec, vec, mat, vec, mat, expert, expert, expert, seq,
    )
    out_specs = (
        seq, seq, vec, mat, mat, mat, vec, vec, mat, vec, mat, seq, seq, seq,
    )
    return jax.shard_map(body, mesh=mesh, in_specs=in_specs, out_specs=out_specs, check_vma=False)
```

```python
import functools

import jax
import jax.numpy as jnp
from jax import lax
from jax.experimental import pallas as pl
from jax.experimental.pallas import tpu as pltpu
from jax.sharding import PartitionSpec as P

HEAD_DIM = 128
EPS = 1e-05
THETA = 10000.0
NEG_FILL = -1e30
F32 = jnp.float32
BF16 = jnp.bfloat16
MIB = 1 << 20
COVER = 20


def product(left, right):
    return jnp.dot(left, right, preferred_element_type=F32)


def product_left(left, right):
    return lax.dot_general(left, right, (((0,), (0,)), ((), ())), preferred_element_type=F32)


def product_right(left, right):
    return lax.dot_general(left, right, (((1,), (1,)), ((), ())), preferred_element_type=F32)


def row_sums(values_in):
    sums = jnp.sum(values_in, axis=1, keepdims=True)
    return jnp.transpose(jnp.broadcast_to(sums, (sums.shape[0], HEAD_DIM)))[:8]


def call(kernel, out_shape, args, flops, name, scratch=(), scalars=(), grid=(1,), in_specs=None,
         out_specs=None, aliases=None, vmem=60, after=()):
    single = not isinstance(out_shape, (list, tuple))
    shapes = [out_shape] if single else list(out_shape)
    count = len(grid)

    def fixed(shape):
        rank = len(shape)
        return pl.BlockSpec(tuple(shape), lambda *ids: (0,) * rank)

    in_specs = in_specs or [None] * len(args)
    out_specs = out_specs or [None] * len(shapes)
    in_specs = [s if s is not None else fixed(a.shape) for s, a in zip(in_specs, args)]
    out_specs = [s if s is not None else fixed(o.shape) for s, o in zip(out_specs, shapes)]
    waited = len(after)
    args = [*args, *after]
    in_specs = in_specs + [pl.BlockSpec(memory_space=pl.ANY)] * waited
    if waited:
        inner, first = kernel, len(scalars) + len(args) - waited

        def kernel(*refs):
            inner(*refs[:first], *refs[first + waited :])

    moved = sum(a.size * a.dtype.itemsize for a in args[: len(args) - waited])
    moved += sum(o.size * o.dtype.itemsize for o in shapes)
    result = pl.pallas_call(
        kernel,
        grid_spec=pltpu.PrefetchScalarGridSpec(
            num_scalar_prefetch=len(scalars), grid=grid, in_specs=in_specs, out_specs=out_specs,
            scratch_shapes=list(scratch),
        ),
        out_shape=shapes,
        input_output_aliases={k + len(scalars): v for k, v in (aliases or {}).items()},
        compiler_params=pltpu.CompilerParams(
            vmem_limit_bytes=vmem * MIB, dimension_semantics=("arbitrary",) * count
        ),
        cost_estimate=pl.CostEstimate(flops=int(COVER * flops), bytes_accessed=int(moved), transcendentals=0),
        name=name,
    )(*scalars, *args)
    return result[0] if single else result


def like(shape, dtype):
    return jax.ShapeDtypeStruct(tuple(shape), dtype)


def tie(*values):
    return lax.optimization_barrier(values)


def swap(value, bits):
    return lax.ppermute(value, "ep", [(i, i ^ bits) for i in range(8)])


def swap_sp(value, bits):
    return lax.ppermute(value, "sp", [(i, i ^ bits) for i in range(4)])


def piece_blocks(n_ep, ep_index):
    ids = jnp.arange(n_ep, dtype=jnp.int32)
    return jnp.bitwise_xor(ids, ep_index) if n_ep == 8 else ids


def along_z(value):
    far = swap(value, 4)
    return [value, swap(value, 2), far, swap(far, 2)]


def across_x(blocks):
    pieces = []
    for own in blocks:
        pieces += [own, swap(own, 1)]
    return pieces


def gather_whole(value):
    whole = lax.all_gather(value, "ep", axis=0, tiled=False)
    return [whole[i] for i in range(whole.shape[0])]


def gather(value, n_ep):
    return across_x(along_z(value)) if n_ep == 8 else gather_whole(value)


def plus(left, right):
    return (left.astype(F32) + right.astype(F32)).astype(left.dtype)


def crossed_sums(pieces):
    return [plus(pieces[i], swap(pieces[i + 1], 1)) for i in range(0, len(pieces), 2)]


def scatter_z(own, near, far, farther):
    far = plus(far, swap(farther, 2))
    return own.astype(F32) + swap(near, 2).astype(F32) + swap(far, 4).astype(F32), far


def scatter(pieces, n_ep):
    if n_ep != 8:
        stacked = jnp.stack(pieces)
        return lax.psum_scatter(stacked, "ep", scatter_dimension=0, tiled=False).astype(F32)
    return scatter_z(*crossed_sums(pieces))[0]


def gather_sp(value):
    over = swap_sp(value, 2)
    return [value, swap_sp(value, 1), over, swap_sp(over, 1)]


def sum_sp(value):
    value = value + swap_sp(value, 1)
    return value + swap_sp(value, 2)


def block_at(ids, position, size):
    if size % HEAD_DIM:
        return pl.ds(position * size, size)
    return pl.ds(pl.multiple_of(ids[position] * size, size), size)


def qk_kernel(count, ids, h_ref, *refs):
    pieces, (q_ref, k_ref, squares_ref, w_ref) = refs[:count], refs[count:]
    shard = pieces[0].shape[0]

    @pl.when(pl.program_id(0) == 0)
    def _():
        for k in range(count):
            w_ref[block_at(ids, k, shard), :] = pieces[k][...]

    width = q_ref.shape[1]
    for at, ref in enumerate((q_ref, k_ref)):
        part = product(h_ref[...], w_ref[:, at * width : (at + 1) * width])
        ref[...] = part
        squares_ref[8 * at : 8 * at + 8, :] = row_sums(part * part)


def qk_project(ids, h_all, pieces):
    total, depth = h_all.shape
    shard, both = pieces[0].shape
    width = both // 2
    rows = min(256, total)
    block = pl.BlockSpec((rows, width), lambda i, ids: (i, 0))
    return call(
        functools.partial(qk_kernel, len(pieces)),
        [like((total, width), F32)] * 2 + [like((16, total), F32), like((depth, both), BF16)],
        [h_all, *pieces],
        2 * total * depth * both,
        "qk_project",
        scalars=(ids,),
        grid=(total // rows,),
        in_specs=[pl.BlockSpec((rows, depth), lambda i, ids: (i, 0))] + [None] * len(pieces),
        out_specs=[block, block, pl.BlockSpec((16, rows), lambda i, ids: (0, i)), None],
    )


def v_kernel(count, ids, h_ref, *refs):
    pieces, (v_ref, w_ref, out_ref) = refs[:count], refs[count:]
    shard = pieces[0].shape[0]
    width = v_ref.shape[1]

    @pl.when(pl.program_id(0) == 0)
    def _():
        for k in range(count):
            rows = block_at(ids, k, shard)
            w_ref[rows, :] = pieces[k][:, :width]
            out_ref[rows, :] = pieces[k][:, width:]

    v_ref[...] = product(h_ref[...], w_ref[...]).astype(BF16)


def v_project(ids, h_all, pieces, after):
    total, depth = h_all.shape
    width = pieces[0].shape[1] // 2
    rows = min(256, total)
    return call(
        functools.partial(v_kernel, len(pieces)),
        [like((total, width), BF16), like((depth, width), BF16), like((depth, width), BF16)],
        [h_all, *pieces],
        2 * total * depth * width,
        "v_project",
        after=after,
        scalars=(ids,),
        grid=(total // rows,),
        in_specs=[pl.BlockSpec((rows, depth), lambda i, ids: (i, 0))] + [None] * len(pieces),
        out_specs=[pl.BlockSpec((rows, width), lambda i, ids: (i, 0)), None, None],
    )


def out_kernel(n_ep, ids, attn_ref, x_ref, gain_ref, *refs):
    weights, (one_ref, low_ref) = refs[:-2], refs[-2:]
    width = weights[0].shape[1]
    for j, weight in enumerate(weights):
        cols = block_at(ids, n_ep + j, width)
        one_ref[:, cols] = x_ref[:, cols].astype(F32) + product(attn_ref[...], weight[...])
    one = one_ref[...]
    scale = lax.rsqrt(jnp.mean(one * one, axis=1, keepdims=True) + EPS)
    low_ref[...] = (one * scale * gain_ref[...]).astype(BF16)


def out_project(ids, n_ep, attn_tok, tokens, gain, weights, after):
    return call(
        functools.partial(out_kernel, n_ep),
        [like(tokens.shape, F32), like(tokens.shape, BF16)],
        [attn_tok, tokens, gain, *weights],
        2 * tokens.size * attn_tok.shape[1],
        "out_project",
        after=after,
        scalars=(ids,),
    )


def out_back_kernel(n_ep, ids, d_ref, *refs):
    weights, d_attn_ref = refs[:-1], refs[-1]
    width = weights[0].shape[1]
    total = None
    for j, weight in enumerate(weights):
        part = product_right(d_ref[:, block_at(ids, n_ep + j, width)], weight[...])
        total = part if total is None else total + part
    d_attn_ref[...] = total.astype(BF16)


def out_back(ids, n_ep, d_z, weights, after):
    return call(
        functools.partial(out_back_kernel, n_ep),
        like((d_z.shape[0], weights[0].shape[0]), BF16),
        [d_z, *weights],
        2 * d_z.size * weights[0].shape[0],
        "out_back",
        after=after,
        scalars=(ids,),
    )


def vo_grads_kernel(count, ids, h_ref, dv_ref, attn_ref, dz_ref, *pieces):
    shard = pieces[0].shape[0]
    width = dv_ref.shape[1]
    for k in range(count):
        block = block_at(ids, k, shard)
        pieces[k][:, :width] = product_left(h_ref[:, block], dv_ref[...]).astype(BF16)
        pieces[k][:, width:] = product_left(attn_ref[:, block], dz_ref[...]).astype(BF16)


def vo_grads(ids, count, h_all, d_v, attn_all, d_z_cols):
    shard = h_all.shape[1] // count
    width = d_v.shape[1]
    return call(
        functools.partial(vo_grads_kernel, count),
        [like((shard, 2 * width), BF16)] * count,
        [h_all, d_v, attn_all, d_z_cols],
        4 * h_all.size * width,
        "vo_grads",
        scalars=(ids,),
    )


def qk_back_kernel(
    count, width_all, ids, h_ref, dqn_ref, dkn_ref, qr_ref, kr_ref, scale_ref, sums_ref,
    tiny_ref, *refs
):
    pieces, d_ref = refs[:count], refs[count]
    width = dqn_ref.shape[1]
    scales = jnp.transpose(scale_ref[...])
    means = jnp.transpose(sums_ref[...]) * (1.0 / width_all)
    for at, (d_normed, raw) in enumerate(((dqn_ref, qr_ref), (dkn_ref, kr_ref))):
        scale, mean = scales[:, 8 * at : 8 * at + 1], means[:, 8 * at : 8 * at + 1]
        d_ref[:, at * width : (at + 1) * width] = (
            scale * (d_normed[...] - raw[...] * scale * mean)
        ).astype(BF16)
    shard = h_ref.shape[1] // count
    per_row = 2 * width // shard
    for k in range(count):
        block = block_at(ids, k, shard)
        pieces[k][:shard, :] = product_left(h_ref[:, block], d_ref[...]).astype(BF16)
        pieces[k][shard:, :] = jnp.zeros_like(pieces[k][shard:, :])
        for at in range(tiny_ref.shape[0]):
            row, col = shard + at // per_row, (at % per_row) * shard
            pieces[k][row : row + 1, col : col + shard] = tiny_ref[at : at + 1, block].astype(BF16)


def qk_back(ids, count, h_all, d_qn, d_kn, q_raw, k_raw, scales, sums, tiny, after):
    total, depth = h_all.shape
    width = d_qn.shape[1]
    shard = depth // count
    extra = -(-tiny.shape[0] // (2 * width // shard))
    extra = -(-extra // 16) * 16
    return call(
        functools.partial(qk_back_kernel, count, depth),
        [like((shard + extra, 2 * width), BF16)] * count + [like((total, 2 * width), BF16)],
        [h_all, d_qn, d_kn, q_raw, k_raw, scales, sums, tiny],
        2 * h_all.size * 2 * width,
        "qk_back",
        scalars=(ids,),
        after=after,
    )


def d_h_kernel(d_ref, dv_ref, qk_ref, v_ref, out_ref):
    out_ref[...] = (
        product_right(d_ref[...], qk_ref[...]) + product_right(dv_ref[...], v_ref[...])
    ).astype(BF16)


def d_h_rows(d_qk, d_v, w_qk, w_v, after):
    total, wide = d_qk.shape
    depth = w_qk.shape[0]
    rows = min(256, total)
    return call(
        d_h_kernel,
        like((total, depth), BF16),
        [d_qk, d_v, w_qk, w_v],
        3 * d_qk.size * depth,
        "d_h",
        after=after,
        grid=(total // rows,),
        in_specs=[
            pl.BlockSpec((rows, wide), lambda i: (i, 0)),
            pl.BlockSpec((rows, d_v.shape[1]), lambda i: (i, 0)), None, None,
        ],
        out_specs=[pl.BlockSpec((rows, depth), lambda i: (i, 0))],
    )


def finish_kernel(n_ep, n_sp, ids, wq_ref, wk_ref, wv_ref, gain_ref, *refs):
    firsts, seconds = refs[:n_sp], refs[n_sp : 2 * n_sp]
    gq_ref, gk_ref, gv_ref, go_ref, tiny_ref, attn_ref = refs[2 * n_sp :]
    shard = wq_ref.shape[0]
    width = firsts[0].shape[1] // 2
    dots = jnp.zeros((shard, 1), F32)
    tiny = jnp.zeros(tiny_ref.shape, F32)
    for j in range(n_sp):
        cols = block_at(ids, n_ep + j, width)
        for at, grad, weight in ((0, gq_ref, wq_ref), (1, gk_ref, wk_ref), (2, gv_ref, wv_ref)):
            part = firsts[j][:shard, at * width : (at + 1) * width] if at < 2 else seconds[j][:, :width]
            value = part.astype(F32)
            grad[:, cols] = value * gain_ref[...]
            dots += jnp.sum(value * weight[:, cols].astype(F32), axis=1, keepdims=True)
        go_ref[:, cols] = seconds[j][:, width:].astype(F32)
        tiny += firsts[j][shard:, :].astype(F32)
    tiny_ref[...] = tiny
    attn_ref[...] = dots


def finish(ids, n_ep, w_query, w_key, w_value, gain, firsts, seconds, after):
    shard, depth = w_query.shape
    extra = firsts[0].shape[0] - shard
    return call(
        functools.partial(finish_kernel, n_ep, len(firsts)),
        [like((shard, depth), F32)] * 4 + [like((extra, firsts[0].shape[1]), F32), like((shard, 1), F32)],
        [w_query, w_key, w_value, gain, *firsts, *seconds],
        shard * depth * 6,
        "finish",
        after=after,
        scalars=(ids,),
    )


def turn(values_in):
    return pltpu.roll(values_in, HEAD_DIM // 2, 1)


def masked_probs(q_ref, k_ref, start_ref, block, rows):
    first, last = block * rows, (block + 1) * rows
    scores = product_right(q_ref[first:last, :], k_ref[0:last, :]) * (HEAD_DIM ** (-0.5))
    row_ids = first + lax.broadcasted_iota(jnp.int32, scores.shape, 0)
    places = lax.broadcasted_iota(jnp.int32, scores.shape, 1)
    allowed = (places <= row_ids) & (places >= start_ref[first:last, :])
    scores = jnp.where(allowed, scores, NEG_FILL)
    top = jnp.max(scores, axis=1, keepdims=True)
    weights = jnp.exp(scores - top)
    return weights * (1.0 / jnp.sum(weights, axis=1, keepdims=True))


def attend_kernel(
    rows, qr_ref, kr_ref, v_ref, scale_ref, gq_ref, gk_ref, cos_ref, sin_ref, start_ref,
    q_ref, k_ref, out_ref,
):
    scales = jnp.transpose(scale_ref[...])
    for at, (raw, gain, low) in enumerate(((qr_ref, gq_ref, q_ref), (kr_ref, gk_ref, k_ref))):
        normed = raw[...] * scales[:, 8 * at : 8 * at + 1] * gain[...]
        low[...] = (normed * cos_ref[...] + turn(normed) * sin_ref[...]).astype(BF16)
    for block in range(q_ref.shape[0] // rows):
        probs = masked_probs(q_ref, k_ref, start_ref, block, rows)
        last = (block + 1) * rows
        out_ref[block * rows : last, :] = product(
            probs.astype(BF16), v_ref[0:last, :]
        ).astype(BF16)


def head_spec(rows):
    return pl.BlockSpec((rows, HEAD_DIM), lambda h: (0, h))


def attend(q_raw, k_raw, v_low, scales, q_gain, k_gain, cosine, sine, starts):
    total, width = v_low.shape
    heads = width // HEAD_DIM
    head, gain = head_spec(total), head_spec(1)
    return call(
        functools.partial(attend_kernel, min(256, total)),
        [like((total, width), BF16)] * 3,
        [q_raw, k_raw, v_low, scales, q_gain, k_gain, cosine, sine, starts],
        3 * heads * total * total * HEAD_DIM,
        "attend",
        grid=(heads,),
        in_specs=[head, head, head, None, gain, gain, None, None, None],
        out_specs=[head, head, head],
    )


def attend_back_kernel(
    rows, q_ref, k_ref, v_ref, do_ref, qr_ref, kr_ref, scale_ref, gq_ref, gk_ref,
    cos_ref, sin_ref, start_ref,
    dq_ref, dk_ref, dv_ref, sums_ref, dgq_ref, dgk_ref, q_acc, k_acc, v_acc,
):
    k_acc[...] = jnp.zeros_like(k_acc)
    v_acc[...] = jnp.zeros_like(v_acc)
    for block in range(q_ref.shape[0] // rows):
        first, last = block * rows, (block + 1) * rows
        probs = masked_probs(q_ref, k_ref, start_ref, block, rows)
        d_rows = do_ref[first:last, :]
        d_probs = product_right(d_rows, v_ref[0:last, :])
        delta = jnp.sum(probs * d_probs, axis=1, keepdims=True)
        d_scores = (probs * (d_probs - delta) * (HEAD_DIM ** (-0.5))).astype(BF16)
        q_acc[first:last, :] = product(d_scores, k_ref[0:last, :])
        k_acc[0:last, :] += product_left(d_scores, q_ref[first:last, :])
        v_acc[0:last, :] += product_left(probs.astype(BF16), d_rows)
    dv_ref[...] = v_acc[...].astype(BF16)

    @pl.when(pl.program_id(0) == 0)
    def _():
        sums_ref[...] = jnp.zeros_like(sums_ref)

    scales = jnp.transpose(scale_ref[...])
    for at, (acc, raw, gain, d_ref, dg_ref) in enumerate(
        ((q_acc, qr_ref, gq_ref, dq_ref, dgq_ref), (k_acc, kr_ref, gk_ref, dk_ref, dgk_ref))
    ):
        turned = acc[...].astype(BF16).astype(F32)
        back = turned * cos_ref[...] + turn(turned * sin_ref[...])
        normed = raw[...] * scales[:, 8 * at : 8 * at + 1]
        both = back * normed
        dg_ref[...] = jnp.sum(both, axis=0, keepdims=True)
        d_ref[...] = back * gain[...]
        sums_ref[8 * at : 8 * at + 8, :] += row_sums(both * gain[...])


def attend_back(
    q_rot, k_rot, v_low, d_heads, q_raw, k_raw, scales, q_gain, k_gain, cosine, sine, starts
):
    total, width = v_low.shape
    heads = width // HEAD_DIM
    head, gain = head_spec(total), head_spec(1)
    wide, thin = like((total, width), F32), like((1, width), F32)
    return call(
        functools.partial(attend_back_kernel, min(256, total)),
        [wide, wide, like((total, width), BF16), like((16, total), F32), thin, thin],
        [q_rot, k_rot, v_low, d_heads, q_raw, k_raw, scales, q_gain, k_gain, cosine, sine, starts],
        7 * heads * total * total * HEAD_DIM,
        "attend_back",
        scratch=[pltpu.VMEM((total, HEAD_DIM), F32)] * 3,
        grid=(heads,),
        in_specs=[head] * 6 + [None, gain, gain, None, None, None],
        out_specs=[head, head, head, None, gain, gain],
    )


def chooser(places_ref, at, cap):
    row = places_ref[at : at + 1, :]
    slots = lax.broadcasted_iota(jnp.int32, (cap, row.shape[1]), 0)
    return slots == row


def dispatch_kernel(
    pieces_here, local, cap, gated, mine, *refs
):
    pieces, refs = refs[:pieces_here], refs[pieces_here:]
    places_ref, refs = refs[0], refs[1:]
    if gated:
        (picked_ref, router_ref), refs = refs[:2], refs[2:]
        rows_ref, gate_ref, all_ref = refs[-3:]
    else:
        rows_ref = refs[-1]
    for p in range(pieces_here):
        if gated:
            logits = product_right(router_ref[...], pieces[p][...])
            experts = logits.shape[0]
            picked = picked_ref[p * experts : (p + 1) * experts, :] > 0
            logits = jnp.where(picked, logits, NEG_FILL)
            weights = jnp.exp(logits - jnp.max(logits, axis=0, keepdims=True))
            weights = jnp.where(picked, weights, 0.0)
            gates = weights / jnp.sum(weights, axis=0, keepdims=True)
            all_ref[p * experts : (p + 1) * experts, :] = gates
        for e in range(local):
            chosen = chooser(places_ref, p * local + e, cap)
            rows_ref[e, p * cap : (p + 1) * cap, :] = product(
                chosen.astype(BF16), pieces[p][...]
            ).astype(BF16)
            if gated:
                row = all_ref[pl.ds(p * experts + mine[0] * local + e, 1), :]
                gate_ref[e, p * cap : (p + 1) * cap, :] = jnp.sum(
                    jnp.where(chosen, row, 0.0), axis=1, keepdims=True
                )


def dispatch(mine, pieces, places, picked, router, local, cap, group, at, rows, gates, after=()):
    gated = router is not None
    here = len(pieces)
    width = pieces[0].shape[1]
    args = [*pieces, places]
    shapes = [like((local, group * cap, width), BF16)]
    spec = pl.BlockSpec((local, here * cap, width), lambda i, mine: (0, at, 0))
    out_specs = [spec]
    if gated:
        args += [picked, router]
        shapes += [like((local, group * cap, 1), F32), like((picked.shape[0], places.shape[1]), F32)]
        out_specs += [pl.BlockSpec((local, here * cap, 1), lambda i, mine: (0, at, 0)), None]
    in_specs = [None] * len(args)
    aliases = {}
    if rows is not None:
        aliases[len(args)] = 0
        args.append(rows)
        in_specs.append(pl.BlockSpec(memory_space=pl.ANY))
        if gated:
            aliases[len(args)] = 1
            args.append(gates)
            in_specs.append(pl.BlockSpec(memory_space=pl.ANY))
    return call(
        functools.partial(dispatch_kernel, here, local, cap, gated),
        shapes,
        args,
        2 * here * local * cap * places.shape[1] * width,
        "dispatch",
        scalars=(mine,),
        in_specs=in_specs,
        out_specs=out_specs,
        aliases=aliases,
        after=after,
    )


def expert_kernel(
    x_ref, d_ref, gate_ref, wg_ref, wu_ref, wd_ref,
    act_ref, dg_ref, du_ref, dots_ref, mix_ref, back_ref, mix_acc, back_acc,
):
    step = pl.program_id(1)
    last = pl.num_programs(1) - 1
    x_rows, d_rows, gate = x_ref[0], d_ref[0], gate_ref[0]
    pre = product(x_rows, wg_ref[0])
    up = product(x_rows, wu_ref[0])
    pulled = product_right(d_rows, wd_ref[0])
    sigma = jax.nn.sigmoid(pre)
    silu = pre * sigma
    act = silu * up
    dots = jnp.sum(act * pulled, axis=1, keepdims=True)
    act_low = (act * gate).astype(BF16)
    act_ref[0] = act_low
    d_act = pulled * gate
    du_low = (d_act * silu).astype(BF16)
    dg_low = (d_act * up * sigma * (1.0 + pre * (1.0 - sigma))).astype(BF16)
    dg_ref[0] = dg_low
    du_ref[0] = du_low
    mix = product(act_low, wd_ref[0])
    back = product_right(dg_low, wg_ref[0]) + product_right(du_low, wu_ref[0])

    @pl.when(step == 0)
    def _():
        dots_ref[0] = dots
        mix_acc[...] = mix
        back_acc[...] = back

    @pl.when((step > 0) & (step < last))
    def _():
        dots_ref[0] += dots
        mix_acc[...] += mix
        back_acc[...] += back

    @pl.when(step == last)
    def _():
        dots_ref[0] += dots
        mix_ref[0] = (mix_acc[...] + mix).astype(BF16)
        back_ref[0] = (back_acc[...] + back).astype(BF16)


def experts(rows, d_rows, gates, w_gate, w_up, w_down, after=()):
    local, count, width = rows.shape
    hidden = w_gate.shape[2]
    part = hidden // 2
    wide = pl.BlockSpec((1, count, width), lambda e, f: (e, 0, 0))
    column = pl.BlockSpec((1, count, 1), lambda e, f: (e, 0, 0))
    thin = pl.BlockSpec((1, count, part), lambda e, f: (e, 0, f))
    into = pl.BlockSpec((1, width, part), lambda e, f: (e, 0, f))
    outof = pl.BlockSpec((1, part, width), lambda e, f: (e, f, 0))
    return call(
        expert_kernel,
        [like((local, count, hidden), BF16)] * 3
        + [like((local, count, 1), F32)]
        + [like((local, count, width), BF16)] * 2,
        [rows, d_rows, gates, w_gate, w_up, w_down],
        12 * rows.size * hidden,
        "experts",
        after=after,
        scratch=[pltpu.VMEM((count, width), F32)] * 2,
        grid=(local, 2),
        in_specs=[wide, wide, column, into, into, outof],
        out_specs=[thin, thin, thin, column, wide, wide],
    )


def combine_kernel(here, local, cap, dotted, places_ref, rows_ref, *refs):
    pieces = refs[int(dotted) : int(dotted) + here]
    for p in range(here):
        chosen = [chooser(places_ref, p * local + e, cap) for e in range(local)]
        total = None
        for e in range(local):
            part = product_left(chosen[e].astype(BF16), rows_ref[e, p * cap : (p + 1) * cap, :])
            total = part if total is None else total + part
            if dotted:
                refs[-1][p * local + e : p * local + e + 1, :] = jnp.sum(
                    jnp.where(chosen[e], refs[0][e, p * cap : (p + 1) * cap, :], 0.0),
                    axis=0, keepdims=True,
                )
        pieces[p][...] = total.astype(BF16)


def combine(places, rows, here, local, cap, at, dots=None, after=()):
    width = rows.shape[2]
    tokens = places.shape[1]
    dotted = dots is not None
    args = [places, rows] + ([dots] if dotted else [])
    in_specs = [None, pl.BlockSpec((local, here * cap, width), lambda i: (0, at, 0))]
    if dotted:
        in_specs.append(pl.BlockSpec((local, here * cap, 1), lambda i: (0, at, 0)))
    shapes = [like((tokens, width), BF16)] * here
    if dotted:
        shapes.append(like(places.shape, F32))
    return call(
        functools.partial(combine_kernel, here, local, cap, dotted),
        shapes,
        args,
        2 * here * local * cap * tokens * width,
        "combine",
        after=after,
        in_specs=in_specs,
    )


def weight_grad_kernel(groups, *refs):
    lefts, rights = refs[:groups], refs[groups : 2 * groups]
    total = None
    for left, right in zip(lefts, rights):
        part = product_left(left[0], right[0])
        total = part if total is None else total + part
    refs[-1][0] = total.astype(BF16)


def weight_grad(lefts, rights, after=()):
    local, count, tall = lefts[0].shape
    wide = rights[0].shape[2]
    part = min(512, tall)
    left = pl.BlockSpec((1, count, part), lambda e, i: (e, 0, i))
    right = pl.BlockSpec((1, count, wide), lambda e, i: (e, 0, 0))
    return call(
        functools.partial(weight_grad_kernel, len(lefts)),
        like((local, tall, wide), BF16),
        [*lefts, *rights],
        2 * len(lefts) * lefts[0].size * wide,
        "weight_grad",
        after=after,
        grid=(local, tall // part),
        in_specs=[left] * len(lefts) + [right] * len(lefts),
        out_specs=[pl.BlockSpec((1, part, wide), lambda e, i: (e, i, 0))],
    )


def body(
    tokens, doc_lengths, routes, attn_gain, w_query, w_key, w_value, q_gain, k_gain, w_out,
    ffn_gain, w_router, w_gate, w_up, w_down, cotangent,
):
    n_sp = lax.axis_size("sp")
    n_ep = lax.axis_size("ep")
    sp_index = lax.axis_index("sp")
    ep_index = lax.axis_index("ep")
    tok_dev, width = tokens.shape[1:]
    total = tok_dev * n_sp
    shard = width // n_ep
    head_width = width // n_sp
    top_count = routes.shape[2]
    local = w_gate.shape[0]
    expert_count = local * n_ep
    capacity = 9 * tok_dev * top_count // (8 * expert_count)
    cap = -(-capacity // 16) * 16
    group = 4
    blocks = piece_blocks(n_ep, ep_index)
    partners = jnp.bitwise_xor(jnp.arange(n_sp, dtype=jnp.int32), sp_index)
    ids = jnp.concatenate([blocks, partners]).astype(jnp.int32)
    mine = ep_index.astype(jnp.int32).reshape(1)

    def own_columns(value):
        return lax.dynamic_slice_in_dim(value, sp_index * head_width, head_width, 1)

    def by_block(value):
        order = jnp.bitwise_xor(jnp.arange(n_ep, dtype=jnp.int32), ep_index) if n_ep == 8 else blocks
        return jnp.stack(
            [lax.dynamic_index_in_dim(value, order[i], 0, keepdims=False) for i in range(n_ep)]
        )

    row_gain = attn_gain.astype(F32)[:, None]

    def scaled(value):
        return (own_columns(value).astype(F32) * row_gain).astype(BF16)

    qk_own = jnp.concatenate([scaled(w_query), scaled(w_key)], axis=1)
    vo_own = jnp.concatenate([scaled(w_value), own_columns(w_out)], axis=1)
    cot_own = cotangent[0]
    x_rows = tokens[0].astype(F32)
    x_scale = lax.rsqrt(jnp.mean(x_rows * x_rows, axis=-1, keepdims=True) + EPS)
    x_normed = x_rows * x_scale
    h_all = lax.all_gather(x_normed.astype(BF16), "sp", axis=0, tiled=True)

    expert_ids = jnp.arange(expert_count, dtype=jnp.int32)
    picked = jnp.any(routes[0][:, :, None] == expert_ids[None, None, :], axis=1)
    small = jnp.concatenate(
        [
            jnp.stack([q_gain, k_gain, ffn_gain]),
            jnp.zeros((13, shard), BF16),
            w_router.T,
        ],
        axis=0,
    )
    picked_low = picked.T.astype(BF16)
    if n_ep == 8:
        qk_blocks = along_z(qk_own)
        qk_blocks[2], vo_own, small = tie(qk_blocks[2], vo_own, small)
        vo_blocks = along_z(vo_own)
        vo_blocks[2], cot_own = tie(vo_blocks[2], cot_own)
        cot_blocks = along_z(cot_own)
        qk_pieces = across_x(qk_blocks)
        qk_pieces[7], vo_blocks[0], vo_blocks[1] = tie(qk_pieces[7], vo_blocks[0], vo_blocks[1])
        vo_pieces = across_x(vo_blocks)
        vo_pieces[7], cot_blocks[0], cot_blocks[1] = tie(vo_pieces[7], cot_blocks[0], cot_blocks[1])
        cot_pieces = across_x(cot_blocks)
    else:
        qk_pieces, vo_pieces, cot_pieces = (
            gather_whole(value) for value in (qk_own, vo_own, cot_own)
        )
    if shard == tok_dev:
        both = jnp.stack(gather(jnp.concatenate([small, picked_low], axis=0), n_ep))
        small_all, picked_all = both[:, : 16 + expert_count], both[:, 16 + expert_count :]
    else:
        small_all = jnp.stack(gather(small, n_ep))
        picked_all = jnp.stack(gather(picked_low, n_ep))
    small_rows = jnp.swapaxes(by_block(small_all), 0, 1).reshape(16 + expert_count, width)
    gains = small_rows[:3].astype(F32)
    full_router = small_rows[16:]

    upper = (
        jnp.arange(tok_dev, dtype=jnp.int32)[:, None] < jnp.arange(tok_dev, dtype=jnp.int32)[None, :]
    ).astype(BF16)
    picked_mine = lax.dynamic_slice_in_dim(picked_all, ep_index * local, local, 1)
    picked_mine = picked_mine.reshape(n_ep * local, tok_dev)
    earlier = product(picked_mine, upper).astype(jnp.int32)
    places = jnp.where((picked_mine > 0) & (earlier < capacity), earlier, -1)
    picked_flat = picked_all.reshape(n_ep * expert_count, tok_dev).astype(F32)

    positions = jnp.arange(total, dtype=jnp.int32)
    lengths = doc_lengths[0]
    doc_ends = jnp.cumsum(lengths)
    starts = jnp.sum(
        jnp.where(doc_ends[None, :] <= positions[:, None], lengths[None, :], 0), axis=1
    )
    half = HEAD_DIM // 2
    frequency = THETA ** (-(2.0 * jnp.arange(half, dtype=F32)) / HEAD_DIM)
    angles = (positions - starts).astype(F32)[:, None] * frequency[None, :]
    cosine = jnp.concatenate([jnp.cos(angles), jnp.cos(angles)], axis=1)
    sine = jnp.concatenate([-jnp.sin(angles), jnp.sin(angles)], axis=1)
    starts = starts[:, None].astype(jnp.int32)

    q_raw, k_raw, squares, w_qk = qk_project(ids, h_all, qk_pieces)
    scales = lax.rsqrt(sum_sp(squares) / width + EPS)
    v_low, w_v, w_o = v_project(ids, h_all, vo_pieces, [q_raw])
    w_o_parts = gather_sp(w_o)
    gain_q, gain_k = own_columns(gains)[0:1], own_columns(gains)[1:2]
    q_rot, k_rot, mixed = attend(
        q_raw, k_raw, v_low, scales, gain_q, gain_k, cosine, sine, starts
    )

    def pair_places(p):
        return places[p * local : (p + 2) * local]

    def cot_rows(g, after):
        d_rows = None
        for at, p in enumerate(range(g, g + group, 2)):
            (d_rows,) = dispatch(
                mine, cot_pieces[p : p + 2], pair_places(p), None, None, local, cap, group, at,
                d_rows, None, after,
            )
        return d_rows

    attn_tok = lax.all_to_all(mixed, "sp", split_axis=0, concat_axis=1, tiled=True)
    near_rows = cot_rows(0, [mixed])
    x_one, h2_low = out_project(
        ids, n_ep, attn_tok, tokens[0], gains[2:3], w_o_parts, [near_rows]
    )
    attn_all = lax.all_gather(attn_tok, "sp", axis=0, tiled=True)

    h2_pieces = gather(h2_low, n_ep)
    cots = [near_rows] + [cot_rows(g, [x_one]) for g in range(group, n_ep, group)]
    groups, d_pieces, d_gates, d_sums = [], [], [], []
    home_gates = None

    def rows_of(g, after):
        rows = gates = first_gates = None
        for at, p in enumerate(range(g, g + group, 2)):
            rows, gates, piece_gates = dispatch(
                mine, h2_pieces[p : p + 2], pair_places(p),
                picked_flat[p * expert_count : (p + 2) * expert_count], full_router, local, cap,
                group, at, rows, gates, after,
            )
            first_gates = piece_gates if first_gates is None else first_gates
        return rows, gates, first_gates

    rows, gates, home_gates = rows_of(0, [])
    for g in range(0, n_ep, group):
        d_rows = cots[g // group]
        made = experts(rows, d_rows, gates, w_gate, w_up, w_down, d_pieces[-group:] + cots)
        groups.append((rows, d_rows, made))
        following = []
        if g + group < n_ep:
            rows, gates, _ = rows_of(g + group, [made[5]])
            following = [rows]
        sums_before = list(d_sums)
        for at in range(group // 2):
            *two, dots = combine(
                pair_places(g + 2 * at), made[5], 2, local, cap, at, made[3],
                sums_before + following,
            )
            d_pieces += two
            d_gates.append(dots)
        if n_ep == 8:
            d_sums += crossed_sums(d_pieces[-group:])

    acts = [made[0] for _, _, made in groups]
    d_gate_rows = [made[1] for _, _, made in groups]
    d_up_rows = [made[2] for _, _, made in groups]
    ins = [rows for rows, _, _ in groups]
    outs = [d_rows for _, d_rows, _ in groups]
    if n_ep == 8:
        d_h2, inside = scatter_z(*d_sums)
        inside = [inside]
    else:
        d_h2, inside = scatter(d_pieces, n_ep), []
    grad_down = weight_grad(acts, outs, d_pieces)
    grad_gate = weight_grad(ins, d_gate_rows)
    grad_up = weight_grad(ins, d_up_rows, [*d_sums, grad_down, grad_gate])

    def over_sp(value):
        return lax.psum_scatter(value, "sp", scatter_dimension=1, tiled=True).astype(F32)

    d_gates = by_block(jnp.concatenate(d_gates, axis=0).reshape(n_ep, local, tok_dev))
    d_gates = lax.all_to_all(d_gates, "ep", split_axis=0, concat_axis=0, tiled=True)
    d_gates = d_gates.reshape(expert_count, tok_dev)

    mix_pieces = []
    for g, (_, _, made) in enumerate(groups):
        for at in range(group // 2):
            mix_pieces += combine(
                pair_places(g * group + 2 * at), made[4], 2, local, cap, at, None,
                [grad_up, *inside],
            )

    if n_ep == 8:
        gates_here = home_gates[:expert_count]
    else:
        logits = product_right(full_router, h2_low)
        logits = jnp.where(picked.T, logits, NEG_FILL)
        gates_here = jax.nn.softmax(logits, axis=0)
    d_logits = gates_here * (d_gates - jnp.sum(gates_here * d_gates, axis=0, keepdims=True))
    d_logits = jnp.where(picked.T, d_logits, 0.0).astype(BF16)
    grad_router = product(d_logits, h2_low)
    d_h2 = d_h2 + product_left(d_logits, full_router)
    one_scale = lax.rsqrt(jnp.mean(x_one * x_one, axis=-1, keepdims=True) + EPS)
    one_normed = x_one * one_scale
    grad_ffn = jnp.sum(d_h2 * one_normed, axis=0)
    d_normed = d_h2 * gains[2][None, :]
    d_one = cotangent[0].astype(F32) + one_scale * (
        d_normed - one_normed * jnp.mean(d_normed * one_normed, axis=-1, keepdims=True)
    )
    d_z = d_one.astype(BF16)
    d_attn = out_back(ids, n_ep, d_z, w_o_parts, [grad_up, grad_gate, grad_down, *mix_pieces])
    d_heads = lax.all_to_all(d_attn, "sp", split_axis=1, concat_axis=0, tiled=True)
    d_z_cols = lax.all_to_all(d_z, "sp", split_axis=1, concat_axis=0, tiled=True)
    if n_ep == 8:
        mix_sums = crossed_sums(mix_pieces)
        mix_sums[3], d_heads = tie(mix_sums[3], d_heads)
    grad_down, grad_gate, grad_up = over_sp(grad_down), over_sp(grad_gate), over_sp(grad_up)

    d_qn, d_kn, d_v, sums, grad_qg, grad_kg = attend_back(
        q_rot, k_rot, v_low, d_heads, q_raw, k_raw, scales, gain_q, gain_k, cosine, sine, starts
    )
    if n_ep == 8:
        mix_sums[2], mix_sums[1], d_v = tie(mix_sums[2], mix_sums[1], d_v)
        mix = scatter_z(*mix_sums)[0]
    else:
        mix = scatter(mix_pieces, n_ep)
    output = (x_one + mix).astype(BF16)
    vo_pieces = vo_grads(ids, n_ep, h_all, d_v, attn_all, d_z_cols)
    grad_vo = scatter(vo_pieces, n_ep).astype(BF16)

    def placed(value):
        return lax.dynamic_update_slice_in_dim(
            jnp.zeros((1, width), F32), value, sp_index * head_width, 1
        )

    tiny = jnp.concatenate(
        [placed(grad_qg), placed(grad_kg), grad_ffn[None], grad_router], axis=0
    )
    *qk_pieces, d_qk = qk_back(
        ids, n_ep, h_all, d_qn, d_kn, q_raw, k_raw, scales, sum_sp(sums), tiny, vo_pieces[-1:]
    )
    grad_qk = scatter(qk_pieces, n_ep).astype(BF16)

    d_h = d_h_rows(d_qk, d_v, w_qk, w_v, [output]).reshape(n_sp, tok_dev, width)
    parts = [
        lax.dynamic_index_in_dim(d_h, partners[j], 0, keepdims=False) for j in range(4)
    ]
    kept = plus(parts[0], swap_sp(parts[1], 1))
    sent = plus(parts[2], swap_sp(parts[3], 1))
    d_h = kept.astype(F32) + swap_sp(sent, 2).astype(F32)
    input_grad = d_one + x_scale * (
        d_h - x_normed * jnp.mean(d_h * x_normed, axis=-1, keepdims=True)
    )

    g_query, g_key, g_value, g_out, tiny, g_attn = finish(
        ids, n_ep, w_query, w_key, w_value, row_gain,
        gather_sp(grad_qk), gather_sp(grad_vo), [grad_down, grad_gate, grad_up, input_grad],
    )
    per_row = 2 * head_width // shard

    def vector(at):
        col = (at % per_row) * shard
        return tiny[at // per_row, col : col + shard]

    g_router = jnp.stack([vector(3 + i) for i in range(expert_count)], axis=1)
    return (
        output[None], input_grad[None], g_attn[:, 0], g_query, g_key, g_value, vector(0), vector(1),
        g_out, vector(2), g_router, grad_gate, grad_up, grad_down,
    )


def solution(mesh):
    seq = P("ep", "sp", None)
    vec = P("ep")
    mat = P("ep", None)
    expert = P("ep", None, None)
    in_specs = (
        seq, mat, seq, vec, mat, mat, mat, vec, vec, mat, vec, mat, expert, expert, expert, seq,
    )
    out_specs = (
        seq, seq, vec, mat, mat, mat, vec, vec, mat, vec, mat, seq, seq, seq,
    )
    return jax.shard_map(body, mesh=mesh, in_specs=in_specs, out_specs=out_specs, check_vma=False)
```

```python
import functools

import jax
import jax.numpy as jnp
from jax import lax
from jax.experimental import pallas as pl
from jax.experimental.pallas import tpu as pltpu
from jax.sharding import PartitionSpec as P

HEAD_DIM = 128
EPS = 1e-05
THETA = 10000.0
NEG_FILL = -1e30
F32 = jnp.float32
BF16 = jnp.bfloat16
MIB = 1 << 20
COVER = 20


def product(left, right):
    return jnp.dot(left, right, preferred_element_type=F32)


def product_left(left, right):
    return lax.dot_general(left, right, (((0,), (0,)), ((), ())), preferred_element_type=F32)


def product_right(left, right):
    return lax.dot_general(left, right, (((1,), (1,)), ((), ())), preferred_element_type=F32)


def row_sums(values_in):
    sums = jnp.sum(values_in, axis=1, keepdims=True)
    return jnp.transpose(jnp.broadcast_to(sums, (sums.shape[0], HEAD_DIM)))[:8]


def call(kernel, out_shape, args, flops, name, scratch=(), scalars=(), grid=(1,), in_specs=None,
         out_specs=None, aliases=None, vmem=60, after=()):
    single = not isinstance(out_shape, (list, tuple))
    shapes = [out_shape] if single else list(out_shape)
    count = len(grid)

    def fixed(shape):
        rank = len(shape)
        return pl.BlockSpec(tuple(shape), lambda *ids: (0,) * rank)

    in_specs = in_specs or [None] * len(args)
    out_specs = out_specs or [None] * len(shapes)
    in_specs = [s if s is not None else fixed(a.shape) for s, a in zip(in_specs, args)]
    out_specs = [s if s is not None else fixed(o.shape) for s, o in zip(out_specs, shapes)]
    waited = len(after)
    args = [*args, *after]
    in_specs = in_specs + [pl.BlockSpec(memory_space=pl.ANY)] * waited
    if waited:
        inner, first = kernel, len(scalars) + len(args) - waited

        def kernel(*refs):
            inner(*refs[:first], *refs[first + waited :])

    moved = sum(a.size * a.dtype.itemsize for a in args[: len(args) - waited])
    moved += sum(o.size * o.dtype.itemsize for o in shapes)
    result = pl.pallas_call(
        kernel,
        grid_spec=pltpu.PrefetchScalarGridSpec(
            num_scalar_prefetch=len(scalars), grid=grid, in_specs=in_specs, out_specs=out_specs,
            scratch_shapes=list(scratch),
        ),
        out_shape=shapes,
        input_output_aliases={k + len(scalars): v for k, v in (aliases or {}).items()},
        compiler_params=pltpu.CompilerParams(
            vmem_limit_bytes=vmem * MIB, dimension_semantics=("arbitrary",) * count
        ),
        cost_estimate=pl.CostEstimate(flops=int(COVER * flops), bytes_accessed=int(moved), transcendentals=0),
        name=name,
    )(*scalars, *args)
    return result[0] if single else result


def like(shape, dtype):
    return jax.ShapeDtypeStruct(tuple(shape), dtype)


def tie(*values):
    return lax.optimization_barrier(values)


def swap(value, bits):
    return lax.ppermute(value, "ep", [(i, i ^ bits) for i in range(8)])


def swap_sp(value, bits):
    return lax.ppermute(value, "sp", [(i, i ^ bits) for i in range(4)])


def piece_blocks(n_ep, ep_index):
    ids = jnp.arange(n_ep, dtype=jnp.int32)
    return jnp.bitwise_xor(ids, ep_index) if n_ep == 8 else ids


def along_z(value):
    far = swap(value, 4)
    return [value, swap(value, 2), far, swap(far, 2)]


def across_x(blocks):
    pieces = []
    for own in blocks:
        pieces += [own, swap(own, 1)]
    return pieces


def gather_whole(value):
    whole = lax.all_gather(value, "ep", axis=0, tiled=False)
    return [whole[i] for i in range(whole.shape[0])]


def gather(value, n_ep):
    if n_ep != 8:
        return gather_whole(value)
    blocks = along_z(value)
    near = across_x(blocks[:2])
    near[3], blocks[2], blocks[3] = tie(near[3], blocks[2], blocks[3])
    return near + across_x(blocks[2:])


def plus(left, right):
    return (left.astype(F32) + right.astype(F32)).astype(left.dtype)


def crossed_sums(pieces):
    return [plus(pieces[i], swap(pieces[i + 1], 1)) for i in range(0, len(pieces), 2)]


def scatter_z(own, near, far, farther):
    far = plus(far, swap(farther, 2))
    return own.astype(F32) + swap(near, 2).astype(F32) + swap(far, 4).astype(F32)


def scatter(pieces, n_ep):
    if n_ep != 8:
        stacked = jnp.stack(pieces)
        return lax.psum_scatter(stacked, "ep", scatter_dimension=0, tiled=False).astype(F32)
    return scatter_z(*crossed_sums(pieces))


def gather_sp(value):
    over = swap_sp(value, 2)
    return [value, swap_sp(value, 1), over, swap_sp(over, 1)]


def sum_sp(value):
    value = value + swap_sp(value, 1)
    return value + swap_sp(value, 2)


def block_at(ids, position, size):
    if size % HEAD_DIM:
        return pl.ds(position * size, size)
    return pl.ds(pl.multiple_of(ids[position] * size, size), size)


def qk_kernel(count, ids, x_ref, gain_ref, *refs):
    pieces, (q_ref, k_ref, squares_ref, w_ref, h_ref) = refs[:count], refs[count:]
    shard = pieces[0].shape[0]

    @pl.when(pl.program_id(0) == 0)
    def _():
        for k in range(count):
            w_ref[block_at(ids, k, shard), :] = pieces[k][...]

    x_rows = x_ref[...].astype(F32)
    scale = lax.rsqrt(jnp.mean(x_rows * x_rows, axis=1, keepdims=True) + EPS)
    h_ref[...] = (x_rows * scale * gain_ref[...]).astype(BF16)
    width = q_ref.shape[1]
    for at, ref in enumerate((q_ref, k_ref)):
        part = product(h_ref[...], w_ref[:, at * width : (at + 1) * width])
        ref[...] = part
        squares_ref[8 * at : 8 * at + 8, :] = row_sums(part * part)


def qk_project(ids, x_all, gain, pieces):
    total, depth = x_all.shape
    shard, both = pieces[0].shape
    width = both // 2
    rows = min(256, total)
    block = pl.BlockSpec((rows, width), lambda i, ids: (i, 0))
    wide = pl.BlockSpec((rows, depth), lambda i, ids: (i, 0))
    return call(
        functools.partial(qk_kernel, len(pieces)),
        [like((total, width), F32)] * 2
        + [like((16, total), F32), like((depth, both), BF16), like((total, depth), BF16)],
        [x_all, gain, *pieces],
        2 * total * depth * both,
        "qk_project",
        scalars=(ids,),
        grid=(total // rows,),
        in_specs=[wide] + [None] * (len(pieces) + 1),
        out_specs=[block, block, pl.BlockSpec((16, rows), lambda i, ids: (0, i)), None, wide],
    )


def v_kernel(count, ids, h_ref, *refs):
    pieces, (v_ref, w_ref, out_ref) = refs[:count], refs[count:]
    shard = pieces[0].shape[0]
    width = v_ref.shape[1]

    @pl.when(pl.program_id(0) == 0)
    def _():
        for k in range(count):
            rows = block_at(ids, k, shard)
            w_ref[rows, :] = pieces[k][:, :width]
            out_ref[rows, :] = pieces[k][:, width:]

    v_ref[...] = product(h_ref[...], w_ref[...]).astype(BF16)


def v_project(ids, h_all, pieces, after):
    total, depth = h_all.shape
    width = pieces[0].shape[1] // 2
    rows = min(256, total)
    return call(
        functools.partial(v_kernel, len(pieces)),
        [like((total, width), BF16), like((depth, width), BF16), like((depth, width), BF16)],
        [h_all, *pieces],
        2 * total * depth * width,
        "v_project",
        after=after,
        scalars=(ids,),
        grid=(total // rows,),
        in_specs=[pl.BlockSpec((rows, depth), lambda i, ids: (i, 0))] + [None] * len(pieces),
        out_specs=[pl.BlockSpec((rows, width), lambda i, ids: (i, 0)), None, None],
    )


def out_kernel(n_ep, ids, attn_ref, x_ref, gain_ref, *refs):
    weights, (one_ref, low_ref) = refs[:-2], refs[-2:]
    width = weights[0].shape[1]
    for j, weight in enumerate(weights):
        cols = block_at(ids, n_ep + j, width)
        one_ref[:, cols] = x_ref[:, cols].astype(F32) + product(attn_ref[...], weight[...])
    one = one_ref[...]
    scale = lax.rsqrt(jnp.mean(one * one, axis=1, keepdims=True) + EPS)
    low_ref[...] = (one * scale * gain_ref[...]).astype(BF16)


def out_project(ids, n_ep, attn_tok, tokens, gain, weights, after):
    return call(
        functools.partial(out_kernel, n_ep),
        [like(tokens.shape, F32), like(tokens.shape, BF16)],
        [attn_tok, tokens, gain, *weights],
        2 * tokens.size * attn_tok.shape[1],
        "out_project",
        after=after,
        scalars=(ids,),
    )


def out_back_kernel(n_ep, ids, d_ref, *refs):
    weights, d_attn_ref = refs[:-1], refs[-1]
    width = weights[0].shape[1]
    total = None
    for j, weight in enumerate(weights):
        part = product_right(d_ref[:, block_at(ids, n_ep + j, width)], weight[...])
        total = part if total is None else total + part
    d_attn_ref[...] = total.astype(BF16)


def out_back(ids, n_ep, d_z, weights, after):
    return call(
        functools.partial(out_back_kernel, n_ep),
        like((d_z.shape[0], weights[0].shape[0]), BF16),
        [d_z, *weights],
        2 * d_z.size * weights[0].shape[0],
        "out_back",
        after=after,
        scalars=(ids,),
    )


def vo_grads_kernel(count, ids, h_ref, dv_ref, attn_ref, dz_ref, *pieces):
    shard = pieces[0].shape[0]
    width = dv_ref.shape[1]
    for k in range(count):
        block = block_at(ids, k, shard)
        pieces[k][:, :width] = product_left(h_ref[:, block], dv_ref[...]).astype(BF16)
        pieces[k][:, width:] = product_left(attn_ref[:, block], dz_ref[...]).astype(BF16)


def vo_grads(ids, count, h_all, d_v, attn_all, d_z_cols):
    shard = h_all.shape[1] // count
    width = d_v.shape[1]
    return call(
        functools.partial(vo_grads_kernel, count),
        [like((shard, 2 * width), BF16)] * count,
        [h_all, d_v, attn_all, d_z_cols],
        4 * h_all.size * width,
        "vo_grads",
        scalars=(ids,),
    )


def qk_back_kernel(
    count, width_all, ids, h_ref, dqn_ref, dkn_ref, qr_ref, kr_ref, scale_ref, sums_ref,
    tiny_ref, *refs
):
    pieces, d_ref = refs[:count], refs[count]
    width = dqn_ref.shape[1]
    scales = jnp.transpose(scale_ref[...])
    means = jnp.transpose(sums_ref[...]) * (1.0 / width_all)
    for at, (d_normed, raw) in enumerate(((dqn_ref, qr_ref), (dkn_ref, kr_ref))):
        scale, mean = scales[:, 8 * at : 8 * at + 1], means[:, 8 * at : 8 * at + 1]
        d_ref[:, at * width : (at + 1) * width] = (
            scale * (d_normed[...] - raw[...] * scale * mean)
        ).astype(BF16)
    shard = h_ref.shape[1] // count
    per_row = 2 * width // shard
    for k in range(count):
        block = block_at(ids, k, shard)
        pieces[k][:shard, :] = product_left(h_ref[:, block], d_ref[...]).astype(BF16)
        pieces[k][shard:, :] = jnp.zeros_like(pieces[k][shard:, :])
        for at in range(tiny_ref.shape[0]):
            row, col = shard + at // per_row, (at % per_row) * shard
            pieces[k][row : row + 1, col : col + shard] = tiny_ref[at : at + 1, block].astype(BF16)


def qk_back(ids, count, h_all, d_qn, d_kn, q_raw, k_raw, scales, sums, tiny, after):
    total, depth = h_all.shape
    width = d_qn.shape[1]
    shard = depth // count
    extra = -(-tiny.shape[0] // (2 * width // shard))
    extra = -(-extra // 16) * 16
    return call(
        functools.partial(qk_back_kernel, count, depth),
        [like((shard + extra, 2 * width), BF16)] * count + [like((total, 2 * width), BF16)],
        [h_all, d_qn, d_kn, q_raw, k_raw, scales, sums, tiny],
        2 * h_all.size * 2 * width,
        "qk_back",
        scalars=(ids,),
        after=after,
    )


def d_h_kernel(d_ref, dv_ref, qk_ref, v_ref, out_ref):
    out_ref[...] = (
        product_right(d_ref[...], qk_ref[...]) + product_right(dv_ref[...], v_ref[...])
    ).astype(BF16)


def d_h_rows(d_qk, d_v, w_qk, w_v, after):
    total, wide = d_qk.shape
    depth = w_qk.shape[0]
    rows = min(256, total)
    return call(
        d_h_kernel,
        like((total, depth), BF16),
        [d_qk, d_v, w_qk, w_v],
        3 * d_qk.size * depth,
        "d_h",
        after=after,
        grid=(total // rows,),
        in_specs=[
            pl.BlockSpec((rows, wide), lambda i: (i, 0)),
            pl.BlockSpec((rows, d_v.shape[1]), lambda i: (i, 0)), None, None,
        ],
        out_specs=[pl.BlockSpec((rows, depth), lambda i: (i, 0))],
    )


def finish_kernel(n_ep, n_sp, ids, wq_ref, wk_ref, wv_ref, gain_ref, *refs):
    firsts, seconds = refs[:n_sp], refs[n_sp : 2 * n_sp]
    gq_ref, gk_ref, gv_ref, go_ref, tiny_ref, attn_ref = refs[2 * n_sp :]
    shard = wq_ref.shape[0]
    width = firsts[0].shape[1] // 2
    dots = jnp.zeros((shard, 1), F32)
    tiny = jnp.zeros(tiny_ref.shape, F32)
    for j in range(n_sp):
        cols = block_at(ids, n_ep + j, width)
        for at, grad, weight in ((0, gq_ref, wq_ref), (1, gk_ref, wk_ref), (2, gv_ref, wv_ref)):
            part = firsts[j][:shard, at * width : (at + 1) * width] if at < 2 else seconds[j][:, :width]
            value = part.astype(F32)
            grad[:, cols] = value
            dots += jnp.sum(value * weight[:, cols].astype(F32), axis=1, keepdims=True)
        go_ref[:, cols] = seconds[j][:, width:].astype(F32)
        tiny += firsts[j][shard:, :].astype(F32)
    tiny_ref[...] = tiny
    attn_ref[...] = dots / gain_ref[...]


def finish(ids, n_ep, w_query, w_key, w_value, gain, firsts, seconds, after):
    shard, depth = w_query.shape
    extra = firsts[0].shape[0] - shard
    return call(
        functools.partial(finish_kernel, n_ep, len(firsts)),
        [like((shard, depth), F32)] * 4 + [like((extra, firsts[0].shape[1]), F32), like((shard, 1), F32)],
        [w_query, w_key, w_value, gain, *firsts, *seconds],
        shard * depth * 6,
        "finish",
        after=after,
        scalars=(ids,),
    )


def turn(values_in):
    return pltpu.roll(values_in, HEAD_DIM // 2, 1)


def masked_probs(q_ref, k_ref, start_ref, block, rows):
    first, last = block * rows, (block + 1) * rows
    scores = product_right(q_ref[first:last, :], k_ref[0:last, :]) * (HEAD_DIM ** (-0.5))
    row_ids = first + lax.broadcasted_iota(jnp.int32, scores.shape, 0)
    places = lax.broadcasted_iota(jnp.int32, scores.shape, 1)
    allowed = (places <= row_ids) & (places >= start_ref[first:last, :])
    scores = jnp.where(allowed, scores, NEG_FILL)
    top = jnp.max(scores, axis=1, keepdims=True)
    weights = jnp.exp(scores - top)
    return weights * (1.0 / jnp.sum(weights, axis=1, keepdims=True))


def attend_kernel(
    rows, qr_ref, kr_ref, v_ref, scale_ref, gq_ref, gk_ref, cos_ref, sin_ref, start_ref,
    q_ref, k_ref, out_ref,
):
    scales = jnp.transpose(scale_ref[...])
    for at, (raw, gain, low) in enumerate(((qr_ref, gq_ref, q_ref), (kr_ref, gk_ref, k_ref))):
        normed = raw[...] * scales[:, 8 * at : 8 * at + 1] * gain[...]
        low[...] = (normed * cos_ref[...] + turn(normed) * sin_ref[...]).astype(BF16)
    for block in range(q_ref.shape[0] // rows):
        probs = masked_probs(q_ref, k_ref, start_ref, block, rows)
        last = (block + 1) * rows
        out_ref[block * rows : last, :] = product(
            probs.astype(BF16), v_ref[0:last, :]
        ).astype(BF16)


def head_spec(rows):
    return pl.BlockSpec((rows, HEAD_DIM), lambda h: (0, h))


def attend(q_raw, k_raw, v_low, scales, q_gain, k_gain, cosine, sine, starts):
    total, width = v_low.shape
    heads = width // HEAD_DIM
    head, gain = head_spec(total), head_spec(1)
    return call(
        functools.partial(attend_kernel, min(256, total)),
        [like((total, width), BF16)] * 3,
        [q_raw, k_raw, v_low, scales, q_gain, k_gain, cosine, sine, starts],
        3 * heads * total * total * HEAD_DIM,
        "attend",
        grid=(heads,),
        in_specs=[head, head, head, None, gain, gain, None, None, None],
        out_specs=[head, head, head],
    )


def attend_back_kernel(
    rows, q_ref, k_ref, v_ref, do_ref, qr_ref, kr_ref, scale_ref, gq_ref, gk_ref,
    cos_ref, sin_ref, start_ref,
    dq_ref, dk_ref, dv_ref, sums_ref, dgq_ref, dgk_ref, q_acc, k_acc, v_acc,
):
    k_acc[...] = jnp.zeros_like(k_acc)
    v_acc[...] = jnp.zeros_like(v_acc)
    for block in range(q_ref.shape[0] // rows):
        first, last = block * rows, (block + 1) * rows
        probs = masked_probs(q_ref, k_ref, start_ref, block, rows)
        d_rows = do_ref[first:last, :]
        d_probs = product_right(d_rows, v_ref[0:last, :])
        delta = jnp.sum(probs * d_probs, axis=1, keepdims=True)
        d_scores = (probs * (d_probs - delta) * (HEAD_DIM ** (-0.5))).astype(BF16)
        q_acc[first:last, :] = product(d_scores, k_ref[0:last, :])
        k_acc[0:last, :] += product_left(d_scores, q_ref[first:last, :])
        v_acc[0:last, :] += product_left(probs.astype(BF16), d_rows)
    dv_ref[...] = v_acc[...].astype(BF16)

    @pl.when(pl.program_id(0) == 0)
    def _():
        sums_ref[...] = jnp.zeros_like(sums_ref)

    scales = jnp.transpose(scale_ref[...])
    for at, (acc, raw, gain, d_ref, dg_ref) in enumerate(
        ((q_acc, qr_ref, gq_ref, dq_ref, dgq_ref), (k_acc, kr_ref, gk_ref, dk_ref, dgk_ref))
    ):
        turned = acc[...].astype(BF16).astype(F32)
        back = turned * cos_ref[...] + turn(turned * sin_ref[...])
        normed = raw[...] * scales[:, 8 * at : 8 * at + 1]
        both = back * normed
        dg_ref[...] = jnp.sum(both, axis=0, keepdims=True)
        d_ref[...] = back * gain[...]
        sums_ref[8 * at : 8 * at + 8, :] += row_sums(both * gain[...])


def attend_back(
    q_rot, k_rot, v_low, d_heads, q_raw, k_raw, scales, q_gain, k_gain, cosine, sine, starts
):
    total, width = v_low.shape
    heads = width // HEAD_DIM
    head, gain = head_spec(total), head_spec(1)
    wide, thin = like((total, width), F32), like((1, width), F32)
    return call(
        functools.partial(attend_back_kernel, min(256, total)),
        [wide, wide, like((total, width), BF16), like((16, total), F32), thin, thin],
        [q_rot, k_rot, v_low, d_heads, q_raw, k_raw, scales, q_gain, k_gain, cosine, sine, starts],
        7 * heads * total * total * HEAD_DIM,
        "attend_back",
        scratch=[pltpu.VMEM((total, HEAD_DIM), F32)] * 3,
        grid=(heads,),
        in_specs=[head] * 6 + [None, gain, gain, None, None, None],
        out_specs=[head, head, head, None, gain, gain],
    )


def chooser(places_ref, at, cap):
    row = places_ref[at : at + 1, :]
    slots = lax.broadcasted_iota(jnp.int32, (cap, row.shape[1]), 0)
    return slots == row


def dispatch_kernel(
    pieces_here, local, cap, gated, mine, *refs
):
    pieces, refs = refs[:pieces_here], refs[pieces_here:]
    places_ref, refs = refs[0], refs[1:]
    if gated:
        (picked_ref, router_ref), refs = refs[:2], refs[2:]
        rows_ref, gate_ref, all_ref = refs[-3:]
    else:
        rows_ref = refs[-1]
    for p in range(pieces_here):
        if gated:
            logits = product_right(router_ref[...], pieces[p][...])
            experts = logits.shape[0]
            picked = picked_ref[p * experts : (p + 1) * experts, :] > 0
            logits = jnp.where(picked, logits, NEG_FILL)
            weights = jnp.exp(logits - jnp.max(logits, axis=0, keepdims=True))
            weights = jnp.where(picked, weights, 0.0)
            gates = weights / jnp.sum(weights, axis=0, keepdims=True)
            all_ref[p * experts : (p + 1) * experts, :] = gates
        for e in range(local):
            chosen = chooser(places_ref, p * local + e, cap)
            rows_ref[e, p * cap : (p + 1) * cap, :] = product(
                chosen.astype(BF16), pieces[p][...]
            ).astype(BF16)
            if gated:
                row = all_ref[pl.ds(p * experts + mine[0] * local + e, 1), :]
                gate_ref[e, p * cap : (p + 1) * cap, :] = jnp.sum(
                    jnp.where(chosen, row, 0.0), axis=1, keepdims=True
                )


def dispatch(mine, pieces, places, picked, router, local, cap, group, at, rows, gates, after=()):
    gated = router is not None
    here = len(pieces)
    width = pieces[0].shape[1]
    args = [*pieces, places]
    shapes = [like((local, group * cap, width), BF16)]
    spec = pl.BlockSpec((local, here * cap, width), lambda i, mine: (0, at, 0))
    out_specs = [spec]
    if gated:
        args += [picked, router]
        shapes += [like((local, group * cap, 1), F32), like((picked.shape[0], places.shape[1]), F32)]
        out_specs += [pl.BlockSpec((local, here * cap, 1), lambda i, mine: (0, at, 0)), None]
    in_specs = [None] * len(args)
    aliases = {}
    if rows is not None:
        aliases[len(args)] = 0
        args.append(rows)
        in_specs.append(pl.BlockSpec(memory_space=pl.ANY))
        if gated:
            aliases[len(args)] = 1
            args.append(gates)
            in_specs.append(pl.BlockSpec(memory_space=pl.ANY))
    return call(
        functools.partial(dispatch_kernel, here, local, cap, gated),
        shapes,
        args,
        2 * here * local * cap * places.shape[1] * width,
        "dispatch",
        scalars=(mine,),
        in_specs=in_specs,
        out_specs=out_specs,
        aliases=aliases,
        after=after,
    )


def expert_kernel(
    x_ref, d_ref, gate_ref, wg_ref, wu_ref, wd_ref,
    act_ref, dg_ref, du_ref, dots_ref, mix_ref, back_ref, mix_acc, back_acc,
):
    step = pl.program_id(1)
    last = pl.num_programs(1) - 1
    x_rows, d_rows, gate = x_ref[0], d_ref[0], gate_ref[0]
    pre = product(x_rows, wg_ref[0])
    up = product(x_rows, wu_ref[0])
    pulled = product_right(d_rows, wd_ref[0])
    sigma = jax.nn.sigmoid(pre)
    silu = pre * sigma
    act = silu * up
    dots = jnp.sum(act * pulled, axis=1, keepdims=True)
    act_low = (act * gate).astype(BF16)
    act_ref[0] = act_low
    d_act = pulled * gate
    du_low = (d_act * silu).astype(BF16)
    dg_low = (d_act * up * sigma * (1.0 + pre * (1.0 - sigma))).astype(BF16)
    dg_ref[0] = dg_low
    du_ref[0] = du_low
    mix = product(act_low, wd_ref[0])
    back = product_right(dg_low, wg_ref[0]) + product_right(du_low, wu_ref[0])

    @pl.when(step == 0)
    def _():
        dots_ref[0] = dots
        mix_acc[...] = mix
        back_acc[...] = back

    @pl.when((step > 0) & (step < last))
    def _():
        dots_ref[0] += dots
        mix_acc[...] += mix
        back_acc[...] += back

    @pl.when(step == last)
    def _():
        dots_ref[0] += dots
        mix_ref[0] = (mix_acc[...] + mix).astype(BF16)
        back_ref[0] = (back_acc[...] + back).astype(BF16)


def experts(rows, d_rows, gates, w_gate, w_up, w_down, after=()):
    local, count, width = rows.shape
    hidden = w_gate.shape[2]
    part = hidden // 2
    wide = pl.BlockSpec((1, count, width), lambda e, f: (e, 0, 0))
    column = pl.BlockSpec((1, count, 1), lambda e, f: (e, 0, 0))
    thin = pl.BlockSpec((1, count, part), lambda e, f: (e, 0, f))
    into = pl.BlockSpec((1, width, part), lambda e, f: (e, 0, f))
    outof = pl.BlockSpec((1, part, width), lambda e, f: (e, f, 0))
    return call(
        expert_kernel,
        [like((local, count, hidden), BF16)] * 3
        + [like((local, count, 1), F32)]
        + [like((local, count, width), BF16)] * 2,
        [rows, d_rows, gates, w_gate, w_up, w_down],
        12 * rows.size * hidden,
        "experts",
        after=after,
        scratch=[pltpu.VMEM((count, width), F32)] * 2,
        grid=(local, 2),
        in_specs=[wide, wide, column, into, into, outof],
        out_specs=[thin, thin, thin, column, wide, wide],
    )


def combine_kernel(here, local, cap, dotted, places_ref, rows_ref, *refs):
    pieces = refs[int(dotted) : int(dotted) + here]
    for p in range(here):
        chosen = [chooser(places_ref, p * local + e, cap) for e in range(local)]
        total = None
        for e in range(local):
            part = product_left(chosen[e].astype(BF16), rows_ref[e, p * cap : (p + 1) * cap, :])
            total = part if total is None else total + part
            if dotted:
                refs[-1][p * local + e : p * local + e + 1, :] = jnp.sum(
                    jnp.where(chosen[e], refs[0][e, p * cap : (p + 1) * cap, :], 0.0),
                    axis=0, keepdims=True,
                )
        pieces[p][...] = total.astype(BF16)


def combine(places, rows, here, local, cap, at, dots=None, after=()):
    width = rows.shape[2]
    tokens = places.shape[1]
    dotted = dots is not None
    args = [places, rows] + ([dots] if dotted else [])
    in_specs = [None, pl.BlockSpec((local, here * cap, width), lambda i: (0, at, 0))]
    if dotted:
        in_specs.append(pl.BlockSpec((local, here * cap, 1), lambda i: (0, at, 0)))
    shapes = [like((tokens, width), BF16)] * here
    if dotted:
        shapes.append(like(places.shape, F32))
    return call(
        functools.partial(combine_kernel, here, local, cap, dotted),
        shapes,
        args,
        2 * here * local * cap * tokens * width,
        "combine",
        after=after,
        in_specs=in_specs,
    )


def weight_grad_kernel(groups, *refs):
    lefts, rights = refs[:groups], refs[groups : 2 * groups]
    total = None
    for left, right in zip(lefts, rights):
        part = product_left(left[0], right[0])
        total = part if total is None else total + part
    refs[-1][0] = total.astype(BF16)


def weight_grad(lefts, rights, after=()):
    local, count, tall = lefts[0].shape
    wide = rights[0].shape[2]
    part = min(512, tall)
    left = pl.BlockSpec((1, count, part), lambda e, i: (e, 0, i))
    right = pl.BlockSpec((1, count, wide), lambda e, i: (e, 0, 0))
    return call(
        functools.partial(weight_grad_kernel, len(lefts)),
        like((local, tall, wide), BF16),
        [*lefts, *rights],
        2 * len(lefts) * lefts[0].size * wide,
        "weight_grad",
        after=after,
        grid=(local, tall // part),
        in_specs=[left] * len(lefts) + [right] * len(lefts),
        out_specs=[pl.BlockSpec((1, part, wide), lambda e, i: (e, i, 0))],
    )


def body(
    tokens, doc_lengths, routes, attn_gain, w_query, w_key, w_value, q_gain, k_gain, w_out,
    ffn_gain, w_router, w_gate, w_up, w_down, cotangent,
):
    n_sp = lax.axis_size("sp")
    n_ep = lax.axis_size("ep")
    sp_index = lax.axis_index("sp")
    ep_index = lax.axis_index("ep")
    tok_dev, width = tokens.shape[1:]
    total = tok_dev * n_sp
    shard = width // n_ep
    head_width = width // n_sp
    top_count = routes.shape[2]
    local = w_gate.shape[0]
    expert_count = local * n_ep
    capacity = 9 * tok_dev * top_count // (8 * expert_count)
    cap = -(-capacity // 16) * 16
    group = 4
    blocks = piece_blocks(n_ep, ep_index)
    partners = jnp.bitwise_xor(jnp.arange(n_sp, dtype=jnp.int32), sp_index)
    ids = jnp.concatenate([blocks, partners]).astype(jnp.int32)
    mine = ep_index.astype(jnp.int32).reshape(1)

    def own_columns(value):
        return lax.dynamic_slice_in_dim(value, sp_index * head_width, head_width, 1)

    def by_piece(value):
        return jnp.stack(
            [lax.dynamic_index_in_dim(value, blocks[i], 0, keepdims=False) for i in range(n_ep)]
        )

    expert_ids = jnp.arange(expert_count, dtype=jnp.int32)
    picked = jnp.any(routes[0][:, :, None] == expert_ids[None, None, :], axis=1)
    picked_low = picked.T.astype(BF16)
    small = jnp.concatenate(
        [
            jnp.stack([attn_gain, q_gain, k_gain, ffn_gain]),
            jnp.zeros((12, shard), BF16),
            w_router.T,
        ],
        axis=0,
    )

    def to_all(value):
        value = jnp.broadcast_to(value[None], (n_ep, *value.shape))
        return lax.all_to_all(value, "ep", split_axis=0, concat_axis=0, tiled=True)

    if shard == tok_dev:
        both = to_all(jnp.concatenate([small, picked_low], axis=0))
        small_all, picked_all = both[:, : 16 + expert_count], both[:, 16 + expert_count :]
    else:
        small_all, picked_all = to_all(small), to_all(picked_low)
    small_rows = jnp.swapaxes(small_all, 0, 1).reshape(16 + expert_count, width)
    gains = small_rows[:4].astype(F32)
    full_router = small_rows[16:]
    picked_all = by_piece(picked_all)

    qk_own = jnp.concatenate([own_columns(w_query), own_columns(w_key)], axis=1)
    vo_own = jnp.concatenate([own_columns(w_value), own_columns(w_out)], axis=1)
    cot_own = cotangent[0]
    if n_ep == 8:
        own_x, near, far = swap(qk_own, 1), swap(qk_own, 2), swap(qk_own, 4)
        own_x, near, far, vo_own = tie(own_x, near, far, vo_own)
        vo_blocks = along_z(vo_own)
        qk_pieces = [qk_own, own_x] + across_x([near, far, swap(far, 2)])
        vo_blocks[2], cot_own = tie(vo_blocks[2], cot_own)
        cot_blocks = along_z(cot_own)
        qk_pieces[7], vo_blocks[0], vo_blocks[1] = tie(qk_pieces[7], vo_blocks[0], vo_blocks[1])
        vo_pieces = across_x(vo_blocks)
        vo_pieces[7], cot_blocks[0], cot_blocks[1] = tie(vo_pieces[7], cot_blocks[0], cot_blocks[1])
        cot_pieces = across_x(cot_blocks)
    else:
        qk_pieces, vo_pieces, cot_pieces = (
            gather_whole(value) for value in (qk_own, vo_own, cot_own)
        )
    x_all = lax.all_gather(tokens[0], "sp", axis=0, tiled=True)

    upper = (
        jnp.arange(tok_dev, dtype=jnp.int32)[:, None] < jnp.arange(tok_dev, dtype=jnp.int32)[None, :]
    ).astype(BF16)
    picked_mine = lax.dynamic_slice_in_dim(picked_all, ep_index * local, local, 1)
    picked_mine = picked_mine.reshape(n_ep * local, tok_dev)
    earlier = product(picked_mine, upper).astype(jnp.int32)
    places = jnp.where((picked_mine > 0) & (earlier < capacity), earlier, -1)
    picked_flat = picked_all.reshape(n_ep * expert_count, tok_dev).astype(F32)

    positions = jnp.arange(total, dtype=jnp.int32)
    lengths = doc_lengths[0]
    doc_ends = jnp.cumsum(lengths)
    starts = jnp.sum(
        jnp.where(doc_ends[None, :] <= positions[:, None], lengths[None, :], 0), axis=1
    )
    half = HEAD_DIM // 2
    frequency = THETA ** (-(2.0 * jnp.arange(half, dtype=F32)) / HEAD_DIM)
    angles = (positions - starts).astype(F32)[:, None] * frequency[None, :]
    cosine = jnp.concatenate([jnp.cos(angles), jnp.cos(angles)], axis=1)
    sine = jnp.concatenate([-jnp.sin(angles), jnp.sin(angles)], axis=1)
    starts = starts[:, None].astype(jnp.int32)

    q_raw, k_raw, squares, w_qk, h_all = qk_project(ids, x_all, gains[0:1], qk_pieces)
    scales = lax.rsqrt(sum_sp(squares) / width + EPS)
    v_low, w_v, w_o = v_project(ids, h_all, vo_pieces, [q_raw])
    w_o_parts = gather_sp(w_o)
    gain_q, gain_k = own_columns(gains)[1:2], own_columns(gains)[2:3]
    q_rot, k_rot, mixed = attend(
        q_raw, k_raw, v_low, scales, gain_q, gain_k, cosine, sine, starts
    )

    def pair_places(p):
        return places[p * local : (p + 2) * local]

    def cot_rows(g, after):
        d_rows = None
        for at, p in enumerate(range(g, g + group, 2)):
            (d_rows,) = dispatch(
                mine, cot_pieces[p : p + 2], pair_places(p), None, None, local, cap, group, at,
                d_rows, None, after,
            )
        return d_rows

    attn_tok = lax.all_to_all(mixed, "sp", split_axis=0, concat_axis=1, tiled=True)
    near_rows = cot_rows(0, [mixed])
    x_one, h2_low = out_project(
        ids, n_ep, attn_tok, tokens[0], gains[3:4], w_o_parts, [near_rows]
    )
    attn_all = lax.all_gather(attn_tok, "sp", axis=0, tiled=True)

    h2_pieces = gather(h2_low, n_ep)
    cots = [near_rows] + [cot_rows(g, [x_one]) for g in range(group, n_ep, group)]
    groups, d_pieces, d_gates, d_sums = [], [], [], []
    home_gates = None

    def rows_of(g, after):
        rows = gates = first_gates = None
        for at, p in enumerate(range(g, g + group, 2)):
            rows, gates, piece_gates = dispatch(
                mine, h2_pieces[p : p + 2], pair_places(p),
                picked_flat[p * expert_count : (p + 2) * expert_count], full_router, local, cap,
                group, at, rows, gates, after,
            )
            first_gates = piece_gates if first_gates is None else first_gates
        return rows, gates, first_gates

    rows, gates, home_gates = rows_of(0, [])
    for g in range(0, n_ep, group):
        d_rows = cots[g // group]
        made = experts(rows, d_rows, gates, w_gate, w_up, w_down, d_pieces[-group:] + cots)
        groups.append((rows, d_rows, made))
        following = []
        if g + group < n_ep:
            rows, gates, _ = rows_of(g + group, [made[5]])
            following = [rows]
        sums_before = list(d_sums)
        for at in range(group // 2):
            *two, dots = combine(
                pair_places(g + 2 * at), made[5], 2, local, cap, at, made[3],
                sums_before + following,
            )
            d_pieces += two
            d_gates.append(dots)
        if n_ep == 8:
            d_sums += crossed_sums(d_pieces[-group:])

    acts = [made[0] for _, _, made in groups]
    d_gate_rows = [made[1] for _, _, made in groups]
    d_up_rows = [made[2] for _, _, made in groups]
    ins = [rows for rows, _, _ in groups]
    outs = [d_rows for _, d_rows, _ in groups]
    grad_down = weight_grad(acts, outs, d_pieces)
    grad_gate = weight_grad(ins, d_gate_rows, [grad_down])
    mix_pieces = []
    for g, (_, _, made) in enumerate(groups):
        for at in range(group // 2):
            mix_pieces += combine(
                pair_places(g * group + 2 * at), made[4], 2, local, cap, at, None,
                [grad_gate, *d_sums],
            )
    if n_ep == 8:
        *d_sums, mix_pieces[1], mix_pieces[3], mix_pieces[5], mix_pieces[7] = tie(
            *d_sums, mix_pieces[1], mix_pieces[3], mix_pieces[5], mix_pieces[7]
        )
        mix_sums = crossed_sums(mix_pieces)
        d_h2 = scatter_z(*d_sums)
    else:
        d_h2 = scatter(d_pieces, n_ep)
    grad_up = weight_grad(ins, d_up_rows, mix_pieces)

    def over_sp(value):
        return lax.psum_scatter(value, "sp", scatter_dimension=1, tiled=True).astype(F32)

    d_gates = by_piece(jnp.concatenate(d_gates, axis=0).reshape(n_ep, local, tok_dev))
    d_gates = lax.all_to_all(d_gates, "ep", split_axis=0, concat_axis=0, tiled=True)
    d_gates = d_gates.reshape(expert_count, tok_dev)

    if n_ep == 8:
        gates_here = home_gates[:expert_count]
    else:
        logits = product_right(full_router, h2_low)
        logits = jnp.where(picked.T, logits, NEG_FILL)
        gates_here = jax.nn.softmax(logits, axis=0)
    d_logits = gates_here * (d_gates - jnp.sum(gates_here * d_gates, axis=0, keepdims=True))
    d_logits = jnp.where(picked.T, d_logits, 0.0).astype(BF16)
    grad_router = product(d_logits, h2_low)
    d_h2 = d_h2 + product_left(d_logits, full_router)
    one_scale = lax.rsqrt(jnp.mean(x_one * x_one, axis=-1, keepdims=True) + EPS)
    one_normed = x_one * one_scale
    grad_ffn = jnp.sum(d_h2 * one_normed, axis=0)
    d_normed = d_h2 * gains[3][None, :]
    d_one = cotangent[0].astype(F32) + one_scale * (
        d_normed - one_normed * jnp.mean(d_normed * one_normed, axis=-1, keepdims=True)
    )
    d_z = d_one.astype(BF16)
    d_attn = out_back(ids, n_ep, d_z, w_o_parts, [grad_up, grad_gate, grad_down, *mix_pieces])
    d_heads = lax.all_to_all(d_attn, "sp", split_axis=1, concat_axis=0, tiled=True)
    d_z_cols = lax.all_to_all(d_z, "sp", split_axis=1, concat_axis=0, tiled=True)
    if n_ep == 8:
        *mix_sums, d_heads = tie(*mix_sums, d_heads)
    grad_down, grad_gate, grad_up = over_sp(grad_down), over_sp(grad_gate), over_sp(grad_up)

    d_qn, d_kn, d_v, sums, grad_qg, grad_kg = attend_back(
        q_rot, k_rot, v_low, d_heads, q_raw, k_raw, scales, gain_q, gain_k, cosine, sine, starts
    )
    if n_ep == 8:
        own, near, far, farther = mix_sums
        far, d_v = tie(plus(far, swap(farther, 2)), d_v)
        mix = own.astype(F32) + swap(near, 2).astype(F32) + swap(far, 4).astype(F32)
    else:
        mix = scatter(mix_pieces, n_ep)
    output = (x_one + mix).astype(BF16)
    vo_pieces = vo_grads(ids, n_ep, h_all, d_v, attn_all, d_z_cols)
    grad_vo = scatter(vo_pieces, n_ep).astype(BF16)

    def placed(value):
        return lax.dynamic_update_slice_in_dim(
            jnp.zeros((1, width), F32), value, sp_index * head_width, 1
        )

    tiny = jnp.concatenate(
        [placed(grad_qg), placed(grad_kg), grad_ffn[None], grad_router], axis=0
    )
    *qk_pieces, d_qk = qk_back(
        ids, n_ep, h_all, d_qn, d_kn, q_raw, k_raw, scales, sum_sp(sums), tiny, vo_pieces[-1:]
    )
    grad_qk = scatter(qk_pieces, n_ep).astype(BF16)

    d_h = d_h_rows(d_qk, d_v, w_qk, w_v, [output]).reshape(n_sp, tok_dev, width)
    parts = [
        lax.dynamic_index_in_dim(d_h, partners[j], 0, keepdims=False) for j in range(4)
    ]
    kept = plus(parts[0], swap_sp(parts[1], 1))
    sent = plus(parts[2], swap_sp(parts[3], 1))
    d_h = kept.astype(F32) + swap_sp(sent, 2).astype(F32)
    x_rows = tokens[0].astype(F32)
    x_scale = lax.rsqrt(jnp.mean(x_rows * x_rows, axis=-1, keepdims=True) + EPS)
    x_normed = x_rows * x_scale
    d_normed = d_h * gains[0][None, :]
    input_grad = d_one + x_scale * (
        d_normed - x_normed * jnp.mean(d_normed * x_normed, axis=-1, keepdims=True)
    )

    g_query, g_key, g_value, g_out, tiny, g_attn = finish(
        ids, n_ep, w_query, w_key, w_value, attn_gain.astype(F32)[:, None],
        gather_sp(grad_qk), gather_sp(grad_vo), [grad_down, grad_gate, grad_up, input_grad],
    )
    per_row = 2 * head_width // shard

    def vector(at):
        col = (at % per_row) * shard
        return tiny[at // per_row, col : col + shard]

    g_router = jnp.stack([vector(3 + i) for i in range(expert_count)], axis=1)
    return (
        output[None], input_grad[None], g_attn[:, 0], g_query, g_key, g_value, vector(0), vector(1),
        g_out, vector(2), g_router, grad_gate, grad_up, grad_down,
    )


def solution(mesh):
    seq = P("ep", "sp", None)
    vec = P("ep")
    mat = P("ep", None)
    expert = P("ep", None, None)
    in_specs = (
        seq, mat, seq, vec, mat, mat, mat, vec, vec, mat, vec, mat, expert, expert, expert, seq,
    )
    out_specs = (
        seq, seq, vec, mat, mat, mat, vec, vec, mat, vec, mat, seq, seq, seq,
    )
    return jax.shard_map(body, mesh=mesh, in_specs=in_specs, out_specs=out_specs, check_vma=False)
```

```python
import functools

import jax
import jax.numpy as jnp
from jax import lax
from jax.experimental import pallas as pl
from jax.experimental.pallas import tpu as pltpu
from jax.sharding import PartitionSpec as P

HEAD_DIM = 128
EPS = 1e-05
THETA = 10000.0
NEG_FILL = -1e30
F32 = jnp.float32
BF16 = jnp.bfloat16
MIB = 1 << 20
COVER = 20


def product(left, right):
    return jnp.dot(left, right, preferred_element_type=F32)


def product_left(left, right):
    return lax.dot_general(left, right, (((0,), (0,)), ((), ())), preferred_element_type=F32)


def product_right(left, right):
    return lax.dot_general(left, right, (((1,), (1,)), ((), ())), preferred_element_type=F32)


def row_sums(values_in):
    sums = jnp.sum(values_in, axis=1, keepdims=True)
    return jnp.transpose(jnp.broadcast_to(sums, (sums.shape[0], HEAD_DIM)))[:8]


def call(kernel, out_shape, args, flops, name, scratch=(), scalars=(), grid=(1,), in_specs=None,
         out_specs=None, aliases=None, vmem=60, after=()):
    single = not isinstance(out_shape, (list, tuple))
    shapes = [out_shape] if single else list(out_shape)
    count = len(grid)

    def fixed(shape):
        rank = len(shape)
        return pl.BlockSpec(tuple(shape), lambda *ids: (0,) * rank)

    in_specs = in_specs or [None] * len(args)
    out_specs = out_specs or [None] * len(shapes)
    in_specs = [s if s is not None else fixed(a.shape) for s, a in zip(in_specs, args)]
    out_specs = [s if s is not None else fixed(o.shape) for s, o in zip(out_specs, shapes)]
    waited = len(after)
    args = [*args, *after]
    in_specs = in_specs + [pl.BlockSpec(memory_space=pl.ANY)] * waited
    if waited:
        inner, first = kernel, len(scalars) + len(args) - waited

        def kernel(*refs):
            inner(*refs[:first], *refs[first + waited :])

    moved = sum(a.size * a.dtype.itemsize for a in args[: len(args) - waited])
    moved += sum(o.size * o.dtype.itemsize for o in shapes)
    result = pl.pallas_call(
        kernel,
        grid_spec=pltpu.PrefetchScalarGridSpec(
            num_scalar_prefetch=len(scalars), grid=grid, in_specs=in_specs, out_specs=out_specs,
            scratch_shapes=list(scratch),
        ),
        out_shape=shapes,
        input_output_aliases={k + len(scalars): v for k, v in (aliases or {}).items()},
        compiler_params=pltpu.CompilerParams(
            vmem_limit_bytes=vmem * MIB, dimension_semantics=("arbitrary",) * count
        ),
        cost_estimate=pl.CostEstimate(flops=int(COVER * flops), bytes_accessed=int(moved), transcendentals=0),
        name=name,
    )(*scalars, *args)
    return result[0] if single else result


def like(shape, dtype):
    return jax.ShapeDtypeStruct(tuple(shape), dtype)


def tie(*values):
    return lax.optimization_barrier(values)


def swap(value, bits):
    return lax.ppermute(value, "ep", [(i, i ^ bits) for i in range(8)])


def swap_sp(value, bits):
    return lax.ppermute(value, "sp", [(i, i ^ bits) for i in range(4)])


def piece_blocks(n_ep, ep_index):
    ids = jnp.arange(n_ep, dtype=jnp.int32)
    return jnp.bitwise_xor(ids, ep_index) if n_ep == 8 else ids


def along_z(value):
    far = swap(value, 4)
    return [value, swap(value, 2), far, swap(far, 2)]


def across_x(blocks):
    pieces = []
    for own in blocks:
        pieces += [own, swap(own, 1)]
    return pieces


def gather_whole(value):
    whole = lax.all_gather(value, "ep", axis=0, tiled=False)
    return [whole[i] for i in range(whole.shape[0])]


def gather(value, n_ep):
    if n_ep != 8:
        return gather_whole(value)
    blocks = along_z(value)
    near = across_x(blocks[:2])
    near[3], blocks[2], blocks[3] = tie(near[3], blocks[2], blocks[3])
    return near + across_x(blocks[2:])


def plus(left, right):
    return (left.astype(F32) + right.astype(F32)).astype(left.dtype)


def crossed_sums(pieces):
    return [plus(pieces[i], swap(pieces[i + 1], 1)) for i in range(0, len(pieces), 2)]


def scatter_z(own, near, far, farther):
    far = plus(far, swap(farther, 2))
    return own.astype(F32) + swap(near, 2).astype(F32) + swap(far, 4).astype(F32)


def scatter_x_last(pieces, n_ep):
    if n_ep != 8:
        return scatter(pieces, n_ep)
    kept, sent = scatter_z(*pieces[0::2]), scatter_z(*pieces[1::2])
    return kept + swap(sent.astype(BF16), 1).astype(F32)


def scatter(pieces, n_ep):
    if n_ep != 8:
        stacked = jnp.stack(pieces)
        return lax.psum_scatter(stacked, "ep", scatter_dimension=0, tiled=False).astype(F32)
    return scatter_z(*crossed_sums(pieces))


def gather_sp(value):
    over = swap_sp(value, 2)
    return [value, swap_sp(value, 1), over, swap_sp(over, 1)]


def sum_sp(value):
    return (value + swap_sp(value, 1)) + (swap_sp(value, 2) + swap_sp(value, 3))


def block_at(ids, position, size):
    if size % HEAD_DIM:
        return pl.ds(position * size, size)
    return pl.ds(pl.multiple_of(ids[position] * size, size), size)


def qk_kernel(count, ids, x_ref, gain_ref, *refs):
    pieces, (q_ref, k_ref, squares_ref, w_ref, h_ref) = refs[:count], refs[count:]
    shard = pieces[0].shape[0]

    @pl.when(pl.program_id(0) == 0)
    def _():
        for k in range(count):
            w_ref[block_at(ids, k, shard), :] = pieces[k][...]

    x_rows = x_ref[...].astype(F32)
    scale = lax.rsqrt(jnp.mean(x_rows * x_rows, axis=1, keepdims=True) + EPS)
    h_ref[...] = (x_rows * scale * gain_ref[...]).astype(BF16)
    width = q_ref.shape[1]
    for at, ref in enumerate((q_ref, k_ref)):
        part = product(h_ref[...], w_ref[:, at * width : (at + 1) * width])
        ref[...] = part
        squares_ref[8 * at : 8 * at + 8, :] = row_sums(part * part)


def qk_project(ids, x_all, gain, pieces):
    total, depth = x_all.shape
    shard, both = pieces[0].shape
    width = both // 2
    rows = min(256, total)
    block = pl.BlockSpec((rows, width), lambda i, ids: (i, 0))
    wide = pl.BlockSpec((rows, depth), lambda i, ids: (i, 0))
    return call(
        functools.partial(qk_kernel, len(pieces)),
        [like((total, width), F32)] * 2
        + [like((16, total), F32), like((depth, both), BF16), like((total, depth), BF16)],
        [x_all, gain, *pieces],
        2 * total * depth * both,
        "qk_project",
        scalars=(ids,),
        grid=(total // rows,),
        in_specs=[wide] + [None] * (len(pieces) + 1),
        out_specs=[block, block, pl.BlockSpec((16, rows), lambda i, ids: (0, i)), None, wide],
    )


def v_kernel(count, ids, h_ref, *refs):
    pieces, (v_ref, w_ref, out_ref) = refs[:count], refs[count:]
    shard = pieces[0].shape[0]
    width = v_ref.shape[1]

    @pl.when(pl.program_id(0) == 0)
    def _():
        for k in range(count):
            rows = block_at(ids, k, shard)
            w_ref[rows, :] = pieces[k][:, :width]
            out_ref[rows, :] = pieces[k][:, width:]

    v_ref[...] = product(h_ref[...], w_ref[...]).astype(BF16)


def v_project(ids, h_all, pieces, after):
    total, depth = h_all.shape
    width = pieces[0].shape[1] // 2
    rows = min(256, total)
    return call(
        functools.partial(v_kernel, len(pieces)),
        [like((total, width), BF16), like((depth, width), BF16), like((depth, width), BF16)],
        [h_all, *pieces],
        2 * total * depth * width,
        "v_project",
        after=after,
        scalars=(ids,),
        grid=(total // rows,),
        in_specs=[pl.BlockSpec((rows, depth), lambda i, ids: (i, 0))] + [None] * len(pieces),
        out_specs=[pl.BlockSpec((rows, width), lambda i, ids: (i, 0)), None, None],
    )


def out_kernel(n_ep, ids, attn_ref, x_ref, gain_ref, *refs):
    weights, (one_ref, low_ref) = refs[:-2], refs[-2:]
    width = weights[0].shape[1]
    for j, weight in enumerate(weights):
        cols = block_at(ids, n_ep + j, width)
        one_ref[:, cols] = x_ref[:, cols].astype(F32) + product(attn_ref[...], weight[...])
    one = one_ref[...]
    scale = lax.rsqrt(jnp.mean(one * one, axis=1, keepdims=True) + EPS)
    low_ref[...] = (one * scale * gain_ref[...]).astype(BF16)


def out_project(ids, n_ep, attn_tok, tokens, gain, weights, after):
    return call(
        functools.partial(out_kernel, n_ep),
        [like(tokens.shape, F32), like(tokens.shape, BF16)],
        [attn_tok, tokens, gain, *weights],
        2 * tokens.size * attn_tok.shape[1],
        "out_project",
        after=after,
        scalars=(ids,),
    )


def out_back_kernel(n_ep, ids, d_ref, *refs):
    weights, d_attn_ref = refs[:-1], refs[-1]
    width = weights[0].shape[1]
    total = None
    for j, weight in enumerate(weights):
        part = product_right(d_ref[:, block_at(ids, n_ep + j, width)], weight[...])
        total = part if total is None else total + part
    d_attn_ref[...] = total.astype(BF16)


def out_back(ids, n_ep, d_z, weights, after):
    return call(
        functools.partial(out_back_kernel, n_ep),
        like((d_z.shape[0], weights[0].shape[0]), BF16),
        [d_z, *weights],
        2 * d_z.size * weights[0].shape[0],
        "out_back",
        after=after,
        scalars=(ids,),
    )


def vo_grads_kernel(count, ids, h_ref, dv_ref, attn_ref, dz_ref, *pieces):
    shard = pieces[0].shape[0]
    width = dv_ref.shape[1]
    for k in range(count):
        block = block_at(ids, k, shard)
        pieces[k][:, :width] = product_left(h_ref[:, block], dv_ref[...]).astype(BF16)
        pieces[k][:, width:] = product_left(attn_ref[:, block], dz_ref[...]).astype(BF16)


def vo_grads(ids, count, h_all, d_v, attn_all, d_z_cols):
    shard = h_all.shape[1] // count
    width = d_v.shape[1]
    return call(
        functools.partial(vo_grads_kernel, count),
        [like((shard, 2 * width), BF16)] * count,
        [h_all, d_v, attn_all, d_z_cols],
        4 * h_all.size * width,
        "vo_grads",
        scalars=(ids,),
    )


def qk_back_kernel(
    count, width_all, ids, h_ref, dqn_ref, dkn_ref, qr_ref, kr_ref, scale_ref, sums_ref,
    tiny_ref, *refs
):
    pieces, d_ref = refs[:count], refs[count]
    width = dqn_ref.shape[1]
    scales = jnp.transpose(scale_ref[...])
    means = jnp.transpose(sums_ref[...]) * (1.0 / width_all)
    for at, (d_normed, raw) in enumerate(((dqn_ref, qr_ref), (dkn_ref, kr_ref))):
        scale, mean = scales[:, 8 * at : 8 * at + 1], means[:, 8 * at : 8 * at + 1]
        d_ref[:, at * width : (at + 1) * width] = (
            scale * (d_normed[...] - raw[...] * scale * mean)
        ).astype(BF16)
    shard = h_ref.shape[1] // count
    per_row = 2 * width // shard
    for k in range(count):
        block = block_at(ids, k, shard)
        pieces[k][:shard, :] = product_left(h_ref[:, block], d_ref[...]).astype(BF16)
        pieces[k][shard:, :] = jnp.zeros_like(pieces[k][shard:, :])
        for at in range(tiny_ref.shape[0]):
            row, col = shard + at // per_row, (at % per_row) * shard
            pieces[k][row : row + 1, col : col + shard] = tiny_ref[at : at + 1, block].astype(BF16)


def qk_back(ids, count, h_all, d_qn, d_kn, q_raw, k_raw, scales, sums, tiny, after):
    total, depth = h_all.shape
    width = d_qn.shape[1]
    shard = depth // count
    extra = -(-tiny.shape[0] // (2 * width // shard))
    extra = -(-extra // 16) * 16
    return call(
        functools.partial(qk_back_kernel, count, depth),
        [like((shard + extra, 2 * width), BF16)] * count + [like((total, 2 * width), BF16)],
        [h_all, d_qn, d_kn, q_raw, k_raw, scales, sums, tiny],
        2 * h_all.size * 2 * width,
        "qk_back",
        scalars=(ids,),
        after=after,
    )


def d_h_kernel(d_ref, dv_ref, qk_ref, v_ref, out_ref):
    out_ref[...] = (
        product_right(d_ref[...], qk_ref[...]) + product_right(dv_ref[...], v_ref[...])
    ).astype(BF16)


def d_h_rows(d_qk, d_v, w_qk, w_v, after):
    total, wide = d_qk.shape
    depth = w_qk.shape[0]
    rows = min(256, total)
    return call(
        d_h_kernel,
        like((total, depth), BF16),
        [d_qk, d_v, w_qk, w_v],
        3 * d_qk.size * depth,
        "d_h",
        after=after,
        grid=(total // rows,),
        in_specs=[
            pl.BlockSpec((rows, wide), lambda i: (i, 0)),
            pl.BlockSpec((rows, d_v.shape[1]), lambda i: (i, 0)), None, None,
        ],
        out_specs=[pl.BlockSpec((rows, depth), lambda i: (i, 0))],
    )


def finish_kernel(n_ep, n_sp, ids, wq_ref, wk_ref, wv_ref, gain_ref, *refs):
    firsts, seconds = refs[:n_sp], refs[n_sp : 2 * n_sp]
    gq_ref, gk_ref, gv_ref, go_ref, tiny_ref, attn_ref = refs[2 * n_sp :]
    shard = wq_ref.shape[0]
    width = firsts[0].shape[1] // 2
    dots = jnp.zeros((shard, 1), F32)
    tiny = jnp.zeros(tiny_ref.shape, F32)
    for j in range(n_sp):
        cols = block_at(ids, n_ep + j, width)
        for at, grad, weight in ((0, gq_ref, wq_ref), (1, gk_ref, wk_ref), (2, gv_ref, wv_ref)):
            part = firsts[j][:shard, at * width : (at + 1) * width] if at < 2 else seconds[j][:, :width]
            value = part.astype(F32)
            grad[:, cols] = value
            dots += jnp.sum(value * weight[:, cols].astype(F32), axis=1, keepdims=True)
        go_ref[:, cols] = seconds[j][:, width:].astype(F32)
        tiny += firsts[j][shard:, :].astype(F32)
    tiny_ref[...] = tiny
    attn_ref[...] = dots / gain_ref[...]


def finish(ids, n_ep, w_query, w_key, w_value, gain, firsts, seconds, after):
    shard, depth = w_query.shape
    extra = firsts[0].shape[0] - shard
    return call(
        functools.partial(finish_kernel, n_ep, len(firsts)),
        [like((shard, depth), F32)] * 4 + [like((extra, firsts[0].shape[1]), F32), like((shard, 1), F32)],
        [w_query, w_key, w_value, gain, *firsts, *seconds],
        shard * depth * 6,
        "finish",
        after=after,
        scalars=(ids,),
    )


def turn(values_in):
    return pltpu.roll(values_in, HEAD_DIM // 2, 1)


def masked_probs(q_ref, k_ref, start_ref, block, rows):
    first, last = block * rows, (block + 1) * rows
    scores = product_right(q_ref[first:last, :], k_ref[0:last, :]) * (HEAD_DIM ** (-0.5))
    row_ids = first + lax.broadcasted_iota(jnp.int32, scores.shape, 0)
    places = lax.broadcasted_iota(jnp.int32, scores.shape, 1)
    allowed = (places <= row_ids) & (places >= start_ref[first:last, :])
    scores = jnp.where(allowed, scores, NEG_FILL)
    top = jnp.max(scores, axis=1, keepdims=True)
    weights = jnp.exp(scores - top)
    return weights * (1.0 / jnp.sum(weights, axis=1, keepdims=True))


def attend_kernel(
    rows, qr_ref, kr_ref, v_ref, scale_ref, gq_ref, gk_ref, cos_ref, sin_ref, start_ref,
    q_ref, k_ref, out_ref,
):
    scales = jnp.transpose(scale_ref[...])
    for at, (raw, gain, low) in enumerate(((qr_ref, gq_ref, q_ref), (kr_ref, gk_ref, k_ref))):
        normed = raw[...] * scales[:, 8 * at : 8 * at + 1] * gain[...]
        low[...] = (normed * cos_ref[...] + turn(normed) * sin_ref[...]).astype(BF16)
    for block in range(q_ref.shape[0] // rows):
        probs = masked_probs(q_ref, k_ref, start_ref, block, rows)
        last = (block + 1) * rows
        out_ref[block * rows : last, :] = product(
            probs.astype(BF16), v_ref[0:last, :]
        ).astype(BF16)


def head_spec(rows):
    return pl.BlockSpec((rows, HEAD_DIM), lambda h: (0, h))


def attend(q_raw, k_raw, v_low, scales, q_gain, k_gain, cosine, sine, starts):
    total, width = v_low.shape
    heads = width // HEAD_DIM
    head, gain = head_spec(total), head_spec(1)
    return call(
        functools.partial(attend_kernel, min(256, total)),
        [like((total, width), BF16)] * 3,
        [q_raw, k_raw, v_low, scales, q_gain, k_gain, cosine, sine, starts],
        3 * heads * total * total * HEAD_DIM,
        "attend",
        grid=(heads,),
        in_specs=[head, head, head, None, gain, gain, None, None, None],
        out_specs=[head, head, head],
    )


def attend_back_kernel(
    rows, q_ref, k_ref, v_ref, do_ref, qr_ref, kr_ref, scale_ref, gq_ref, gk_ref,
    cos_ref, sin_ref, start_ref,
    dq_ref, dk_ref, dv_ref, sums_ref, dgq_ref, dgk_ref, q_acc, k_acc, v_acc,
):
    k_acc[...] = jnp.zeros_like(k_acc)
    v_acc[...] = jnp.zeros_like(v_acc)
    for block in range(q_ref.shape[0] // rows):
        first, last = block * rows, (block + 1) * rows
        probs = masked_probs(q_ref, k_ref, start_ref, block, rows)
        d_rows = do_ref[first:last, :]
        d_probs = product_right(d_rows, v_ref[0:last, :])
        delta = jnp.sum(probs * d_probs, axis=1, keepdims=True)
        d_scores = (probs * (d_probs - delta) * (HEAD_DIM ** (-0.5))).astype(BF16)
        q_acc[first:last, :] = product(d_scores, k_ref[0:last, :])
        k_acc[0:last, :] += product_left(d_scores, q_ref[first:last, :])
        v_acc[0:last, :] += product_left(probs.astype(BF16), d_rows)
    dv_ref[...] = v_acc[...].astype(BF16)

    @pl.when(pl.program_id(0) == 0)
    def _():
        sums_ref[...] = jnp.zeros_like(sums_ref)

    scales = jnp.transpose(scale_ref[...])
    for at, (acc, raw, gain, d_ref, dg_ref) in enumerate(
        ((q_acc, qr_ref, gq_ref, dq_ref, dgq_ref), (k_acc, kr_ref, gk_ref, dk_ref, dgk_ref))
    ):
        turned = acc[...].astype(BF16).astype(F32)
        back = turned * cos_ref[...] + turn(turned * sin_ref[...])
        normed = raw[...] * scales[:, 8 * at : 8 * at + 1]
        both = back * normed
        dg_ref[...] = jnp.sum(both, axis=0, keepdims=True)
        d_ref[...] = back * gain[...]
        sums_ref[8 * at : 8 * at + 8, :] += row_sums(both * gain[...])


def attend_back(
    q_rot, k_rot, v_low, d_heads, q_raw, k_raw, scales, q_gain, k_gain, cosine, sine, starts
):
    total, width = v_low.shape
    heads = width // HEAD_DIM
    head, gain = head_spec(total), head_spec(1)
    wide, thin = like((total, width), F32), like((1, width), F32)
    return call(
        functools.partial(attend_back_kernel, min(256, total)),
        [wide, wide, like((total, width), BF16), like((16, total), F32), thin, thin],
        [q_rot, k_rot, v_low, d_heads, q_raw, k_raw, scales, q_gain, k_gain, cosine, sine, starts],
        7 * heads * total * total * HEAD_DIM,
        "attend_back",
        scratch=[pltpu.VMEM((total, HEAD_DIM), F32)] * 3,
        grid=(heads,),
        in_specs=[head] * 6 + [None, gain, gain, None, None, None],
        out_specs=[head, head, head, None, gain, gain],
    )


def chooser(places_ref, at, cap):
    row = places_ref[at : at + 1, :]
    slots = lax.broadcasted_iota(jnp.int32, (cap, row.shape[1]), 0)
    return slots == row


def dispatch_kernel(
    pieces_here, local, cap, gated, mine, *refs
):
    pieces, refs = refs[:pieces_here], refs[pieces_here:]
    places_ref, refs = refs[0], refs[1:]
    if gated:
        (picked_ref, router_ref), refs = refs[:2], refs[2:]
        rows_ref, gate_ref, all_ref = refs[-3:]
    else:
        rows_ref = refs[-1]
    for p in range(pieces_here):
        if gated:
            logits = product_right(router_ref[...], pieces[p][...])
            experts = logits.shape[0]
            picked = picked_ref[p * experts : (p + 1) * experts, :] > 0
            logits = jnp.where(picked, logits, NEG_FILL)
            weights = jnp.exp(logits - jnp.max(logits, axis=0, keepdims=True))
            weights = jnp.where(picked, weights, 0.0)
            gates = weights / jnp.sum(weights, axis=0, keepdims=True)
            all_ref[p * experts : (p + 1) * experts, :] = gates
        for e in range(local):
            chosen = chooser(places_ref, p * local + e, cap)
            rows_ref[e, p * cap : (p + 1) * cap, :] = product(
                chosen.astype(BF16), pieces[p][...]
            ).astype(BF16)
            if gated:
                row = all_ref[pl.ds(p * experts + mine[0] * local + e, 1), :]
                gate_ref[e, p * cap : (p + 1) * cap, :] = jnp.sum(
                    jnp.where(chosen, row, 0.0), axis=1, keepdims=True
                )


def dispatch(mine, pieces, places, picked, router, local, cap, group, at, rows, gates, after=()):
    gated = router is not None
    here = len(pieces)
    width = pieces[0].shape[1]
    args = [*pieces, places]
    shapes = [like((local, group * cap, width), BF16)]
    spec = pl.BlockSpec((local, here * cap, width), lambda i, mine: (0, at, 0))
    out_specs = [spec]
    if gated:
        args += [picked, router]
        shapes += [like((local, group * cap, 1), F32), like((picked.shape[0], places.shape[1]), F32)]
        out_specs += [pl.BlockSpec((local, here * cap, 1), lambda i, mine: (0, at, 0)), None]
    in_specs = [None] * len(args)
    aliases = {}
    if rows is not None:
        aliases[len(args)] = 0
        args.append(rows)
        in_specs.append(pl.BlockSpec(memory_space=pl.ANY))
        if gated:
            aliases[len(args)] = 1
            args.append(gates)
            in_specs.append(pl.BlockSpec(memory_space=pl.ANY))
    return call(
        functools.partial(dispatch_kernel, here, local, cap, gated),
        shapes,
        args,
        2 * here * local * cap * places.shape[1] * width,
        "dispatch",
        scalars=(mine,),
        in_specs=in_specs,
        out_specs=out_specs,
        aliases=aliases,
        after=after,
    )


def expert_kernel(
    x_ref, d_ref, gate_ref, wg_ref, wu_ref, wd_ref,
    act_ref, dg_ref, du_ref, dots_ref, mix_ref, back_ref, mix_acc, back_acc,
):
    step = pl.program_id(1)
    last = pl.num_programs(1) - 1
    x_rows, d_rows, gate = x_ref[0], d_ref[0], gate_ref[0]
    pre = product(x_rows, wg_ref[0])
    up = product(x_rows, wu_ref[0])
    pulled = product_right(d_rows, wd_ref[0])
    sigma = jax.nn.sigmoid(pre)
    silu = pre * sigma
    act = silu * up
    dots = jnp.sum(act * pulled, axis=1, keepdims=True)
    act_low = (act * gate).astype(BF16)
    act_ref[0] = act_low
    d_act = pulled * gate
    du_low = (d_act * silu).astype(BF16)
    dg_low = (d_act * up * sigma * (1.0 + pre * (1.0 - sigma))).astype(BF16)
    dg_ref[0] = dg_low
    du_ref[0] = du_low
    mix = product(act_low, wd_ref[0])
    back = product_right(dg_low, wg_ref[0]) + product_right(du_low, wu_ref[0])

    @pl.when(step == 0)
    def _():
        dots_ref[0] = dots
        mix_acc[...] = mix
        back_acc[...] = back

    @pl.when((step > 0) & (step < last))
    def _():
        dots_ref[0] += dots
        mix_acc[...] += mix
        back_acc[...] += back

    @pl.when(step == last)
    def _():
        dots_ref[0] += dots
        mix_ref[0] = (mix_acc[...] + mix).astype(BF16)
        back_ref[0] = (back_acc[...] + back).astype(BF16)


def experts(rows, d_rows, gates, w_gate, w_up, w_down, after=()):
    local, count, width = rows.shape
    hidden = w_gate.shape[2]
    part = hidden // 2
    wide = pl.BlockSpec((1, count, width), lambda e, f: (e, 0, 0))
    column = pl.BlockSpec((1, count, 1), lambda e, f: (e, 0, 0))
    thin = pl.BlockSpec((1, count, part), lambda e, f: (e, 0, f))
    into = pl.BlockSpec((1, width, part), lambda e, f: (e, 0, f))
    outof = pl.BlockSpec((1, part, width), lambda e, f: (e, f, 0))
    return call(
        expert_kernel,
        [like((local, count, hidden), BF16)] * 3
        + [like((local, count, 1), F32)]
        + [like((local, count, width), BF16)] * 2,
        [rows, d_rows, gates, w_gate, w_up, w_down],
        12 * rows.size * hidden,
        "experts",
        after=after,
        scratch=[pltpu.VMEM((count, width), F32)] * 2,
        grid=(local, 2),
        in_specs=[wide, wide, column, into, into, outof],
        out_specs=[thin, thin, thin, column, wide, wide],
    )


def combine_kernel(here, local, cap, dotted, places_ref, rows_ref, *refs):
    pieces = refs[int(dotted) : int(dotted) + here]
    for p in range(here):
        chosen = [chooser(places_ref, p * local + e, cap) for e in range(local)]
        total = None
        for e in range(local):
            part = product_left(chosen[e].astype(BF16), rows_ref[e, p * cap : (p + 1) * cap, :])
            total = part if total is None else total + part
            if dotted:
                refs[-1][p * local + e : p * local + e + 1, :] = jnp.sum(
                    jnp.where(chosen[e], refs[0][e, p * cap : (p + 1) * cap, :], 0.0),
                    axis=0, keepdims=True,
                )
        pieces[p][...] = total.astype(BF16)


def combine(places, rows, here, local, cap, at, dots=None, after=()):
    width = rows.shape[2]
    tokens = places.shape[1]
    dotted = dots is not None
    args = [places, rows] + ([dots] if dotted else [])
    in_specs = [None, pl.BlockSpec((local, here * cap, width), lambda i: (0, at, 0))]
    if dotted:
        in_specs.append(pl.BlockSpec((local, here * cap, 1), lambda i: (0, at, 0)))
    shapes = [like((tokens, width), BF16)] * here
    if dotted:
        shapes.append(like(places.shape, F32))
    return call(
        functools.partial(combine_kernel, here, local, cap, dotted),
        shapes,
        args,
        2 * here * local * cap * tokens * width,
        "combine",
        after=after,
        in_specs=in_specs,
    )


def weight_grad_kernel(groups, *refs):
    lefts, rights = refs[:groups], refs[groups : 2 * groups]
    total = None
    for left, right in zip(lefts, rights):
        part = product_left(left[0], right[0])
        total = part if total is None else total + part
    refs[-1][0] = total.astype(BF16)


def weight_grad(lefts, rights, after=()):
    local, count, tall = lefts[0].shape
    wide = rights[0].shape[2]
    part = min(512, tall)
    left = pl.BlockSpec((1, count, part), lambda e, i: (e, 0, i))
    right = pl.BlockSpec((1, count, wide), lambda e, i: (e, 0, 0))
    return call(
        functools.partial(weight_grad_kernel, len(lefts)),
        like((local, tall, wide), BF16),
        [*lefts, *rights],
        2 * len(lefts) * lefts[0].size * wide,
        "weight_grad",
        after=after,
        grid=(local, tall // part),
        in_specs=[left] * len(lefts) + [right] * len(lefts),
        out_specs=[pl.BlockSpec((1, part, wide), lambda e, i: (e, i, 0))],
    )


def body(
    tokens, doc_lengths, routes, attn_gain, w_query, w_key, w_value, q_gain, k_gain, w_out,
    ffn_gain, w_router, w_gate, w_up, w_down, cotangent,
):
    n_sp = lax.axis_size("sp")
    n_ep = lax.axis_size("ep")
    sp_index = lax.axis_index("sp")
    ep_index = lax.axis_index("ep")
    tok_dev, width = tokens.shape[1:]
    total = tok_dev * n_sp
    shard = width // n_ep
    head_width = width // n_sp
    top_count = routes.shape[2]
    local = w_gate.shape[0]
    expert_count = local * n_ep
    capacity = 9 * tok_dev * top_count // (8 * expert_count)
    cap = -(-capacity // 16) * 16
    group = 4
    blocks = piece_blocks(n_ep, ep_index)
    partners = jnp.bitwise_xor(jnp.arange(n_sp, dtype=jnp.int32), sp_index)
    ids = jnp.concatenate([blocks, partners]).astype(jnp.int32)
    mine = ep_index.astype(jnp.int32).reshape(1)

    def own_columns(value):
        return lax.dynamic_slice_in_dim(value, sp_index * head_width, head_width, 1)

    def by_piece(value):
        return jnp.stack(
            [lax.dynamic_index_in_dim(value, blocks[i], 0, keepdims=False) for i in range(n_ep)]
        )

    expert_ids = jnp.arange(expert_count, dtype=jnp.int32)
    picked = jnp.any(routes[0][:, :, None] == expert_ids[None, None, :], axis=1)
    picked_low = picked.T.astype(BF16)
    small = jnp.concatenate(
        [
            jnp.stack([attn_gain, q_gain, k_gain, ffn_gain]),
            jnp.zeros((12, shard), BF16),
            w_router.T,
        ],
        axis=0,
    )

    def to_all(value):
        value = jnp.broadcast_to(value[None], (n_ep, *value.shape))
        return lax.all_to_all(value, "ep", split_axis=0, concat_axis=0, tiled=True)

    if shard == tok_dev:
        both = to_all(jnp.concatenate([small, picked_low], axis=0))
        small_all, picked_all = both[:, : 16 + expert_count], both[:, 16 + expert_count :]
    else:
        small_all, picked_all = to_all(small), to_all(picked_low)
    small_rows = jnp.swapaxes(small_all, 0, 1).reshape(16 + expert_count, width)
    gains = small_rows[:4].astype(F32)
    full_router = small_rows[16:]
    picked_all = by_piece(picked_all)

    x_all = lax.all_gather(tokens[0], "sp", axis=0, tiled=True)
    qk_own = jnp.concatenate([own_columns(w_query), own_columns(w_key)], axis=1)
    vo_own = jnp.concatenate([own_columns(w_value), own_columns(w_out)], axis=1)
    cot_own = cotangent[0]
    if n_ep == 8:
        own_x, near, far = swap(qk_own, 1), swap(qk_own, 2), swap(qk_own, 4)
        own_x, near, far = tie(own_x, near, far)
        farther = swap(far, 2)
        farther, vo_own = tie(farther, vo_own)
        near_x, far_x, farther_x = swap(near, 1), swap(far, 1), swap(farther, 1)
        near_x, far_x, farther_x, vo_own_x = tie(near_x, far_x, farther_x, vo_own)
        qk_pieces = [qk_own, own_x, near, near_x, far, far_x, farther, farther_x]
        vo_blocks = along_z(vo_own)
        vo_crossed, vo_blocks[2] = tie(swap(vo_own_x, 1), vo_blocks[2])
        vo_blocks[3] = swap(vo_blocks[2], 2)
        vo_crossed, vo_blocks[1], vo_blocks[3] = tie(vo_crossed, vo_blocks[1], vo_blocks[3])
        q_raw, k_raw, squares, w_qk, h_all = qk_project(ids, x_all, gains[0:1], qk_pieces)
        vo_crossed, squares = tie(vo_crossed, squares)
        vo_others = along_z(vo_crossed)
        vo_pieces = [piece for two in zip(vo_blocks, vo_others) for piece in two]
        vo_pieces[7], cot_own = tie(vo_pieces[7], cot_own)
        cot_blocks = along_z(cot_own)
        cot_pieces = across_x(cot_blocks)
    else:
        qk_pieces, vo_pieces, cot_pieces = (
            gather_whole(value) for value in (qk_own, vo_own, cot_own)
        )
        q_raw, k_raw, squares, w_qk, h_all = qk_project(ids, x_all, gains[0:1], qk_pieces)
    upper = (
        jnp.arange(tok_dev, dtype=jnp.int32)[:, None] < jnp.arange(tok_dev, dtype=jnp.int32)[None, :]
    ).astype(BF16)
    picked_mine = lax.dynamic_slice_in_dim(picked_all, ep_index * local, local, 1)
    picked_mine = picked_mine.reshape(n_ep * local, tok_dev)
    earlier = product(picked_mine, upper).astype(jnp.int32)
    places = jnp.where((picked_mine > 0) & (earlier < capacity), earlier, -1)
    picked_flat = picked_all.reshape(n_ep * expert_count, tok_dev).astype(F32)

    positions = jnp.arange(total, dtype=jnp.int32)
    lengths = doc_lengths[0]
    doc_ends = jnp.cumsum(lengths)
    starts = jnp.sum(
        jnp.where(doc_ends[None, :] <= positions[:, None], lengths[None, :], 0), axis=1
    )
    half = HEAD_DIM // 2
    frequency = THETA ** (-(2.0 * jnp.arange(half, dtype=F32)) / HEAD_DIM)
    angles = (positions - starts).astype(F32)[:, None] * frequency[None, :]
    cosine = jnp.concatenate([jnp.cos(angles), jnp.cos(angles)], axis=1)
    sine = jnp.concatenate([-jnp.sin(angles), jnp.sin(angles)], axis=1)
    starts = starts[:, None].astype(jnp.int32)

    scales = lax.rsqrt(sum_sp(squares) / width + EPS)
    v_low, w_v, w_o = v_project(ids, h_all, vo_pieces, [q_raw])
    w_o_parts = gather_sp(w_o)
    gain_q, gain_k = own_columns(gains)[1:2], own_columns(gains)[2:3]
    q_rot, k_rot, mixed = attend(
        q_raw, k_raw, v_low, scales, gain_q, gain_k, cosine, sine, starts
    )

    def pair_places(p):
        return places[p * local : (p + 2) * local]

    def cot_rows(g, after):
        d_rows = None
        for at, p in enumerate(range(g, g + group, 2)):
            (d_rows,) = dispatch(
                mine, cot_pieces[p : p + 2], pair_places(p), None, None, local, cap, group, at,
                d_rows, None, after,
            )
        return d_rows

    attn_tok = lax.all_to_all(mixed, "sp", split_axis=0, concat_axis=1, tiled=True)
    near_rows = cot_rows(0, [mixed])
    x_one, h2_low = out_project(
        ids, n_ep, attn_tok, tokens[0], gains[3:4], w_o_parts, [near_rows]
    )
    attn_all = lax.all_gather(attn_tok, "sp", axis=0, tiled=True)

    h2_pieces = gather(h2_low, n_ep)
    cots = [near_rows] + [cot_rows(g, [x_one]) for g in range(group, n_ep, group)]
    groups, d_pieces, d_gates, d_sums = [], [], [], []
    home_gates = None

    def rows_of(g, after):
        rows = gates = first_gates = None
        for at, p in enumerate(range(g, g + group, 2)):
            rows, gates, piece_gates = dispatch(
                mine, h2_pieces[p : p + 2], pair_places(p),
                picked_flat[p * expert_count : (p + 2) * expert_count], full_router, local, cap,
                group, at, rows, gates, after,
            )
            first_gates = piece_gates if first_gates is None else first_gates
        return rows, gates, first_gates

    rows, gates, home_gates = rows_of(0, [])
    for g in range(0, n_ep, group):
        d_rows = cots[g // group]
        made = experts(rows, d_rows, gates, w_gate, w_up, w_down, d_pieces[-group:] + cots)
        groups.append((rows, d_rows, made))
        following = []
        if g + group < n_ep:
            rows, gates, _ = rows_of(g + group, [made[5]])
            following = [rows]
        sums_before = list(d_sums)
        for at in range(group // 2):
            *two, dots = combine(
                pair_places(g + 2 * at), made[5], 2, local, cap, at, made[3],
                sums_before + following,
            )
            d_pieces += two
            d_gates.append(dots)
        if n_ep == 8:
            d_sums += crossed_sums(d_pieces[-group:])

    acts = [made[0] for _, _, made in groups]
    d_gate_rows = [made[1] for _, _, made in groups]
    d_up_rows = [made[2] for _, _, made in groups]
    ins = [rows for rows, _, _ in groups]
    outs = [d_rows for _, d_rows, _ in groups]
    grad_down = weight_grad(acts, outs, d_pieces)
    d_gates = by_piece(jnp.concatenate(d_gates, axis=0).reshape(n_ep, local, tok_dev))
    d_gates = lax.all_to_all(d_gates, "ep", split_axis=0, concat_axis=0, tiled=True)
    d_gates = d_gates.reshape(expert_count, tok_dev)
    grad_gate = weight_grad(ins, d_gate_rows, [grad_down, d_gates])
    mix_pieces = []
    for g, (_, _, made) in enumerate(groups):
        for at in range(group // 2):
            mix_pieces += combine(
                pair_places(g * group + 2 * at), made[4], 2, local, cap, at, None,
                [grad_gate, *d_sums],
            )
    if n_ep == 8:
        *d_sums, mix_pieces[1], mix_pieces[3], mix_pieces[5], mix_pieces[7] = tie(
            *d_sums, mix_pieces[1], mix_pieces[3], mix_pieces[5], mix_pieces[7]
        )
        mix_pieces[0], grad_down, grad_gate = tie(mix_pieces[0], grad_down, grad_gate)
        mix_sums = crossed_sums(mix_pieces)
        d_h2 = scatter_z(*d_sums)
    else:
        d_h2 = scatter(d_pieces, n_ep)
    grad_up = weight_grad(ins, d_up_rows, mix_pieces)

    def over_sp(value):
        return lax.psum_scatter(value, "sp", scatter_dimension=1, tiled=True).astype(F32)


    if n_ep == 8:
        gates_here = home_gates[:expert_count]
    else:
        logits = product_right(full_router, h2_low)
        logits = jnp.where(picked.T, logits, NEG_FILL)
        gates_here = jax.nn.softmax(logits, axis=0)
    d_logits = gates_here * (d_gates - jnp.sum(gates_here * d_gates, axis=0, keepdims=True))
    d_logits = jnp.where(picked.T, d_logits, 0.0).astype(BF16)
    grad_router = product(d_logits, h2_low)
    d_h2 = d_h2 + product_left(d_logits, full_router)
    one_scale = lax.rsqrt(jnp.mean(x_one * x_one, axis=-1, keepdims=True) + EPS)
    one_normed = x_one * one_scale
    grad_ffn = jnp.sum(d_h2 * one_normed, axis=0)
    d_normed = d_h2 * gains[3][None, :]
    d_one = cotangent[0].astype(F32) + one_scale * (
        d_normed - one_normed * jnp.mean(d_normed * one_normed, axis=-1, keepdims=True)
    )
    d_z, grad_up = tie(d_one.astype(BF16), grad_up)
    d_attn = out_back(ids, n_ep, d_z, w_o_parts, [grad_up, grad_gate, grad_down, *mix_pieces])
    d_heads = lax.all_to_all(d_attn, "sp", split_axis=1, concat_axis=0, tiled=True)
    d_z_cols = lax.all_to_all(d_z, "sp", split_axis=1, concat_axis=0, tiled=True)
    if n_ep == 8:
        *mix_sums, d_heads = tie(*mix_sums, d_heads)
    grad_down, grad_gate, grad_up = over_sp(grad_down), over_sp(grad_gate), over_sp(grad_up)

    d_qn, d_kn, d_v, sums, grad_qg, grad_kg = attend_back(
        q_rot, k_rot, v_low, d_heads, q_raw, k_raw, scales, gain_q, gain_k, cosine, sine, starts
    )
    if n_ep == 8:
        own, near, far, farther = mix_sums
        far, d_v = tie(plus(far, swap(farther, 2)), d_v)
        mix = own.astype(F32) + swap(near, 2).astype(F32) + swap(far, 4).astype(F32)
    else:
        mix = scatter(mix_pieces, n_ep)
    output = (x_one + mix).astype(BF16)
    vo_pieces = vo_grads(ids, n_ep, h_all, d_v, attn_all, d_z_cols)
    grad_vo = scatter_x_last(vo_pieces, n_ep).astype(BF16)

    def placed(value):
        return lax.dynamic_update_slice_in_dim(
            jnp.zeros((1, width), F32), value, sp_index * head_width, 1
        )

    tiny = jnp.concatenate(
        [placed(grad_qg), placed(grad_kg), grad_ffn[None], grad_router], axis=0
    )
    *qk_pieces, d_qk = qk_back(
        ids, n_ep, h_all, d_qn, d_kn, q_raw, k_raw, scales, sum_sp(sums), tiny, vo_pieces[-1:]
    )
    grad_qk = scatter(qk_pieces, n_ep).astype(BF16)

    d_h = d_h_rows(d_qk, d_v, w_qk, w_v, [])
    output, d_h = tie(output, d_h)
    d_h = d_h.reshape(n_sp, tok_dev, width)
    parts = [
        lax.dynamic_index_in_dim(d_h, partners[j], 0, keepdims=False) for j in range(4)
    ]
    kept = plus(parts[0], swap_sp(parts[1], 1))
    sent = plus(parts[2], swap_sp(parts[3], 1))
    d_h = kept.astype(F32) + swap_sp(sent, 2).astype(F32)
    x_rows = tokens[0].astype(F32)
    x_scale = lax.rsqrt(jnp.mean(x_rows * x_rows, axis=-1, keepdims=True) + EPS)
    x_normed = x_rows * x_scale
    d_normed = d_h * gains[0][None, :]
    input_grad = d_one + x_scale * (
        d_normed - x_normed * jnp.mean(d_normed * x_normed, axis=-1, keepdims=True)
    )

    g_query, g_key, g_value, g_out, tiny, g_attn = finish(
        ids, n_ep, w_query, w_key, w_value, attn_gain.astype(F32)[:, None],
        gather_sp(grad_qk), gather_sp(grad_vo), [grad_down, grad_gate, grad_up, input_grad],
    )
    per_row = 2 * head_width // shard

    def vector(at):
        col = (at % per_row) * shard
        return tiny[at // per_row, col : col + shard]

    g_router = jnp.stack([vector(3 + i) for i in range(expert_count)], axis=1)
    return (
        output[None], input_grad[None], g_attn[:, 0], g_query, g_key, g_value, vector(0), vector(1),
        g_out, vector(2), g_router, grad_gate, grad_up, grad_down,
    )


def solution(mesh):
    seq = P("ep", "sp", None)
    vec = P("ep")
    mat = P("ep", None)
    expert = P("ep", None, None)
    in_specs = (
        seq, mat, seq, vec, mat, mat, mat, vec, vec, mat, vec, mat, expert, expert, expert, seq,
    )
    out_specs = (
        seq, seq, vec, mat, mat, mat, vec, vec, mat, vec, mat, seq, seq, seq,
    )
    return jax.shard_map(body, mesh=mesh, in_specs=in_specs, out_specs=out_specs, check_vma=False)
```

```python
import functools

import jax
import jax.numpy as jnp
from jax import lax
from jax.experimental import pallas as pl
from jax.experimental.pallas import tpu as pltpu
from jax.sharding import PartitionSpec as P

HEAD_DIM = 128
EPS = 1e-05
THETA = 10000.0
NEG_FILL = -1e30
F32 = jnp.float32
BF16 = jnp.bfloat16
MIB = 1 << 20
COVER = 20


def product(left, right):
    return jnp.dot(left, right, preferred_element_type=F32)


def product_left(left, right):
    return lax.dot_general(left, right, (((0,), (0,)), ((), ())), preferred_element_type=F32)


def product_right(left, right):
    return lax.dot_general(left, right, (((1,), (1,)), ((), ())), preferred_element_type=F32)


def row_sums(values_in):
    sums = jnp.sum(values_in, axis=1, keepdims=True)
    return jnp.transpose(jnp.broadcast_to(sums, (sums.shape[0], HEAD_DIM)))[:8]


def call(kernel, out_shape, args, flops, name, scratch=(), scalars=(), grid=(1,), in_specs=None,
         out_specs=None, aliases=None, vmem=60, after=()):
    single = not isinstance(out_shape, (list, tuple))
    shapes = [out_shape] if single else list(out_shape)
    count = len(grid)

    def fixed(shape):
        rank = len(shape)
        return pl.BlockSpec(tuple(shape), lambda *ids: (0,) * rank)

    in_specs = in_specs or [None] * len(args)
    out_specs = out_specs or [None] * len(shapes)
    in_specs = [s if s is not None else fixed(a.shape) for s, a in zip(in_specs, args)]
    out_specs = [s if s is not None else fixed(o.shape) for s, o in zip(out_specs, shapes)]
    waited = len(after)
    args = [*args, *after]
    in_specs = in_specs + [pl.BlockSpec(memory_space=pl.ANY)] * waited
    if waited:
        inner, first = kernel, len(scalars) + len(args) - waited

        def kernel(*refs):
            inner(*refs[:first], *refs[first + waited :])

    moved = sum(a.size * a.dtype.itemsize for a in args[: len(args) - waited])
    moved += sum(o.size * o.dtype.itemsize for o in shapes)
    result = pl.pallas_call(
        kernel,
        grid_spec=pltpu.PrefetchScalarGridSpec(
            num_scalar_prefetch=len(scalars), grid=grid, in_specs=in_specs, out_specs=out_specs,
            scratch_shapes=list(scratch),
        ),
        out_shape=shapes,
        input_output_aliases={k + len(scalars): v for k, v in (aliases or {}).items()},
        compiler_params=pltpu.CompilerParams(
            vmem_limit_bytes=vmem * MIB, dimension_semantics=("arbitrary",) * count
        ),
        cost_estimate=pl.CostEstimate(flops=int(COVER * flops), bytes_accessed=int(moved), transcendentals=0),
        name=name,
    )(*scalars, *args)
    return result[0] if single else list(result)


def like(shape, dtype):
    return jax.ShapeDtypeStruct(tuple(shape), dtype)


def tie(*values):
    return lax.optimization_barrier(values)


def swap(value, bits):
    return lax.ppermute(value, "ep", [(i, i ^ bits) for i in range(8)])


def swap_sp(value, bits):
    return lax.ppermute(value, "sp", [(i, i ^ bits) for i in range(4)])


def piece_blocks(n_ep, ep_index):
    ids = jnp.arange(n_ep, dtype=jnp.int32)
    return jnp.bitwise_xor(ids, ep_index) if n_ep == 8 else ids


def along_z(value):
    far = swap(value, 4)
    return [value, swap(value, 2), far, swap(far, 2)]


def across_x(blocks):
    pieces = []
    for own in blocks:
        pieces += [own, swap(own, 1)]
    return pieces


def gather_whole(value):
    whole = lax.all_gather(value, "ep", axis=0, tiled=False)
    return [whole[i] for i in range(whole.shape[0])]


def gather(value, n_ep):
    if n_ep != 8:
        return gather_whole(value)
    blocks = along_z(value)
    near = across_x(blocks[:2])
    near[3], blocks[2], blocks[3] = tie(near[3], blocks[2], blocks[3])
    return near + across_x(blocks[2:])


def plus(left, right):
    return (left.astype(F32) + right.astype(F32)).astype(left.dtype)


def crossed_sums(pieces):
    return [plus(pieces[i], swap(pieces[i + 1], 1)) for i in range(0, len(pieces), 2)]


def scatter_z(own, near, far, farther):
    far = plus(far, swap(farther, 2))
    return own.astype(F32) + swap(near, 2).astype(F32) + swap(far, 4).astype(F32)


def scatter(pieces, n_ep):
    if n_ep != 8:
        stacked = jnp.stack(pieces)
        return lax.psum_scatter(stacked, "ep", scatter_dimension=0, tiled=False).astype(F32)
    return scatter_z(*crossed_sums(pieces))


def stack_at(piece, n_ep):
    if n_ep != 8:
        return 0, piece
    return 2 * (piece % 2) + (piece // 2) % 2, piece // 4


def stack_shapes(n_ep, shape):
    return [like((2, *shape), BF16)] * 4 if n_ep == 8 else [like((n_ep, *shape), BF16)]


def scatter_stacks(stacks, n_ep):
    if n_ep != 8:
        total = lax.psum_scatter(stacks[0], "ep", scatter_dimension=0, tiled=False)
        return total.astype(F32), None
    even, odd, even_sent, odd_sent = stacks
    odd = plus(odd, swap(odd_sent, 1))
    even = even.astype(F32) + swap(even_sent, 1).astype(F32) + swap(odd, 2).astype(F32)
    return even[0], even[1].astype(BF16)


def last_hop(total, far):
    return total if far is None else total + swap(far, 4).astype(F32)


def gather_sp(value):
    over = swap_sp(value, 2)
    return [value, swap_sp(value, 1), over, swap_sp(over, 1)]


def sum_sp(value):
    return (value + swap_sp(value, 1)) + (swap_sp(value, 2) + swap_sp(value, 3))


def block_at(ids, position, size):
    if size % HEAD_DIM:
        return pl.ds(position * size, size)
    return pl.ds(pl.multiple_of(ids[position] * size, size), size)


def qkv_kernel(count, ids, x_ref, gain_ref, *refs):
    pieces, refs = refs[:count], refs[count:]
    q_ref, k_ref, v_ref, squares_ref, w_ref, out_ref, h_ref = refs
    shard = pieces[0].shape[0]
    width = q_ref.shape[1]

    @pl.when(pl.program_id(0) == 0)
    def _():
        for k in range(count):
            rows = block_at(ids, k, shard)
            w_ref[rows, :] = pieces[k][:, : 3 * width]
            out_ref[rows, :] = pieces[k][:, 3 * width :]

    x_rows = x_ref[...].astype(F32)
    scale = lax.rsqrt(jnp.mean(x_rows * x_rows, axis=1, keepdims=True) + EPS)
    h_ref[...] = (x_rows * scale * gain_ref[...]).astype(BF16)
    for at, ref in enumerate((q_ref, k_ref)):
        part = product(h_ref[...], w_ref[:, at * width : (at + 1) * width])
        ref[...] = part
        squares_ref[8 * at : 8 * at + 8, :] = row_sums(part * part)
    v_ref[...] = product(h_ref[...], w_ref[:, 2 * width :]).astype(BF16)


def qkv_project(ids, x_all, gain, pieces):
    total, depth = x_all.shape
    width = pieces[0].shape[1] // 4
    rows = min(256, total)
    block = pl.BlockSpec((rows, width), lambda i, ids: (i, 0))
    wide = pl.BlockSpec((rows, depth), lambda i, ids: (i, 0))
    return call(
        functools.partial(qkv_kernel, len(pieces)),
        [like((total, width), F32)] * 2
        + [like((total, width), BF16), like((16, total), F32), like((depth, 3 * width), BF16)]
        + [like((depth, width), BF16), like((total, depth), BF16)],
        [x_all, gain, *pieces],
        6 * total * depth * width,
        "qkv_project",
        scalars=(ids,),
        grid=(total // rows,),
        in_specs=[wide] + [None] * (len(pieces) + 1),
        out_specs=[
            block, block, block, pl.BlockSpec((16, rows), lambda i, ids: (0, i)), None, None, wide,
        ],
    )


def out_kernel(n_ep, ids, attn_ref, x_ref, gain_ref, *refs):
    weights, (one_ref, low_ref) = refs[:-2], refs[-2:]
    width = weights[0].shape[1]
    for j, weight in enumerate(weights):
        cols = block_at(ids, n_ep + j, width)
        one_ref[:, cols] = x_ref[:, cols].astype(F32) + product(attn_ref[...], weight[...])
    one = one_ref[...]
    scale = lax.rsqrt(jnp.mean(one * one, axis=1, keepdims=True) + EPS)
    low_ref[...] = (one * scale * gain_ref[...]).astype(BF16)


def out_project(ids, n_ep, attn_tok, tokens, gain, weights, after):
    return call(
        functools.partial(out_kernel, n_ep),
        [like(tokens.shape, F32), like(tokens.shape, BF16)],
        [attn_tok, tokens, gain, *weights],
        2 * tokens.size * attn_tok.shape[1],
        "out_project",
        after=after,
        scalars=(ids,),
    )


def out_back_kernel(n_ep, ids, d_ref, *refs):
    weights, d_attn_ref = refs[:-1], refs[-1]
    width = weights[0].shape[1]
    total = None
    for j, weight in enumerate(weights):
        part = product_right(d_ref[:, block_at(ids, n_ep + j, width)], weight[...])
        total = part if total is None else total + part
    d_attn_ref[...] = total.astype(BF16)


def out_back(ids, n_ep, d_z, weights, after):
    return call(
        functools.partial(out_back_kernel, n_ep),
        like((d_z.shape[0], weights[0].shape[0]), BF16),
        [d_z, *weights],
        2 * d_z.size * weights[0].shape[0],
        "out_back",
        after=after,
        scalars=(ids,),
    )


def vo_grads_kernel(count, shard, ids, h_ref, dv_ref, attn_ref, dz_ref, *stacks):
    width = dv_ref.shape[1]
    for k in range(count):
        block = block_at(ids, k, shard)
        array, place = stack_at(k, count)
        stacks[array][place, :, :width] = product_left(h_ref[:, block], dv_ref[...]).astype(BF16)
        stacks[array][place, :, width:] = product_left(attn_ref[:, block], dz_ref[...]).astype(BF16)


def vo_grads(ids, count, h_all, d_v, attn_all, d_z_cols):
    shard = h_all.shape[1] // count
    width = d_v.shape[1]
    return call(
        functools.partial(vo_grads_kernel, count, shard),
        stack_shapes(count, (shard, 2 * width)),
        [h_all, d_v, attn_all, d_z_cols],
        4 * h_all.size * width,
        "vo_grads",
        scalars=(ids,),
    )


def qk_back_kernel(
    count, shard, ids, h_ref, dqn_ref, dkn_ref, qr_ref, kr_ref, scale_ref, sums_ref, tiny_ref, *refs
):
    stacks, d_ref = refs[:-1], refs[-1]
    width = dqn_ref.shape[1]
    scales = jnp.transpose(scale_ref[...])
    means = jnp.transpose(sums_ref[...]) * (1.0 / h_ref.shape[1])
    for at, (d_normed, raw) in enumerate(((dqn_ref, qr_ref), (dkn_ref, kr_ref))):
        scale, mean = scales[:, 8 * at : 8 * at + 1], means[:, 8 * at : 8 * at + 1]
        d_ref[:, at * width : (at + 1) * width] = (
            scale * (d_normed[...] - raw[...] * scale * mean)
        ).astype(BF16)
    per_row = 2 * width // shard
    extra = stacks[0].shape[1] - shard
    for k in range(count):
        block = block_at(ids, k, shard)
        array, place = stack_at(k, count)
        ref = stacks[array]
        ref[place, :shard, :] = product_left(h_ref[:, block], d_ref[...]).astype(BF16)
        ref[place, shard:, :] = jnp.zeros((extra, 2 * width), BF16)
        for at in range(tiny_ref.shape[0]):
            row, col = shard + at // per_row, (at % per_row) * shard
            ref[place, row : row + 1, col : col + shard] = tiny_ref[at : at + 1, block].astype(BF16)


def qk_back(ids, count, h_all, d_qn, d_kn, q_raw, k_raw, scales, sums, tiny, after):
    total, depth = h_all.shape
    width = d_qn.shape[1]
    shard = depth // count
    extra = -(-tiny.shape[0] // (2 * width // shard))
    extra = -(-extra // 16) * 16
    return call(
        functools.partial(qk_back_kernel, count, shard),
        stack_shapes(count, (shard + extra, 2 * width)) + [like((total, 2 * width), BF16)],
        [h_all, d_qn, d_kn, q_raw, k_raw, scales, sums, tiny],
        2 * h_all.size * 2 * width,
        "qk_back",
        scalars=(ids,),
        after=after,
    )


def d_h_kernel(ids, d_ref, dv_ref, w_ref, out_ref):
    both = d_ref.shape[1]
    out_ref[0] = (
        product_right(d_ref[...], w_ref[:, :both]) + product_right(dv_ref[...], w_ref[:, both:])
    ).astype(BF16)


def d_h_rows(ids, n_ep, n_sp, d_qk, d_v, w_qkv):
    total, wide = d_qk.shape
    depth = w_qkv.shape[0]
    rows = total // n_sp

    def partner(j, ids):
        return ids[n_ep + (j % 2) * 2 + j // 2], 0

    return call(
        d_h_kernel,
        like((n_sp, rows, depth), BF16),
        [d_qk, d_v, w_qkv],
        3 * d_qk.size * depth,
        "d_h",
        scalars=(ids,),
        grid=(n_sp,),
        in_specs=[
            pl.BlockSpec((rows, wide), partner), pl.BlockSpec((rows, d_v.shape[1]), partner), None,
        ],
        out_specs=[pl.BlockSpec((1, rows, depth), lambda j, ids: (j, 0, 0))],
    )


def finish_kernel(n_ep, n_sp, ids, wq_ref, wk_ref, wv_ref, gain_ref, *refs):
    firsts, seconds = refs[:n_sp], refs[n_sp : 2 * n_sp]
    gq_ref, gk_ref, gv_ref, go_ref, tiny_ref, attn_ref = refs[2 * n_sp :]
    shard = wq_ref.shape[0]
    width = firsts[0].shape[1] // 2
    dots = jnp.zeros((shard, 1), F32)
    tiny = jnp.zeros(tiny_ref.shape, F32)
    for j in range(n_sp):
        cols = block_at(ids, n_ep + j, width)
        for at, grad, weight in ((0, gq_ref, wq_ref), (1, gk_ref, wk_ref), (2, gv_ref, wv_ref)):
            part = firsts[j][:shard, at * width : (at + 1) * width] if at < 2 else seconds[j][:, :width]
            value = part.astype(F32)
            grad[:, cols] = value
            dots += jnp.sum(value * weight[:, cols].astype(F32), axis=1, keepdims=True)
        go_ref[:, cols] = seconds[j][:, width:].astype(F32)
        tiny += firsts[j][shard:, :].astype(F32)
    tiny_ref[...] = tiny
    attn_ref[...] = dots / gain_ref[...]


def finish(ids, n_ep, w_query, w_key, w_value, gain, firsts, seconds, after):
    shard, depth = w_query.shape
    extra = firsts[0].shape[0] - shard
    return call(
        functools.partial(finish_kernel, n_ep, len(firsts)),
        [like((shard, depth), F32)] * 4 + [like((extra, firsts[0].shape[1]), F32), like((shard, 1), F32)],
        [w_query, w_key, w_value, gain, *firsts, *seconds],
        shard * depth * 6,
        "finish",
        after=after,
        scalars=(ids,),
    )


def turn(values_in):
    return pltpu.roll(values_in, HEAD_DIM // 2, 1)


def masked_probs(q_ref, k_ref, start_ref, block, rows):
    first, last = block * rows, (block + 1) * rows
    scores = product_right(q_ref[first:last, :], k_ref[0:last, :]) * (HEAD_DIM ** (-0.5))
    row_ids = first + lax.broadcasted_iota(jnp.int32, scores.shape, 0)
    places = lax.broadcasted_iota(jnp.int32, scores.shape, 1)
    allowed = (places <= row_ids) & (places >= start_ref[first:last, :])
    scores = jnp.where(allowed, scores, NEG_FILL)
    top = jnp.max(scores, axis=1, keepdims=True)
    weights = jnp.exp(scores - top)
    return weights * (1.0 / jnp.sum(weights, axis=1, keepdims=True))


def attend_kernel(
    rows, qr_ref, kr_ref, v_ref, scale_ref, gq_ref, gk_ref, cos_ref, sin_ref, start_ref,
    q_ref, k_ref, out_ref,
):
    scales = jnp.transpose(scale_ref[...])
    for at, (raw, gain, low) in enumerate(((qr_ref, gq_ref, q_ref), (kr_ref, gk_ref, k_ref))):
        normed = raw[...] * scales[:, 8 * at : 8 * at + 1] * gain[...]
        low[...] = (normed * cos_ref[...] + turn(normed) * sin_ref[...]).astype(BF16)
    for block in range(q_ref.shape[0] // rows):
        probs = masked_probs(q_ref, k_ref, start_ref, block, rows)
        last = (block + 1) * rows
        out_ref[block * rows : last, :] = product(
            probs.astype(BF16), v_ref[0:last, :]
        ).astype(BF16)


def head_spec(rows):
    return pl.BlockSpec((rows, HEAD_DIM), lambda h: (0, h))


def attend(q_raw, k_raw, v_low, scales, q_gain, k_gain, cosine, sine, starts):
    total, width = v_low.shape
    heads = width // HEAD_DIM
    head, gain = head_spec(total), head_spec(1)
    return call(
        functools.partial(attend_kernel, min(256, total)),
        [like((total, width), BF16)] * 3,
        [q_raw, k_raw, v_low, scales, q_gain, k_gain, cosine, sine, starts],
        3 * heads * total * total * HEAD_DIM,
        "attend",
        grid=(heads,),
        in_specs=[head, head, head, None, gain, gain, None, None, None],
        out_specs=[head, head, head],
    )


def attend_back_kernel(
    rows, q_ref, k_ref, v_ref, do_ref, qr_ref, kr_ref, scale_ref, gq_ref, gk_ref,
    cos_ref, sin_ref, start_ref,
    dq_ref, dk_ref, dv_ref, sums_ref, dgq_ref, dgk_ref, q_acc, k_acc, v_acc,
):
    k_acc[...] = jnp.zeros_like(k_acc)
    v_acc[...] = jnp.zeros_like(v_acc)
    for block in range(q_ref.shape[0] // rows):
        first, last = block * rows, (block + 1) * rows
        probs = masked_probs(q_ref, k_ref, start_ref, block, rows)
        d_rows = do_ref[first:last, :]
        d_probs = product_right(d_rows, v_ref[0:last, :])
        delta = jnp.sum(probs * d_probs, axis=1, keepdims=True)
        d_scores = (probs * (d_probs - delta) * (HEAD_DIM ** (-0.5))).astype(BF16)
        q_acc[first:last, :] = product(d_scores, k_ref[0:last, :])
        k_acc[0:last, :] += product_left(d_scores, q_ref[first:last, :])
        v_acc[0:last, :] += product_left(probs.astype(BF16), d_rows)
    dv_ref[...] = v_acc[...].astype(BF16)

    @pl.when(pl.program_id(0) == 0)
    def _():
        sums_ref[...] = jnp.zeros_like(sums_ref)

    scales = jnp.transpose(scale_ref[...])
    for at, (acc, raw, gain, d_ref, dg_ref) in enumerate(
        ((q_acc, qr_ref, gq_ref, dq_ref, dgq_ref), (k_acc, kr_ref, gk_ref, dk_ref, dgk_ref))
    ):
        turned = acc[...].astype(BF16).astype(F32)
        back = turned * cos_ref[...] + turn(turned * sin_ref[...])
        normed = raw[...] * scales[:, 8 * at : 8 * at + 1]
        both = back * normed
        dg_ref[...] = jnp.sum(both, axis=0, keepdims=True)
        d_ref[...] = back * gain[...]
        sums_ref[8 * at : 8 * at + 8, :] += row_sums(both * gain[...])


def attend_back(
    q_rot, k_rot, v_low, d_heads, q_raw, k_raw, scales, q_gain, k_gain, cosine, sine, starts
):
    total, width = v_low.shape
    heads = width // HEAD_DIM
    head, gain = head_spec(total), head_spec(1)
    wide, thin = like((total, width), F32), like((1, width), F32)
    return call(
        functools.partial(attend_back_kernel, min(256, total)),
        [wide, wide, like((total, width), BF16), like((16, total), F32), thin, thin],
        [q_rot, k_rot, v_low, d_heads, q_raw, k_raw, scales, q_gain, k_gain, cosine, sine, starts],
        7 * heads * total * total * HEAD_DIM,
        "attend_back",
        scratch=[pltpu.VMEM((total, HEAD_DIM), F32)] * 3,
        grid=(heads,),
        in_specs=[head] * 6 + [None, gain, gain, None, None, None],
        out_specs=[head, head, head, None, gain, gain],
    )


def chooser(places_ref, at, cap):
    row = places_ref[at : at + 1, :]
    slots = lax.broadcasted_iota(jnp.int32, (cap, row.shape[1]), 0)
    return slots == row


def dispatch_kernel(
    pieces_here, local, cap, gated, mine, *refs
):
    pieces, refs = refs[:pieces_here], refs[pieces_here:]
    places_ref, refs = refs[0], refs[1:]
    if gated:
        (picked_ref, router_ref), refs = refs[:2], refs[2:]
        rows_ref, gate_ref, all_ref = refs[-3:]
    else:
        rows_ref = refs[-1]
    for p in range(pieces_here):
        if gated:
            logits = product_right(router_ref[...], pieces[p][...])
            experts = logits.shape[0]
            picked = picked_ref[p * experts : (p + 1) * experts, :] > 0
            logits = jnp.where(picked, logits, NEG_FILL)
            weights = jnp.exp(logits - jnp.max(logits, axis=0, keepdims=True))
            weights = jnp.where(picked, weights, 0.0)
            gates = weights / jnp.sum(weights, axis=0, keepdims=True)
            all_ref[p * experts : (p + 1) * experts, :] = gates
        for e in range(local):
            chosen = chooser(places_ref, p * local + e, cap)
            rows_ref[e, p * cap : (p + 1) * cap, :] = product(
                chosen.astype(BF16), pieces[p][...]
            ).astype(BF16)
            if gated:
                row = all_ref[pl.ds(p * experts + mine[0] * local + e, 1), :]
                gate_ref[e, p * cap : (p + 1) * cap, :] = jnp.sum(
                    jnp.where(chosen, row, 0.0), axis=1, keepdims=True
                )


def dispatch(mine, pieces, places, picked, router, local, cap, group, at, rows, gates, after=()):
    gated = router is not None
    here = len(pieces)
    width = pieces[0].shape[1]
    args = [*pieces, places]
    shapes = [like((local, group * cap, width), BF16)]
    spec = pl.BlockSpec((local, here * cap, width), lambda i, mine: (0, at, 0))
    out_specs = [spec]
    if gated:
        args += [picked, router]
        shapes += [like((local, group * cap, 1), F32), like((picked.shape[0], places.shape[1]), F32)]
        out_specs += [pl.BlockSpec((local, here * cap, 1), lambda i, mine: (0, at, 0)), None]
    in_specs = [None] * len(args)
    aliases = {}
    if rows is not None:
        aliases[len(args)] = 0
        args.append(rows)
        in_specs.append(pl.BlockSpec(memory_space=pl.ANY))
        if gated:
            aliases[len(args)] = 1
            args.append(gates)
            in_specs.append(pl.BlockSpec(memory_space=pl.ANY))
    return call(
        functools.partial(dispatch_kernel, here, local, cap, gated),
        shapes,
        args,
        2 * here * local * cap * places.shape[1] * width,
        "dispatch",
        scalars=(mine,),
        in_specs=in_specs,
        out_specs=out_specs,
        aliases=aliases,
        after=after,
    )


def expert_kernel(
    x_ref, d_ref, gate_ref, wg_ref, wu_ref, wd_ref,
    act_ref, dg_ref, du_ref, dots_ref, mix_ref, back_ref, mix_acc, back_acc,
):
    step = pl.program_id(1)
    last = pl.num_programs(1) - 1
    x_rows, d_rows, gate = x_ref[0], d_ref[0], gate_ref[0]
    pre = product(x_rows, wg_ref[0])
    up = product(x_rows, wu_ref[0])
    pulled = product_right(d_rows, wd_ref[0])
    sigma = jax.nn.sigmoid(pre)
    silu = pre * sigma
    act = silu * up
    dots = jnp.sum(act * pulled, axis=1, keepdims=True)
    act_low = (act * gate).astype(BF16)
    act_ref[0] = act_low
    d_act = pulled * gate
    du_low = (d_act * silu).astype(BF16)
    dg_low = (d_act * up * sigma * (1.0 + pre * (1.0 - sigma))).astype(BF16)
    dg_ref[0] = dg_low
    du_ref[0] = du_low
    mix = product(act_low, wd_ref[0])
    back = product_right(dg_low, wg_ref[0]) + product_right(du_low, wu_ref[0])

    @pl.when(step == 0)
    def _():
        dots_ref[0] = dots
        mix_acc[...] = mix
        back_acc[...] = back

    @pl.when((step > 0) & (step < last))
    def _():
        dots_ref[0] += dots
        mix_acc[...] += mix
        back_acc[...] += back

    @pl.when(step == last)
    def _():
        dots_ref[0] += dots
        mix_ref[0] = (mix_acc[...] + mix).astype(BF16)
        back_ref[0] = (back_acc[...] + back).astype(BF16)


def experts(rows, d_rows, gates, w_gate, w_up, w_down, after=()):
    local, count, width = rows.shape
    hidden = w_gate.shape[2]
    part = hidden // 2
    wide = pl.BlockSpec((1, count, width), lambda e, f: (e, 0, 0))
    column = pl.BlockSpec((1, count, 1), lambda e, f: (e, 0, 0))
    thin = pl.BlockSpec((1, count, part), lambda e, f: (e, 0, f))
    into = pl.BlockSpec((1, width, part), lambda e, f: (e, 0, f))
    outof = pl.BlockSpec((1, part, width), lambda e, f: (e, f, 0))
    return call(
        expert_kernel,
        [like((local, count, hidden), BF16)] * 3
        + [like((local, count, 1), F32)]
        + [like((local, count, width), BF16)] * 2,
        [rows, d_rows, gates, w_gate, w_up, w_down],
        12 * rows.size * hidden,
        "experts",
        after=after,
        scratch=[pltpu.VMEM((count, width), F32)] * 2,
        grid=(local, 2),
        in_specs=[wide, wide, column, into, into, outof],
        out_specs=[thin, thin, thin, column, wide, wide],
    )


def combine_kernel(here, local, cap, dotted, places_ref, rows_ref, *refs):
    pieces = refs[int(dotted) : int(dotted) + here]
    for p in range(here):
        chosen = [chooser(places_ref, p * local + e, cap) for e in range(local)]
        total = None
        for e in range(local):
            part = product_left(chosen[e].astype(BF16), rows_ref[e, p * cap : (p + 1) * cap, :])
            total = part if total is None else total + part
            if dotted:
                refs[-1][p * local + e : p * local + e + 1, :] = jnp.sum(
                    jnp.where(chosen[e], refs[0][e, p * cap : (p + 1) * cap, :], 0.0),
                    axis=0, keepdims=True,
                )
        pieces[p][...] = total.astype(BF16)


def combine(places, rows, here, local, cap, at, dots=None, after=()):
    width = rows.shape[2]
    tokens = places.shape[1]
    dotted = dots is not None
    args = [places, rows] + ([dots] if dotted else [])
    in_specs = [None, pl.BlockSpec((local, here * cap, width), lambda i: (0, at, 0))]
    if dotted:
        in_specs.append(pl.BlockSpec((local, here * cap, 1), lambda i: (0, at, 0)))
    shapes = [like((tokens, width), BF16)] * here
    if dotted:
        shapes.append(like(places.shape, F32))
    return call(
        functools.partial(combine_kernel, here, local, cap, dotted),
        shapes,
        args,
        2 * here * local * cap * tokens * width,
        "combine",
        after=after,
        in_specs=in_specs,
    )


def combine_stacks_kernel(count, local, cap, group, places_ref, *refs):
    groups = count // group
    for k in range(count):
        rows = refs[k // group]
        at = (k % group) * cap
        total = None
        for e in range(local):
            chosen = chooser(places_ref, k * local + e, cap).astype(BF16)
            part = product_left(chosen, rows[e, at : at + cap, :])
            total = part if total is None else total + part
        array, place = stack_at(k, count)
        refs[groups + array][place] = total.astype(BF16)


def combine_stacks(places, rows, count, local, cap, group, after):
    tokens, width = places.shape[1], rows[0].shape[2]
    return call(
        functools.partial(combine_stacks_kernel, count, local, cap, group),
        stack_shapes(count, (tokens, width)),
        [places, *rows],
        2 * count * local * cap * tokens * width,
        "combine_stacks",
        after=after,
    )


def weight_grad_kernel(groups, *refs):
    lefts, rights = refs[:groups], refs[groups : 2 * groups]
    total = None
    for left, right in zip(lefts, rights):
        part = product_left(left[0], right[0])
        total = part if total is None else total + part
    refs[-1][0] = total.astype(BF16)


def weight_grad(lefts, rights, after=()):
    local, count, tall = lefts[0].shape
    wide = rights[0].shape[2]
    part = min(512, tall)
    left = pl.BlockSpec((1, count, part), lambda e, i: (e, 0, i))
    right = pl.BlockSpec((1, count, wide), lambda e, i: (e, 0, 0))
    return call(
        functools.partial(weight_grad_kernel, len(lefts)),
        like((local, tall, wide), BF16),
        [*lefts, *rights],
        2 * len(lefts) * lefts[0].size * wide,
        "weight_grad",
        after=after,
        grid=(local, tall // part),
        in_specs=[left] * len(lefts) + [right] * len(lefts),
        out_specs=[pl.BlockSpec((1, part, wide), lambda e, i: (e, i, 0))],
    )


def body(
    tokens, doc_lengths, routes, attn_gain, w_query, w_key, w_value, q_gain, k_gain, w_out,
    ffn_gain, w_router, w_gate, w_up, w_down, cotangent,
):
    n_sp = lax.axis_size("sp")
    n_ep = lax.axis_size("ep")
    sp_index = lax.axis_index("sp")
    ep_index = lax.axis_index("ep")
    tok_dev, width = tokens.shape[1:]
    total = tok_dev * n_sp
    shard = width // n_ep
    head_width = width // n_sp
    top_count = routes.shape[2]
    local = w_gate.shape[0]
    expert_count = local * n_ep
    capacity = 9 * tok_dev * top_count // (8 * expert_count)
    cap = -(-capacity // 16) * 16
    group = 4
    blocks = piece_blocks(n_ep, ep_index)
    partners = jnp.bitwise_xor(jnp.arange(n_sp, dtype=jnp.int32), sp_index)
    ids = jnp.concatenate([blocks, partners]).astype(jnp.int32)
    mine = ep_index.astype(jnp.int32).reshape(1)

    def own_columns(value):
        return lax.dynamic_slice_in_dim(value, sp_index * head_width, head_width, 1)

    def by_piece(value):
        return jnp.stack(
            [lax.dynamic_index_in_dim(value, blocks[i], 0, keepdims=False) for i in range(n_ep)]
        )

    expert_ids = jnp.arange(expert_count, dtype=jnp.int32)
    picked = jnp.any(routes[0][:, :, None] == expert_ids[None, None, :], axis=1)
    picked_low = picked.T.astype(BF16)
    small = jnp.concatenate(
        [
            jnp.stack([attn_gain, q_gain, k_gain, ffn_gain]),
            jnp.zeros((12, shard), BF16),
            w_router.T,
        ],
        axis=0,
    )

    def to_all(value):
        value = jnp.broadcast_to(value[None], (n_ep, *value.shape))
        return lax.all_to_all(value, "ep", split_axis=0, concat_axis=0, tiled=True)

    if shard == tok_dev:
        both = to_all(jnp.concatenate([small, picked_low], axis=0))
        small_all, picked_all = both[:, : 16 + expert_count], both[:, 16 + expert_count :]
    else:
        small_all, picked_all = to_all(small), to_all(picked_low)
    small_rows = jnp.swapaxes(small_all, 0, 1).reshape(16 + expert_count, width)
    gains = small_rows[:4].astype(F32)
    full_router = small_rows[16:]
    picked_all = by_piece(picked_all)

    x_all = lax.all_gather(tokens[0], "sp", axis=0, tiled=True)
    w_own = jnp.concatenate([own_columns(w) for w in (w_query, w_key, w_value, w_out)], axis=1)
    cot_own = cotangent[0]
    if n_ep == 8:
        blocks_z = along_z(w_own)
        blocks_z[3], cot_own = tie(blocks_z[3], cot_own)
        cot_blocks = along_z(cot_own)
        w_pieces = across_x(blocks_z)
        w_pieces[7], cot_blocks[0], cot_blocks[1] = tie(w_pieces[7], cot_blocks[0], cot_blocks[1])
        cot_pieces = across_x(cot_blocks)
    else:
        w_pieces, cot_pieces = gather_whole(w_own), gather_whole(cot_own)

    upper = (
        jnp.arange(tok_dev, dtype=jnp.int32)[:, None] < jnp.arange(tok_dev, dtype=jnp.int32)[None, :]
    ).astype(BF16)
    picked_mine = lax.dynamic_slice_in_dim(picked_all, ep_index * local, local, 1)
    picked_mine = picked_mine.reshape(n_ep * local, tok_dev)
    earlier = product(picked_mine, upper).astype(jnp.int32)
    places = jnp.where((picked_mine > 0) & (earlier < capacity), earlier, -1)
    picked_flat = picked_all.reshape(n_ep * expert_count, tok_dev).astype(F32)

    positions = jnp.arange(total, dtype=jnp.int32)
    lengths = doc_lengths[0]
    doc_ends = jnp.cumsum(lengths)
    starts = jnp.sum(
        jnp.where(doc_ends[None, :] <= positions[:, None], lengths[None, :], 0), axis=1
    )
    half = HEAD_DIM // 2
    frequency = THETA ** (-(2.0 * jnp.arange(half, dtype=F32)) / HEAD_DIM)
    angles = (positions - starts).astype(F32)[:, None] * frequency[None, :]
    cosine = jnp.concatenate([jnp.cos(angles), jnp.cos(angles)], axis=1)
    sine = jnp.concatenate([-jnp.sin(angles), jnp.sin(angles)], axis=1)
    starts = starts[:, None].astype(jnp.int32)

    q_raw, k_raw, v_low, squares, w_qkv, w_o, h_all = qkv_project(ids, x_all, gains[0:1], w_pieces)
    scales = lax.rsqrt(sum_sp(squares) / width + EPS)
    w_o_parts = gather_sp(w_o)
    gain_q, gain_k = own_columns(gains)[1:2], own_columns(gains)[2:3]
    q_rot, k_rot, mixed = attend(
        q_raw, k_raw, v_low, scales, gain_q, gain_k, cosine, sine, starts
    )

    def pair_places(p):
        return places[p * local : (p + 2) * local]

    def cot_rows(g, after):
        d_rows = None
        for at, p in enumerate(range(g, g + group, 2)):
            (d_rows,) = dispatch(
                mine, cot_pieces[p : p + 2], pair_places(p), None, None, local, cap, group, at,
                d_rows, None, after,
            )
        return d_rows

    attn_tok = lax.all_to_all(mixed, "sp", split_axis=0, concat_axis=1, tiled=True)
    near_rows = cot_rows(0, [])
    x_one, h2_low = out_project(
        ids, n_ep, attn_tok, tokens[0], gains[3:4], w_o_parts, []
    )
    attn_all = lax.all_gather(attn_tok, "sp", axis=0, tiled=True)

    h2_pieces = gather(h2_low, n_ep)
    cots = [near_rows] + [cot_rows(g, [x_one]) for g in range(group, n_ep, group)]
    groups, d_pieces, d_gates, d_sums = [], [], [], []
    home_gates = None

    def rows_of(g, after):
        rows = gates = first_gates = None
        for at, p in enumerate(range(g, g + group, 2)):
            rows, gates, piece_gates = dispatch(
                mine, h2_pieces[p : p + 2], pair_places(p),
                picked_flat[p * expert_count : (p + 2) * expert_count], full_router, local, cap,
                group, at, rows, gates, after,
            )
            first_gates = piece_gates if first_gates is None else first_gates
        return rows, gates, first_gates

    rows, gates, home_gates = rows_of(0, [])
    for g in range(0, n_ep, group):
        d_rows = cots[g // group]
        made = experts(rows, d_rows, gates, w_gate, w_up, w_down, d_pieces[-group:] + cots)
        groups.append((rows, d_rows, made))
        following = []
        if g + group < n_ep:
            rows, gates, _ = rows_of(g + group, [made[5]])
            following = [rows]
        sums_before = list(d_sums)
        for at in range(group // 2):
            *two, dots = combine(
                pair_places(g + 2 * at), made[5], 2, local, cap, at, made[3],
                sums_before + following,
            )
            d_pieces += two
            d_gates.append(dots)
        if n_ep == 8:
            d_sums += crossed_sums(d_pieces[-group:])

    acts = [made[0] for _, _, made in groups]
    d_gate_rows = [made[1] for _, _, made in groups]
    d_up_rows = [made[2] for _, _, made in groups]
    ins = [rows for rows, _, _ in groups]
    outs = [d_rows for _, d_rows, _ in groups]
    grad_down = weight_grad(acts, outs, d_pieces)
    d_gates = by_piece(jnp.concatenate(d_gates, axis=0).reshape(n_ep, local, tok_dev))
    d_gates = lax.all_to_all(d_gates, "ep", split_axis=0, concat_axis=0, tiled=True)
    d_gates = d_gates.reshape(expert_count, tok_dev)
    grad_gate = weight_grad(ins, d_gate_rows, [grad_down, d_gates])
    mix_stacks = combine_stacks(
        places, [made[4] for _, _, made in groups], n_ep, local, cap, group, [grad_gate, *d_sums]
    )
    mix_stacks[0], grad_down, grad_gate = tie(mix_stacks[0], grad_down, grad_gate)
    d_h2 = scatter_z(*d_sums) if n_ep == 8 else scatter(d_pieces, n_ep)
    grad_up = weight_grad(ins, d_up_rows, mix_stacks[:1])

    def over_sp(value):
        return lax.psum_scatter(value, "sp", scatter_dimension=1, tiled=True).astype(F32)


    if n_ep == 8:
        gates_here = home_gates[:expert_count]
    else:
        logits = product_right(full_router, h2_low)
        logits = jnp.where(picked.T, logits, NEG_FILL)
        gates_here = jax.nn.softmax(logits, axis=0)
    d_logits = gates_here * (d_gates - jnp.sum(gates_here * d_gates, axis=0, keepdims=True))
    d_logits = jnp.where(picked.T, d_logits, 0.0).astype(BF16)
    grad_router = product(d_logits, h2_low)
    d_h2 = d_h2 + product_left(d_logits, full_router)
    one_scale = lax.rsqrt(jnp.mean(x_one * x_one, axis=-1, keepdims=True) + EPS)
    one_normed = x_one * one_scale
    grad_ffn = jnp.sum(d_h2 * one_normed, axis=0)
    d_normed = d_h2 * gains[3][None, :]
    d_one = cotangent[0].astype(F32) + one_scale * (
        d_normed - one_normed * jnp.mean(d_normed * one_normed, axis=-1, keepdims=True)
    )
    d_z, grad_up = tie(d_one.astype(BF16), grad_up)
    d_attn = out_back(ids, n_ep, d_z, w_o_parts, [])
    d_heads = lax.all_to_all(d_attn, "sp", split_axis=1, concat_axis=0, tiled=True)
    d_z_cols = lax.all_to_all(d_z, "sp", split_axis=1, concat_axis=0, tiled=True)
    mix, mix_far = scatter_stacks(mix_stacks, n_ep)
    if n_ep == 8:
        mix, mix_far, d_heads = tie(mix, mix_far, d_heads)
    grad_down, grad_gate, grad_up = over_sp(grad_down), over_sp(grad_gate), over_sp(grad_up)

    d_qn, d_kn, d_v, sums, grad_qg, grad_kg = attend_back(
        q_rot, k_rot, v_low, d_heads, q_raw, k_raw, scales, gain_q, gain_k, cosine, sine, starts
    )
    output = (x_one + last_hop(mix, mix_far)).astype(BF16)
    vo_stacks = vo_grads(ids, n_ep, h_all, d_v, attn_all, d_z_cols)
    grad_vo = last_hop(*scatter_stacks(vo_stacks, n_ep)).astype(BF16)

    def placed(value):
        return lax.dynamic_update_slice_in_dim(
            jnp.zeros((1, width), F32), value, sp_index * head_width, 1
        )

    tiny = jnp.concatenate(
        [placed(grad_qg), placed(grad_kg), grad_ffn[None], grad_router], axis=0
    )
    *qk_stacks, d_qk = qk_back(
        ids, n_ep, h_all, d_qn, d_kn, q_raw, k_raw, scales, sum_sp(sums), tiny, vo_stacks[:1]
    )
    grad_qk = last_hop(*scatter_stacks(qk_stacks, n_ep)).astype(BF16)

    d_h = d_h_rows(ids, n_ep, n_sp, d_qk, d_v, w_qkv)
    output, d_h = tie(output, d_h)
    halves = plus(d_h[:2], swap_sp(d_h[2:], 1))
    d_h = halves[0].astype(F32) + swap_sp(halves[1], 2).astype(F32)
    x_rows = tokens[0].astype(F32)
    x_scale = lax.rsqrt(jnp.mean(x_rows * x_rows, axis=-1, keepdims=True) + EPS)
    x_normed = x_rows * x_scale
    d_normed = d_h * gains[0][None, :]
    input_grad = d_one + x_scale * (
        d_normed - x_normed * jnp.mean(d_normed * x_normed, axis=-1, keepdims=True)
    )

    g_query, g_key, g_value, g_out, tiny, g_attn = finish(
        ids, n_ep, w_query, w_key, w_value, attn_gain.astype(F32)[:, None],
        gather_sp(grad_qk), gather_sp(grad_vo), [grad_down, grad_gate, grad_up, input_grad],
    )
    per_row = 2 * head_width // shard

    def vector(at):
        col = (at % per_row) * shard
        return tiny[at // per_row, col : col + shard]

    g_router = jnp.stack([vector(3 + i) for i in range(expert_count)], axis=1)
    return (
        output[None], input_grad[None], g_attn[:, 0], g_query, g_key, g_value, vector(0), vector(1),
        g_out, vector(2), g_router, grad_gate, grad_up, grad_down,
    )


def solution(mesh):
    seq = P("ep", "sp", None)
    vec = P("ep")
    mat = P("ep", None)
    expert = P("ep", None, None)
    in_specs = (
        seq, mat, seq, vec, mat, mat, mat, vec, vec, mat, vec, mat, expert, expert, expert, seq,
    )
    out_specs = (
        seq, seq, vec, mat, mat, mat, vec, vec, mat, vec, mat, seq, seq, seq,
    )
    return jax.shard_map(body, mesh=mesh, in_specs=in_specs, out_specs=out_specs, check_vma=False)
```

```python
import functools

import jax
import jax.numpy as jnp
from jax import lax
from jax.experimental import pallas as pl
from jax.experimental.pallas import tpu as pltpu
from jax.sharding import PartitionSpec as P

HEAD_DIM = 128
EPS = 1e-05
THETA = 10000.0
NEG_FILL = -1e30
F32 = jnp.float32
BF16 = jnp.bfloat16
MIB = 1 << 20
COVER = 20


def product(left, right):
    return jnp.dot(left, right, preferred_element_type=F32)


def product_left(left, right):
    return lax.dot_general(left, right, (((0,), (0,)), ((), ())), preferred_element_type=F32)


def product_right(left, right):
    return lax.dot_general(left, right, (((1,), (1,)), ((), ())), preferred_element_type=F32)


def row_sums(values_in):
    sums = jnp.sum(values_in, axis=1, keepdims=True)
    return jnp.transpose(jnp.broadcast_to(sums, (sums.shape[0], HEAD_DIM)))[:8]


def call(kernel, out_shape, args, flops, name, scratch=(), scalars=(), grid=(1,), in_specs=None,
         out_specs=None, aliases=None, vmem=60, after=()):
    single = not isinstance(out_shape, (list, tuple))
    shapes = [out_shape] if single else list(out_shape)
    count = len(grid)

    def fixed(shape):
        rank = len(shape)
        return pl.BlockSpec(tuple(shape), lambda *ids: (0,) * rank)

    in_specs = in_specs or [None] * len(args)
    out_specs = out_specs or [None] * len(shapes)
    in_specs = [s if s is not None else fixed(a.shape) for s, a in zip(in_specs, args)]
    out_specs = [s if s is not None else fixed(o.shape) for s, o in zip(out_specs, shapes)]
    waited = len(after)
    args = [*args, *after]
    in_specs = in_specs + [pl.BlockSpec(memory_space=pl.ANY)] * waited
    if waited:
        inner, first = kernel, len(scalars) + len(args) - waited

        def kernel(*refs):
            inner(*refs[:first], *refs[first + waited :])

    moved = sum(a.size * a.dtype.itemsize for a in args[: len(args) - waited])
    moved += sum(o.size * o.dtype.itemsize for o in shapes)
    result = pl.pallas_call(
        kernel,
        grid_spec=pltpu.PrefetchScalarGridSpec(
            num_scalar_prefetch=len(scalars), grid=grid, in_specs=in_specs, out_specs=out_specs,
            scratch_shapes=list(scratch),
        ),
        out_shape=shapes,
        input_output_aliases={k + len(scalars): v for k, v in (aliases or {}).items()},
        compiler_params=pltpu.CompilerParams(
            vmem_limit_bytes=vmem * MIB, dimension_semantics=("arbitrary",) * count
        ),
        cost_estimate=pl.CostEstimate(flops=int(COVER * flops), bytes_accessed=int(moved), transcendentals=0),
        name=name,
    )(*scalars, *args)
    return result[0] if single else list(result)


def like(shape, dtype):
    return jax.ShapeDtypeStruct(tuple(shape), dtype)


def tie(*values):
    return lax.optimization_barrier(values)


def swap(value, bits):
    return lax.ppermute(value, "ep", [(i, i ^ bits) for i in range(8)])


def swap_sp(value, bits):
    return lax.ppermute(value, "sp", [(i, i ^ bits) for i in range(4)])


def piece_blocks(n_ep, ep_index):
    ids = jnp.arange(n_ep, dtype=jnp.int32)
    return jnp.bitwise_xor(ids, ep_index) if n_ep == 8 else ids


def gather_steps(value, after=None):
    near, far = swap(value, 2), swap(value, 4)
    crossed = value
    if after is not None:
        after, crossed, near = tie(after, value, near)
    near_x = swap(near, 1)
    near_x, far = tie(near_x, far)
    farther = swap(far, 2)
    pieces = [value, swap(crossed, 1), near, near_x, far, swap(far, 1), farther, swap(farther, 1)]
    return pieces, after


def gather_whole(value):
    whole = lax.all_gather(value, "ep", axis=0, tiled=False)
    return [whole[i] for i in range(whole.shape[0])]


def gather(value, n_ep):
    return gather_steps(value)[0] if n_ep == 8 else gather_whole(value)


def plus(left, right):
    return (left.astype(F32) + right.astype(F32)).astype(left.dtype)


def crossed_sums(pieces):
    return [plus(pieces[i], swap(pieces[i + 1], 1)) for i in range(0, len(pieces), 2)]


def scatter_z(own, near, far, farther):
    far = plus(far, swap(farther, 2))
    return own.astype(F32) + swap(near, 2).astype(F32) + swap(far, 4).astype(F32)


def scatter(pieces, n_ep):
    if n_ep != 8:
        stacked = jnp.stack(pieces)
        return lax.psum_scatter(stacked, "ep", scatter_dimension=0, tiled=False).astype(F32)
    return scatter_z(*crossed_sums(pieces))


def stack_at(piece, n_ep):
    if n_ep != 8:
        return 0, piece
    return 2 * (piece % 2) + (piece // 2) % 2, piece // 4


def stack_shapes(n_ep, shape):
    return [like((2, *shape), BF16)] * 4 if n_ep == 8 else [like((n_ep, *shape), BF16)]


def scatter_stacks(stacks, n_ep):
    if n_ep != 8:
        total = lax.psum_scatter(stacks[0], "ep", scatter_dimension=0, tiled=False)
        return total.astype(F32), None
    even, odd, even_sent, odd_sent = stacks
    odd = plus(odd, swap(odd_sent, 1))
    even = even.astype(F32) + swap(even_sent, 1).astype(F32) + swap(odd, 2).astype(F32)
    return even[0], even[1].astype(BF16)


def last_hop(total, far):
    return total if far is None else total + swap(far, 4).astype(F32)


def gather_sp(value):
    over = swap_sp(value, 2)
    return [value, swap_sp(value, 1), over, swap_sp(over, 1)]


def sum_sp(value):
    return (value + swap_sp(value, 1)) + (swap_sp(value, 2) + swap_sp(value, 3))


def block_at(ids, position, size):
    if size % HEAD_DIM:
        return pl.ds(position * size, size)
    return pl.ds(pl.multiple_of(ids[position] * size, size), size)


def qkv_kernel(count, ids, x_ref, gain_ref, *refs):
    pieces, refs = refs[:count], refs[count:]
    q_ref, k_ref, v_ref, squares_ref, w_ref, out_ref, h_ref = refs
    shard = pieces[0].shape[0]
    width = q_ref.shape[1]

    @pl.when(pl.program_id(0) == 0)
    def _():
        for k in range(count):
            rows = block_at(ids, k, shard)
            w_ref[rows, :] = pieces[k][:, : 3 * width]
            out_ref[rows, :] = pieces[k][:, 3 * width :]

    x_rows = x_ref[...].astype(F32)
    scale = lax.rsqrt(jnp.mean(x_rows * x_rows, axis=1, keepdims=True) + EPS)
    h_ref[...] = (x_rows * scale * gain_ref[...]).astype(BF16)
    for at, ref in enumerate((q_ref, k_ref)):
        part = product(h_ref[...], w_ref[:, at * width : (at + 1) * width])
        ref[...] = part
        squares_ref[8 * at : 8 * at + 8, :] = row_sums(part * part)
    v_ref[...] = product(h_ref[...], w_ref[:, 2 * width :]).astype(BF16)


def qkv_project(ids, x_all, gain, pieces):
    total, depth = x_all.shape
    width = pieces[0].shape[1] // 4
    rows = min(256, total)
    block = pl.BlockSpec((rows, width), lambda i, ids: (i, 0))
    wide = pl.BlockSpec((rows, depth), lambda i, ids: (i, 0))
    return call(
        functools.partial(qkv_kernel, len(pieces)),
        [like((total, width), F32)] * 2
        + [like((total, width), BF16), like((16, total), F32), like((depth, 3 * width), BF16)]
        + [like((depth, width), BF16), like((total, depth), BF16)],
        [x_all, gain, *pieces],
        6 * total * depth * width,
        "qkv_project",
        scalars=(ids,),
        grid=(total // rows,),
        in_specs=[wide] + [None] * (len(pieces) + 1),
        out_specs=[
            block, block, block, pl.BlockSpec((16, rows), lambda i, ids: (0, i)), None, None, wide,
        ],
    )


def out_kernel(n_ep, ids, attn_ref, x_ref, gain_ref, *refs):
    weights, (one_ref, low_ref) = refs[:-2], refs[-2:]
    width = weights[0].shape[1]
    for j, weight in enumerate(weights):
        cols = block_at(ids, n_ep + j, width)
        one_ref[:, cols] = x_ref[:, cols].astype(F32) + product(attn_ref[...], weight[...])
    one = one_ref[...]
    scale = lax.rsqrt(jnp.mean(one * one, axis=1, keepdims=True) + EPS)
    low_ref[...] = (one * scale * gain_ref[...]).astype(BF16)


def out_project(ids, n_ep, attn_tok, tokens, gain, weights, after):
    return call(
        functools.partial(out_kernel, n_ep),
        [like(tokens.shape, F32), like(tokens.shape, BF16)],
        [attn_tok, tokens, gain, *weights],
        2 * tokens.size * attn_tok.shape[1],
        "out_project",
        after=after,
        scalars=(ids,),
    )


def out_back_kernel(n_ep, ids, d_ref, *refs):
    weights, d_attn_ref = refs[:-1], refs[-1]
    width = weights[0].shape[1]
    total = None
    for j, weight in enumerate(weights):
        part = product_right(d_ref[:, block_at(ids, n_ep + j, width)], weight[...])
        total = part if total is None else total + part
    d_attn_ref[...] = total.astype(BF16)


def out_back(ids, n_ep, d_z, weights, after):
    return call(
        functools.partial(out_back_kernel, n_ep),
        like((d_z.shape[0], weights[0].shape[0]), BF16),
        [d_z, *weights],
        2 * d_z.size * weights[0].shape[0],
        "out_back",
        after=after,
        scalars=(ids,),
    )


def vo_grads_kernel(count, shard, ids, h_ref, dv_ref, attn_ref, dz_ref, *stacks):
    width = dv_ref.shape[1]
    for k in range(count):
        block = block_at(ids, k, shard)
        array, place = stack_at(k, count)
        stacks[array][place, :, :width] = product_left(h_ref[:, block], dv_ref[...]).astype(BF16)
        stacks[array][place, :, width:] = product_left(attn_ref[:, block], dz_ref[...]).astype(BF16)


def vo_grads(ids, count, h_all, d_v, attn_all, d_z_cols):
    shard = h_all.shape[1] // count
    width = d_v.shape[1]
    return call(
        functools.partial(vo_grads_kernel, count, shard),
        stack_shapes(count, (shard, 2 * width)),
        [h_all, d_v, attn_all, d_z_cols],
        4 * h_all.size * width,
        "vo_grads",
        scalars=(ids,),
    )


def qk_back_kernel(
    count, shard, ids, h_ref, dqn_ref, dkn_ref, qr_ref, kr_ref, scale_ref, sums_ref, tiny_ref, *refs
):
    stacks, d_ref = refs[:-1], refs[-1]
    width = dqn_ref.shape[1]
    scales = jnp.transpose(scale_ref[...])
    means = jnp.transpose(sums_ref[...]) * (1.0 / h_ref.shape[1])
    for at, (d_normed, raw) in enumerate(((dqn_ref, qr_ref), (dkn_ref, kr_ref))):
        scale, mean = scales[:, 8 * at : 8 * at + 1], means[:, 8 * at : 8 * at + 1]
        d_ref[:, at * width : (at + 1) * width] = (
            scale * (d_normed[...] - raw[...] * scale * mean)
        ).astype(BF16)
    per_row = 2 * width // shard
    extra = stacks[0].shape[1] - shard
    for k in range(count):
        block = block_at(ids, k, shard)
        array, place = stack_at(k, count)
        ref = stacks[array]
        ref[place, :shard, :] = product_left(h_ref[:, block], d_ref[...]).astype(BF16)
        ref[place, shard:, :] = jnp.zeros((extra, 2 * width), BF16)
        for at in range(tiny_ref.shape[0]):
            row, col = shard + at // per_row, (at % per_row) * shard
            ref[place, row : row + 1, col : col + shard] = tiny_ref[at : at + 1, block].astype(BF16)


def qk_back(ids, count, h_all, d_qn, d_kn, q_raw, k_raw, scales, sums, tiny, after):
    total, depth = h_all.shape
    width = d_qn.shape[1]
    shard = depth // count
    extra = -(-tiny.shape[0] // (2 * width // shard))
    extra = -(-extra // 16) * 16
    return call(
        functools.partial(qk_back_kernel, count, shard),
        stack_shapes(count, (shard + extra, 2 * width)) + [like((total, 2 * width), BF16)],
        [h_all, d_qn, d_kn, q_raw, k_raw, scales, sums, tiny],
        2 * h_all.size * 2 * width,
        "qk_back",
        scalars=(ids,),
        after=after,
    )


def d_h_kernel(ids, d_ref, dv_ref, w_ref, out_ref):
    both = d_ref.shape[1]
    out_ref[0] = (
        product_right(d_ref[...], w_ref[:, :both]) + product_right(dv_ref[...], w_ref[:, both:])
    ).astype(BF16)


def d_h_rows(ids, n_ep, n_sp, d_qk, d_v, w_qkv):
    total, wide = d_qk.shape
    depth = w_qkv.shape[0]
    rows = total // n_sp

    def partner(j, ids):
        return ids[n_ep + (j % 2) * 2 + j // 2], 0

    return call(
        d_h_kernel,
        like((n_sp, rows, depth), BF16),
        [d_qk, d_v, w_qkv],
        3 * d_qk.size * depth,
        "d_h",
        scalars=(ids,),
        grid=(n_sp,),
        in_specs=[
            pl.BlockSpec((rows, wide), partner), pl.BlockSpec((rows, d_v.shape[1]), partner), None,
        ],
        out_specs=[pl.BlockSpec((1, rows, depth), lambda j, ids: (j, 0, 0))],
    )


def finish_kernel(n_ep, n_sp, ids, wq_ref, wk_ref, wv_ref, gain_ref, *refs):
    firsts, seconds = refs[:n_sp], refs[n_sp : 2 * n_sp]
    gq_ref, gk_ref, gv_ref, go_ref, tiny_ref, attn_ref = refs[2 * n_sp :]
    shard = wq_ref.shape[0]
    width = firsts[0].shape[1] // 2
    dots = jnp.zeros((shard, 1), F32)
    tiny = jnp.zeros(tiny_ref.shape, F32)
    for j in range(n_sp):
        cols = block_at(ids, n_ep + j, width)
        for at, grad, weight in ((0, gq_ref, wq_ref), (1, gk_ref, wk_ref), (2, gv_ref, wv_ref)):
            part = firsts[j][:shard, at * width : (at + 1) * width] if at < 2 else seconds[j][:, :width]
            value = part.astype(F32)
            grad[:, cols] = value
            dots += jnp.sum(value * weight[:, cols].astype(F32), axis=1, keepdims=True)
        go_ref[:, cols] = seconds[j][:, width:].astype(F32)
        tiny += firsts[j][shard:, :].astype(F32)
    tiny_ref[...] = tiny
    attn_ref[...] = dots / gain_ref[...]


def finish(ids, n_ep, w_query, w_key, w_value, gain, firsts, seconds, after):
    shard, depth = w_query.shape
    extra = firsts[0].shape[0] - shard
    return call(
        functools.partial(finish_kernel, n_ep, len(firsts)),
        [like((shard, depth), F32)] * 4 + [like((extra, firsts[0].shape[1]), F32), like((shard, 1), F32)],
        [w_query, w_key, w_value, gain, *firsts, *seconds],
        shard * depth * 6,
        "finish",
        after=after,
        scalars=(ids,),
    )


def turn(values_in):
    return pltpu.roll(values_in, HEAD_DIM // 2, 1)


def masked_probs(q_ref, k_ref, start_ref, block, rows):
    first, last = block * rows, (block + 1) * rows
    scores = product_right(q_ref[first:last, :], k_ref[0:last, :]) * (HEAD_DIM ** (-0.5))
    row_ids = first + lax.broadcasted_iota(jnp.int32, scores.shape, 0)
    places = lax.broadcasted_iota(jnp.int32, scores.shape, 1)
    allowed = (places <= row_ids) & (places >= start_ref[first:last, :])
    scores = jnp.where(allowed, scores, NEG_FILL)
    top = jnp.max(scores, axis=1, keepdims=True)
    weights = jnp.exp(scores - top)
    return weights * (1.0 / jnp.sum(weights, axis=1, keepdims=True))


def attend_kernel(
    rows, qr_ref, kr_ref, v_ref, scale_ref, gq_ref, gk_ref, cos_ref, sin_ref, start_ref,
    q_ref, k_ref, out_ref,
):
    scales = jnp.transpose(scale_ref[...])
    for at, (raw, gain, low) in enumerate(((qr_ref, gq_ref, q_ref), (kr_ref, gk_ref, k_ref))):
        normed = raw[...] * scales[:, 8 * at : 8 * at + 1] * gain[...]
        low[...] = (normed * cos_ref[...] + turn(normed) * sin_ref[...]).astype(BF16)
    for block in range(q_ref.shape[0] // rows):
        probs = masked_probs(q_ref, k_ref, start_ref, block, rows)
        last = (block + 1) * rows
        out_ref[block * rows : last, :] = product(
            probs.astype(BF16), v_ref[0:last, :]
        ).astype(BF16)


def head_spec(rows):
    return pl.BlockSpec((rows, HEAD_DIM), lambda h: (0, h))


def attend(q_raw, k_raw, v_low, scales, q_gain, k_gain, cosine, sine, starts):
    total, width = v_low.shape
    heads = width // HEAD_DIM
    head, gain = head_spec(total), head_spec(1)
    return call(
        functools.partial(attend_kernel, min(256, total)),
        [like((total, width), BF16)] * 3,
        [q_raw, k_raw, v_low, scales, q_gain, k_gain, cosine, sine, starts],
        3 * heads * total * total * HEAD_DIM,
        "attend",
        grid=(heads,),
        in_specs=[head, head, head, None, gain, gain, None, None, None],
        out_specs=[head, head, head],
    )


def attend_back_kernel(
    rows, q_ref, k_ref, v_ref, do_ref, qr_ref, kr_ref, scale_ref, gq_ref, gk_ref,
    cos_ref, sin_ref, start_ref,
    dq_ref, dk_ref, dv_ref, sums_ref, dgq_ref, dgk_ref, q_acc, k_acc, v_acc,
):
    k_acc[...] = jnp.zeros_like(k_acc)
    v_acc[...] = jnp.zeros_like(v_acc)
    for block in range(q_ref.shape[0] // rows):
        first, last = block * rows, (block + 1) * rows
        probs = masked_probs(q_ref, k_ref, start_ref, block, rows)
        d_rows = do_ref[first:last, :]
        d_probs = product_right(d_rows, v_ref[0:last, :])
        delta = jnp.sum(probs * d_probs, axis=1, keepdims=True)
        d_scores = (probs * (d_probs - delta) * (HEAD_DIM ** (-0.5))).astype(BF16)
        q_acc[first:last, :] = product(d_scores, k_ref[0:last, :])
        k_acc[0:last, :] += product_left(d_scores, q_ref[first:last, :])
        v_acc[0:last, :] += product_left(probs.astype(BF16), d_rows)
    dv_ref[...] = v_acc[...].astype(BF16)

    @pl.when(pl.program_id(0) == 0)
    def _():
        sums_ref[...] = jnp.zeros_like(sums_ref)

    scales = jnp.transpose(scale_ref[...])
    for at, (acc, raw, gain, d_ref, dg_ref) in enumerate(
        ((q_acc, qr_ref, gq_ref, dq_ref, dgq_ref), (k_acc, kr_ref, gk_ref, dk_ref, dgk_ref))
    ):
        turned = acc[...].astype(BF16).astype(F32)
        back = turned * cos_ref[...] + turn(turned * sin_ref[...])
        normed = raw[...] * scales[:, 8 * at : 8 * at + 1]
        both = back * normed
        dg_ref[...] = jnp.sum(both, axis=0, keepdims=True)
        d_ref[...] = back * gain[...]
        sums_ref[8 * at : 8 * at + 8, :] += row_sums(both * gain[...])


def attend_back(
    q_rot, k_rot, v_low, d_heads, q_raw, k_raw, scales, q_gain, k_gain, cosine, sine, starts
):
    total, width = v_low.shape
    heads = width // HEAD_DIM
    head, gain = head_spec(total), head_spec(1)
    wide, thin = like((total, width), F32), like((1, width), F32)
    return call(
        functools.partial(attend_back_kernel, min(256, total)),
        [wide, wide, like((total, width), BF16), like((16, total), F32), thin, thin],
        [q_rot, k_rot, v_low, d_heads, q_raw, k_raw, scales, q_gain, k_gain, cosine, sine, starts],
        7 * heads * total * total * HEAD_DIM,
        "attend_back",
        scratch=[pltpu.VMEM((total, HEAD_DIM), F32)] * 3,
        grid=(heads,),
        in_specs=[head] * 6 + [None, gain, gain, None, None, None],
        out_specs=[head, head, head, None, gain, gain],
    )


def chooser(places_ref, at, cap):
    row = places_ref[at : at + 1, :]
    slots = lax.broadcasted_iota(jnp.int32, (cap, row.shape[1]), 0)
    return slots == row


def dispatch_kernel(
    pieces_here, local, cap, gated, mine, *refs
):
    pieces, refs = refs[:pieces_here], refs[pieces_here:]
    places_ref, refs = refs[0], refs[1:]
    if gated:
        (picked_ref, router_ref), refs = refs[:2], refs[2:]
        rows_ref, gate_ref, all_ref = refs[-3:]
    else:
        rows_ref = refs[-1]
    for p in range(pieces_here):
        if gated:
            logits = product_right(router_ref[...], pieces[p][...])
            experts = logits.shape[0]
            picked = picked_ref[p * experts : (p + 1) * experts, :] > 0
            logits = jnp.where(picked, logits, NEG_FILL)
            weights = jnp.exp(logits - jnp.max(logits, axis=0, keepdims=True))
            weights = jnp.where(picked, weights, 0.0)
            gates = weights / jnp.sum(weights, axis=0, keepdims=True)
            all_ref[p * experts : (p + 1) * experts, :] = gates
        for e in range(local):
            chosen = chooser(places_ref, p * local + e, cap)
            rows_ref[e, p * cap : (p + 1) * cap, :] = product(
                chosen.astype(BF16), pieces[p][...]
            ).astype(BF16)
            if gated:
                row = all_ref[pl.ds(p * experts + mine[0] * local + e, 1), :]
                gate_ref[e, p * cap : (p + 1) * cap, :] = jnp.sum(
                    jnp.where(chosen, row, 0.0), axis=1, keepdims=True
                )


def dispatch(mine, pieces, places, picked, router, local, cap, group, at, rows, gates, after=()):
    gated = router is not None
    here = len(pieces)
    width = pieces[0].shape[1]
    args = [*pieces, places]
    shapes = [like((local, group * cap, width), BF16)]
    spec = pl.BlockSpec((local, here * cap, width), lambda i, mine: (0, at, 0))
    out_specs = [spec]
    if gated:
        args += [picked, router]
        shapes += [like((local, group * cap, 1), F32), like((picked.shape[0], places.shape[1]), F32)]
        out_specs += [pl.BlockSpec((local, here * cap, 1), lambda i, mine: (0, at, 0)), None]
    in_specs = [None] * len(args)
    aliases = {}
    if rows is not None:
        aliases[len(args)] = 0
        args.append(rows)
        in_specs.append(pl.BlockSpec(memory_space=pl.ANY))
        if gated:
            aliases[len(args)] = 1
            args.append(gates)
            in_specs.append(pl.BlockSpec(memory_space=pl.ANY))
    return call(
        functools.partial(dispatch_kernel, here, local, cap, gated),
        shapes,
        args,
        2 * here * local * cap * places.shape[1] * width,
        "dispatch",
        scalars=(mine,),
        in_specs=in_specs,
        out_specs=out_specs,
        aliases=aliases,
        after=after,
    )


def expert_kernel(
    x_ref, d_ref, gate_ref, wg_ref, wu_ref, wd_ref,
    act_ref, dg_ref, du_ref, dots_ref, mix_ref, back_ref, mix_acc, back_acc,
):
    step = pl.program_id(1)
    last = pl.num_programs(1) - 1
    x_rows, d_rows, gate = x_ref[0], d_ref[0], gate_ref[0]
    pre = product(x_rows, wg_ref[0])
    up = product(x_rows, wu_ref[0])
    pulled = product_right(d_rows, wd_ref[0])
    sigma = jax.nn.sigmoid(pre)
    silu = pre * sigma
    act = silu * up
    dots = jnp.sum(act * pulled, axis=1, keepdims=True)
    act_low = (act * gate).astype(BF16)
    act_ref[0] = act_low
    d_act = pulled * gate
    du_low = (d_act * silu).astype(BF16)
    dg_low = (d_act * up * sigma * (1.0 + pre * (1.0 - sigma))).astype(BF16)
    dg_ref[0] = dg_low
    du_ref[0] = du_low
    mix = product(act_low, wd_ref[0])
    back = product_right(dg_low, wg_ref[0]) + product_right(du_low, wu_ref[0])

    @pl.when(step == 0)
    def _():
        dots_ref[0] = dots
        mix_acc[...] = mix
        back_acc[...] = back

    @pl.when((step > 0) & (step < last))
    def _():
        dots_ref[0] += dots
        mix_acc[...] += mix
        back_acc[...] += back

    @pl.when(step == last)
    def _():
        dots_ref[0] += dots
        mix_ref[0] = (mix_acc[...] + mix).astype(BF16)
        back_ref[0] = (back_acc[...] + back).astype(BF16)


def experts(rows, d_rows, gates, w_gate, w_up, w_down, after=()):
    local, count, width = rows.shape
    hidden = w_gate.shape[2]
    part = hidden // 2
    wide = pl.BlockSpec((1, count, width), lambda e, f: (e, 0, 0))
    column = pl.BlockSpec((1, count, 1), lambda e, f: (e, 0, 0))
    thin = pl.BlockSpec((1, count, part), lambda e, f: (e, 0, f))
    into = pl.BlockSpec((1, width, part), lambda e, f: (e, 0, f))
    outof = pl.BlockSpec((1, part, width), lambda e, f: (e, f, 0))
    return call(
        expert_kernel,
        [like((local, count, hidden), BF16)] * 3
        + [like((local, count, 1), F32)]
        + [like((local, count, width), BF16)] * 2,
        [rows, d_rows, gates, w_gate, w_up, w_down],
        12 * rows.size * hidden,
        "experts",
        after=after,
        scratch=[pltpu.VMEM((count, width), F32)] * 2,
        grid=(local, 2),
        in_specs=[wide, wide, column, into, into, outof],
        out_specs=[thin, thin, thin, column, wide, wide],
    )


def combine_kernel(here, local, cap, dotted, places_ref, rows_ref, *refs):
    pieces = refs[int(dotted) : int(dotted) + here]
    for p in range(here):
        chosen = [chooser(places_ref, p * local + e, cap) for e in range(local)]
        total = None
        for e in range(local):
            part = product_left(chosen[e].astype(BF16), rows_ref[e, p * cap : (p + 1) * cap, :])
            total = part if total is None else total + part
            if dotted:
                refs[-1][p * local + e : p * local + e + 1, :] = jnp.sum(
                    jnp.where(chosen[e], refs[0][e, p * cap : (p + 1) * cap, :], 0.0),
                    axis=0, keepdims=True,
                )
        pieces[p][...] = total.astype(BF16)


def combine(places, rows, here, local, cap, at, dots=None, after=()):
    width = rows.shape[2]
    tokens = places.shape[1]
    dotted = dots is not None
    args = [places, rows] + ([dots] if dotted else [])
    in_specs = [None, pl.BlockSpec((local, here * cap, width), lambda i: (0, at, 0))]
    if dotted:
        in_specs.append(pl.BlockSpec((local, here * cap, 1), lambda i: (0, at, 0)))
    shapes = [like((tokens, width), BF16)] * here
    if dotted:
        shapes.append(like(places.shape, F32))
    return call(
        functools.partial(combine_kernel, here, local, cap, dotted),
        shapes,
        args,
        2 * here * local * cap * tokens * width,
        "combine",
        after=after,
        in_specs=in_specs,
    )


def combine_stacks_kernel(count, local, cap, group, places_ref, *refs):
    groups = count // group
    for k in range(count):
        rows = refs[k // group]
        at = (k % group) * cap
        total = None
        for e in range(local):
            chosen = chooser(places_ref, k * local + e, cap).astype(BF16)
            part = product_left(chosen, rows[e, at : at + cap, :])
            total = part if total is None else total + part
        array, place = stack_at(k, count)
        refs[groups + array][place] = total.astype(BF16)


def combine_stacks(places, rows, count, local, cap, group, after):
    tokens, width = places.shape[1], rows[0].shape[2]
    return call(
        functools.partial(combine_stacks_kernel, count, local, cap, group),
        stack_shapes(count, (tokens, width)),
        [places, *rows],
        2 * count * local * cap * tokens * width,
        "combine_stacks",
        after=after,
    )


def weight_grad_kernel(groups, *refs):
    lefts, rights = refs[:groups], refs[groups : 2 * groups]
    total = None
    for left, right in zip(lefts, rights):
        part = product_left(left[0], right[0])
        total = part if total is None else total + part
    refs[-1][0] = total.astype(BF16)


def weight_grad(lefts, rights, after=()):
    local, count, tall = lefts[0].shape
    wide = rights[0].shape[2]
    part = min(512, tall)
    left = pl.BlockSpec((1, count, part), lambda e, i: (e, 0, i))
    right = pl.BlockSpec((1, count, wide), lambda e, i: (e, 0, 0))
    return call(
        functools.partial(weight_grad_kernel, len(lefts)),
        like((local, tall, wide), BF16),
        [*lefts, *rights],
        2 * len(lefts) * lefts[0].size * wide,
        "weight_grad",
        after=after,
        grid=(local, tall // part),
        in_specs=[left] * len(lefts) + [right] * len(lefts),
        out_specs=[pl.BlockSpec((1, part, wide), lambda e, i: (e, i, 0))],
    )


def body(
    tokens, doc_lengths, routes, attn_gain, w_query, w_key, w_value, q_gain, k_gain, w_out,
    ffn_gain, w_router, w_gate, w_up, w_down, cotangent,
):
    n_sp = lax.axis_size("sp")
    n_ep = lax.axis_size("ep")
    sp_index = lax.axis_index("sp")
    ep_index = lax.axis_index("ep")
    tok_dev, width = tokens.shape[1:]
    total = tok_dev * n_sp
    shard = width // n_ep
    head_width = width // n_sp
    top_count = routes.shape[2]
    local = w_gate.shape[0]
    expert_count = local * n_ep
    capacity = 9 * tok_dev * top_count // (8 * expert_count)
    cap = -(-capacity // 16) * 16
    group = 4
    blocks = piece_blocks(n_ep, ep_index)
    partners = jnp.bitwise_xor(jnp.arange(n_sp, dtype=jnp.int32), sp_index)
    ids = jnp.concatenate([blocks, partners]).astype(jnp.int32)
    mine = ep_index.astype(jnp.int32).reshape(1)

    def own_columns(value):
        return lax.dynamic_slice_in_dim(value, sp_index * head_width, head_width, 1)

    def by_piece(value):
        return jnp.stack(
            [lax.dynamic_index_in_dim(value, blocks[i], 0, keepdims=False) for i in range(n_ep)]
        )

    expert_ids = jnp.arange(expert_count, dtype=jnp.int32)
    picked = jnp.any(routes[0][:, :, None] == expert_ids[None, None, :], axis=1)
    picked_low = picked.T.astype(BF16)
    small = jnp.concatenate(
        [
            jnp.stack([attn_gain, q_gain, k_gain, ffn_gain]),
            jnp.zeros((12, shard), BF16),
            w_router.T,
        ],
        axis=0,
    )

    def to_all(value):
        value = jnp.broadcast_to(value[None], (n_ep, *value.shape))
        return lax.all_to_all(value, "ep", split_axis=0, concat_axis=0, tiled=True)

    if shard == tok_dev:
        both = to_all(jnp.concatenate([small, picked_low], axis=0))
        small_all, picked_all = both[:, : 16 + expert_count], both[:, 16 + expert_count :]
    else:
        small_all, picked_all = to_all(small), to_all(picked_low)
    small_rows = jnp.swapaxes(small_all, 0, 1).reshape(16 + expert_count, width)
    gains = small_rows[:4].astype(F32)
    full_router = small_rows[16:]
    picked_all = by_piece(picked_all)

    x_all = lax.all_gather(tokens[0], "sp", axis=0, tiled=True)
    w_own = jnp.concatenate([own_columns(w) for w in (w_query, w_key, w_value, w_out)], axis=1)
    cot_own = cotangent[0]
    if n_ep == 8:
        w_pieces = gather_steps(w_own)[0]
        w_pieces[6], cot_own = tie(w_pieces[6], cot_own)
        cot_pieces, w_pieces[7] = gather_steps(cot_own, w_pieces[7])
    else:
        w_pieces, cot_pieces = gather_whole(w_own), gather_whole(cot_own)

    upper = (
        jnp.arange(tok_dev, dtype=jnp.int32)[:, None] < jnp.arange(tok_dev, dtype=jnp.int32)[None, :]
    ).astype(BF16)
    picked_mine = lax.dynamic_slice_in_dim(picked_all, ep_index * local, local, 1)
    picked_mine = picked_mine.reshape(n_ep * local, tok_dev)
    earlier = product(picked_mine, upper).astype(jnp.int32)
    places = jnp.where((picked_mine > 0) & (earlier < capacity), earlier, -1)
    picked_flat = picked_all.reshape(n_ep * expert_count, tok_dev).astype(F32)

    positions = jnp.arange(total, dtype=jnp.int32)
    lengths = doc_lengths[0]
    doc_ends = jnp.cumsum(lengths)
    starts = jnp.sum(
        jnp.where(doc_ends[None, :] <= positions[:, None], lengths[None, :], 0), axis=1
    )
    half = HEAD_DIM // 2
    frequency = THETA ** (-(2.0 * jnp.arange(half, dtype=F32)) / HEAD_DIM)
    angles = (positions - starts).astype(F32)[:, None] * frequency[None, :]
    cosine = jnp.concatenate([jnp.cos(angles), jnp.cos(angles)], axis=1)
    sine = jnp.concatenate([-jnp.sin(angles), jnp.sin(angles)], axis=1)
    starts = starts[:, None].astype(jnp.int32)

    q_raw, k_raw, v_low, squares, w_qkv, w_o, h_all = qkv_project(ids, x_all, gains[0:1], w_pieces)
    scales = lax.rsqrt(sum_sp(squares) / width + EPS)
    w_o_parts = gather_sp(w_o)
    gain_q, gain_k = own_columns(gains)[1:2], own_columns(gains)[2:3]
    q_rot, k_rot, mixed = attend(
        q_raw, k_raw, v_low, scales, gain_q, gain_k, cosine, sine, starts
    )

    def pair_places(p):
        return places[p * local : (p + 2) * local]

    def cot_rows(g, after):
        d_rows = None
        for at, p in enumerate(range(g, g + group, 2)):
            (d_rows,) = dispatch(
                mine, cot_pieces[p : p + 2], pair_places(p), None, None, local, cap, group, at,
                d_rows, None, after,
            )
        return d_rows

    attn_tok = lax.all_to_all(mixed, "sp", split_axis=0, concat_axis=1, tiled=True)
    near_rows = cot_rows(0, [])
    x_one, h2_low = out_project(
        ids, n_ep, attn_tok, tokens[0], gains[3:4], w_o_parts, []
    )
    attn_all = lax.all_gather(attn_tok, "sp", axis=0, tiled=True)

    h2_pieces = gather(h2_low, n_ep)
    cots = [near_rows] + [cot_rows(g, [x_one]) for g in range(group, n_ep, group)]
    groups, d_pieces, d_gates, d_sums = [], [], [], []
    home_gates = None

    def rows_of(g, after):
        rows = gates = first_gates = None
        for at, p in enumerate(range(g, g + group, 2)):
            rows, gates, piece_gates = dispatch(
                mine, h2_pieces[p : p + 2], pair_places(p),
                picked_flat[p * expert_count : (p + 2) * expert_count], full_router, local, cap,
                group, at, rows, gates, after,
            )
            first_gates = piece_gates if first_gates is None else first_gates
        return rows, gates, first_gates

    rows, gates, home_gates = rows_of(0, [])
    for g in range(0, n_ep, group):
        d_rows = cots[g // group]
        made = experts(rows, d_rows, gates, w_gate, w_up, w_down, d_pieces[-group:] + cots + h2_pieces[6:7])
        groups.append((rows, d_rows, made))
        following = []
        if g + group < n_ep:
            rows, gates, _ = rows_of(g + group, [made[5]])
            following = [rows]
        sums_before = list(d_sums)
        for at in range(group // 2):
            *two, dots = combine(
                pair_places(g + 2 * at), made[5], 2, local, cap, at, made[3],
                sums_before + following,
            )
            d_pieces += two
            d_gates.append(dots)
        if n_ep == 8:
            d_sums += crossed_sums(d_pieces[-group:])

    acts = [made[0] for _, _, made in groups]
    d_gate_rows = [made[1] for _, _, made in groups]
    d_up_rows = [made[2] for _, _, made in groups]
    ins = [rows for rows, _, _ in groups]
    outs = [d_rows for _, d_rows, _ in groups]
    mix_stacks = combine_stacks(
        places, [made[4] for _, _, made in groups], n_ep, local, cap, group, d_pieces
    )
    grad_down = weight_grad(acts, outs, mix_stacks[:1])
    d_gates = by_piece(jnp.concatenate(d_gates, axis=0).reshape(n_ep, local, tok_dev))
    d_gates = lax.all_to_all(d_gates, "ep", split_axis=0, concat_axis=0, tiled=True)
    d_gates = d_gates.reshape(expert_count, tok_dev)
    grad_gate = weight_grad(ins, d_gate_rows, [grad_down, d_gates, *d_sums[3:]])
    if n_ep == 8:
        d_sums[2], mix_stacks[2], mix_stacks[3], grad_down, grad_gate = tie(
            d_sums[2], mix_stacks[2], mix_stacks[3], grad_down, grad_gate
        )
    d_h2 = scatter_z(*d_sums) if n_ep == 8 else scatter(d_pieces, n_ep)
    grad_up = weight_grad(ins, d_up_rows, [*d_sums, grad_gate])

    def over_sp(value):
        return lax.psum_scatter(value, "sp", scatter_dimension=1, tiled=True).astype(F32)


    if n_ep == 8:
        gates_here = home_gates[:expert_count]
    else:
        logits = product_right(full_router, h2_low)
        logits = jnp.where(picked.T, logits, NEG_FILL)
        gates_here = jax.nn.softmax(logits, axis=0)
    d_logits = gates_here * (d_gates - jnp.sum(gates_here * d_gates, axis=0, keepdims=True))
    d_logits = jnp.where(picked.T, d_logits, 0.0).astype(BF16)
    grad_router = product(d_logits, h2_low)
    d_h2 = d_h2 + product_left(d_logits, full_router)
    one_scale = lax.rsqrt(jnp.mean(x_one * x_one, axis=-1, keepdims=True) + EPS)
    one_normed = x_one * one_scale
    grad_ffn = jnp.sum(d_h2 * one_normed, axis=0)
    d_normed = d_h2 * gains[3][None, :]
    d_one = cotangent[0].astype(F32) + one_scale * (
        d_normed - one_normed * jnp.mean(d_normed * one_normed, axis=-1, keepdims=True)
    )
    d_z, grad_up = tie(d_one.astype(BF16), grad_up)
    d_attn = out_back(ids, n_ep, d_z, w_o_parts, [])
    d_heads = lax.all_to_all(d_attn, "sp", split_axis=1, concat_axis=0, tiled=True)
    d_z_cols = lax.all_to_all(d_z, "sp", split_axis=1, concat_axis=0, tiled=True)
    mix, mix_far = scatter_stacks(mix_stacks, n_ep)
    if n_ep == 8:
        mix, mix_far, d_heads = tie(mix, mix_far, d_heads)
    grad_down, grad_gate, grad_up = over_sp(grad_down), over_sp(grad_gate), over_sp(grad_up)

    d_qn, d_kn, d_v, sums, grad_qg, grad_kg = attend_back(
        q_rot, k_rot, v_low, d_heads, q_raw, k_raw, scales, gain_q, gain_k, cosine, sine, starts
    )
    output = (x_one + last_hop(mix, mix_far)).astype(BF16)
    vo_stacks = vo_grads(ids, n_ep, h_all, d_v, attn_all, d_z_cols)
    grad_vo = last_hop(*scatter_stacks(vo_stacks, n_ep)).astype(BF16)

    def placed(value):
        return lax.dynamic_update_slice_in_dim(
            jnp.zeros((1, width), F32), value, sp_index * head_width, 1
        )

    tiny = jnp.concatenate(
        [placed(grad_qg), placed(grad_kg), grad_ffn[None], grad_router], axis=0
    )
    *qk_stacks, d_qk = qk_back(
        ids, n_ep, h_all, d_qn, d_kn, q_raw, k_raw, scales, sum_sp(sums), tiny, vo_stacks[:1]
    )
    grad_qk, qk_far = scatter_stacks(qk_stacks, n_ep)
    if n_ep == 8:
        qk_far, grad_vo = tie(qk_far, grad_vo)
    grad_qk = last_hop(grad_qk, qk_far).astype(BF16)
    grad_qk, grad_down, grad_gate, grad_up = tie(grad_qk, grad_down, grad_gate, grad_up)

    d_h = d_h_rows(ids, n_ep, n_sp, d_qk, d_v, w_qkv)
    output, d_h = tie(output, d_h)
    halves = plus(d_h[:2], swap_sp(d_h[2:], 1))
    d_h = halves[0].astype(F32) + swap_sp(halves[1], 2).astype(F32)
    x_rows = tokens[0].astype(F32)
    x_scale = lax.rsqrt(jnp.mean(x_rows * x_rows, axis=-1, keepdims=True) + EPS)
    x_normed = x_rows * x_scale
    d_normed = d_h * gains[0][None, :]
    input_grad = d_one + x_scale * (
        d_normed - x_normed * jnp.mean(d_normed * x_normed, axis=-1, keepdims=True)
    )

    g_query, g_key, g_value, g_out, tiny, g_attn = finish(
        ids, n_ep, w_query, w_key, w_value, attn_gain.astype(F32)[:, None],
        gather_sp(grad_qk), gather_sp(grad_vo), [grad_down, grad_gate, grad_up, input_grad],
    )
    per_row = 2 * head_width // shard

    def vector(at):
        col = (at % per_row) * shard
        return tiny[at // per_row, col : col + shard]

    g_router = jnp.stack([vector(3 + i) for i in range(expert_count)], axis=1)
    return (
        output[None], input_grad[None], g_attn[:, 0], g_query, g_key, g_value, vector(0), vector(1),
        g_out, vector(2), g_router, grad_gate, grad_up, grad_down,
    )


def solution(mesh):
    seq = P("ep", "sp", None)
    vec = P("ep")
    mat = P("ep", None)
    expert = P("ep", None, None)
    in_specs = (
        seq, mat, seq, vec, mat, mat, mat, vec, vec, mat, vec, mat, expert, expert, expert, seq,
    )
    out_specs = (
        seq, seq, vec, mat, mat, mat, vec, vec, mat, vec, mat, seq, seq, seq,
    )
    return jax.shard_map(body, mesh=mesh, in_specs=in_specs, out_specs=out_specs, check_vma=False)
```

```python
import functools

import jax
import jax.numpy as jnp
from jax import lax
from jax.experimental import pallas as pl
from jax.experimental.pallas import tpu as pltpu
from jax.sharding import PartitionSpec as P

HEAD_DIM = 128
EPS = 1e-05
THETA = 10000.0
NEG_FILL = -1e30
F32 = jnp.float32
BF16 = jnp.bfloat16
MIB = 1 << 20
COVER = 20


def product(left, right):
    return jnp.dot(left, right, preferred_element_type=F32)


def product_left(left, right):
    return lax.dot_general(left, right, (((0,), (0,)), ((), ())), preferred_element_type=F32)


def product_right(left, right):
    return lax.dot_general(left, right, (((1,), (1,)), ((), ())), preferred_element_type=F32)


def row_sums(values_in):
    sums = jnp.sum(values_in, axis=1, keepdims=True)
    return jnp.transpose(jnp.broadcast_to(sums, (sums.shape[0], HEAD_DIM)))[:8]


def call(kernel, out_shape, args, flops, name, scratch=(), scalars=(), grid=(1,), in_specs=None,
         out_specs=None, aliases=None, vmem=60, after=()):
    single = not isinstance(out_shape, (list, tuple))
    shapes = [out_shape] if single else list(out_shape)
    count = len(grid)

    def fixed(shape):
        rank = len(shape)
        return pl.BlockSpec(tuple(shape), lambda *ids: (0,) * rank)

    in_specs = in_specs or [None] * len(args)
    out_specs = out_specs or [None] * len(shapes)
    in_specs = [s if s is not None else fixed(a.shape) for s, a in zip(in_specs, args)]
    out_specs = [s if s is not None else fixed(o.shape) for s, o in zip(out_specs, shapes)]
    waited = len(after)
    args = [*args, *after]
    in_specs = in_specs + [pl.BlockSpec(memory_space=pl.ANY)] * waited
    if waited:
        inner, first = kernel, len(scalars) + len(args) - waited

        def kernel(*refs):
            inner(*refs[:first], *refs[first + waited :])

    moved = sum(a.size * a.dtype.itemsize for a in args[: len(args) - waited])
    moved += sum(o.size * o.dtype.itemsize for o in shapes)
    result = pl.pallas_call(
        kernel,
        grid_spec=pltpu.PrefetchScalarGridSpec(
            num_scalar_prefetch=len(scalars), grid=grid, in_specs=in_specs, out_specs=out_specs,
            scratch_shapes=list(scratch),
        ),
        out_shape=shapes,
        input_output_aliases={k + len(scalars): v for k, v in (aliases or {}).items()},
        compiler_params=pltpu.CompilerParams(
            vmem_limit_bytes=vmem * MIB, dimension_semantics=("arbitrary",) * count
        ),
        cost_estimate=pl.CostEstimate(flops=int(COVER * flops), bytes_accessed=int(moved), transcendentals=0),
        name=name,
    )(*scalars, *args)
    return result[0] if single else list(result)


def like(shape, dtype):
    return jax.ShapeDtypeStruct(tuple(shape), dtype)


def tie(*values):
    return lax.optimization_barrier(values)


def swap(value, bits):
    return lax.ppermute(value, "ep", [(i, i ^ bits) for i in range(8)])


def swap_sp(value, bits):
    return lax.ppermute(value, "sp", [(i, i ^ bits) for i in range(4)])


def piece_blocks(n_ep, ep_index):
    ids = jnp.arange(n_ep, dtype=jnp.int32)
    return jnp.bitwise_xor(ids, ep_index) if n_ep == 8 else ids


MIDDLE = [(2, 4), (3, 5), (4, 2), (5, 3)]
OUTWARD = [(2, 0), (3, 1), (4, 6), (5, 7)]


def gather_line(value):
    crossed = swap(value, 1)
    near = swap(value, 2)
    inner = lax.ppermute(value, "ep", MIDDLE)
    near_x, outer = swap(near, 1), lax.ppermute(near, "ep", MIDDLE)
    near_x, crossed, outer = tie(near_x, crossed, outer)
    far = outer + lax.ppermute(inner, "ep", OUTWARD)
    farther = inner + lax.ppermute(outer, "ep", OUTWARD)
    return [value, crossed, near, near_x, far, swap(far, 1), farther, swap(farther, 1)]


def gather_double(value, after):
    near, far = swap(value, 2), swap(value, 4)
    farther = swap(far, 2)
    after, crossed, near = tie(after, value, near)
    return [
        value, swap(crossed, 1), near, swap(near, 1), far, swap(far, 1), farther, swap(farther, 1)
    ], after


def gather_whole(value):
    whole = lax.all_gather(value, "ep", axis=0, tiled=False)
    return [whole[i] for i in range(whole.shape[0])]


def gather(value, n_ep):
    return gather_line(value) if n_ep == 8 else gather_whole(value)


def plus(left, right):
    return (left.astype(F32) + right.astype(F32)).astype(left.dtype)


def crossed_sums(pieces):
    return [plus(pieces[i], swap(pieces[i + 1], 1)) for i in range(0, len(pieces), 2)]


def scatter_z(own, near, far, farther):
    far = plus(far, swap(farther, 2))
    far, near = tie(far, near)
    return own.astype(F32) + swap(near, 2).astype(F32) + swap(far, 4).astype(F32), far


def scatter(pieces, n_ep):
    if n_ep != 8:
        stacked = jnp.stack(pieces)
        return lax.psum_scatter(stacked, "ep", scatter_dimension=0, tiled=False).astype(F32)
    return scatter_z(*crossed_sums(pieces))[0]


def stack_at(piece, n_ep):
    if n_ep != 8:
        return 0, piece
    return 2 * (piece % 2) + (piece // 2) % 2, piece // 4


def stack_at_z(piece, n_ep):
    if n_ep != 8:
        return 0, piece
    return (piece // 2) % 2, 2 * (piece % 2) + piece // 4


def stack_shapes_z(n_ep, shape):
    return [like((4, *shape), BF16)] * 2 if n_ep == 8 else [like((n_ep, *shape), BF16)]


def scatter_stacks_z(stacks, n_ep):
    if n_ep != 8:
        return scatter_stacks(stacks, n_ep)[0]
    even = stacks[0].astype(F32) + swap(stacks[1], 2).astype(F32)
    far = jnp.concatenate([even[1:2], even[3:4]]).astype(BF16)
    far = swap(far, 4).astype(F32)
    return even[0] + far[0] + swap((even[2] + far[1]).astype(BF16), 1).astype(F32)


def stack_shapes(n_ep, shape):
    return [like((2, *shape), BF16)] * 4 if n_ep == 8 else [like((n_ep, *shape), BF16)]


def scatter_stacks(stacks, n_ep):
    if n_ep != 8:
        total = lax.psum_scatter(stacks[0], "ep", scatter_dimension=0, tiled=False)
        return total.astype(F32), None
    even, odd, even_sent, odd_sent = stacks
    odd = plus(odd, swap(odd_sent, 1))
    even = even.astype(F32) + swap(even_sent, 1).astype(F32) + swap(odd, 2).astype(F32)
    return even[0], even[1].astype(BF16)


def last_hop(total, far):
    return total if far is None else total + swap(far, 4).astype(F32)


def gather_sp(value):
    over = swap_sp(value, 2)
    return [value, swap_sp(value, 1), over, swap_sp(over, 1)]


def sum_sp(value):
    return (value + swap_sp(value, 1)) + (swap_sp(value, 2) + swap_sp(value, 3))


def block_at(ids, position, size):
    if size % HEAD_DIM:
        return pl.ds(position * size, size)
    return pl.ds(pl.multiple_of(ids[position] * size, size), size)


def qkv_kernel(count, ids, x_ref, gain_ref, *refs):
    pieces, refs = refs[:count], refs[count:]
    q_ref, k_ref, v_ref, squares_ref, w_ref, out_ref, h_ref = refs
    shard = pieces[0].shape[0]
    width = q_ref.shape[1]

    @pl.when(pl.program_id(0) == 0)
    def _():
        for k in range(count):
            rows = block_at(ids, k, shard)
            w_ref[rows, :] = pieces[k][:, : 3 * width]
            out_ref[rows, :] = pieces[k][:, 3 * width :]

    x_rows = x_ref[...].astype(F32)
    scale = lax.rsqrt(jnp.mean(x_rows * x_rows, axis=1, keepdims=True) + EPS)
    h_ref[...] = (x_rows * scale * gain_ref[...]).astype(BF16)
    for at, ref in enumerate((q_ref, k_ref)):
        part = product(h_ref[...], w_ref[:, at * width : (at + 1) * width])
        ref[...] = part
        squares_ref[8 * at : 8 * at + 8, :] = row_sums(part * part)
    v_ref[...] = product(h_ref[...], w_ref[:, 2 * width :]).astype(BF16)


def qkv_project(ids, x_all, gain, pieces):
    total, depth = x_all.shape
    width = pieces[0].shape[1] // 4
    rows = min(256, total)
    block = pl.BlockSpec((rows, width), lambda i, ids: (i, 0))
    wide = pl.BlockSpec((rows, depth), lambda i, ids: (i, 0))
    return call(
        functools.partial(qkv_kernel, len(pieces)),
        [like((total, width), F32)] * 2
        + [like((total, width), BF16), like((16, total), F32), like((depth, 3 * width), BF16)]
        + [like((depth, width), BF16), like((total, depth), BF16)],
        [x_all, gain, *pieces],
        6 * total * depth * width,
        "qkv_project",
        scalars=(ids,),
        grid=(total // rows,),
        in_specs=[wide] + [None] * (len(pieces) + 1),
        out_specs=[
            block, block, block, pl.BlockSpec((16, rows), lambda i, ids: (0, i)), None, None, wide,
        ],
    )


def out_kernel(n_ep, ids, attn_ref, x_ref, gain_ref, *refs):
    weights, (one_ref, low_ref) = refs[:-2], refs[-2:]
    width = weights[0].shape[1]
    for j, weight in enumerate(weights):
        cols = block_at(ids, n_ep + j, width)
        one_ref[:, cols] = x_ref[:, cols].astype(F32) + product(attn_ref[...], weight[...])
    one = one_ref[...]
    scale = lax.rsqrt(jnp.mean(one * one, axis=1, keepdims=True) + EPS)
    low_ref[...] = (one * scale * gain_ref[...]).astype(BF16)


def out_project(ids, n_ep, attn_tok, tokens, gain, weights, after):
    return call(
        functools.partial(out_kernel, n_ep),
        [like(tokens.shape, F32), like(tokens.shape, BF16)],
        [attn_tok, tokens, gain, *weights],
        2 * tokens.size * attn_tok.shape[1],
        "out_project",
        after=after,
        scalars=(ids,),
    )


def out_back_kernel(n_ep, ids, d_ref, *refs):
    weights, d_attn_ref = refs[:-1], refs[-1]
    width = weights[0].shape[1]
    total = None
    for j, weight in enumerate(weights):
        part = product_right(d_ref[:, block_at(ids, n_ep + j, width)], weight[...])
        total = part if total is None else total + part
    d_attn_ref[...] = total.astype(BF16)


def out_back(ids, n_ep, d_z, weights, after):
    return call(
        functools.partial(out_back_kernel, n_ep),
        like((d_z.shape[0], weights[0].shape[0]), BF16),
        [d_z, *weights],
        2 * d_z.size * weights[0].shape[0],
        "out_back",
        after=after,
        scalars=(ids,),
    )


def vo_grads_kernel(count, shard, ids, h_ref, dv_ref, attn_ref, dz_ref, *stacks):
    width = dv_ref.shape[1]
    for k in range(count):
        block = block_at(ids, k, shard)
        array, place = stack_at_z(k, count)
        stacks[array][place, :, :width] = product_left(h_ref[:, block], dv_ref[...]).astype(BF16)
        stacks[array][place, :, width:] = product_left(attn_ref[:, block], dz_ref[...]).astype(BF16)


def vo_grads(ids, count, h_all, d_v, attn_all, d_z_cols):
    shard = h_all.shape[1] // count
    width = d_v.shape[1]
    return call(
        functools.partial(vo_grads_kernel, count, shard),
        stack_shapes_z(count, (shard, 2 * width)),
        [h_all, d_v, attn_all, d_z_cols],
        4 * h_all.size * width,
        "vo_grads",
        scalars=(ids,),
    )


def qk_back_kernel(
    count, shard, ids, h_ref, dqn_ref, dkn_ref, qr_ref, kr_ref, scale_ref, sums_ref, tiny_ref, *refs
):
    stacks, d_ref = refs[:-1], refs[-1]
    width = dqn_ref.shape[1]
    scales = jnp.transpose(scale_ref[...])
    means = jnp.transpose(sums_ref[...]) * (1.0 / h_ref.shape[1])
    for at, (d_normed, raw) in enumerate(((dqn_ref, qr_ref), (dkn_ref, kr_ref))):
        scale, mean = scales[:, 8 * at : 8 * at + 1], means[:, 8 * at : 8 * at + 1]
        d_ref[:, at * width : (at + 1) * width] = (
            scale * (d_normed[...] - raw[...] * scale * mean)
        ).astype(BF16)
    per_row = 2 * width // shard
    extra = stacks[0].shape[1] - shard
    for k in range(count):
        block = block_at(ids, k, shard)
        array, place = stack_at(k, count)
        ref = stacks[array]
        ref[place, :shard, :] = product_left(h_ref[:, block], d_ref[...]).astype(BF16)
        ref[place, shard:, :] = jnp.zeros((extra, 2 * width), BF16)
        for at in range(tiny_ref.shape[0]):
            row, col = shard + at // per_row, (at % per_row) * shard
            ref[place, row : row + 1, col : col + shard] = tiny_ref[at : at + 1, block].astype(BF16)


def qk_back(ids, count, h_all, d_qn, d_kn, q_raw, k_raw, scales, sums, tiny, after):
    total, depth = h_all.shape
    width = d_qn.shape[1]
    shard = depth // count
    extra = -(-tiny.shape[0] // (2 * width // shard))
    extra = -(-extra // 16) * 16
    return call(
        functools.partial(qk_back_kernel, count, shard),
        stack_shapes(count, (shard + extra, 2 * width)) + [like((total, 2 * width), BF16)],
        [h_all, d_qn, d_kn, q_raw, k_raw, scales, sums, tiny],
        2 * h_all.size * 2 * width,
        "qk_back",
        scalars=(ids,),
        after=after,
    )


def d_h_kernel(ids, d_ref, dv_ref, w_ref, out_ref):
    both = d_ref.shape[1]
    out_ref[0] = (
        product_right(d_ref[...], w_ref[:, :both]) + product_right(dv_ref[...], w_ref[:, both:])
    ).astype(BF16)


def d_h_rows(ids, n_ep, n_sp, d_qk, d_v, w_qkv):
    total, wide = d_qk.shape
    depth = w_qkv.shape[0]
    rows = total // n_sp

    def partner(j, ids):
        return ids[n_ep + (j % 2) * 2 + j // 2], 0

    return call(
        d_h_kernel,
        like((n_sp, rows, depth), BF16),
        [d_qk, d_v, w_qkv],
        3 * d_qk.size * depth,
        "d_h",
        scalars=(ids,),
        grid=(n_sp,),
        in_specs=[
            pl.BlockSpec((rows, wide), partner), pl.BlockSpec((rows, d_v.shape[1]), partner), None,
        ],
        out_specs=[pl.BlockSpec((1, rows, depth), lambda j, ids: (j, 0, 0))],
    )


def finish_kernel(n_ep, n_sp, ids, wq_ref, wk_ref, wv_ref, gain_ref, *refs):
    firsts, seconds = refs[:n_sp], refs[n_sp : 2 * n_sp]
    gq_ref, gk_ref, gv_ref, go_ref, tiny_ref, attn_ref = refs[2 * n_sp :]
    shard = wq_ref.shape[0]
    width = firsts[0].shape[1] // 2
    dots = jnp.zeros((shard, 1), F32)
    tiny = jnp.zeros(tiny_ref.shape, F32)
    for j in range(n_sp):
        cols = block_at(ids, n_ep + j, width)
        for at, grad, weight in ((0, gq_ref, wq_ref), (1, gk_ref, wk_ref), (2, gv_ref, wv_ref)):
            part = firsts[j][:shard, at * width : (at + 1) * width] if at < 2 else seconds[j][:, :width]
            value = part.astype(F32)
            grad[:, cols] = value
            dots += jnp.sum(value * weight[:, cols].astype(F32), axis=1, keepdims=True)
        go_ref[:, cols] = seconds[j][:, width:].astype(F32)
        tiny += firsts[j][shard:, :].astype(F32)
    tiny_ref[...] = tiny
    attn_ref[...] = dots / gain_ref[...]


def finish(ids, n_ep, w_query, w_key, w_value, gain, firsts, seconds, after):
    shard, depth = w_query.shape
    extra = firsts[0].shape[0] - shard
    return call(
        functools.partial(finish_kernel, n_ep, len(firsts)),
        [like((shard, depth), F32)] * 4 + [like((extra, firsts[0].shape[1]), F32), like((shard, 1), F32)],
        [w_query, w_key, w_value, gain, *firsts, *seconds],
        shard * depth * 6,
        "finish",
        after=after,
        scalars=(ids,),
    )


def turn(values_in):
    return pltpu.roll(values_in, HEAD_DIM // 2, 1)


def masked_probs(q_ref, k_ref, start_ref, block, rows):
    first, last = block * rows, (block + 1) * rows
    scores = product_right(q_ref[first:last, :], k_ref[0:last, :]) * (HEAD_DIM ** (-0.5))
    row_ids = first + lax.broadcasted_iota(jnp.int32, scores.shape, 0)
    places = lax.broadcasted_iota(jnp.int32, scores.shape, 1)
    allowed = (places <= row_ids) & (places >= start_ref[first:last, :])
    scores = jnp.where(allowed, scores, NEG_FILL)
    top = jnp.max(scores, axis=1, keepdims=True)
    weights = jnp.exp(scores - top)
    return weights * (1.0 / jnp.sum(weights, axis=1, keepdims=True))


def attend_kernel(
    rows, qr_ref, kr_ref, v_ref, scale_ref, gq_ref, gk_ref, cos_ref, sin_ref, start_ref,
    q_ref, k_ref, out_ref,
):
    scales = jnp.transpose(scale_ref[...])
    for at, (raw, gain, low) in enumerate(((qr_ref, gq_ref, q_ref), (kr_ref, gk_ref, k_ref))):
        normed = raw[...] * scales[:, 8 * at : 8 * at + 1] * gain[...]
        low[...] = (normed * cos_ref[...] + turn(normed) * sin_ref[...]).astype(BF16)
    for block in range(q_ref.shape[0] // rows):
        probs = masked_probs(q_ref, k_ref, start_ref, block, rows)
        last = (block + 1) * rows
        out_ref[block * rows : last, :] = product(
            probs.astype(BF16), v_ref[0:last, :]
        ).astype(BF16)


def head_spec(rows):
    return pl.BlockSpec((rows, HEAD_DIM), lambda h: (0, h))


def attend(q_raw, k_raw, v_low, scales, q_gain, k_gain, cosine, sine, starts):
    total, width = v_low.shape
    heads = width // HEAD_DIM
    head, gain = head_spec(total), head_spec(1)
    return call(
        functools.partial(attend_kernel, min(256, total)),
        [like((total, width), BF16)] * 3,
        [q_raw, k_raw, v_low, scales, q_gain, k_gain, cosine, sine, starts],
        3 * heads * total * total * HEAD_DIM,
        "attend",
        grid=(heads,),
        in_specs=[head, head, head, None, gain, gain, None, None, None],
        out_specs=[head, head, head],
    )


def attend_back_kernel(
    rows, q_ref, k_ref, v_ref, do_ref, qr_ref, kr_ref, scale_ref, gq_ref, gk_ref,
    cos_ref, sin_ref, start_ref,
    dq_ref, dk_ref, dv_ref, sums_ref, dgq_ref, dgk_ref, q_acc, k_acc, v_acc,
):
    k_acc[...] = jnp.zeros_like(k_acc)
    v_acc[...] = jnp.zeros_like(v_acc)
    for block in range(q_ref.shape[0] // rows):
        first, last = block * rows, (block + 1) * rows
        probs = masked_probs(q_ref, k_ref, start_ref, block, rows)
        d_rows = do_ref[first:last, :]
        d_probs = product_right(d_rows, v_ref[0:last, :])
        delta = jnp.sum(probs * d_probs, axis=1, keepdims=True)
        d_scores = (probs * (d_probs - delta) * (HEAD_DIM ** (-0.5))).astype(BF16)
        q_acc[first:last, :] = product(d_scores, k_ref[0:last, :])
        k_acc[0:last, :] += product_left(d_scores, q_ref[first:last, :])
        v_acc[0:last, :] += product_left(probs.astype(BF16), d_rows)
    dv_ref[...] = v_acc[...].astype(BF16)

    @pl.when(pl.program_id(0) == 0)
    def _():
        sums_ref[...] = jnp.zeros_like(sums_ref)

    scales = jnp.transpose(scale_ref[...])
    for at, (acc, raw, gain, d_ref, dg_ref) in enumerate(
        ((q_acc, qr_ref, gq_ref, dq_ref, dgq_ref), (k_acc, kr_ref, gk_ref, dk_ref, dgk_ref))
    ):
        turned = acc[...].astype(BF16).astype(F32)
        back = turned * cos_ref[...] + turn(turned * sin_ref[...])
        normed = raw[...] * scales[:, 8 * at : 8 * at + 1]
        both = back * normed
        dg_ref[...] = jnp.sum(both, axis=0, keepdims=True)
        d_ref[...] = back * gain[...]
        sums_ref[8 * at : 8 * at + 8, :] += row_sums(both * gain[...])


def attend_back(
    q_rot, k_rot, v_low, d_heads, q_raw, k_raw, scales, q_gain, k_gain, cosine, sine, starts
):
    total, width = v_low.shape
    heads = width // HEAD_DIM
    head, gain = head_spec(total), head_spec(1)
    wide, thin = like((total, width), F32), like((1, width), F32)
    return call(
        functools.partial(attend_back_kernel, min(256, total)),
        [wide, wide, like((total, width), BF16), like((16, total), F32), thin, thin],
        [q_rot, k_rot, v_low, d_heads, q_raw, k_raw, scales, q_gain, k_gain, cosine, sine, starts],
        7 * heads * total * total * HEAD_DIM,
        "attend_back",
        scratch=[pltpu.VMEM((total, HEAD_DIM), F32)] * 3,
        grid=(heads,),
        in_specs=[head] * 6 + [None, gain, gain, None, None, None],
        out_specs=[head, head, head, None, gain, gain],
    )


def chooser(places_ref, at, cap):
    row = places_ref[at : at + 1, :]
    slots = lax.broadcasted_iota(jnp.int32, (cap, row.shape[1]), 0)
    return slots == row


def dispatch_kernel(
    pieces_here, local, cap, gated, mine, *refs
):
    pieces, refs = refs[:pieces_here], refs[pieces_here:]
    places_ref, refs = refs[0], refs[1:]
    if gated:
        (picked_ref, router_ref), refs = refs[:2], refs[2:]
        rows_ref, gate_ref, all_ref = refs[-3:]
    else:
        rows_ref = refs[-1]
    for p in range(pieces_here):
        if gated:
            logits = product_right(router_ref[...], pieces[p][...])
            experts = logits.shape[0]
            picked = picked_ref[p * experts : (p + 1) * experts, :] > 0
            logits = jnp.where(picked, logits, NEG_FILL)
            weights = jnp.exp(logits - jnp.max(logits, axis=0, keepdims=True))
            weights = jnp.where(picked, weights, 0.0)
            gates = weights / jnp.sum(weights, axis=0, keepdims=True)
            all_ref[p * experts : (p + 1) * experts, :] = gates
        for e in range(local):
            chosen = chooser(places_ref, p * local + e, cap)
            rows_ref[e, p * cap : (p + 1) * cap, :] = product(
                chosen.astype(BF16), pieces[p][...]
            ).astype(BF16)
            if gated:
                row = all_ref[pl.ds(p * experts + mine[0] * local + e, 1), :]
                gate_ref[e, p * cap : (p + 1) * cap, :] = jnp.sum(
                    jnp.where(chosen, row, 0.0), axis=1, keepdims=True
                )


def dispatch(mine, pieces, places, picked, router, local, cap, group, at, rows, gates, after=()):
    gated = router is not None
    here = len(pieces)
    width = pieces[0].shape[1]
    args = [*pieces, places]
    shapes = [like((local, group * cap, width), BF16)]
    spec = pl.BlockSpec((local, here * cap, width), lambda i, mine: (0, at, 0))
    out_specs = [spec]
    if gated:
        args += [picked, router]
        shapes += [like((local, group * cap, 1), F32), like((picked.shape[0], places.shape[1]), F32)]
        out_specs += [pl.BlockSpec((local, here * cap, 1), lambda i, mine: (0, at, 0)), None]
    in_specs = [None] * len(args)
    aliases = {}
    if rows is not None:
        aliases[len(args)] = 0
        args.append(rows)
        in_specs.append(pl.BlockSpec(memory_space=pl.ANY))
        if gated:
            aliases[len(args)] = 1
            args.append(gates)
            in_specs.append(pl.BlockSpec(memory_space=pl.ANY))
    return call(
        functools.partial(dispatch_kernel, here, local, cap, gated),
        shapes,
        args,
        2 * here * local * cap * places.shape[1] * width,
        "dispatch",
        scalars=(mine,),
        in_specs=in_specs,
        out_specs=out_specs,
        aliases=aliases,
        after=after,
    )


def expert_kernel(
    x_ref, d_ref, gate_ref, wg_ref, wu_ref, wd_ref,
    act_ref, dg_ref, du_ref, dots_ref, mix_ref, back_ref, mix_acc, back_acc,
):
    step = pl.program_id(1)
    last = pl.num_programs(1) - 1
    x_rows, d_rows, gate = x_ref[0], d_ref[0], gate_ref[0]
    pre = product(x_rows, wg_ref[0])
    up = product(x_rows, wu_ref[0])
    pulled = product_right(d_rows, wd_ref[0])
    sigma = jax.nn.sigmoid(pre)
    silu = pre * sigma
    act = silu * up
    dots = jnp.sum(act * pulled, axis=1, keepdims=True)
    act_low = (act * gate).astype(BF16)
    act_ref[0] = act_low
    d_act = pulled * gate
    du_low = (d_act * silu).astype(BF16)
    dg_low = (d_act * up * sigma * (1.0 + pre * (1.0 - sigma))).astype(BF16)
    dg_ref[0] = dg_low
    du_ref[0] = du_low
    mix = product(act_low, wd_ref[0])
    back = product_right(dg_low, wg_ref[0]) + product_right(du_low, wu_ref[0])

    @pl.when(step == 0)
    def _():
        dots_ref[0] = dots
        mix_acc[...] = mix
        back_acc[...] = back

    @pl.when((step > 0) & (step < last))
    def _():
        dots_ref[0] += dots
        mix_acc[...] += mix
        back_acc[...] += back

    @pl.when(step == last)
    def _():
        dots_ref[0] += dots
        mix_ref[0] = (mix_acc[...] + mix).astype(BF16)
        back_ref[0] = (back_acc[...] + back).astype(BF16)


def experts(rows, d_rows, gates, w_gate, w_up, w_down, after=()):
    local, count, width = rows.shape
    hidden = w_gate.shape[2]
    part = hidden // 2
    wide = pl.BlockSpec((1, count, width), lambda e, f: (e, 0, 0))
    column = pl.BlockSpec((1, count, 1), lambda e, f: (e, 0, 0))
    thin = pl.BlockSpec((1, count, part), lambda e, f: (e, 0, f))
    into = pl.BlockSpec((1, width, part), lambda e, f: (e, 0, f))
    outof = pl.BlockSpec((1, part, width), lambda e, f: (e, f, 0))
    return call(
        expert_kernel,
        [like((local, count, hidden), BF16)] * 3
        + [like((local, count, 1), F32)]
        + [like((local, count, width), BF16)] * 2,
        [rows, d_rows, gates, w_gate, w_up, w_down],
        12 * rows.size * hidden,
        "experts",
        after=after,
        scratch=[pltpu.VMEM((count, width), F32)] * 2,
        grid=(local, 2),
        in_specs=[wide, wide, column, into, into, outof],
        out_specs=[thin, thin, thin, column, wide, wide],
    )


def combine_kernel(here, local, cap, dotted, places_ref, rows_ref, *refs):
    pieces = refs[int(dotted) : int(dotted) + here]
    for p in range(here):
        chosen = [chooser(places_ref, p * local + e, cap) for e in range(local)]
        total = None
        for e in range(local):
            part = product_left(chosen[e].astype(BF16), rows_ref[e, p * cap : (p + 1) * cap, :])
            total = part if total is None else total + part
            if dotted:
                refs[-1][p * local + e : p * local + e + 1, :] = jnp.sum(
                    jnp.where(chosen[e], refs[0][e, p * cap : (p + 1) * cap, :], 0.0),
                    axis=0, keepdims=True,
                )
        pieces[p][...] = total.astype(BF16)


def combine(places, rows, here, local, cap, at, dots=None, after=()):
    width = rows.shape[2]
    tokens = places.shape[1]
    dotted = dots is not None
    args = [places, rows] + ([dots] if dotted else [])
    in_specs = [None, pl.BlockSpec((local, here * cap, width), lambda i: (0, at, 0))]
    if dotted:
        in_specs.append(pl.BlockSpec((local, here * cap, 1), lambda i: (0, at, 0)))
    shapes = [like((tokens, width), BF16)] * here
    if dotted:
        shapes.append(like(places.shape, F32))
    return call(
        functools.partial(combine_kernel, here, local, cap, dotted),
        shapes,
        args,
        2 * here * local * cap * tokens * width,
        "combine",
        after=after,
        in_specs=in_specs,
    )


def combine_stacks_kernel(count, local, cap, group, places_ref, *refs):
    groups = count // group
    for k in range(count):
        rows = refs[k // group]
        at = (k % group) * cap
        total = None
        for e in range(local):
            chosen = chooser(places_ref, k * local + e, cap).astype(BF16)
            part = product_left(chosen, rows[e, at : at + cap, :])
            total = part if total is None else total + part
        array, place = stack_at(k, count)
        refs[groups + array][place] = total.astype(BF16)


def combine_stacks(places, rows, count, local, cap, group, after):
    tokens, width = places.shape[1], rows[0].shape[2]
    return call(
        functools.partial(combine_stacks_kernel, count, local, cap, group),
        stack_shapes(count, (tokens, width)),
        [places, *rows],
        2 * count * local * cap * tokens * width,
        "combine_stacks",
        after=after,
    )


def weight_grad_kernel(groups, *refs):
    lefts, rights = refs[:groups], refs[groups : 2 * groups]
    total = None
    for left, right in zip(lefts, rights):
        part = product_left(left[0], right[0])
        total = part if total is None else total + part
    refs[-1][0] = total.astype(BF16)


def weight_grad(lefts, rights, after=()):
    local, count, tall = lefts[0].shape
    wide = rights[0].shape[2]
    part = min(512, tall)
    left = pl.BlockSpec((1, count, part), lambda e, i: (e, 0, i))
    right = pl.BlockSpec((1, count, wide), lambda e, i: (e, 0, 0))
    return call(
        functools.partial(weight_grad_kernel, len(lefts)),
        like((local, tall, wide), BF16),
        [*lefts, *rights],
        2 * len(lefts) * lefts[0].size * wide,
        "weight_grad",
        after=after,
        grid=(local, tall // part),
        in_specs=[left] * len(lefts) + [right] * len(lefts),
        out_specs=[pl.BlockSpec((1, part, wide), lambda e, i: (e, i, 0))],
    )


def body(
    tokens, doc_lengths, routes, attn_gain, w_query, w_key, w_value, q_gain, k_gain, w_out,
    ffn_gain, w_router, w_gate, w_up, w_down, cotangent,
):
    n_sp = lax.axis_size("sp")
    n_ep = lax.axis_size("ep")
    sp_index = lax.axis_index("sp")
    ep_index = lax.axis_index("ep")
    tok_dev, width = tokens.shape[1:]
    total = tok_dev * n_sp
    shard = width // n_ep
    head_width = width // n_sp
    top_count = routes.shape[2]
    local = w_gate.shape[0]
    expert_count = local * n_ep
    capacity = 9 * tok_dev * top_count // (8 * expert_count)
    cap = -(-capacity // 16) * 16
    group = 4
    blocks = piece_blocks(n_ep, ep_index)
    partners = jnp.bitwise_xor(jnp.arange(n_sp, dtype=jnp.int32), sp_index)
    ids = jnp.concatenate([blocks, partners]).astype(jnp.int32)
    mine = ep_index.astype(jnp.int32).reshape(1)

    def own_columns(value):
        return lax.dynamic_slice_in_dim(value, sp_index * head_width, head_width, 1)

    def by_piece(value):
        return jnp.stack(
            [lax.dynamic_index_in_dim(value, blocks[i], 0, keepdims=False) for i in range(n_ep)]
        )

    expert_ids = jnp.arange(expert_count, dtype=jnp.int32)
    picked = jnp.any(routes[0][:, :, None] == expert_ids[None, None, :], axis=1)
    picked_low = picked.T.astype(BF16)
    small = jnp.concatenate(
        [
            jnp.stack([attn_gain, q_gain, k_gain, ffn_gain]),
            jnp.zeros((12, shard), BF16),
            w_router.T,
        ],
        axis=0,
    )

    def to_all(value):
        value = jnp.broadcast_to(value[None], (n_ep, *value.shape))
        return lax.all_to_all(value, "ep", split_axis=0, concat_axis=0, tiled=True)

    if shard == tok_dev:
        both = to_all(jnp.concatenate([small, picked_low], axis=0))
        small_all, picked_all = both[:, : 16 + expert_count], both[:, 16 + expert_count :]
    else:
        small_all, picked_all = to_all(small), to_all(picked_low)
    small_rows = jnp.swapaxes(small_all, 0, 1).reshape(16 + expert_count, width)
    gains = small_rows[:4].astype(F32)
    full_router = small_rows[16:]
    picked_all = by_piece(picked_all)

    x_all = lax.all_gather(tokens[0], "sp", axis=0, tiled=True)
    w_own = jnp.concatenate([own_columns(w) for w in (w_query, w_key, w_value, w_out)], axis=1)
    cot_own = cotangent[0]
    if n_ep == 8:
        w_pieces = gather_line(w_own)
        w_pieces[6], cot_own = tie(w_pieces[6], cot_own)
        cot_pieces, w_pieces[7] = gather_double(cot_own, w_pieces[7])
    else:
        w_pieces, cot_pieces = gather_whole(w_own), gather_whole(cot_own)

    upper = (
        jnp.arange(tok_dev, dtype=jnp.int32)[:, None] < jnp.arange(tok_dev, dtype=jnp.int32)[None, :]
    ).astype(BF16)
    picked_mine = lax.dynamic_slice_in_dim(picked_all, ep_index * local, local, 1)
    picked_mine = picked_mine.reshape(n_ep * local, tok_dev)
    earlier = product(picked_mine, upper).astype(jnp.int32)
    places = jnp.where((picked_mine > 0) & (earlier < capacity), earlier, -1)
    picked_flat = picked_all.reshape(n_ep * expert_count, tok_dev).astype(F32)

    positions = jnp.arange(total, dtype=jnp.int32)
    lengths = doc_lengths[0]
    doc_ends = jnp.cumsum(lengths)
    starts = jnp.sum(
        jnp.where(doc_ends[None, :] <= positions[:, None], lengths[None, :], 0), axis=1
    )
    half = HEAD_DIM // 2
    frequency = THETA ** (-(2.0 * jnp.arange(half, dtype=F32)) / HEAD_DIM)
    angles = (positions - starts).astype(F32)[:, None] * frequency[None, :]
    cosine = jnp.concatenate([jnp.cos(angles), jnp.cos(angles)], axis=1)
    sine = jnp.concatenate([-jnp.sin(angles), jnp.sin(angles)], axis=1)
    starts = starts[:, None].astype(jnp.int32)

    q_raw, k_raw, v_low, squares, w_qkv, w_o, h_all = qkv_project(ids, x_all, gains[0:1], w_pieces)
    scales = lax.rsqrt(sum_sp(squares) / width + EPS)
    w_o_parts = gather_sp(w_o)
    gain_q, gain_k = own_columns(gains)[1:2], own_columns(gains)[2:3]
    q_rot, k_rot, mixed = attend(
        q_raw, k_raw, v_low, scales, gain_q, gain_k, cosine, sine, starts
    )

    def pair_places(p):
        return places[p * local : (p + 2) * local]

    def cot_rows(g, after):
        d_rows = None
        for at, p in enumerate(range(g, g + group, 2)):
            (d_rows,) = dispatch(
                mine, cot_pieces[p : p + 2], pair_places(p), None, None, local, cap, group, at,
                d_rows, None, after,
            )
        return d_rows

    attn_tok = lax.all_to_all(mixed, "sp", split_axis=0, concat_axis=1, tiled=True)
    near_rows = cot_rows(0, [])
    x_one, h2_low = out_project(
        ids, n_ep, attn_tok, tokens[0], gains[3:4], w_o_parts, []
    )
    attn_all = lax.all_gather(attn_tok, "sp", axis=0, tiled=True)

    h2_pieces = gather(h2_low, n_ep)
    cots = [near_rows] + [cot_rows(g, [x_one]) for g in range(group, n_ep, group)]
    groups, d_pieces, d_gates, d_sums = [], [], [], []
    home_gates = None

    def rows_of(g, after):
        rows = gates = first_gates = None
        for at, p in enumerate(range(g, g + group, 2)):
            rows, gates, piece_gates = dispatch(
                mine, h2_pieces[p : p + 2], pair_places(p),
                picked_flat[p * expert_count : (p + 2) * expert_count], full_router, local, cap,
                group, at, rows, gates, after,
            )
            first_gates = piece_gates if first_gates is None else first_gates
        return rows, gates, first_gates

    rows, gates, home_gates = rows_of(0, [])
    for g in range(0, n_ep, group):
        d_rows = cots[g // group]
        made = experts(rows, d_rows, gates, w_gate, w_up, w_down, d_pieces[-group:] + cots + h2_pieces[4:7:2])
        groups.append((rows, d_rows, made))
        following = []
        if g + group < n_ep:
            rows, gates, _ = rows_of(g + group, [made[5]])
            following = [rows]
        sums_before = list(d_sums)
        for at in range(group // 2):
            *two, dots = combine(
                pair_places(g + 2 * at), made[5], 2, local, cap, at, made[3],
                sums_before + following,
            )
            d_pieces += two
            d_gates.append(dots)
        if n_ep == 8:
            d_sums += crossed_sums(d_pieces[-group:])

    acts = [made[0] for _, _, made in groups]
    d_gate_rows = [made[1] for _, _, made in groups]
    d_up_rows = [made[2] for _, _, made in groups]
    ins = [rows for rows, _, _ in groups]
    outs = [d_rows for _, d_rows, _ in groups]
    mix_stacks = combine_stacks(
        places, [made[4] for _, _, made in groups], n_ep, local, cap, group, d_pieces
    )
    grad_down = weight_grad(acts, outs, mix_stacks[:1])
    d_gates = by_piece(jnp.concatenate(d_gates, axis=0).reshape(n_ep, local, tok_dev))
    d_gates = lax.all_to_all(d_gates, "ep", split_axis=0, concat_axis=0, tiled=True)
    d_gates = d_gates.reshape(expert_count, tok_dev)
    if n_ep == 8:
        d_sums[2], mix_stacks[2], mix_stacks[3], grad_down = tie(
            d_sums[2], mix_stacks[2], mix_stacks[3], grad_down
        )
        d_h2, d_far = scatter_z(*d_sums)
        d_last = [d_far]
    else:
        d_h2, d_last = scatter(d_pieces, n_ep), []
    grad_gate = weight_grad(ins, d_gate_rows, [grad_down, d_gates, *d_last])
    grad_up = weight_grad(ins, d_up_rows, [grad_gate])

    def over_sp(value):
        return lax.psum_scatter(value, "sp", scatter_dimension=1, tiled=True).astype(F32)


    if n_ep == 8:
        gates_here = home_gates[:expert_count]
    else:
        logits = product_right(full_router, h2_low)
        logits = jnp.where(picked.T, logits, NEG_FILL)
        gates_here = jax.nn.softmax(logits, axis=0)
    d_logits = gates_here * (d_gates - jnp.sum(gates_here * d_gates, axis=0, keepdims=True))
    d_logits = jnp.where(picked.T, d_logits, 0.0).astype(BF16)
    grad_router = product(d_logits, h2_low)
    d_h2 = d_h2 + product_left(d_logits, full_router)
    one_scale = lax.rsqrt(jnp.mean(x_one * x_one, axis=-1, keepdims=True) + EPS)
    one_normed = x_one * one_scale
    grad_ffn = jnp.sum(d_h2 * one_normed, axis=0)
    d_normed = d_h2 * gains[3][None, :]
    d_one = cotangent[0].astype(F32) + one_scale * (
        d_normed - one_normed * jnp.mean(d_normed * one_normed, axis=-1, keepdims=True)
    )
    d_z, grad_up = tie(d_one.astype(BF16), grad_up)
    d_attn = out_back(ids, n_ep, d_z, w_o_parts, [])
    d_heads = lax.all_to_all(d_attn, "sp", split_axis=1, concat_axis=0, tiled=True)
    d_z_cols = lax.all_to_all(d_z, "sp", split_axis=1, concat_axis=0, tiled=True)
    mix, mix_far = scatter_stacks(mix_stacks, n_ep)
    if n_ep == 8:
        mix, mix_far, d_heads = tie(mix, mix_far, d_heads)
    grad_down, grad_gate, grad_up = over_sp(grad_down), over_sp(grad_gate), over_sp(grad_up)

    d_qn, d_kn, d_v, sums, grad_qg, grad_kg = attend_back(
        q_rot, k_rot, v_low, d_heads, q_raw, k_raw, scales, gain_q, gain_k, cosine, sine, starts
    )
    output = (x_one + last_hop(mix, mix_far)).astype(BF16)
    vo_stacks = vo_grads(ids, n_ep, h_all, d_v, attn_all, d_z_cols)
    grad_vo = scatter_stacks_z(vo_stacks, n_ep).astype(BF16)

    def placed(value):
        return lax.dynamic_update_slice_in_dim(
            jnp.zeros((1, width), F32), value, sp_index * head_width, 1
        )

    tiny = jnp.concatenate(
        [placed(grad_qg), placed(grad_kg), grad_ffn[None], grad_router], axis=0
    )
    *qk_stacks, d_qk = qk_back(
        ids, n_ep, h_all, d_qn, d_kn, q_raw, k_raw, scales, sum_sp(sums), tiny, vo_stacks[:1]
    )
    grad_qk, qk_far = scatter_stacks(qk_stacks, n_ep)
    grad_qk = last_hop(grad_qk, qk_far).astype(BF16)

    d_h = d_h_rows(ids, n_ep, n_sp, d_qk, d_v, w_qkv)
    output, d_h = tie(output, d_h)
    halves = plus(d_h[:2], swap_sp(d_h[2:], 1))
    d_h = halves[0].astype(F32) + swap_sp(halves[1], 2).astype(F32)
    x_rows = tokens[0].astype(F32)
    x_scale = lax.rsqrt(jnp.mean(x_rows * x_rows, axis=-1, keepdims=True) + EPS)
    x_normed = x_rows * x_scale
    d_normed = d_h * gains[0][None, :]
    input_grad = d_one + x_scale * (
        d_normed - x_normed * jnp.mean(d_normed * x_normed, axis=-1, keepdims=True)
    )

    g_query, g_key, g_value, g_out, tiny, g_attn = finish(
        ids, n_ep, w_query, w_key, w_value, attn_gain.astype(F32)[:, None],
        gather_sp(grad_qk), gather_sp(grad_vo), [grad_down, grad_gate, grad_up, input_grad],
    )
    per_row = 2 * head_width // shard

    def vector(at):
        col = (at % per_row) * shard
        return tiny[at // per_row, col : col + shard]

    g_router = jnp.stack([vector(3 + i) for i in range(expert_count)], axis=1)
    return (
        output[None], input_grad[None], g_attn[:, 0], g_query, g_key, g_value, vector(0), vector(1),
        g_out, vector(2), g_router, grad_gate, grad_up, grad_down,
    )


def solution(mesh):
    seq = P("ep", "sp", None)
    vec = P("ep")
    mat = P("ep", None)
    expert = P("ep", None, None)
    in_specs = (
        seq, mat, seq, vec, mat, mat, mat, vec, vec, mat, vec, mat, expert, expert, expert, seq,
    )
    out_specs = (
        seq, seq, vec, mat, mat, mat, vec, vec, mat, vec, mat, seq, seq, seq,
    )
    return jax.shard_map(body, mesh=mesh, in_specs=in_specs, out_specs=out_specs, check_vma=False)
```

```python
import functools

import jax
import jax.numpy as jnp
from jax import lax
from jax.experimental import pallas as pl
from jax.experimental.pallas import tpu as pltpu
from jax.sharding import PartitionSpec as P

HEAD_DIM = 128
EPS = 1e-05
THETA = 10000.0
NEG_FILL = -1e30
F32 = jnp.float32
BF16 = jnp.bfloat16
MIB = 1 << 20
COVER = 20


def product(left, right):
    return jnp.dot(left, right, preferred_element_type=F32)


def product_left(left, right):
    return lax.dot_general(left, right, (((0,), (0,)), ((), ())), preferred_element_type=F32)


def product_right(left, right):
    return lax.dot_general(left, right, (((1,), (1,)), ((), ())), preferred_element_type=F32)


def row_sums(values_in):
    sums = jnp.sum(values_in, axis=1, keepdims=True)
    return jnp.transpose(jnp.broadcast_to(sums, (sums.shape[0], HEAD_DIM)))[:8]


def call(kernel, out_shape, args, flops, name, scratch=(), scalars=(), grid=(1,), in_specs=None,
         out_specs=None, aliases=None, vmem=60, after=()):
    single = not isinstance(out_shape, (list, tuple))
    shapes = [out_shape] if single else list(out_shape)
    count = len(grid)

    def fixed(shape):
        rank = len(shape)
        return pl.BlockSpec(tuple(shape), lambda *ids: (0,) * rank)

    in_specs = in_specs or [None] * len(args)
    out_specs = out_specs or [None] * len(shapes)
    in_specs = [s if s is not None else fixed(a.shape) for s, a in zip(in_specs, args)]
    out_specs = [s if s is not None else fixed(o.shape) for s, o in zip(out_specs, shapes)]
    waited = len(after)
    args = [*args, *after]
    in_specs = in_specs + [pl.BlockSpec(memory_space=pl.ANY)] * waited
    if waited:
        inner, first = kernel, len(scalars) + len(args) - waited

        def kernel(*refs):
            inner(*refs[:first], *refs[first + waited :])

    moved = sum(a.size * a.dtype.itemsize for a in args[: len(args) - waited])
    moved += sum(o.size * o.dtype.itemsize for o in shapes)
    result = pl.pallas_call(
        kernel,
        grid_spec=pltpu.PrefetchScalarGridSpec(
            num_scalar_prefetch=len(scalars), grid=grid, in_specs=in_specs, out_specs=out_specs,
            scratch_shapes=list(scratch),
        ),
        out_shape=shapes,
        input_output_aliases={k + len(scalars): v for k, v in (aliases or {}).items()},
        compiler_params=pltpu.CompilerParams(
            vmem_limit_bytes=vmem * MIB, dimension_semantics=("arbitrary",) * count
        ),
        cost_estimate=pl.CostEstimate(flops=int(COVER * flops), bytes_accessed=int(moved), transcendentals=0),
        name=name,
    )(*scalars, *args)
    return result[0] if single else list(result)


def like(shape, dtype):
    return jax.ShapeDtypeStruct(tuple(shape), dtype)


def tie(*values):
    return lax.optimization_barrier(values)


def swap(value, bits):
    return lax.ppermute(value, "ep", [(i, i ^ bits) for i in range(8)])


def swap_sp(value, bits):
    return lax.ppermute(value, "sp", [(i, i ^ bits) for i in range(4)])


def piece_blocks(n_ep, ep_index):
    ids = jnp.arange(n_ep, dtype=jnp.int32)
    return jnp.bitwise_xor(ids, ep_index) if n_ep == 8 else ids


MIDDLE = [(2, 4), (3, 5), (4, 2), (5, 3)]
OUTWARD = [(2, 0), (3, 1), (4, 6), (5, 7)]


def gather_line(value):
    crossed = swap(value, 1)
    near = swap(value, 2)
    inner = lax.ppermute(value, "ep", MIDDLE)
    near_x, outer = swap(near, 1), lax.ppermute(near, "ep", MIDDLE)
    near_x, crossed, outer = tie(near_x, crossed, outer)
    far = outer + lax.ppermute(inner, "ep", OUTWARD)
    farther = inner + lax.ppermute(outer, "ep", OUTWARD)
    return [value, crossed, near, near_x, far, swap(far, 1), farther, swap(farther, 1)]


def gather_double(value, after):
    after, held = tie(after, value)
    crossed = swap(held, 1)
    near, far = swap(value, 2), swap(value, 4)
    farther = swap(far, 2)
    return [
        value, crossed, near, swap(near, 1), far, swap(far, 1), farther, swap(farther, 1)
    ], after


def gather_whole(value):
    whole = lax.all_gather(value, "ep", axis=0, tiled=False)
    return [whole[i] for i in range(whole.shape[0])]


def gather(value, n_ep):
    return gather_line(value) if n_ep == 8 else gather_whole(value)


def plus(left, right):
    return (left.astype(F32) + right.astype(F32)).astype(left.dtype)


def crossed_sums(pieces):
    return [plus(pieces[i], swap(pieces[i + 1], 1)) for i in range(0, len(pieces), 2)]


def scatter_z(own, near, far, farther):
    far = plus(far, swap(farther, 2))
    far, near = tie(far, near)
    return own.astype(F32) + swap(near, 2).astype(F32) + swap(far, 4).astype(F32), far


def scatter(pieces, n_ep):
    if n_ep != 8:
        stacked = jnp.stack(pieces)
        return lax.psum_scatter(stacked, "ep", scatter_dimension=0, tiled=False).astype(F32)
    return scatter_z(*crossed_sums(pieces))[0]


def stack_at(piece, n_ep):
    if n_ep != 8:
        return 0, piece
    return 2 * (piece % 2) + (piece // 2) % 2, piece // 4


def stack_shapes(n_ep, shape):
    return [like((2, *shape), BF16)] * 4 if n_ep == 8 else [like((n_ep, *shape), BF16)]


def scatter_stacks(stacks, n_ep):
    if n_ep != 8:
        total = lax.psum_scatter(stacks[0], "ep", scatter_dimension=0, tiled=False)
        return total.astype(F32), None
    even, odd, even_sent, odd_sent = stacks
    odd = plus(odd, swap(odd_sent, 1))
    even = even.astype(F32) + swap(even_sent, 1).astype(F32) + swap(odd, 2).astype(F32)
    return even[0], even[1].astype(BF16)


def last_hop(total, far):
    return total if far is None else total + swap(far, 4).astype(F32)


def gather_sp(value):
    over = swap_sp(value, 2)
    return [value, swap_sp(value, 1), over, swap_sp(over, 1)]


def sum_sp(value):
    n_sp = lax.axis_size("sp")
    value = jnp.broadcast_to(value[None], (n_sp, *value.shape))
    return jnp.sum(lax.all_to_all(value, "sp", split_axis=0, concat_axis=0, tiled=True), axis=0)


def sum_sp_swaps(value):
    return (value + swap_sp(value, 1)) + (swap_sp(value, 2) + swap_sp(value, 3))


def block_at(ids, position, size):
    if size % HEAD_DIM:
        return pl.ds(position * size, size)
    return pl.ds(pl.multiple_of(ids[position] * size, size), size)


def qkv_kernel(count, ids, x_ref, gain_ref, *refs):
    pieces, refs = refs[:count], refs[count:]
    q_ref, k_ref, v_ref, squares_ref, w_ref, out_ref, h_ref = refs
    shard = pieces[0].shape[0]
    width = q_ref.shape[1]

    @pl.when(pl.program_id(0) == 0)
    def _():
        for k in range(count):
            rows = block_at(ids, k, shard)
            w_ref[rows, :] = pieces[k][:, : 3 * width]
            out_ref[rows, :] = pieces[k][:, 3 * width :]

    x_rows = x_ref[...].astype(F32)
    scale = lax.rsqrt(jnp.mean(x_rows * x_rows, axis=1, keepdims=True) + EPS)
    h_ref[...] = (x_rows * scale * gain_ref[...]).astype(BF16)
    for at, ref in enumerate((q_ref, k_ref)):
        part = product(h_ref[...], w_ref[:, at * width : (at + 1) * width])
        ref[...] = part
        squares_ref[8 * at : 8 * at + 8, :] = row_sums(part * part)
    v_ref[...] = product(h_ref[...], w_ref[:, 2 * width :]).astype(BF16)


def qkv_project(ids, x_all, gain, pieces):
    total, depth = x_all.shape
    width = pieces[0].shape[1] // 4
    rows = min(256, total)
    block = pl.BlockSpec((rows, width), lambda i, ids: (i, 0))
    wide = pl.BlockSpec((rows, depth), lambda i, ids: (i, 0))
    return call(
        functools.partial(qkv_kernel, len(pieces)),
        [like((total, width), F32)] * 2
        + [like((total, width), BF16), like((16, total), F32), like((depth, 3 * width), BF16)]
        + [like((depth, width), BF16), like((total, depth), BF16)],
        [x_all, gain, *pieces],
        6 * total * depth * width,
        "qkv_project",
        scalars=(ids,),
        grid=(total // rows,),
        in_specs=[wide] + [None] * (len(pieces) + 1),
        out_specs=[
            block, block, block, pl.BlockSpec((16, rows), lambda i, ids: (0, i)), None, None, wide,
        ],
    )


def out_kernel(n_ep, ids, attn_ref, x_ref, gain_ref, *refs):
    weights, (one_ref, low_ref) = refs[:-2], refs[-2:]
    width = weights[0].shape[1]
    for j, weight in enumerate(weights):
        cols = block_at(ids, n_ep + j, width)
        one_ref[:, cols] = x_ref[:, cols].astype(F32) + product(attn_ref[...], weight[...])
    one = one_ref[...]
    scale = lax.rsqrt(jnp.mean(one * one, axis=1, keepdims=True) + EPS)
    low_ref[...] = (one * scale * gain_ref[...]).astype(BF16)


def out_project(ids, n_ep, attn_tok, tokens, gain, weights, after):
    return call(
        functools.partial(out_kernel, n_ep),
        [like(tokens.shape, F32), like(tokens.shape, BF16)],
        [attn_tok, tokens, gain, *weights],
        2 * tokens.size * attn_tok.shape[1],
        "out_project",
        after=after,
        scalars=(ids,),
    )


def out_back_kernel(n_ep, ids, d_ref, *refs):
    weights, d_attn_ref = refs[:-1], refs[-1]
    width = weights[0].shape[1]
    total = None
    for j, weight in enumerate(weights):
        part = product_right(d_ref[:, block_at(ids, n_ep + j, width)], weight[...])
        total = part if total is None else total + part
    d_attn_ref[...] = total.astype(BF16)


def out_back(ids, n_ep, d_z, weights, after):
    return call(
        functools.partial(out_back_kernel, n_ep),
        like((d_z.shape[0], weights[0].shape[0]), BF16),
        [d_z, *weights],
        2 * d_z.size * weights[0].shape[0],
        "out_back",
        after=after,
        scalars=(ids,),
    )


def vo_grads_kernel(count, shard, ids, h_ref, dv_ref, attn_ref, dz_ref, *stacks):
    width = dv_ref.shape[1]
    for k in range(count):
        block = block_at(ids, k, shard)
        array, place = stack_at(k, count)
        stacks[array][place, :, :width] = product_left(h_ref[:, block], dv_ref[...]).astype(BF16)
        stacks[array][place, :, width:] = product_left(attn_ref[:, block], dz_ref[...]).astype(BF16)


def vo_grads(ids, count, h_all, d_v, attn_all, d_z_cols):
    shard = h_all.shape[1] // count
    width = d_v.shape[1]
    return call(
        functools.partial(vo_grads_kernel, count, shard),
        stack_shapes(count, (shard, 2 * width)),
        [h_all, d_v, attn_all, d_z_cols],
        4 * h_all.size * width,
        "vo_grads",
        scalars=(ids,),
    )


def qk_back_kernel(
    count, shard, ids, h_ref, dqn_ref, dkn_ref, qr_ref, kr_ref, scale_ref, sums_ref, tiny_ref, *refs
):
    stacks, d_ref = refs[:-1], refs[-1]
    width = dqn_ref.shape[1]
    scales = jnp.transpose(scale_ref[...])
    means = jnp.transpose(sums_ref[...]) * (1.0 / h_ref.shape[1])
    for at, (d_normed, raw) in enumerate(((dqn_ref, qr_ref), (dkn_ref, kr_ref))):
        scale, mean = scales[:, 8 * at : 8 * at + 1], means[:, 8 * at : 8 * at + 1]
        d_ref[:, at * width : (at + 1) * width] = (
            scale * (d_normed[...] - raw[...] * scale * mean)
        ).astype(BF16)
    per_row = 2 * width // shard
    extra = stacks[0].shape[1] - shard
    for k in range(count):
        block = block_at(ids, k, shard)
        array, place = stack_at(k, count)
        ref = stacks[array]
        ref[place, :shard, :] = product_left(h_ref[:, block], d_ref[...]).astype(BF16)
        ref[place, shard:, :] = jnp.zeros((extra, 2 * width), BF16)
        for at in range(tiny_ref.shape[0]):
            row, col = shard + at // per_row, (at % per_row) * shard
            ref[place, row : row + 1, col : col + shard] = tiny_ref[at : at + 1, block].astype(BF16)


def qk_back(ids, count, h_all, d_qn, d_kn, q_raw, k_raw, scales, sums, tiny, after):
    total, depth = h_all.shape
    width = d_qn.shape[1]
    shard = depth // count
    extra = -(-tiny.shape[0] // (2 * width // shard))
    extra = -(-extra // 16) * 16
    return call(
        functools.partial(qk_back_kernel, count, shard),
        stack_shapes(count, (shard + extra, 2 * width)) + [like((total, 2 * width), BF16)],
        [h_all, d_qn, d_kn, q_raw, k_raw, scales, sums, tiny],
        2 * h_all.size * 2 * width,
        "qk_back",
        scalars=(ids,),
        after=after,
    )


def d_h_kernel(ids, d_ref, dv_ref, w_ref, out_ref):
    both = d_ref.shape[1]
    out_ref[0] = (
        product_right(d_ref[...], w_ref[:, :both]) + product_right(dv_ref[...], w_ref[:, both:])
    ).astype(BF16)


def d_h_rows(ids, n_ep, n_sp, d_qk, d_v, w_qkv, after):
    total, wide = d_qk.shape
    depth = w_qkv.shape[0]
    rows = total // n_sp

    def partner(j, ids):
        return ids[n_ep + (j % 2) * 2 + j // 2], 0

    return call(
        d_h_kernel,
        like((n_sp, rows, depth), BF16),
        [d_qk, d_v, w_qkv],
        3 * d_qk.size * depth,
        "d_h",
        after=after,
        scalars=(ids,),
        grid=(n_sp,),
        in_specs=[
            pl.BlockSpec((rows, wide), partner), pl.BlockSpec((rows, d_v.shape[1]), partner), None,
        ],
        out_specs=[pl.BlockSpec((1, rows, depth), lambda j, ids: (j, 0, 0))],
    )


def finish_kernel(n_ep, n_sp, ids, wq_ref, wk_ref, wv_ref, gain_ref, *refs):
    firsts, seconds = refs[:n_sp], refs[n_sp : 2 * n_sp]
    gq_ref, gk_ref, gv_ref, go_ref, tiny_ref, attn_ref = refs[2 * n_sp :]
    shard = wq_ref.shape[0]
    width = firsts[0].shape[1] // 2
    dots = jnp.zeros((shard, 1), F32)
    tiny = jnp.zeros(tiny_ref.shape, F32)
    for j in range(n_sp):
        cols = block_at(ids, n_ep + j, width)
        for at, grad, weight in ((0, gq_ref, wq_ref), (1, gk_ref, wk_ref), (2, gv_ref, wv_ref)):
            part = firsts[j][:shard, at * width : (at + 1) * width] if at < 2 else seconds[j][:, :width]
            value = part.astype(F32)
            grad[:, cols] = value
            dots += jnp.sum(value * weight[:, cols].astype(F32), axis=1, keepdims=True)
        go_ref[:, cols] = seconds[j][:, width:].astype(F32)
        tiny += firsts[j][shard:, :].astype(F32)
    tiny_ref[...] = tiny
    attn_ref[...] = dots / gain_ref[...]


def finish(ids, n_ep, w_query, w_key, w_value, gain, firsts, seconds, after):
    shard, depth = w_query.shape
    extra = firsts[0].shape[0] - shard
    return call(
        functools.partial(finish_kernel, n_ep, len(firsts)),
        [like((shard, depth), F32)] * 4 + [like((extra, firsts[0].shape[1]), F32), like((shard, 1), F32)],
        [w_query, w_key, w_value, gain, *firsts, *seconds],
        shard * depth * 6,
        "finish",
        after=after,
        scalars=(ids,),
    )


def turn(values_in):
    return pltpu.roll(values_in, HEAD_DIM // 2, 1)


def masked_probs(q_ref, k_ref, start_ref, block, rows):
    first, last = block * rows, (block + 1) * rows
    scores = product_right(q_ref[first:last, :], k_ref[0:last, :]) * (HEAD_DIM ** (-0.5))
    row_ids = first + lax.broadcasted_iota(jnp.int32, scores.shape, 0)
    places = lax.broadcasted_iota(jnp.int32, scores.shape, 1)
    allowed = (places <= row_ids) & (places >= start_ref[first:last, :])
    scores = jnp.where(allowed, scores, NEG_FILL)
    top = jnp.max(scores, axis=1, keepdims=True)
    weights = jnp.exp(scores - top)
    return weights * (1.0 / jnp.sum(weights, axis=1, keepdims=True))


def attend_kernel(
    rows, qr_ref, kr_ref, v_ref, scale_ref, gq_ref, gk_ref, cos_ref, sin_ref, start_ref,
    q_ref, k_ref, out_ref,
):
    scales = jnp.transpose(scale_ref[...])
    for at, (raw, gain, low) in enumerate(((qr_ref, gq_ref, q_ref), (kr_ref, gk_ref, k_ref))):
        normed = raw[...] * scales[:, 8 * at : 8 * at + 1] * gain[...]
        low[...] = (normed * cos_ref[...] + turn(normed) * sin_ref[...]).astype(BF16)
    for block in range(q_ref.shape[0] // rows):
        probs = masked_probs(q_ref, k_ref, start_ref, block, rows)
        last = (block + 1) * rows
        out_ref[block * rows : last, :] = product(
            probs.astype(BF16), v_ref[0:last, :]
        ).astype(BF16)


def head_spec(rows):
    return pl.BlockSpec((rows, HEAD_DIM), lambda h: (0, h))


def attend(q_raw, k_raw, v_low, scales, q_gain, k_gain, cosine, sine, starts):
    total, width = v_low.shape
    heads = width // HEAD_DIM
    head, gain = head_spec(total), head_spec(1)
    return call(
        functools.partial(attend_kernel, min(256, total)),
        [like((total, width), BF16)] * 3,
        [q_raw, k_raw, v_low, scales, q_gain, k_gain, cosine, sine, starts],
        3 * heads * total * total * HEAD_DIM,
        "attend",
        grid=(heads,),
        in_specs=[head, head, head, None, gain, gain, None, None, None],
        out_specs=[head, head, head],
    )


def attend_back_kernel(
    rows, q_ref, k_ref, v_ref, do_ref, qr_ref, kr_ref, scale_ref, gq_ref, gk_ref,
    cos_ref, sin_ref, start_ref,
    dq_ref, dk_ref, dv_ref, sums_ref, dgq_ref, dgk_ref, q_acc, k_acc, v_acc,
):
    k_acc[...] = jnp.zeros_like(k_acc)
    v_acc[...] = jnp.zeros_like(v_acc)
    for block in range(q_ref.shape[0] // rows):
        first, last = block * rows, (block + 1) * rows
        probs = masked_probs(q_ref, k_ref, start_ref, block, rows)
        d_rows = do_ref[first:last, :]
        d_probs = product_right(d_rows, v_ref[0:last, :])
        delta = jnp.sum(probs * d_probs, axis=1, keepdims=True)
        d_scores = (probs * (d_probs - delta) * (HEAD_DIM ** (-0.5))).astype(BF16)
        q_acc[first:last, :] = product(d_scores, k_ref[0:last, :])
        k_acc[0:last, :] += product_left(d_scores, q_ref[first:last, :])
        v_acc[0:last, :] += product_left(probs.astype(BF16), d_rows)
    dv_ref[...] = v_acc[...].astype(BF16)

    @pl.when(pl.program_id(0) == 0)
    def _():
        sums_ref[...] = jnp.zeros_like(sums_ref)

    scales = jnp.transpose(scale_ref[...])
    for at, (acc, raw, gain, d_ref, dg_ref) in enumerate(
        ((q_acc, qr_ref, gq_ref, dq_ref, dgq_ref), (k_acc, kr_ref, gk_ref, dk_ref, dgk_ref))
    ):
        turned = acc[...].astype(BF16).astype(F32)
        back = turned * cos_ref[...] + turn(turned * sin_ref[...])
        normed = raw[...] * scales[:, 8 * at : 8 * at + 1]
        both = back * normed
        dg_ref[...] = jnp.sum(both, axis=0, keepdims=True)
        d_ref[...] = back * gain[...]
        sums_ref[8 * at : 8 * at + 8, :] += row_sums(both * gain[...])


def attend_back(
    q_rot, k_rot, v_low, d_heads, q_raw, k_raw, scales, q_gain, k_gain, cosine, sine, starts
):
    total, width = v_low.shape
    heads = width // HEAD_DIM
    head, gain = head_spec(total), head_spec(1)
    wide, thin = like((total, width), F32), like((1, width), F32)
    return call(
        functools.partial(attend_back_kernel, min(256, total)),
        [wide, wide, like((total, width), BF16), like((16, total), F32), thin, thin],
        [q_rot, k_rot, v_low, d_heads, q_raw, k_raw, scales, q_gain, k_gain, cosine, sine, starts],
        7 * heads * total * total * HEAD_DIM,
        "attend_back",
        scratch=[pltpu.VMEM((total, HEAD_DIM), F32)] * 3,
        grid=(heads,),
        in_specs=[head] * 6 + [None, gain, gain, None, None, None],
        out_specs=[head, head, head, None, gain, gain],
    )


def chooser(places_ref, at, cap):
    row = places_ref[at : at + 1, :]
    slots = lax.broadcasted_iota(jnp.int32, (cap, row.shape[1]), 0)
    return slots == row


def dispatch_kernel(
    pieces_here, local, cap, gated, mine, *refs
):
    pieces, refs = refs[:pieces_here], refs[pieces_here:]
    places_ref, refs = refs[0], refs[1:]
    if gated:
        (picked_ref, router_ref), refs = refs[:2], refs[2:]
        rows_ref, gate_ref, all_ref = refs[-3:]
    else:
        rows_ref = refs[-1]
    for p in range(pieces_here):
        if gated:
            logits = product_right(router_ref[...], pieces[p][...])
            experts = logits.shape[0]
            picked = picked_ref[p * experts : (p + 1) * experts, :] > 0
            logits = jnp.where(picked, logits, NEG_FILL)
            weights = jnp.exp(logits - jnp.max(logits, axis=0, keepdims=True))
            weights = jnp.where(picked, weights, 0.0)
            gates = weights / jnp.sum(weights, axis=0, keepdims=True)
            all_ref[p * experts : (p + 1) * experts, :] = gates
        for e in range(local):
            chosen = chooser(places_ref, p * local + e, cap)
            rows_ref[e, p * cap : (p + 1) * cap, :] = product(
                chosen.astype(BF16), pieces[p][...]
            ).astype(BF16)
            if gated:
                row = all_ref[pl.ds(p * experts + mine[0] * local + e, 1), :]
                gate_ref[e, p * cap : (p + 1) * cap, :] = jnp.sum(
                    jnp.where(chosen, row, 0.0), axis=1, keepdims=True
                )


def dispatch(mine, pieces, places, picked, router, local, cap, group, at, rows, gates, after=()):
    gated = router is not None
    here = len(pieces)
    width = pieces[0].shape[1]
    args = [*pieces, places]
    shapes = [like((local, group * cap, width), BF16)]
    spec = pl.BlockSpec((local, here * cap, width), lambda i, mine: (0, at, 0))
    out_specs = [spec]
    if gated:
        args += [picked, router]
        shapes += [like((local, group * cap, 1), F32), like((picked.shape[0], places.shape[1]), F32)]
        out_specs += [pl.BlockSpec((local, here * cap, 1), lambda i, mine: (0, at, 0)), None]
    in_specs = [None] * len(args)
    aliases = {}
    if rows is not None:
        aliases[len(args)] = 0
        args.append(rows)
        in_specs.append(pl.BlockSpec(memory_space=pl.ANY))
        if gated:
            aliases[len(args)] = 1
            args.append(gates)
            in_specs.append(pl.BlockSpec(memory_space=pl.ANY))
    return call(
        functools.partial(dispatch_kernel, here, local, cap, gated),
        shapes,
        args,
        2 * here * local * cap * places.shape[1] * width,
        "dispatch",
        scalars=(mine,),
        in_specs=in_specs,
        out_specs=out_specs,
        aliases=aliases,
        after=after,
    )


def expert_kernel(
    x_ref, d_ref, gate_ref, wg_ref, wu_ref, wd_ref,
    act_ref, dg_ref, du_ref, dots_ref, mix_ref, back_ref, mix_acc, back_acc,
):
    step = pl.program_id(1)
    last = pl.num_programs(1) - 1
    x_rows, d_rows, gate = x_ref[0], d_ref[0], gate_ref[0]
    pre = product(x_rows, wg_ref[0])
    up = product(x_rows, wu_ref[0])
    pulled = product_right(d_rows, wd_ref[0])
    sigma = jax.nn.sigmoid(pre)
    silu = pre * sigma
    act = silu * up
    dots = jnp.sum(act * pulled, axis=1, keepdims=True)
    act_low = (act * gate).astype(BF16)
    act_ref[0] = act_low
    d_act = pulled * gate
    du_low = (d_act * silu).astype(BF16)
    dg_low = (d_act * up * sigma * (1.0 + pre * (1.0 - sigma))).astype(BF16)
    dg_ref[0] = dg_low
    du_ref[0] = du_low
    mix = product(act_low, wd_ref[0])
    back = product_right(dg_low, wg_ref[0]) + product_right(du_low, wu_ref[0])

    @pl.when(step == 0)
    def _():
        dots_ref[0] = dots
        mix_acc[...] = mix
        back_acc[...] = back

    @pl.when((step > 0) & (step < last))
    def _():
        dots_ref[0] += dots
        mix_acc[...] += mix
        back_acc[...] += back

    @pl.when(step == last)
    def _():
        dots_ref[0] += dots
        mix_ref[0] = (mix_acc[...] + mix).astype(BF16)
        back_ref[0] = (back_acc[...] + back).astype(BF16)


def experts(rows, d_rows, gates, w_gate, w_up, w_down, after=()):
    local, count, width = rows.shape
    hidden = w_gate.shape[2]
    part = hidden // 2
    wide = pl.BlockSpec((1, count, width), lambda e, f: (e, 0, 0))
    column = pl.BlockSpec((1, count, 1), lambda e, f: (e, 0, 0))
    thin = pl.BlockSpec((1, count, part), lambda e, f: (e, 0, f))
    into = pl.BlockSpec((1, width, part), lambda e, f: (e, 0, f))
    outof = pl.BlockSpec((1, part, width), lambda e, f: (e, f, 0))
    return call(
        expert_kernel,
        [like((local, count, hidden), BF16)] * 3
        + [like((local, count, 1), F32)]
        + [like((local, count, width), BF16)] * 2,
        [rows, d_rows, gates, w_gate, w_up, w_down],
        12 * rows.size * hidden,
        "experts",
        after=after,
        scratch=[pltpu.VMEM((count, width), F32)] * 2,
        grid=(local, 2),
        in_specs=[wide, wide, column, into, into, outof],
        out_specs=[thin, thin, thin, column, wide, wide],
    )


def combine_kernel(here, local, cap, dotted, places_ref, rows_ref, *refs):
    pieces = refs[int(dotted) : int(dotted) + here]
    for p in range(here):
        chosen = [chooser(places_ref, p * local + e, cap) for e in range(local)]
        total = None
        for e in range(local):
            part = product_left(chosen[e].astype(BF16), rows_ref[e, p * cap : (p + 1) * cap, :])
            total = part if total is None else total + part
            if dotted:
                refs[-1][p * local + e : p * local + e + 1, :] = jnp.sum(
                    jnp.where(chosen[e], refs[0][e, p * cap : (p + 1) * cap, :], 0.0),
                    axis=0, keepdims=True,
                )
        pieces[p][...] = total.astype(BF16)


def combine(places, rows, here, local, cap, at, dots=None, after=()):
    width = rows.shape[2]
    tokens = places.shape[1]
    dotted = dots is not None
    args = [places, rows] + ([dots] if dotted else [])
    in_specs = [None, pl.BlockSpec((local, here * cap, width), lambda i: (0, at, 0))]
    if dotted:
        in_specs.append(pl.BlockSpec((local, here * cap, 1), lambda i: (0, at, 0)))
    shapes = [like((tokens, width), BF16)] * here
    if dotted:
        shapes.append(like(places.shape, F32))
    return call(
        functools.partial(combine_kernel, here, local, cap, dotted),
        shapes,
        args,
        2 * here * local * cap * tokens * width,
        "combine",
        after=after,
        in_specs=in_specs,
    )


def combine_stacks_kernel(count, local, cap, group, places_ref, *refs):
    groups = count // group
    for k in range(count):
        rows = refs[k // group]
        at = (k % group) * cap
        total = None
        for e in range(local):
            chosen = chooser(places_ref, k * local + e, cap).astype(BF16)
            part = product_left(chosen, rows[e, at : at + cap, :])
            total = part if total is None else total + part
        array, place = stack_at(k, count)
        refs[groups + array][place] = total.astype(BF16)


def combine_stacks(places, rows, count, local, cap, group, after):
    tokens, width = places.shape[1], rows[0].shape[2]
    return call(
        functools.partial(combine_stacks_kernel, count, local, cap, group),
        stack_shapes(count, (tokens, width)),
        [places, *rows],
        2 * count * local * cap * tokens * width,
        "combine_stacks",
        after=after,
    )


def weight_grad_kernel(groups, *refs):
    lefts, rights = refs[:groups], refs[groups : 2 * groups]
    total = None
    for left, right in zip(lefts, rights):
        part = product_left(left[0], right[0])
        total = part if total is None else total + part
    refs[-1][0] = total.astype(BF16)


def weight_grad(lefts, rights, after=()):
    local, count, tall = lefts[0].shape
    wide = rights[0].shape[2]
    part = min(512, tall)
    left = pl.BlockSpec((1, count, part), lambda e, i: (e, 0, i))
    right = pl.BlockSpec((1, count, wide), lambda e, i: (e, 0, 0))
    return call(
        functools.partial(weight_grad_kernel, len(lefts)),
        like((local, tall, wide), BF16),
        [*lefts, *rights],
        2 * len(lefts) * lefts[0].size * wide,
        "weight_grad",
        after=after,
        grid=(local, tall // part),
        in_specs=[left] * len(lefts) + [right] * len(lefts),
        out_specs=[pl.BlockSpec((1, part, wide), lambda e, i: (e, i, 0))],
    )


def body(
    tokens, doc_lengths, routes, attn_gain, w_query, w_key, w_value, q_gain, k_gain, w_out,
    ffn_gain, w_router, w_gate, w_up, w_down, cotangent,
):
    n_sp = lax.axis_size("sp")
    n_ep = lax.axis_size("ep")
    sp_index = lax.axis_index("sp")
    ep_index = lax.axis_index("ep")
    tok_dev, width = tokens.shape[1:]
    total = tok_dev * n_sp
    shard = width // n_ep
    head_width = width // n_sp
    top_count = routes.shape[2]
    local = w_gate.shape[0]
    expert_count = local * n_ep
    capacity = 9 * tok_dev * top_count // (8 * expert_count)
    cap = -(-capacity // 16) * 16
    group = 4
    blocks = piece_blocks(n_ep, ep_index)
    partners = jnp.bitwise_xor(jnp.arange(n_sp, dtype=jnp.int32), sp_index)
    ids = jnp.concatenate([blocks, partners]).astype(jnp.int32)
    mine = ep_index.astype(jnp.int32).reshape(1)

    def own_columns(value):
        return lax.dynamic_slice_in_dim(value, sp_index * head_width, head_width, 1)

    def by_piece(value):
        return jnp.stack(
            [lax.dynamic_index_in_dim(value, blocks[i], 0, keepdims=False) for i in range(n_ep)]
        )

    expert_ids = jnp.arange(expert_count, dtype=jnp.int32)
    picked = jnp.any(routes[0][:, :, None] == expert_ids[None, None, :], axis=1)
    picked_low = picked.T.astype(BF16)
    small = jnp.concatenate(
        [
            jnp.stack([attn_gain, q_gain, k_gain, ffn_gain]),
            jnp.zeros((12, shard), BF16),
            w_router.T,
        ],
        axis=0,
    )

    def to_all(value):
        value = jnp.broadcast_to(value[None], (n_ep, *value.shape))
        return lax.all_to_all(value, "ep", split_axis=0, concat_axis=0, tiled=True)

    if shard == tok_dev:
        both = to_all(jnp.concatenate([small, picked_low], axis=0))
        small_all, picked_all = both[:, : 16 + expert_count], both[:, 16 + expert_count :]
    else:
        small_all, picked_all = to_all(small), to_all(picked_low)
    small_rows = jnp.swapaxes(small_all, 0, 1).reshape(16 + expert_count, width)
    gains = small_rows[:4].astype(F32)
    full_router = small_rows[16:]
    picked_all = by_piece(picked_all)

    x_all = lax.all_gather(tokens[0], "sp", axis=0, tiled=True)
    w_own = jnp.concatenate([own_columns(w) for w in (w_query, w_key, w_value, w_out)], axis=1)
    cot_own = cotangent[0]
    if n_ep == 8:
        w_pieces = gather_line(w_own)
        w_pieces[6], cot_own = tie(w_pieces[6], cot_own)
        cot_pieces, w_pieces[7] = gather_double(cot_own, w_pieces[7])
    else:
        w_pieces, cot_pieces = gather_whole(w_own), gather_whole(cot_own)

    upper = (
        jnp.arange(tok_dev, dtype=jnp.int32)[:, None] < jnp.arange(tok_dev, dtype=jnp.int32)[None, :]
    ).astype(BF16)
    picked_mine = lax.dynamic_slice_in_dim(picked_all, ep_index * local, local, 1)
    picked_mine = picked_mine.reshape(n_ep * local, tok_dev)
    earlier = product(picked_mine, upper).astype(jnp.int32)
    places = jnp.where((picked_mine > 0) & (earlier < capacity), earlier, -1)
    picked_flat = picked_all.reshape(n_ep * expert_count, tok_dev).astype(F32)

    positions = jnp.arange(total, dtype=jnp.int32)
    lengths = doc_lengths[0]
    doc_ends = jnp.cumsum(lengths)
    starts = jnp.sum(
        jnp.where(doc_ends[None, :] <= positions[:, None], lengths[None, :], 0), axis=1
    )
    half = HEAD_DIM // 2
    frequency = THETA ** (-(2.0 * jnp.arange(half, dtype=F32)) / HEAD_DIM)
    angles = (positions - starts).astype(F32)[:, None] * frequency[None, :]
    cosine = jnp.concatenate([jnp.cos(angles), jnp.cos(angles)], axis=1)
    sine = jnp.concatenate([-jnp.sin(angles), jnp.sin(angles)], axis=1)
    starts = starts[:, None].astype(jnp.int32)

    q_raw, k_raw, v_low, squares, w_qkv, w_o, h_all = qkv_project(ids, x_all, gains[0:1], w_pieces)
    squares, w_o = tie(sum_sp(squares), w_o)
    scales = lax.rsqrt(squares / width + EPS)
    w_o_over = swap_sp(w_o, 2)
    gain_q, gain_k = own_columns(gains)[1:2], own_columns(gains)[2:3]
    q_rot, k_rot, mixed = attend(
        q_raw, k_raw, v_low, scales, gain_q, gain_k, cosine, sine, starts
    )

    def pair_places(p):
        return places[p * local : (p + 2) * local]

    def cot_rows(g, after):
        d_rows = None
        for at, p in enumerate(range(g, g + group, 2)):
            (d_rows,) = dispatch(
                mine, cot_pieces[p : p + 2], pair_places(p), None, None, local, cap, group, at,
                d_rows, None, after,
            )
        return d_rows

    attn_tok = lax.all_to_all(mixed, "sp", split_axis=0, concat_axis=1, tiled=True)
    w_o_over, attn_tok = tie(w_o_over, attn_tok)
    w_o_parts = [w_o, swap_sp(w_o, 1), w_o_over, swap_sp(w_o_over, 1)]
    x_one, h2_low = out_project(
        ids, n_ep, attn_tok, tokens[0], gains[3:4], w_o_parts, []
    )
    attn_all = lax.all_gather(attn_tok, "sp", axis=0, tiled=True)

    h2_pieces = gather(h2_low, n_ep)
    cots = [cot_rows(g, [x_one]) for g in range(0, n_ep, group)]
    groups, d_pieces, d_gates, d_sums = [], [], [], []
    home_gates = None

    def rows_of(g, after):
        rows = gates = first_gates = None
        for at, p in enumerate(range(g, g + group, 2)):
            rows, gates, piece_gates = dispatch(
                mine, h2_pieces[p : p + 2], pair_places(p),
                picked_flat[p * expert_count : (p + 2) * expert_count], full_router, local, cap,
                group, at, rows, gates, after,
            )
            first_gates = piece_gates if first_gates is None else first_gates
        return rows, gates, first_gates

    rows, gates, home_gates = rows_of(0, [])
    for g in range(0, n_ep, group):
        d_rows = cots[g // group]
        made = experts(rows, d_rows, gates, w_gate, w_up, w_down, d_pieces[-group:] + cots + h2_pieces[4:7:2])
        groups.append((rows, d_rows, made))
        following = []
        if g + group < n_ep:
            rows, gates, _ = rows_of(g + group, [made[5]])
            following = [rows]
        sums_before = list(d_sums)
        for at in range(group // 2):
            *two, dots = combine(
                pair_places(g + 2 * at), made[5], 2, local, cap, at, made[3],
                sums_before + following,
            )
            d_pieces += two
            d_gates.append(dots)
        if n_ep == 8:
            d_sums += crossed_sums(d_pieces[-group:])

    acts = [made[0] for _, _, made in groups]
    d_gate_rows = [made[1] for _, _, made in groups]
    d_up_rows = [made[2] for _, _, made in groups]
    ins = [rows for rows, _, _ in groups]
    outs = [d_rows for _, d_rows, _ in groups]
    mix_stacks = combine_stacks(
        places, [made[4] for _, _, made in groups], n_ep, local, cap, group, d_pieces
    )
    grad_down = weight_grad(acts, outs, [mix_stacks[0], *d_sums[3:]])
    d_gates = by_piece(jnp.concatenate(d_gates, axis=0).reshape(n_ep, local, tok_dev))
    d_gates = lax.all_to_all(d_gates, "ep", split_axis=0, concat_axis=0, tiled=True)
    d_gates = d_gates.reshape(expert_count, tok_dev)
    if n_ep == 8:
        d_sums[2], mix_stacks[2], mix_stacks[3], grad_down = tie(
            d_sums[2], mix_stacks[2], mix_stacks[3], grad_down
        )
        d_h2, d_far = scatter_z(*d_sums)
        d_last = [d_far]
    else:
        d_h2, d_last = scatter(d_pieces, n_ep), []
    grad_gate = weight_grad(ins, d_gate_rows, [grad_down, d_gates, *d_last])
    grad_up = weight_grad(ins, d_up_rows, [grad_gate])

    def over_sp(value):
        return lax.psum_scatter(value, "sp", scatter_dimension=1, tiled=True).astype(F32)


    if n_ep == 8:
        gates_here = home_gates[:expert_count]
    else:
        logits = product_right(full_router, h2_low)
        logits = jnp.where(picked.T, logits, NEG_FILL)
        gates_here = jax.nn.softmax(logits, axis=0)
    d_logits = gates_here * (d_gates - jnp.sum(gates_here * d_gates, axis=0, keepdims=True))
    d_logits = jnp.where(picked.T, d_logits, 0.0).astype(BF16)
    grad_router = product(d_logits, h2_low)
    d_h2 = d_h2 + product_left(d_logits, full_router)
    one_scale = lax.rsqrt(jnp.mean(x_one * x_one, axis=-1, keepdims=True) + EPS)
    one_normed = x_one * one_scale
    grad_ffn = jnp.sum(d_h2 * one_normed, axis=0)
    d_normed = d_h2 * gains[3][None, :]
    d_one = cotangent[0].astype(F32) + one_scale * (
        d_normed - one_normed * jnp.mean(d_normed * one_normed, axis=-1, keepdims=True)
    )
    d_z, grad_up = tie(d_one.astype(BF16), grad_up)
    d_attn = out_back(ids, n_ep, d_z, w_o_parts, [])
    d_heads = lax.all_to_all(d_attn, "sp", split_axis=1, concat_axis=0, tiled=True)
    d_z_cols = lax.all_to_all(d_z, "sp", split_axis=1, concat_axis=0, tiled=True)
    mix, mix_far = scatter_stacks(mix_stacks, n_ep)
    if n_ep == 8:
        mix, mix_far, d_heads = tie(mix, mix_far, d_heads)
    grad_down, grad_gate, grad_up = over_sp(grad_down), over_sp(grad_gate), over_sp(grad_up)

    d_qn, d_kn, d_v, sums, grad_qg, grad_kg = attend_back(
        q_rot, k_rot, v_low, d_heads, q_raw, k_raw, scales, gain_q, gain_k, cosine, sine, starts
    )
    output = (x_one + last_hop(mix, mix_far)).astype(BF16)
    vo_stacks = vo_grads(ids, n_ep, h_all, d_v, attn_all, d_z_cols)
    grad_vo = last_hop(*scatter_stacks(vo_stacks, n_ep)).astype(BF16)

    def placed(value):
        return lax.dynamic_update_slice_in_dim(
            jnp.zeros((1, width), F32), value, sp_index * head_width, 1
        )

    tiny = jnp.concatenate(
        [placed(grad_qg), placed(grad_kg), grad_ffn[None], grad_router], axis=0
    )
    *qk_stacks, d_qk = qk_back(
        ids, n_ep, h_all, d_qn, d_kn, q_raw, k_raw, scales, sum_sp_swaps(sums), tiny, vo_stacks[:1]
    )
    grad_qk, qk_far = scatter_stacks(qk_stacks, n_ep)
    grad_qk = last_hop(grad_qk, qk_far).astype(BF16)

    d_h = d_h_rows(ids, n_ep, n_sp, d_qk, d_v, w_qkv, [output, grad_down, grad_gate])
    halves = plus(d_h[:2], swap_sp(d_h[2:], 1))
    d_h = halves[0].astype(F32) + swap_sp(halves[1], 2).astype(F32)
    x_rows = tokens[0].astype(F32)
    x_scale = lax.rsqrt(jnp.mean(x_rows * x_rows, axis=-1, keepdims=True) + EPS)
    x_normed = x_rows * x_scale
    d_normed = d_h * gains[0][None, :]
    input_grad = d_one + x_scale * (
        d_normed - x_normed * jnp.mean(d_normed * x_normed, axis=-1, keepdims=True)
    )

    g_query, g_key, g_value, g_out, tiny, g_attn = finish(
        ids, n_ep, w_query, w_key, w_value, attn_gain.astype(F32)[:, None],
        gather_sp(grad_qk), gather_sp(grad_vo), [grad_down, grad_gate, grad_up, input_grad],
    )
    per_row = 2 * head_width // shard

    def vector(at):
        col = (at % per_row) * shard
        return tiny[at // per_row, col : col + shard]

    g_router = jnp.stack([vector(3 + i) for i in range(expert_count)], axis=1)
    return (
        output[None], input_grad[None], g_attn[:, 0], g_query, g_key, g_value, vector(0), vector(1),
        g_out, vector(2), g_router, grad_gate, grad_up, grad_down,
    )


def solution(mesh):
    seq = P("ep", "sp", None)
    vec = P("ep")
    mat = P("ep", None)
    expert = P("ep", None, None)
    in_specs = (
        seq, mat, seq, vec, mat, mat, mat, vec, vec, mat, vec, mat, expert, expert, expert, seq,
    )
    out_specs = (
        seq, seq, vec, mat, mat, mat, vec, vec, mat, vec, mat, seq, seq, seq,
    )
    return jax.shard_map(body, mesh=mesh, in_specs=in_specs, out_specs=out_specs, check_vma=False)
```

```python
import functools

import jax
import jax.numpy as jnp
from jax import lax
from jax.experimental import pallas as pl
from jax.experimental.pallas import tpu as pltpu
from jax.sharding import PartitionSpec as P

HEAD_DIM = 128
EPS = 1e-05
THETA = 10000.0
NEG_FILL = -1e30
F32 = jnp.float32
BF16 = jnp.bfloat16
MIB = 1 << 20
COVER = 20


def product(left, right):
    return jnp.dot(left, right, preferred_element_type=F32)


def product_left(left, right):
    return lax.dot_general(left, right, (((0,), (0,)), ((), ())), preferred_element_type=F32)


def product_right(left, right):
    return lax.dot_general(left, right, (((1,), (1,)), ((), ())), preferred_element_type=F32)


def row_sums(values_in):
    sums = jnp.sum(values_in, axis=1, keepdims=True)
    return jnp.transpose(jnp.broadcast_to(sums, (sums.shape[0], HEAD_DIM)))[:8]


def call(kernel, out_shape, args, flops, name, scratch=(), scalars=(), grid=(1,), in_specs=None,
         out_specs=None, aliases=None, vmem=60, after=()):
    single = not isinstance(out_shape, (list, tuple))
    shapes = [out_shape] if single else list(out_shape)
    count = len(grid)

    def fixed(shape):
        rank = len(shape)
        return pl.BlockSpec(tuple(shape), lambda *ids: (0,) * rank)

    in_specs = in_specs or [None] * len(args)
    out_specs = out_specs or [None] * len(shapes)
    in_specs = [s if s is not None else fixed(a.shape) for s, a in zip(in_specs, args)]
    out_specs = [s if s is not None else fixed(o.shape) for s, o in zip(out_specs, shapes)]
    waited = len(after)
    args = [*args, *after]
    in_specs = in_specs + [pl.BlockSpec(memory_space=pl.ANY)] * waited
    if waited:
        inner, first = kernel, len(scalars) + len(args) - waited

        def kernel(*refs):
            inner(*refs[:first], *refs[first + waited :])

    moved = sum(a.size * a.dtype.itemsize for a in args[: len(args) - waited])
    moved += sum(o.size * o.dtype.itemsize for o in shapes)
    result = pl.pallas_call(
        kernel,
        grid_spec=pltpu.PrefetchScalarGridSpec(
            num_scalar_prefetch=len(scalars), grid=grid, in_specs=in_specs, out_specs=out_specs,
            scratch_shapes=list(scratch),
        ),
        out_shape=shapes,
        input_output_aliases={k + len(scalars): v for k, v in (aliases or {}).items()},
        compiler_params=pltpu.CompilerParams(
            vmem_limit_bytes=vmem * MIB, dimension_semantics=("arbitrary",) * count
        ),
        cost_estimate=pl.CostEstimate(flops=int(COVER * flops), bytes_accessed=int(moved), transcendentals=0),
        name=name,
    )(*scalars, *args)
    return result[0] if single else list(result)


def like(shape, dtype):
    return jax.ShapeDtypeStruct(tuple(shape), dtype)


def tie(*values):
    return lax.optimization_barrier(values)


def swap(value, bits):
    return lax.ppermute(value, "ep", [(i, i ^ bits) for i in range(8)])


def swap_sp(value, bits):
    return lax.ppermute(value, "sp", [(i, i ^ bits) for i in range(4)])


def piece_blocks(n_ep, ep_index):
    ids = jnp.arange(n_ep, dtype=jnp.int32)
    return jnp.bitwise_xor(ids, ep_index) if n_ep == 8 else ids


MIDDLE = [(2, 4), (3, 5), (4, 2), (5, 3)]
OUTWARD = [(2, 0), (3, 1), (4, 6), (5, 7)]


def gather_line(value):
    crossed = swap(value, 1)
    near = swap(value, 2)
    inner = lax.ppermute(value, "ep", MIDDLE)
    near_x, outer = swap(near, 1), lax.ppermute(near, "ep", MIDDLE)
    near_x, crossed, outer = tie(near_x, crossed, outer)
    far = outer + lax.ppermute(inner, "ep", OUTWARD)
    farther = inner + lax.ppermute(outer, "ep", OUTWARD)
    return [value, crossed, near, near_x, far, swap(far, 1), farther, swap(farther, 1)]


def gather_double(value, after):
    after, held = tie(after, value)
    crossed = swap(held, 1)
    near, far = swap(value, 2), swap(value, 4)
    farther = swap(far, 2)
    return [
        value, crossed, near, swap(near, 1), far, swap(far, 1), farther, swap(farther, 1)
    ], after


def gather_whole(value):
    whole = lax.all_gather(value, "ep", axis=0, tiled=False)
    return [whole[i] for i in range(whole.shape[0])]


def gather(value, n_ep):
    return gather_line(value) if n_ep == 8 else gather_whole(value)


def plus(left, right):
    return (left.astype(F32) + right.astype(F32)).astype(left.dtype)


def crossed_sums(pieces):
    return [plus(pieces[i], swap(pieces[i + 1], 1)) for i in range(0, len(pieces), 2)]


def scatter_z(own, near, far, farther):
    far = plus(far, swap(farther, 2))
    far, near = tie(far, near)
    return own.astype(F32) + swap(near, 2).astype(F32) + swap(far, 4).astype(F32), far


def scatter(pieces, n_ep):
    if n_ep != 8:
        stacked = jnp.stack(pieces)
        return lax.psum_scatter(stacked, "ep", scatter_dimension=0, tiled=False).astype(F32)
    return scatter_z(*crossed_sums(pieces))[0]


def stack_at(piece, n_ep):
    if n_ep != 8:
        return 0, piece
    return 2 * (piece % 2) + (piece // 2) % 2, piece // 4


def stack_shapes(n_ep, shape):
    return [like((2, *shape), BF16)] * 4 if n_ep == 8 else [like((n_ep, *shape), BF16)]


def odd_sums(stacks):
    return plus(stacks[1], swap(stacks[3], 1))


def even_sums(stacks, odd):
    even = stacks[0].astype(F32) + swap(stacks[2], 1).astype(F32) + swap(odd, 2).astype(F32)
    return even[0], even[1].astype(BF16)


def scatter_stacks(stacks, n_ep):
    if n_ep != 8:
        total = lax.psum_scatter(stacks[0], "ep", scatter_dimension=0, tiled=False)
        return total.astype(F32), None
    return even_sums(stacks, odd_sums(stacks))


def last_hop(total, far):
    return total if far is None else total + swap(far, 4).astype(F32)


def gather_sp(value):
    over = swap_sp(value, 2)
    return [value, swap_sp(value, 1), over, swap_sp(over, 1)]


def sum_sp(value):
    n_sp = lax.axis_size("sp")
    value = jnp.broadcast_to(value[None], (n_sp, *value.shape))
    return jnp.sum(lax.all_to_all(value, "sp", split_axis=0, concat_axis=0, tiled=True), axis=0)


def sum_sp_swaps(value):
    return (value + swap_sp(value, 1)) + (swap_sp(value, 2) + swap_sp(value, 3))


def block_at(ids, position, size):
    if size % HEAD_DIM:
        return pl.ds(position * size, size)
    return pl.ds(pl.multiple_of(ids[position] * size, size), size)


def qkv_kernel(count, ids, x_ref, gain_ref, *refs):
    pieces, refs = refs[:count], refs[count:]
    q_ref, k_ref, v_ref, squares_ref, w_ref, out_ref, h_ref = refs
    shard = pieces[0].shape[0]
    width = q_ref.shape[1]

    @pl.when(pl.program_id(0) == 0)
    def _():
        for k in range(count):
            rows = block_at(ids, k, shard)
            w_ref[rows, :] = pieces[k][:, : 3 * width]
            out_ref[rows, :] = pieces[k][:, 3 * width :]

    x_rows = x_ref[...].astype(F32)
    scale = lax.rsqrt(jnp.mean(x_rows * x_rows, axis=1, keepdims=True) + EPS)
    h_ref[...] = (x_rows * scale * gain_ref[...]).astype(BF16)
    for at, ref in enumerate((q_ref, k_ref)):
        part = product(h_ref[...], w_ref[:, at * width : (at + 1) * width])
        ref[...] = part
        squares_ref[8 * at : 8 * at + 8, :] = row_sums(part * part)
    v_ref[...] = product(h_ref[...], w_ref[:, 2 * width :]).astype(BF16)


def qkv_project(ids, x_all, gain, pieces):
    total, depth = x_all.shape
    width = pieces[0].shape[1] // 4
    rows = min(256, total)
    block = pl.BlockSpec((rows, width), lambda i, ids: (i, 0))
    wide = pl.BlockSpec((rows, depth), lambda i, ids: (i, 0))
    return call(
        functools.partial(qkv_kernel, len(pieces)),
        [like((total, width), F32)] * 2
        + [like((total, width), BF16), like((16, total), F32), like((depth, 3 * width), BF16)]
        + [like((depth, width), BF16), like((total, depth), BF16)],
        [x_all, gain, *pieces],
        6 * total * depth * width,
        "qkv_project",
        scalars=(ids,),
        grid=(total // rows,),
        in_specs=[wide] + [None] * (len(pieces) + 1),
        out_specs=[
            block, block, block, pl.BlockSpec((16, rows), lambda i, ids: (0, i)), None, None, wide,
        ],
    )


def out_kernel(n_ep, ids, attn_ref, x_ref, gain_ref, *refs):
    weights, (one_ref, low_ref) = refs[:-2], refs[-2:]
    width = weights[0].shape[1]
    for j, weight in enumerate(weights):
        cols = block_at(ids, n_ep + j, width)
        one_ref[:, cols] = x_ref[:, cols].astype(F32) + product(attn_ref[...], weight[...])
    one = one_ref[...]
    scale = lax.rsqrt(jnp.mean(one * one, axis=1, keepdims=True) + EPS)
    low_ref[...] = (one * scale * gain_ref[...]).astype(BF16)


def out_project(ids, n_ep, attn_tok, tokens, gain, weights, after):
    return call(
        functools.partial(out_kernel, n_ep),
        [like(tokens.shape, F32), like(tokens.shape, BF16)],
        [attn_tok, tokens, gain, *weights],
        2 * tokens.size * attn_tok.shape[1],
        "out_project",
        after=after,
        scalars=(ids,),
    )


def out_back_kernel(n_ep, ids, d_ref, *refs):
    weights, d_attn_ref = refs[:-1], refs[-1]
    width = weights[0].shape[1]
    total = None
    for j, weight in enumerate(weights):
        part = product_right(d_ref[:, block_at(ids, n_ep + j, width)], weight[...])
        total = part if total is None else total + part
    d_attn_ref[...] = total.astype(BF16)


def out_back(ids, n_ep, d_z, weights, after):
    return call(
        functools.partial(out_back_kernel, n_ep),
        like((d_z.shape[0], weights[0].shape[0]), BF16),
        [d_z, *weights],
        2 * d_z.size * weights[0].shape[0],
        "out_back",
        after=after,
        scalars=(ids,),
    )


def vo_grads_kernel(count, shard, ids, h_ref, dv_ref, attn_ref, dz_ref, *stacks):
    width = dv_ref.shape[1]
    for k in range(count):
        block = block_at(ids, k, shard)
        array, place = stack_at(k, count)
        stacks[array][place, :, :width] = product_left(h_ref[:, block], dv_ref[...]).astype(BF16)
        stacks[array][place, :, width:] = product_left(attn_ref[:, block], dz_ref[...]).astype(BF16)


def vo_grads(ids, count, h_all, d_v, attn_all, d_z_cols):
    shard = h_all.shape[1] // count
    width = d_v.shape[1]
    return call(
        functools.partial(vo_grads_kernel, count, shard),
        stack_shapes(count, (shard, 2 * width)),
        [h_all, d_v, attn_all, d_z_cols],
        4 * h_all.size * width,
        "vo_grads",
        scalars=(ids,),
    )


def qk_back_kernel(
    count, shard, ids, h_ref, dqn_ref, dkn_ref, qr_ref, kr_ref, scale_ref, sums_ref, tiny_ref, *refs
):
    stacks, d_ref = refs[:-1], refs[-1]
    width = dqn_ref.shape[1]
    scales = jnp.transpose(scale_ref[...])
    means = jnp.transpose(sums_ref[...]) * (1.0 / h_ref.shape[1])
    for at, (d_normed, raw) in enumerate(((dqn_ref, qr_ref), (dkn_ref, kr_ref))):
        scale, mean = scales[:, 8 * at : 8 * at + 1], means[:, 8 * at : 8 * at + 1]
        d_ref[:, at * width : (at + 1) * width] = (
            scale * (d_normed[...] - raw[...] * scale * mean)
        ).astype(BF16)
    per_row = 2 * width // shard
    extra = stacks[0].shape[1] - shard
    for k in range(count):
        block = block_at(ids, k, shard)
        array, place = stack_at(k, count)
        ref = stacks[array]
        ref[place, :shard, :] = product_left(h_ref[:, block], d_ref[...]).astype(BF16)
        ref[place, shard:, :] = jnp.zeros((extra, 2 * width), BF16)
        for at in range(tiny_ref.shape[0]):
            row, col = shard + at // per_row, (at % per_row) * shard
            ref[place, row : row + 1, col : col + shard] = tiny_ref[at : at + 1, block].astype(BF16)


def qk_back(ids, count, h_all, d_qn, d_kn, q_raw, k_raw, scales, sums, tiny, after):
    total, depth = h_all.shape
    width = d_qn.shape[1]
    shard = depth // count
    extra = -(-tiny.shape[0] // (2 * width // shard))
    extra = -(-extra // 16) * 16
    return call(
        functools.partial(qk_back_kernel, count, shard),
        stack_shapes(count, (shard + extra, 2 * width)) + [like((total, 2 * width), BF16)],
        [h_all, d_qn, d_kn, q_raw, k_raw, scales, sums, tiny],
        2 * h_all.size * 2 * width,
        "qk_back",
        scalars=(ids,),
        after=after,
    )


def d_h_kernel(ids, d_ref, dv_ref, w_ref, out_ref):
    both = d_ref.shape[1]
    out_ref[0] = (
        product_right(d_ref[...], w_ref[:, :both]) + product_right(dv_ref[...], w_ref[:, both:])
    ).astype(BF16)


def d_h_rows(ids, n_ep, n_sp, d_qk, d_v, w_qkv, after):
    total, wide = d_qk.shape
    depth = w_qkv.shape[0]
    rows = total // n_sp

    def partner(j, ids):
        return ids[n_ep + (j % 2) * 2 + j // 2], 0

    return call(
        d_h_kernel,
        like((n_sp, rows, depth), BF16),
        [d_qk, d_v, w_qkv],
        3 * d_qk.size * depth,
        "d_h",
        after=after,
        scalars=(ids,),
        grid=(n_sp,),
        in_specs=[
            pl.BlockSpec((rows, wide), partner), pl.BlockSpec((rows, d_v.shape[1]), partner), None,
        ],
        out_specs=[pl.BlockSpec((1, rows, depth), lambda j, ids: (j, 0, 0))],
    )


def finish_kernel(n_ep, n_sp, ids, wq_ref, wk_ref, wv_ref, gain_ref, *refs):
    firsts, seconds = refs[:n_sp], refs[n_sp : 2 * n_sp]
    gq_ref, gk_ref, gv_ref, go_ref, tiny_ref, attn_ref = refs[2 * n_sp :]
    shard = wq_ref.shape[0]
    width = firsts[0].shape[1] // 2
    dots = jnp.zeros((shard, 1), F32)
    tiny = jnp.zeros(tiny_ref.shape, F32)
    for j in range(n_sp):
        cols = block_at(ids, n_ep + j, width)
        for at, grad, weight in ((0, gq_ref, wq_ref), (1, gk_ref, wk_ref), (2, gv_ref, wv_ref)):
            part = firsts[j][:shard, at * width : (at + 1) * width] if at < 2 else seconds[j][:, :width]
            value = part.astype(F32)
            grad[:, cols] = value
            dots += jnp.sum(value * weight[:, cols].astype(F32), axis=1, keepdims=True)
        go_ref[:, cols] = seconds[j][:, width:].astype(F32)
        tiny += firsts[j][shard:, :].astype(F32)
    tiny_ref[...] = tiny
    attn_ref[...] = dots / gain_ref[...]


def finish(ids, n_ep, w_query, w_key, w_value, gain, firsts, seconds, after):
    shard, depth = w_query.shape
    extra = firsts[0].shape[0] - shard
    return call(
        functools.partial(finish_kernel, n_ep, len(firsts)),
        [like((shard, depth), F32)] * 4 + [like((extra, firsts[0].shape[1]), F32), like((shard, 1), F32)],
        [w_query, w_key, w_value, gain, *firsts, *seconds],
        shard * depth * 6,
        "finish",
        after=after,
        scalars=(ids,),
    )


def turn(values_in):
    return pltpu.roll(values_in, HEAD_DIM // 2, 1)


def masked_probs(q_ref, k_ref, start_ref, block, rows):
    first, last = block * rows, (block + 1) * rows
    scores = product_right(q_ref[first:last, :], k_ref[0:last, :]) * (HEAD_DIM ** (-0.5))
    row_ids = first + lax.broadcasted_iota(jnp.int32, scores.shape, 0)
    places = lax.broadcasted_iota(jnp.int32, scores.shape, 1)
    allowed = (places <= row_ids) & (places >= start_ref[first:last, :])
    scores = jnp.where(allowed, scores, NEG_FILL)
    top = jnp.max(scores, axis=1, keepdims=True)
    weights = jnp.exp(scores - top)
    return weights * (1.0 / jnp.sum(weights, axis=1, keepdims=True))


def attend_kernel(
    rows, qr_ref, kr_ref, v_ref, scale_ref, gq_ref, gk_ref, cos_ref, sin_ref, start_ref,
    q_ref, k_ref, out_ref,
):
    scales = jnp.transpose(scale_ref[...])
    for at, (raw, gain, low) in enumerate(((qr_ref, gq_ref, q_ref), (kr_ref, gk_ref, k_ref))):
        normed = raw[...] * scales[:, 8 * at : 8 * at + 1] * gain[...]
        low[...] = (normed * cos_ref[...] + turn(normed) * sin_ref[...]).astype(BF16)
    for block in range(q_ref.shape[0] // rows):
        probs = masked_probs(q_ref, k_ref, start_ref, block, rows)
        last = (block + 1) * rows
        out_ref[block * rows : last, :] = product(
            probs.astype(BF16), v_ref[0:last, :]
        ).astype(BF16)


def head_spec(rows):
    return pl.BlockSpec((rows, HEAD_DIM), lambda h: (0, h))


def attend(q_raw, k_raw, v_low, scales, q_gain, k_gain, cosine, sine, starts, after):
    total, width = v_low.shape
    heads = width // HEAD_DIM
    head, gain = head_spec(total), head_spec(1)
    return call(
        functools.partial(attend_kernel, min(256, total)),
        [like((total, width), BF16)] * 3,
        [q_raw, k_raw, v_low, scales, q_gain, k_gain, cosine, sine, starts],
        3 * heads * total * total * HEAD_DIM,
        "attend",
        after=after,
        grid=(heads,),
        in_specs=[head, head, head, None, gain, gain, None, None, None],
        out_specs=[head, head, head],
    )


def attend_back_kernel(
    rows, q_ref, k_ref, v_ref, do_ref, qr_ref, kr_ref, scale_ref, gq_ref, gk_ref,
    cos_ref, sin_ref, start_ref,
    dq_ref, dk_ref, dv_ref, sums_ref, dgq_ref, dgk_ref, q_acc, k_acc, v_acc,
):
    k_acc[...] = jnp.zeros_like(k_acc)
    v_acc[...] = jnp.zeros_like(v_acc)
    for block in range(q_ref.shape[0] // rows):
        first, last = block * rows, (block + 1) * rows
        probs = masked_probs(q_ref, k_ref, start_ref, block, rows)
        d_rows = do_ref[first:last, :]
        d_probs = product_right(d_rows, v_ref[0:last, :])
        delta = jnp.sum(probs * d_probs, axis=1, keepdims=True)
        d_scores = (probs * (d_probs - delta) * (HEAD_DIM ** (-0.5))).astype(BF16)
        q_acc[first:last, :] = product(d_scores, k_ref[0:last, :])
        k_acc[0:last, :] += product_left(d_scores, q_ref[first:last, :])
        v_acc[0:last, :] += product_left(probs.astype(BF16), d_rows)
    dv_ref[...] = v_acc[...].astype(BF16)

    @pl.when(pl.program_id(0) == 0)
    def _():
        sums_ref[...] = jnp.zeros_like(sums_ref)

    scales = jnp.transpose(scale_ref[...])
    for at, (acc, raw, gain, d_ref, dg_ref) in enumerate(
        ((q_acc, qr_ref, gq_ref, dq_ref, dgq_ref), (k_acc, kr_ref, gk_ref, dk_ref, dgk_ref))
    ):
        turned = acc[...].astype(BF16).astype(F32)
        back = turned * cos_ref[...] + turn(turned * sin_ref[...])
        normed = raw[...] * scales[:, 8 * at : 8 * at + 1]
        both = back * normed
        dg_ref[...] = jnp.sum(both, axis=0, keepdims=True)
        d_ref[...] = back * gain[...]
        sums_ref[8 * at : 8 * at + 8, :] += row_sums(both * gain[...])


def attend_back(
    q_rot, k_rot, v_low, d_heads, q_raw, k_raw, scales, q_gain, k_gain, cosine, sine, starts
):
    total, width = v_low.shape
    heads = width // HEAD_DIM
    head, gain = head_spec(total), head_spec(1)
    wide, thin = like((total, width), F32), like((1, width), F32)
    return call(
        functools.partial(attend_back_kernel, min(256, total)),
        [wide, wide, like((total, width), BF16), like((16, total), F32), thin, thin],
        [q_rot, k_rot, v_low, d_heads, q_raw, k_raw, scales, q_gain, k_gain, cosine, sine, starts],
        7 * heads * total * total * HEAD_DIM,
        "attend_back",
        scratch=[pltpu.VMEM((total, HEAD_DIM), F32)] * 3,
        grid=(heads,),
        in_specs=[head] * 6 + [None, gain, gain, None, None, None],
        out_specs=[head, head, head, None, gain, gain],
    )


def chooser(places_ref, at, cap):
    row = places_ref[at : at + 1, :]
    slots = lax.broadcasted_iota(jnp.int32, (cap, row.shape[1]), 0)
    return slots == row


def dispatch_kernel(
    pieces_here, local, cap, gated, mine, *refs
):
    pieces, refs = refs[:pieces_here], refs[pieces_here:]
    places_ref, refs = refs[0], refs[1:]
    if gated:
        (picked_ref, router_ref), refs = refs[:2], refs[2:]
        rows_ref, gate_ref, all_ref = refs[-3:]
    else:
        rows_ref = refs[-1]
    for p in range(pieces_here):
        if gated:
            logits = product_right(router_ref[...], pieces[p][...])
            experts = logits.shape[0]
            picked = picked_ref[p * experts : (p + 1) * experts, :] > 0
            logits = jnp.where(picked, logits, NEG_FILL)
            weights = jnp.exp(logits - jnp.max(logits, axis=0, keepdims=True))
            weights = jnp.where(picked, weights, 0.0)
            gates = weights / jnp.sum(weights, axis=0, keepdims=True)
            all_ref[p * experts : (p + 1) * experts, :] = gates
        for e in range(local):
            chosen = chooser(places_ref, p * local + e, cap)
            rows_ref[e, p * cap : (p + 1) * cap, :] = product(
                chosen.astype(BF16), pieces[p][...]
            ).astype(BF16)
            if gated:
                row = all_ref[pl.ds(p * experts + mine[0] * local + e, 1), :]
                gate_ref[e, p * cap : (p + 1) * cap, :] = jnp.sum(
                    jnp.where(chosen, row, 0.0), axis=1, keepdims=True
                )


def dispatch(mine, pieces, places, picked, router, local, cap, group, at, rows, gates, after=()):
    gated = router is not None
    here = len(pieces)
    width = pieces[0].shape[1]
    args = [*pieces, places]
    shapes = [like((local, group * cap, width), BF16)]
    spec = pl.BlockSpec((local, here * cap, width), lambda i, mine: (0, at, 0))
    out_specs = [spec]
    if gated:
        args += [picked, router]
        shapes += [like((local, group * cap, 1), F32), like((picked.shape[0], places.shape[1]), F32)]
        out_specs += [pl.BlockSpec((local, here * cap, 1), lambda i, mine: (0, at, 0)), None]
    in_specs = [None] * len(args)
    aliases = {}
    if rows is not None:
        aliases[len(args)] = 0
        args.append(rows)
        in_specs.append(pl.BlockSpec(memory_space=pl.ANY))
        if gated:
            aliases[len(args)] = 1
            args.append(gates)
            in_specs.append(pl.BlockSpec(memory_space=pl.ANY))
    return call(
        functools.partial(dispatch_kernel, here, local, cap, gated),
        shapes,
        args,
        2 * here * local * cap * places.shape[1] * width,
        "dispatch",
        scalars=(mine,),
        in_specs=in_specs,
        out_specs=out_specs,
        aliases=aliases,
        after=after,
    )


def expert_kernel(
    x_ref, d_ref, gate_ref, wg_ref, wu_ref, wd_ref,
    act_ref, dg_ref, du_ref, dots_ref, mix_ref, back_ref, mix_acc, back_acc,
):
    step = pl.program_id(1)
    last = pl.num_programs(1) - 1
    x_rows, d_rows, gate = x_ref[0], d_ref[0], gate_ref[0]
    pre = product(x_rows, wg_ref[0])
    up = product(x_rows, wu_ref[0])
    pulled = product_right(d_rows, wd_ref[0])
    sigma = jax.nn.sigmoid(pre)
    silu = pre * sigma
    act = silu * up
    dots = jnp.sum(act * pulled, axis=1, keepdims=True)
    act_low = (act * gate).astype(BF16)
    act_ref[0] = act_low
    d_act = pulled * gate
    du_low = (d_act * silu).astype(BF16)
    dg_low = (d_act * up * sigma * (1.0 + pre * (1.0 - sigma))).astype(BF16)
    dg_ref[0] = dg_low
    du_ref[0] = du_low
    mix = product(act_low, wd_ref[0])
    back = product_right(dg_low, wg_ref[0]) + product_right(du_low, wu_ref[0])

    @pl.when(step == 0)
    def _():
        dots_ref[0] = dots
        mix_acc[...] = mix
        back_acc[...] = back

    @pl.when((step > 0) & (step < last))
    def _():
        dots_ref[0] += dots
        mix_acc[...] += mix
        back_acc[...] += back

    @pl.when(step == last)
    def _():
        dots_ref[0] += dots
        mix_ref[0] = (mix_acc[...] + mix).astype(BF16)
        back_ref[0] = (back_acc[...] + back).astype(BF16)


def experts(rows, d_rows, gates, w_gate, w_up, w_down, after=()):
    local, count, width = rows.shape
    hidden = w_gate.shape[2]
    part = hidden // 2
    wide = pl.BlockSpec((1, count, width), lambda e, f: (e, 0, 0))
    column = pl.BlockSpec((1, count, 1), lambda e, f: (e, 0, 0))
    thin = pl.BlockSpec((1, count, part), lambda e, f: (e, 0, f))
    into = pl.BlockSpec((1, width, part), lambda e, f: (e, 0, f))
    outof = pl.BlockSpec((1, part, width), lambda e, f: (e, f, 0))
    return call(
        expert_kernel,
        [like((local, count, hidden), BF16)] * 3
        + [like((local, count, 1), F32)]
        + [like((local, count, width), BF16)] * 2,
        [rows, d_rows, gates, w_gate, w_up, w_down],
        12 * rows.size * hidden,
        "experts",
        after=after,
        scratch=[pltpu.VMEM((count, width), F32)] * 2,
        grid=(local, 2),
        in_specs=[wide, wide, column, into, into, outof],
        out_specs=[thin, thin, thin, column, wide, wide],
    )


def combine_kernel(here, local, cap, dotted, places_ref, rows_ref, *refs):
    pieces = refs[int(dotted) : int(dotted) + here]
    for p in range(here):
        chosen = [chooser(places_ref, p * local + e, cap) for e in range(local)]
        total = None
        for e in range(local):
            part = product_left(chosen[e].astype(BF16), rows_ref[e, p * cap : (p + 1) * cap, :])
            total = part if total is None else total + part
            if dotted:
                refs[-1][p * local + e : p * local + e + 1, :] = jnp.sum(
                    jnp.where(chosen[e], refs[0][e, p * cap : (p + 1) * cap, :], 0.0),
                    axis=0, keepdims=True,
                )
        pieces[p][...] = total.astype(BF16)


def combine(places, rows, here, local, cap, at, dots=None, after=()):
    width = rows.shape[2]
    tokens = places.shape[1]
    dotted = dots is not None
    args = [places, rows] + ([dots] if dotted else [])
    in_specs = [None, pl.BlockSpec((local, here * cap, width), lambda i: (0, at, 0))]
    if dotted:
        in_specs.append(pl.BlockSpec((local, here * cap, 1), lambda i: (0, at, 0)))
    shapes = [like((tokens, width), BF16)] * here
    if dotted:
        shapes.append(like(places.shape, F32))
    return call(
        functools.partial(combine_kernel, here, local, cap, dotted),
        shapes,
        args,
        2 * here * local * cap * tokens * width,
        "combine",
        after=after,
        in_specs=in_specs,
    )


def combine_stacks_kernel(count, local, cap, group, places_ref, *refs):
    groups = count // group
    for k in range(count):
        rows = refs[k // group]
        at = (k % group) * cap
        total = None
        for e in range(local):
            chosen = chooser(places_ref, k * local + e, cap).astype(BF16)
            part = product_left(chosen, rows[e, at : at + cap, :])
            total = part if total is None else total + part
        array, place = stack_at(k, count)
        refs[groups + array][place] = total.astype(BF16)


def combine_stacks(places, rows, count, local, cap, group, after):
    tokens, width = places.shape[1], rows[0].shape[2]
    return call(
        functools.partial(combine_stacks_kernel, count, local, cap, group),
        stack_shapes(count, (tokens, width)),
        [places, *rows],
        2 * count * local * cap * tokens * width,
        "combine_stacks",
        after=after,
    )


def weight_grad_kernel(groups, *refs):
    lefts, rights = refs[:groups], refs[groups : 2 * groups]
    total = None
    for left, right in zip(lefts, rights):
        part = product_left(left[0], right[0])
        total = part if total is None else total + part
    refs[-1][0] = total.astype(BF16)


def weight_grad(lefts, rights, after=()):
    local, count, tall = lefts[0].shape
    wide = rights[0].shape[2]
    part = min(512, tall)
    left = pl.BlockSpec((1, count, part), lambda e, i: (e, 0, i))
    right = pl.BlockSpec((1, count, wide), lambda e, i: (e, 0, 0))
    return call(
        functools.partial(weight_grad_kernel, len(lefts)),
        like((local, tall, wide), BF16),
        [*lefts, *rights],
        2 * len(lefts) * lefts[0].size * wide,
        "weight_grad",
        after=after,
        grid=(local, tall // part),
        in_specs=[left] * len(lefts) + [right] * len(lefts),
        out_specs=[pl.BlockSpec((1, part, wide), lambda e, i: (e, i, 0))],
    )


def body(
    tokens, doc_lengths, routes, attn_gain, w_query, w_key, w_value, q_gain, k_gain, w_out,
    ffn_gain, w_router, w_gate, w_up, w_down, cotangent,
):
    n_sp = lax.axis_size("sp")
    n_ep = lax.axis_size("ep")
    sp_index = lax.axis_index("sp")
    ep_index = lax.axis_index("ep")
    tok_dev, width = tokens.shape[1:]
    total = tok_dev * n_sp
    shard = width // n_ep
    head_width = width // n_sp
    top_count = routes.shape[2]
    local = w_gate.shape[0]
    expert_count = local * n_ep
    capacity = 9 * tok_dev * top_count // (8 * expert_count)
    cap = -(-capacity // 16) * 16
    group = 4
    blocks = piece_blocks(n_ep, ep_index)
    partners = jnp.bitwise_xor(jnp.arange(n_sp, dtype=jnp.int32), sp_index)
    ids = jnp.concatenate([blocks, partners]).astype(jnp.int32)
    mine = ep_index.astype(jnp.int32).reshape(1)

    def own_columns(value):
        return lax.dynamic_slice_in_dim(value, sp_index * head_width, head_width, 1)

    def by_piece(value):
        return jnp.stack(
            [lax.dynamic_index_in_dim(value, blocks[i], 0, keepdims=False) for i in range(n_ep)]
        )

    expert_ids = jnp.arange(expert_count, dtype=jnp.int32)
    picked = jnp.any(routes[0][:, :, None] == expert_ids[None, None, :], axis=1)
    picked_low = picked.T.astype(BF16)
    small = jnp.concatenate(
        [
            jnp.stack([attn_gain, q_gain, k_gain, ffn_gain]),
            jnp.zeros((12, shard), BF16),
            w_router.T,
        ],
        axis=0,
    )

    def to_all(value):
        value = jnp.broadcast_to(value[None], (n_ep, *value.shape))
        return lax.all_to_all(value, "ep", split_axis=0, concat_axis=0, tiled=True)

    if shard == tok_dev:
        both = to_all(jnp.concatenate([small, picked_low], axis=0))
        small_all, picked_all = both[:, : 16 + expert_count], both[:, 16 + expert_count :]
    else:
        small_all, picked_all = to_all(small), to_all(picked_low)
    small_rows = jnp.swapaxes(small_all, 0, 1).reshape(16 + expert_count, width)
    gains = small_rows[:4].astype(F32)
    full_router = small_rows[16:]
    picked_all = by_piece(picked_all)

    x_all = lax.all_gather(tokens[0], "sp", axis=0, tiled=True)
    w_own = jnp.concatenate([own_columns(w) for w in (w_query, w_key, w_value, w_out)], axis=1)
    cot_own = cotangent[0]
    if n_ep == 8:
        w_pieces = gather_line(w_own)
        w_pieces[6], cot_own = tie(w_pieces[6], cot_own)
        cot_pieces, w_pieces[7] = gather_double(cot_own, w_pieces[7])
    else:
        w_pieces, cot_pieces = gather_whole(w_own), gather_whole(cot_own)

    upper = (
        jnp.arange(tok_dev, dtype=jnp.int32)[:, None] < jnp.arange(tok_dev, dtype=jnp.int32)[None, :]
    ).astype(BF16)
    picked_mine = lax.dynamic_slice_in_dim(picked_all, ep_index * local, local, 1)
    picked_mine = picked_mine.reshape(n_ep * local, tok_dev)
    earlier = product(picked_mine, upper).astype(jnp.int32)
    places = jnp.where((picked_mine > 0) & (earlier < capacity), earlier, -1)
    picked_flat = picked_all.reshape(n_ep * expert_count, tok_dev).astype(F32)

    positions = jnp.arange(total, dtype=jnp.int32)
    lengths = doc_lengths[0]
    doc_ends = jnp.cumsum(lengths)
    starts = jnp.sum(
        jnp.where(doc_ends[None, :] <= positions[:, None], lengths[None, :], 0), axis=1
    )
    half = HEAD_DIM // 2
    frequency = THETA ** (-(2.0 * jnp.arange(half, dtype=F32)) / HEAD_DIM)
    angles = (positions - starts).astype(F32)[:, None] * frequency[None, :]
    cosine = jnp.concatenate([jnp.cos(angles), jnp.cos(angles)], axis=1)
    sine = jnp.concatenate([-jnp.sin(angles), jnp.sin(angles)], axis=1)
    starts = starts[:, None].astype(jnp.int32)

    q_raw, k_raw, v_low, squares, w_qkv, w_o, h_all = qkv_project(ids, x_all, gains[0:1], w_pieces)
    squares, w_o = tie(sum_sp(squares), w_o)
    scales = lax.rsqrt(squares / width + EPS)
    w_o_over = swap_sp(w_o, 2)
    gain_q, gain_k = own_columns(gains)[1:2], own_columns(gains)[2:3]
    q_rot, k_rot, mixed = attend(
        q_raw, k_raw, v_low, scales, gain_q, gain_k, cosine, sine, starts,
        [cot_pieces[k] for k in ((1, 2, 4) if n_ep == 8 else ())],
    )

    def pair_places(p):
        return places[p * local : (p + 2) * local]

    def cot_rows(g, after):
        d_rows = None
        for at, p in enumerate(range(g, g + group, 2)):
            (d_rows,) = dispatch(
                mine, cot_pieces[p : p + 2], pair_places(p), None, None, local, cap, group, at,
                d_rows, None, after,
            )
        return d_rows

    if n_ep == 8:
        cot_pieces[3], cot_pieces[6], mixed = tie(cot_pieces[3], cot_pieces[6], mixed)
    attn_tok = lax.all_to_all(mixed, "sp", split_axis=0, concat_axis=1, tiled=True)
    w_o_over, attn_tok = tie(w_o_over, attn_tok)
    w_o_parts = [w_o, swap_sp(w_o, 1), w_o_over, swap_sp(w_o_over, 1)]
    x_one, h2_low = out_project(
        ids, n_ep, attn_tok, tokens[0], gains[3:4], w_o_parts, []
    )
    attn_all = lax.all_gather(attn_tok, "sp", axis=0, tiled=True)

    h2_pieces = gather(h2_low, n_ep)
    cots = [cot_rows(g, [x_one]) for g in range(0, n_ep, group)]
    groups, d_pieces, d_gates, d_sums = [], [], [], []
    home_gates = None

    def rows_of(g, after):
        rows = gates = first_gates = None
        for at, p in enumerate(range(g, g + group, 2)):
            rows, gates, piece_gates = dispatch(
                mine, h2_pieces[p : p + 2], pair_places(p),
                picked_flat[p * expert_count : (p + 2) * expert_count], full_router, local, cap,
                group, at, rows, gates, after,
            )
            first_gates = piece_gates if first_gates is None else first_gates
        return rows, gates, first_gates

    rows, gates, home_gates = rows_of(0, [])
    for g in range(0, n_ep, group):
        d_rows = cots[g // group]
        made = experts(rows, d_rows, gates, w_gate, w_up, w_down, d_pieces[-group:] + cots + h2_pieces[4:7:2])
        groups.append((rows, d_rows, made))
        following = []
        if g + group < n_ep:
            rows, gates, _ = rows_of(g + group, [made[5]])
            following = [rows]
        sums_before = list(d_sums)
        for at in range(group // 2):
            *two, dots = combine(
                pair_places(g + 2 * at), made[5], 2, local, cap, at, made[3],
                sums_before + following,
            )
            d_pieces += two
            d_gates.append(dots)
        if n_ep == 8:
            d_sums += crossed_sums(d_pieces[-group:])

    acts = [made[0] for _, _, made in groups]
    d_gate_rows = [made[1] for _, _, made in groups]
    d_up_rows = [made[2] for _, _, made in groups]
    ins = [rows for rows, _, _ in groups]
    outs = [d_rows for _, d_rows, _ in groups]
    mix_stacks = combine_stacks(
        places, [made[4] for _, _, made in groups], n_ep, local, cap, group, d_pieces
    )
    grad_down = weight_grad(acts, outs, [mix_stacks[0], *d_sums[3:]])
    if n_ep == 8:
        d_sums[2], mix_stacks[2], mix_stacks[3], grad_down = tie(
            d_sums[2], mix_stacks[2], mix_stacks[3], grad_down
        )
        d_h2, d_far = scatter_z(*d_sums)
        d_last = [d_far]
    else:
        d_h2, d_last = scatter(d_pieces, n_ep), []
    d_gates = by_piece(jnp.concatenate(d_gates, axis=0).reshape(n_ep, local, tok_dev))
    if d_last:
        d_gates, d_last[0] = tie(d_gates, d_last[0])
    d_gates = lax.all_to_all(d_gates, "ep", split_axis=0, concat_axis=0, tiled=True)
    d_gates = d_gates.reshape(expert_count, tok_dev)
    grad_gate = weight_grad(ins, d_gate_rows, [grad_down, *d_last])
    grad_up = weight_grad(ins, d_up_rows, [grad_gate, d_gates])

    def over_sp(value):
        return lax.psum_scatter(value, "sp", scatter_dimension=1, tiled=True).astype(F32)


    if n_ep == 8:
        gates_here = home_gates[:expert_count]
    else:
        logits = product_right(full_router, h2_low)
        logits = jnp.where(picked.T, logits, NEG_FILL)
        gates_here = jax.nn.softmax(logits, axis=0)
    d_logits = gates_here * (d_gates - jnp.sum(gates_here * d_gates, axis=0, keepdims=True))
    d_logits = jnp.where(picked.T, d_logits, 0.0).astype(BF16)
    grad_router = product(d_logits, h2_low)
    d_h2 = d_h2 + product_left(d_logits, full_router)
    one_scale = lax.rsqrt(jnp.mean(x_one * x_one, axis=-1, keepdims=True) + EPS)
    one_normed = x_one * one_scale
    grad_ffn = jnp.sum(d_h2 * one_normed, axis=0)
    d_normed = d_h2 * gains[3][None, :]
    d_one = cotangent[0].astype(F32) + one_scale * (
        d_normed - one_normed * jnp.mean(d_normed * one_normed, axis=-1, keepdims=True)
    )
    d_z, grad_up = tie(d_one.astype(BF16), grad_up)
    d_attn = out_back(ids, n_ep, d_z, w_o_parts, [])
    d_heads = lax.all_to_all(d_attn, "sp", split_axis=1, concat_axis=0, tiled=True)
    d_z_cols = lax.all_to_all(d_z, "sp", split_axis=1, concat_axis=0, tiled=True)
    mix, mix_far = scatter_stacks(mix_stacks, n_ep)
    if n_ep == 8:
        mix, mix_far, d_heads = tie(mix, mix_far, d_heads)
    grad_down, grad_gate, grad_up = over_sp(grad_down), over_sp(grad_gate), over_sp(grad_up)

    d_qn, d_kn, d_v, sums, grad_qg, grad_kg = attend_back(
        q_rot, k_rot, v_low, d_heads, q_raw, k_raw, scales, gain_q, gain_k, cosine, sine, starts
    )
    output = (x_one + last_hop(mix, mix_far)).astype(BF16)
    vo_stacks = vo_grads(ids, n_ep, h_all, d_v, attn_all, d_z_cols)

    grad_vo = last_hop(*scatter_stacks(vo_stacks, n_ep)).astype(BF16)

    def placed(value):
        return lax.dynamic_update_slice_in_dim(
            jnp.zeros((1, width), F32), value, sp_index * head_width, 1
        )

    tiny = jnp.concatenate(
        [placed(grad_qg), placed(grad_kg), grad_ffn[None], grad_router], axis=0
    )
    *qk_stacks, d_qk = qk_back(
        ids, n_ep, h_all, d_qn, d_kn, q_raw, k_raw, scales, sum_sp_swaps(sums), tiny, vo_stacks[:1]
    )
    grad_qk = last_hop(*scatter_stacks(qk_stacks, n_ep)).astype(BF16)

    d_h = d_h_rows(ids, n_ep, n_sp, d_qk, d_v, w_qkv, [])
    output, d_h = tie(output, d_h)
    halves = plus(d_h[:2], swap_sp(d_h[2:], 1))
    d_h = halves[0].astype(F32) + swap_sp(halves[1], 2).astype(F32)
    x_rows = tokens[0].astype(F32)
    x_scale = lax.rsqrt(jnp.mean(x_rows * x_rows, axis=-1, keepdims=True) + EPS)
    x_normed = x_rows * x_scale
    d_normed = d_h * gains[0][None, :]
    input_grad = d_one + x_scale * (
        d_normed - x_normed * jnp.mean(d_normed * x_normed, axis=-1, keepdims=True)
    )

    g_query, g_key, g_value, g_out, tiny, g_attn = finish(
        ids, n_ep, w_query, w_key, w_value, attn_gain.astype(F32)[:, None],
        gather_sp(grad_qk), gather_sp(grad_vo), [grad_down, grad_gate, grad_up],
    )
    per_row = 2 * head_width // shard

    def vector(at):
        col = (at % per_row) * shard
        return tiny[at // per_row, col : col + shard]

    g_router = jnp.stack([vector(3 + i) for i in range(expert_count)], axis=1)
    return (
        output[None], input_grad[None], g_attn[:, 0], g_query, g_key, g_value, vector(0), vector(1),
        g_out, vector(2), g_router, grad_gate, grad_up, grad_down,
    )


def solution(mesh):
    seq = P("ep", "sp", None)
    vec = P("ep")
    mat = P("ep", None)
    expert = P("ep", None, None)
    in_specs = (
        seq, mat, seq, vec, mat, mat, mat, vec, vec, mat, vec, mat, expert, expert, expert, seq,
    )
    out_specs = (
        seq, seq, vec, mat, mat, mat, vec, vec, mat, vec, mat, seq, seq, seq,
    )
    return jax.shard_map(body, mesh=mesh, in_specs=in_specs, out_specs=out_specs, check_vma=False)
```

```python
import functools

import jax
import jax.numpy as jnp
from jax import lax
from jax.experimental import pallas as pl
from jax.experimental.pallas import tpu as pltpu
from jax.sharding import PartitionSpec as P

HEAD_DIM = 128
EPS = 1e-05
THETA = 10000.0
NEG_FILL = -1e30
F32 = jnp.float32
BF16 = jnp.bfloat16
MIB = 1 << 20
COVER = 20


def product(left, right):
    return jnp.dot(left, right, preferred_element_type=F32)


def product_left(left, right):
    return lax.dot_general(left, right, (((0,), (0,)), ((), ())), preferred_element_type=F32)


def product_right(left, right):
    return lax.dot_general(left, right, (((1,), (1,)), ((), ())), preferred_element_type=F32)


def row_sums(values_in):
    sums = jnp.sum(values_in, axis=1, keepdims=True)
    return jnp.transpose(jnp.broadcast_to(sums, (sums.shape[0], HEAD_DIM)))[:8]


def call(kernel, out_shape, args, flops, name, scratch=(), scalars=(), grid=(1,), in_specs=None,
         out_specs=None, aliases=None, vmem=60, after=()):
    single = not isinstance(out_shape, (list, tuple))
    shapes = [out_shape] if single else list(out_shape)
    count = len(grid)

    def fixed(shape):
        rank = len(shape)
        return pl.BlockSpec(tuple(shape), lambda *ids: (0,) * rank)

    in_specs = in_specs or [None] * len(args)
    out_specs = out_specs or [None] * len(shapes)
    in_specs = [s if s is not None else fixed(a.shape) for s, a in zip(in_specs, args)]
    out_specs = [s if s is not None else fixed(o.shape) for s, o in zip(out_specs, shapes)]
    waited = len(after)
    args = [*args, *after]
    in_specs = in_specs + [pl.BlockSpec(memory_space=pl.ANY)] * waited
    if waited:
        inner, first = kernel, len(scalars) + len(args) - waited

        def kernel(*refs):
            inner(*refs[:first], *refs[first + waited :])

    moved = sum(a.size * a.dtype.itemsize for a in args[: len(args) - waited])
    moved += sum(o.size * o.dtype.itemsize for o in shapes)
    result = pl.pallas_call(
        kernel,
        grid_spec=pltpu.PrefetchScalarGridSpec(
            num_scalar_prefetch=len(scalars), grid=grid, in_specs=in_specs, out_specs=out_specs,
            scratch_shapes=list(scratch),
        ),
        out_shape=shapes,
        input_output_aliases={k + len(scalars): v for k, v in (aliases or {}).items()},
        compiler_params=pltpu.CompilerParams(
            vmem_limit_bytes=vmem * MIB, dimension_semantics=("arbitrary",) * count
        ),
        cost_estimate=pl.CostEstimate(flops=int(COVER * flops), bytes_accessed=int(moved), transcendentals=0),
        name=name,
    )(*scalars, *args)
    return result[0] if single else list(result)


def like(shape, dtype):
    return jax.ShapeDtypeStruct(tuple(shape), dtype)


def tie(*values):
    return lax.optimization_barrier(values)


def swap(value, bits):
    return lax.ppermute(value, "ep", [(i, i ^ bits) for i in range(8)])


def swap_sp(value, bits):
    return lax.ppermute(value, "sp", [(i, i ^ bits) for i in range(4)])


def piece_blocks(n_ep, ep_index):
    ids = jnp.arange(n_ep, dtype=jnp.int32)
    return jnp.bitwise_xor(ids, ep_index) if n_ep == 8 else ids


MIDDLE = [(2, 4), (3, 5), (4, 2), (5, 3)]
OUTWARD = [(2, 0), (3, 1), (4, 6), (5, 7)]


def gather_line(value):
    crossed = swap(value, 1)
    near = swap(value, 2)
    inner = lax.ppermute(value, "ep", MIDDLE)
    near_x, outer = swap(near, 1), lax.ppermute(near, "ep", MIDDLE)
    near_x, crossed, outer = tie(near_x, crossed, outer)
    far = outer + lax.ppermute(inner, "ep", OUTWARD)
    farther = inner + lax.ppermute(outer, "ep", OUTWARD)
    return [value, crossed, near, near_x, far, swap(far, 1), farther, swap(farther, 1)]


def gather_double(value, after):
    after, held = tie(after, value)
    crossed = swap(held, 1)
    near, far = swap(value, 2), swap(value, 4)
    farther = swap(far, 2)
    return [
        value, crossed, near, swap(near, 1), far, swap(far, 1), farther, swap(farther, 1)
    ], after


def gather_whole(value):
    whole = lax.all_gather(value, "ep", axis=0, tiled=False)
    return [whole[i] for i in range(whole.shape[0])]


def gather(value, n_ep):
    return gather_line(value) if n_ep == 8 else gather_whole(value)


def plus(left, right):
    return (left.astype(F32) + right.astype(F32)).astype(left.dtype)


def crossed_sums(pieces):
    return [plus(pieces[i], swap(pieces[i + 1], 1)) for i in range(0, len(pieces), 2)]


def scatter_z(own, near, far, farther):
    far = plus(far, swap(farther, 2))
    far, near = tie(far, near)
    return own.astype(F32) + swap(near, 2).astype(F32) + swap(far, 4).astype(F32), far


def scatter(pieces, n_ep):
    if n_ep != 8:
        stacked = jnp.stack(pieces)
        return lax.psum_scatter(stacked, "ep", scatter_dimension=0, tiled=False).astype(F32)
    return scatter_z(*crossed_sums(pieces))[0]


def stack_at(piece, n_ep):
    if n_ep != 8:
        return 0, piece
    return 2 * (piece % 2) + (piece // 2) % 2, piece // 4


def stack_shapes(n_ep, shape):
    return [like((2, *shape), BF16)] * 4 if n_ep == 8 else [like((n_ep, *shape), BF16)]


def odd_sums(stacks):
    return plus(stacks[1], swap(stacks[3], 1))


def even_sums(stacks, odd):
    even = stacks[0].astype(F32) + swap(stacks[2], 1).astype(F32) + swap(odd, 2).astype(F32)
    return even[0], even[1].astype(BF16)


def scatter_stacks(stacks, n_ep):
    if n_ep != 8:
        total = lax.psum_scatter(stacks[0], "ep", scatter_dimension=0, tiled=False)
        return total.astype(F32), None
    return even_sums(stacks, odd_sums(stacks))


def last_hop(total, far):
    return total if far is None else total + swap(far, 4).astype(F32)


def gather_sp(value):
    over = swap_sp(value, 2)
    return [value, swap_sp(value, 1), over, swap_sp(over, 1)]


def sum_sp(value):
    n_sp = lax.axis_size("sp")
    value = jnp.broadcast_to(value[None], (n_sp, *value.shape))
    return jnp.sum(lax.all_to_all(value, "sp", split_axis=0, concat_axis=0, tiled=True), axis=0)


def sum_sp_swaps(value):
    return (value + swap_sp(value, 1)) + (swap_sp(value, 2) + swap_sp(value, 3))


def block_at(ids, position, size):
    if size % HEAD_DIM:
        return pl.ds(position * size, size)
    return pl.ds(pl.multiple_of(ids[position] * size, size), size)


def qkv_kernel(count, ids, x_ref, gain_ref, *refs):
    pieces, refs = refs[:count], refs[count:]
    q_ref, k_ref, v_ref, squares_ref, w_ref, h_ref = refs
    shard = pieces[0].shape[0]
    width = q_ref.shape[1]

    @pl.when(pl.program_id(0) == 0)
    def _():
        for k in range(count):
            rows = block_at(ids, k, shard)
            w_ref[rows, :] = pieces[k][:, : 3 * width]

    x_rows = x_ref[...].astype(F32)
    scale = lax.rsqrt(jnp.mean(x_rows * x_rows, axis=1, keepdims=True) + EPS)
    h_ref[...] = (x_rows * scale * gain_ref[...]).astype(BF16)
    for at, ref in enumerate((q_ref, k_ref)):
        part = product(h_ref[...], w_ref[:, at * width : (at + 1) * width])
        ref[...] = part
        squares_ref[8 * at : 8 * at + 8, :] = row_sums(part * part)
    v_ref[...] = product(h_ref[...], w_ref[:, 2 * width :]).astype(BF16)


def qkv_project(ids, x_all, gain, pieces, after):
    total, depth = x_all.shape
    width = pieces[0].shape[1] // 4
    rows = min(256, total)
    block = pl.BlockSpec((rows, width), lambda i, ids: (i, 0))
    wide = pl.BlockSpec((rows, depth), lambda i, ids: (i, 0))
    return call(
        functools.partial(qkv_kernel, len(pieces)),
        [like((total, width), F32)] * 2
        + [like((total, width), BF16), like((16, total), F32), like((depth, 3 * width), BF16)]
        + [like((total, depth), BF16)],
        [x_all, gain, *pieces],
        6 * total * depth * width,
        "qkv_project",
        after=after,
        scalars=(ids,),
        grid=(total // rows,),
        in_specs=[wide] + [None] * (len(pieces) + 1),
        out_specs=[
            block, block, block, pl.BlockSpec((16, rows), lambda i, ids: (0, i)), None, wide,
        ],
    )


def out_kernel(n_ep, n_sp, ids, attn_ref, x_ref, gain_ref, *refs):
    weights, (one_ref, low_ref, turned_ref) = refs[: 2 * n_sp], refs[2 * n_sp :]
    rows, width = weights[0].shape
    shard = 2 * rows // n_ep
    for k in range(n_ep):
        turned_ref[:, k * shard : (k + 1) * shard] = attn_ref[:, block_at(ids, k, shard)]
    for j in range(n_sp):
        cols = block_at(ids, n_ep + j, width)
        one_ref[:, cols] = (
            x_ref[:, cols].astype(F32)
            + product(turned_ref[:, :rows], weights[2 * j][...])
            + product(turned_ref[:, rows:], weights[2 * j + 1][...])
        )
    one = one_ref[...]
    scale = lax.rsqrt(jnp.mean(one * one, axis=1, keepdims=True) + EPS)
    low_ref[...] = (one * scale * gain_ref[...]).astype(BF16)


def out_project(ids, n_ep, attn_tok, tokens, gain, weights):
    return call(
        functools.partial(out_kernel, n_ep, len(weights) // 2),
        [like(tokens.shape, F32), like(tokens.shape, BF16)],
        [attn_tok, tokens, gain, *weights],
        2 * tokens.size * attn_tok.shape[1],
        "out_project",
        scratch=[pltpu.VMEM(attn_tok.shape, BF16)],
        scalars=(ids,),
    )


def out_back_kernel(n_ep, n_sp, ids, d_ref, *refs):
    weights, d_attn_ref = refs[:-1], refs[-1]
    rows, width = weights[0].shape
    shard = 2 * rows // n_ep
    for half in range(2):
        total = None
        for j in range(n_sp):
            part = product_right(
                d_ref[:, block_at(ids, n_ep + j, width)], weights[2 * j + half][...]
            )
            total = part if total is None else total + part
        total = total.astype(BF16)
        for k in range(n_ep // 2):
            block = block_at(ids, half * (n_ep // 2) + k, shard)
            d_attn_ref[:, block] = total[:, k * shard : (k + 1) * shard]


def out_back(ids, n_ep, d_z, weights):
    return call(
        functools.partial(out_back_kernel, n_ep, len(weights) // 2),
        like((d_z.shape[0], 2 * weights[0].shape[0]), BF16),
        [d_z, *weights],
        2 * d_z.size * weights[0].shape[0] * 2,
        "out_back",
        scalars=(ids,),
    )


def vo_grads_kernel(count, shard, ids, h_ref, dv_ref, attn_ref, dz_ref, *stacks):
    width = dv_ref.shape[1]
    for k in range(count):
        block = block_at(ids, k, shard)
        array, place = stack_at(k, count)
        stacks[array][place, :, :width] = product_left(h_ref[:, block], dv_ref[...]).astype(BF16)
        stacks[array][place, :, width:] = product_left(attn_ref[:, block], dz_ref[...]).astype(BF16)


def vo_grads(ids, count, h_all, d_v, attn_all, d_z_cols):
    shard = h_all.shape[1] // count
    width = d_v.shape[1]
    return call(
        functools.partial(vo_grads_kernel, count, shard),
        stack_shapes(count, (shard, 2 * width)),
        [h_all, d_v, attn_all, d_z_cols],
        4 * h_all.size * width,
        "vo_grads",
        scalars=(ids,),
    )


def qk_back_kernel(
    count, shard, ids, h_ref, dqn_ref, dkn_ref, qr_ref, kr_ref, scale_ref, sums_ref, tiny_ref, *refs
):
    stacks, d_ref = refs[:-1], refs[-1]
    width = dqn_ref.shape[1]
    scales = jnp.transpose(scale_ref[...])
    means = jnp.transpose(sums_ref[...]) * (1.0 / h_ref.shape[1])
    for at, (d_normed, raw) in enumerate(((dqn_ref, qr_ref), (dkn_ref, kr_ref))):
        scale, mean = scales[:, 8 * at : 8 * at + 1], means[:, 8 * at : 8 * at + 1]
        d_ref[:, at * width : (at + 1) * width] = (
            scale * (d_normed[...] - raw[...] * scale * mean)
        ).astype(BF16)
    per_row = 2 * width // shard
    extra = stacks[0].shape[1] - shard
    for k in range(count):
        block = block_at(ids, k, shard)
        array, place = stack_at(k, count)
        ref = stacks[array]
        ref[place, :shard, :] = product_left(h_ref[:, block], d_ref[...]).astype(BF16)
        ref[place, shard:, :] = jnp.zeros((extra, 2 * width), BF16)
        for at in range(tiny_ref.shape[0]):
            row, col = shard + at // per_row, (at % per_row) * shard
            ref[place, row : row + 1, col : col + shard] = tiny_ref[at : at + 1, block].astype(BF16)


def qk_back(ids, count, h_all, d_qn, d_kn, q_raw, k_raw, scales, sums, tiny, after):
    total, depth = h_all.shape
    width = d_qn.shape[1]
    shard = depth // count
    extra = -(-tiny.shape[0] // (2 * width // shard))
    extra = -(-extra // 16) * 16
    return call(
        functools.partial(qk_back_kernel, count, shard),
        stack_shapes(count, (shard + extra, 2 * width)) + [like((total, 2 * width), BF16)],
        [h_all, d_qn, d_kn, q_raw, k_raw, scales, sums, tiny],
        2 * h_all.size * 2 * width,
        "qk_back",
        scalars=(ids,),
        after=after,
    )


def d_h_kernel(ids, d_ref, dv_ref, w_ref, out_ref):
    both = d_ref.shape[1]
    out_ref[0] = (
        product_right(d_ref[...], w_ref[:, :both]) + product_right(dv_ref[...], w_ref[:, both:])
    ).astype(BF16)


def d_h_rows(ids, n_ep, n_sp, d_qk, d_v, w_qkv, after):
    total, wide = d_qk.shape
    depth = w_qkv.shape[0]
    rows = total // n_sp

    def partner(j, ids):
        return ids[n_ep + (j % 2) * 2 + j // 2], 0

    return call(
        d_h_kernel,
        like((n_sp, rows, depth), BF16),
        [d_qk, d_v, w_qkv],
        3 * d_qk.size * depth,
        "d_h",
        after=after,
        scalars=(ids,),
        grid=(n_sp,),
        in_specs=[
            pl.BlockSpec((rows, wide), partner), pl.BlockSpec((rows, d_v.shape[1]), partner), None,
        ],
        out_specs=[pl.BlockSpec((1, rows, depth), lambda j, ids: (j, 0, 0))],
    )


def finish_kernel(n_ep, n_sp, ids, wq_ref, wk_ref, wv_ref, gain_ref, *refs):
    firsts, seconds = refs[:n_sp], refs[n_sp : 2 * n_sp]
    gq_ref, gk_ref, gv_ref, go_ref, tiny_ref, attn_ref = refs[2 * n_sp :]
    shard = wq_ref.shape[0]
    width = firsts[0].shape[1] // 2
    dots = jnp.zeros((shard, 1), F32)
    tiny = jnp.zeros(tiny_ref.shape, F32)
    for j in range(n_sp):
        cols = block_at(ids, n_ep + j, width)
        for at, grad, weight in ((0, gq_ref, wq_ref), (1, gk_ref, wk_ref), (2, gv_ref, wv_ref)):
            part = firsts[j][:shard, at * width : (at + 1) * width] if at < 2 else seconds[j][:, :width]
            value = part.astype(F32)
            grad[:, cols] = value
            dots += jnp.sum(value * weight[:, cols].astype(F32), axis=1, keepdims=True)
        go_ref[:, cols] = seconds[j][:, width:].astype(F32)
        tiny += firsts[j][shard:, :].astype(F32)
    tiny_ref[...] = tiny
    attn_ref[...] = dots / gain_ref[...]


def finish(ids, n_ep, w_query, w_key, w_value, gain, firsts, seconds, after):
    shard, depth = w_query.shape
    extra = firsts[0].shape[0] - shard
    return call(
        functools.partial(finish_kernel, n_ep, len(firsts)),
        [like((shard, depth), F32)] * 4 + [like((extra, firsts[0].shape[1]), F32), like((shard, 1), F32)],
        [w_query, w_key, w_value, gain, *firsts, *seconds],
        shard * depth * 6,
        "finish",
        after=after,
        scalars=(ids,),
    )


def turn(values_in):
    return pltpu.roll(values_in, HEAD_DIM // 2, 1)


def masked_probs(q_ref, k_ref, start_ref, block, rows):
    first, last = block * rows, (block + 1) * rows
    scores = product_right(q_ref[first:last, :], k_ref[0:last, :]) * (HEAD_DIM ** (-0.5))
    row_ids = first + lax.broadcasted_iota(jnp.int32, scores.shape, 0)
    places = lax.broadcasted_iota(jnp.int32, scores.shape, 1)
    allowed = (places <= row_ids) & (places >= start_ref[first:last, :])
    scores = jnp.where(allowed, scores, NEG_FILL)
    top = jnp.max(scores, axis=1, keepdims=True)
    weights = jnp.exp(scores - top)
    return weights * (1.0 / jnp.sum(weights, axis=1, keepdims=True))


def attend_kernel(
    rows, qr_ref, kr_ref, v_ref, scale_ref, gq_ref, gk_ref, cos_ref, sin_ref, start_ref,
    q_ref, k_ref, out_ref,
):
    scales = jnp.transpose(scale_ref[...])
    for at, (raw, gain, low) in enumerate(((qr_ref, gq_ref, q_ref), (kr_ref, gk_ref, k_ref))):
        normed = raw[...] * scales[:, 8 * at : 8 * at + 1] * gain[...]
        low[...] = (normed * cos_ref[...] + turn(normed) * sin_ref[...]).astype(BF16)
    for block in range(q_ref.shape[0] // rows):
        probs = masked_probs(q_ref, k_ref, start_ref, block, rows)
        last = (block + 1) * rows
        out_ref[block * rows : last, :] = product(
            probs.astype(BF16), v_ref[0:last, :]
        ).astype(BF16)


def head_spec(rows):
    return pl.BlockSpec((rows, HEAD_DIM), lambda h: (0, h))


def attend(q_raw, k_raw, v_low, scales, q_gain, k_gain, cosine, sine, starts, after):
    total, width = v_low.shape
    heads = width // HEAD_DIM
    head, gain = head_spec(total), head_spec(1)
    return call(
        functools.partial(attend_kernel, min(256, total)),
        [like((total, width), BF16)] * 3,
        [q_raw, k_raw, v_low, scales, q_gain, k_gain, cosine, sine, starts],
        3 * heads * total * total * HEAD_DIM,
        "attend",
        after=after,
        grid=(heads,),
        in_specs=[head, head, head, None, gain, gain, None, None, None],
        out_specs=[head, head, head],
    )


def attend_back_kernel(
    rows, q_ref, k_ref, v_ref, do_ref, qr_ref, kr_ref, scale_ref, gq_ref, gk_ref,
    cos_ref, sin_ref, start_ref,
    dq_ref, dk_ref, dv_ref, sums_ref, dgq_ref, dgk_ref, q_acc, k_acc, v_acc,
):
    k_acc[...] = jnp.zeros_like(k_acc)
    v_acc[...] = jnp.zeros_like(v_acc)
    for block in range(q_ref.shape[0] // rows):
        first, last = block * rows, (block + 1) * rows
        probs = masked_probs(q_ref, k_ref, start_ref, block, rows)
        d_rows = do_ref[first:last, :]
        d_probs = product_right(d_rows, v_ref[0:last, :])
        delta = jnp.sum(probs * d_probs, axis=1, keepdims=True)
        d_scores = (probs * (d_probs - delta) * (HEAD_DIM ** (-0.5))).astype(BF16)
        q_acc[first:last, :] = product(d_scores, k_ref[0:last, :])
        k_acc[0:last, :] += product_left(d_scores, q_ref[first:last, :])
        v_acc[0:last, :] += product_left(probs.astype(BF16), d_rows)
    dv_ref[...] = v_acc[...].astype(BF16)

    @pl.when(pl.program_id(0) == 0)
    def _():
        sums_ref[...] = jnp.zeros_like(sums_ref)

    scales = jnp.transpose(scale_ref[...])
    for at, (acc, raw, gain, d_ref, dg_ref) in enumerate(
        ((q_acc, qr_ref, gq_ref, dq_ref, dgq_ref), (k_acc, kr_ref, gk_ref, dk_ref, dgk_ref))
    ):
        turned = acc[...].astype(BF16).astype(F32)
        back = turned * cos_ref[...] + turn(turned * sin_ref[...])
        normed = raw[...] * scales[:, 8 * at : 8 * at + 1]
        both = back * normed
        dg_ref[...] = jnp.sum(both, axis=0, keepdims=True)
        d_ref[...] = back * gain[...]
        sums_ref[8 * at : 8 * at + 8, :] += row_sums(both * gain[...])


def attend_back(
    q_rot, k_rot, v_low, d_heads, q_raw, k_raw, scales, q_gain, k_gain, cosine, sine, starts
):
    total, width = v_low.shape
    heads = width // HEAD_DIM
    head, gain = head_spec(total), head_spec(1)
    wide, thin = like((total, width), F32), like((1, width), F32)
    return call(
        functools.partial(attend_back_kernel, min(256, total)),
        [wide, wide, like((total, width), BF16), like((16, total), F32), thin, thin],
        [q_rot, k_rot, v_low, d_heads, q_raw, k_raw, scales, q_gain, k_gain, cosine, sine, starts],
        7 * heads * total * total * HEAD_DIM,
        "attend_back",
        scratch=[pltpu.VMEM((total, HEAD_DIM), F32)] * 3,
        grid=(heads,),
        in_specs=[head] * 6 + [None, gain, gain, None, None, None],
        out_specs=[head, head, head, None, gain, gain],
    )


def chooser(places_ref, at, cap):
    row = places_ref[at : at + 1, :]
    slots = lax.broadcasted_iota(jnp.int32, (cap, row.shape[1]), 0)
    return slots == row


def dispatch_kernel(
    pieces_here, local, cap, gated, mine, *refs
):
    pieces, refs = refs[:pieces_here], refs[pieces_here:]
    places_ref, refs = refs[0], refs[1:]
    if gated:
        (picked_ref, router_ref), refs = refs[:2], refs[2:]
        rows_ref, gate_ref, all_ref = refs[-3:]
    else:
        rows_ref = refs[-1]
    for p in range(pieces_here):
        if gated:
            logits = product_right(router_ref[...], pieces[p][...])
            experts = logits.shape[0]
            picked = picked_ref[p * experts : (p + 1) * experts, :] > 0
            logits = jnp.where(picked, logits, NEG_FILL)
            weights = jnp.exp(logits - jnp.max(logits, axis=0, keepdims=True))
            weights = jnp.where(picked, weights, 0.0)
            gates = weights / jnp.sum(weights, axis=0, keepdims=True)
            all_ref[p * experts : (p + 1) * experts, :] = gates
        for e in range(local):
            chosen = chooser(places_ref, p * local + e, cap)
            rows_ref[e, p * cap : (p + 1) * cap, :] = product(
                chosen.astype(BF16), pieces[p][...]
            ).astype(BF16)
            if gated:
                row = all_ref[pl.ds(p * experts + mine[0] * local + e, 1), :]
                gate_ref[e, p * cap : (p + 1) * cap, :] = jnp.sum(
                    jnp.where(chosen, row, 0.0), axis=1, keepdims=True
                )


def dispatch(mine, pieces, places, picked, router, local, cap, group, at, rows, gates, after=()):
    gated = router is not None
    here = len(pieces)
    width = pieces[0].shape[1]
    args = [*pieces, places]
    shapes = [like((local, group * cap, width), BF16)]
    spec = pl.BlockSpec((local, here * cap, width), lambda i, mine: (0, at, 0))
    out_specs = [spec]
    if gated:
        args += [picked, router]
        shapes += [like((local, group * cap, 1), F32), like((picked.shape[0], places.shape[1]), F32)]
        out_specs += [pl.BlockSpec((local, here * cap, 1), lambda i, mine: (0, at, 0)), None]
    in_specs = [None] * len(args)
    aliases = {}
    if rows is not None:
        aliases[len(args)] = 0
        args.append(rows)
        in_specs.append(pl.BlockSpec(memory_space=pl.ANY))
        if gated:
            aliases[len(args)] = 1
            args.append(gates)
            in_specs.append(pl.BlockSpec(memory_space=pl.ANY))
    return call(
        functools.partial(dispatch_kernel, here, local, cap, gated),
        shapes,
        args,
        2 * here * local * cap * places.shape[1] * width,
        "dispatch",
        scalars=(mine,),
        in_specs=in_specs,
        out_specs=out_specs,
        aliases=aliases,
        after=after,
    )


def expert_kernel(
    x_ref, d_ref, gate_ref, wg_ref, wu_ref, wd_ref,
    act_ref, dg_ref, du_ref, dots_ref, mix_ref, back_ref, mix_acc, back_acc,
):
    step = pl.program_id(1)
    last = pl.num_programs(1) - 1
    x_rows, d_rows, gate = x_ref[0], d_ref[0], gate_ref[0]
    pre = product(x_rows, wg_ref[0])
    up = product(x_rows, wu_ref[0])
    pulled = product_right(d_rows, wd_ref[0])
    sigma = jax.nn.sigmoid(pre)
    silu = pre * sigma
    act = silu * up
    dots = jnp.sum(act * pulled, axis=1, keepdims=True)
    act_low = (act * gate).astype(BF16)
    act_ref[0] = act_low
    d_act = pulled * gate
    du_low = (d_act * silu).astype(BF16)
    dg_low = (d_act * up * sigma * (1.0 + pre * (1.0 - sigma))).astype(BF16)
    dg_ref[0] = dg_low
    du_ref[0] = du_low
    mix = product(act_low, wd_ref[0])
    back = product_right(dg_low, wg_ref[0]) + product_right(du_low, wu_ref[0])

    @pl.when(step == 0)
    def _():
        dots_ref[0] = dots
        mix_acc[...] = mix
        back_acc[...] = back

    @pl.when((step > 0) & (step < last))
    def _():
        dots_ref[0] += dots
        mix_acc[...] += mix
        back_acc[...] += back

    @pl.when(step == last)
    def _():
        dots_ref[0] += dots
        mix_ref[0] = (mix_acc[...] + mix).astype(BF16)
        back_ref[0] = (back_acc[...] + back).astype(BF16)


def experts(rows, d_rows, gates, w_gate, w_up, w_down, after=()):
    local, count, width = rows.shape
    hidden = w_gate.shape[2]
    part = hidden // 2
    wide = pl.BlockSpec((1, count, width), lambda e, f: (e, 0, 0))
    column = pl.BlockSpec((1, count, 1), lambda e, f: (e, 0, 0))
    thin = pl.BlockSpec((1, count, part), lambda e, f: (e, 0, f))
    into = pl.BlockSpec((1, width, part), lambda e, f: (e, 0, f))
    outof = pl.BlockSpec((1, part, width), lambda e, f: (e, f, 0))
    return call(
        expert_kernel,
        [like((local, count, hidden), BF16)] * 3
        + [like((local, count, 1), F32)]
        + [like((local, count, width), BF16)] * 2,
        [rows, d_rows, gates, w_gate, w_up, w_down],
        12 * rows.size * hidden,
        "experts",
        after=after,
        scratch=[pltpu.VMEM((count, width), F32)] * 2,
        grid=(local, 2),
        in_specs=[wide, wide, column, into, into, outof],
        out_specs=[thin, thin, thin, column, wide, wide],
    )


def combine_kernel(here, local, cap, dotted, places_ref, rows_ref, *refs):
    pieces = refs[int(dotted) : int(dotted) + here]
    for p in range(here):
        chosen = [chooser(places_ref, p * local + e, cap) for e in range(local)]
        total = None
        for e in range(local):
            part = product_left(chosen[e].astype(BF16), rows_ref[e, p * cap : (p + 1) * cap, :])
            total = part if total is None else total + part
            if dotted:
                refs[-1][p * local + e : p * local + e + 1, :] = jnp.sum(
                    jnp.where(chosen[e], refs[0][e, p * cap : (p + 1) * cap, :], 0.0),
                    axis=0, keepdims=True,
                )
        pieces[p][...] = total.astype(BF16)


def combine(places, rows, here, local, cap, at, dots=None, after=()):
    width = rows.shape[2]
    tokens = places.shape[1]
    dotted = dots is not None
    args = [places, rows] + ([dots] if dotted else [])
    in_specs = [None, pl.BlockSpec((local, here * cap, width), lambda i: (0, at, 0))]
    if dotted:
        in_specs.append(pl.BlockSpec((local, here * cap, 1), lambda i: (0, at, 0)))
    shapes = [like((tokens, width), BF16)] * here
    if dotted:
        shapes.append(like(places.shape, F32))
    return call(
        functools.partial(combine_kernel, here, local, cap, dotted),
        shapes,
        args,
        2 * here * local * cap * tokens * width,
        "combine",
        after=after,
        in_specs=in_specs,
    )


def combine_stacks_kernel(count, local, cap, group, places_ref, *refs):
    groups = count // group
    for k in range(count):
        rows = refs[k // group]
        at = (k % group) * cap
        total = None
        for e in range(local):
            chosen = chooser(places_ref, k * local + e, cap).astype(BF16)
            part = product_left(chosen, rows[e, at : at + cap, :])
            total = part if total is None else total + part
        array, place = stack_at(k, count)
        refs[groups + array][place] = total.astype(BF16)


def combine_stacks(places, rows, count, local, cap, group, after):
    tokens, width = places.shape[1], rows[0].shape[2]
    return call(
        functools.partial(combine_stacks_kernel, count, local, cap, group),
        stack_shapes(count, (tokens, width)),
        [places, *rows],
        2 * count * local * cap * tokens * width,
        "combine_stacks",
        after=after,
    )


def weight_grad_kernel(groups, *refs):
    lefts, rights = refs[:groups], refs[groups : 2 * groups]
    total = None
    for left, right in zip(lefts, rights):
        part = product_left(left[0], right[0])
        total = part if total is None else total + part
    refs[-1][0] = total.astype(BF16)


def weight_grad(lefts, rights, after=()):
    local, count, tall = lefts[0].shape
    wide = rights[0].shape[2]
    part = min(512, tall)
    left = pl.BlockSpec((1, count, part), lambda e, i: (e, 0, i))
    right = pl.BlockSpec((1, count, wide), lambda e, i: (e, 0, 0))
    return call(
        functools.partial(weight_grad_kernel, len(lefts)),
        like((local, tall, wide), BF16),
        [*lefts, *rights],
        2 * len(lefts) * lefts[0].size * wide,
        "weight_grad",
        after=after,
        grid=(local, tall // part),
        in_specs=[left] * len(lefts) + [right] * len(lefts),
        out_specs=[pl.BlockSpec((1, part, wide), lambda e, i: (e, i, 0))],
    )


def body(
    tokens, doc_lengths, routes, attn_gain, w_query, w_key, w_value, q_gain, k_gain, w_out,
    ffn_gain, w_router, w_gate, w_up, w_down, cotangent,
):
    n_sp = lax.axis_size("sp")
    n_ep = lax.axis_size("ep")
    sp_index = lax.axis_index("sp")
    ep_index = lax.axis_index("ep")
    tok_dev, width = tokens.shape[1:]
    total = tok_dev * n_sp
    shard = width // n_ep
    head_width = width // n_sp
    top_count = routes.shape[2]
    local = w_gate.shape[0]
    expert_count = local * n_ep
    capacity = 9 * tok_dev * top_count // (8 * expert_count)
    cap = -(-capacity // 16) * 16
    group = 4
    blocks = piece_blocks(n_ep, ep_index)
    partners = jnp.bitwise_xor(jnp.arange(n_sp, dtype=jnp.int32), sp_index)
    ids = jnp.concatenate([blocks, partners]).astype(jnp.int32)
    mine = ep_index.astype(jnp.int32).reshape(1)

    def own_columns(value):
        return lax.dynamic_slice_in_dim(value, sp_index * head_width, head_width, 1)

    def by_piece(value):
        return jnp.stack(
            [lax.dynamic_index_in_dim(value, blocks[i], 0, keepdims=False) for i in range(n_ep)]
        )

    expert_ids = jnp.arange(expert_count, dtype=jnp.int32)
    picked = jnp.any(routes[0][:, :, None] == expert_ids[None, None, :], axis=1)
    picked_low = picked.T.astype(BF16)
    small = jnp.concatenate(
        [
            jnp.stack([attn_gain, q_gain, k_gain, ffn_gain]),
            jnp.zeros((12, shard), BF16),
            w_router.T,
        ],
        axis=0,
    )

    def to_all(value):
        value = jnp.broadcast_to(value[None], (n_ep, *value.shape))
        return lax.all_to_all(value, "ep", split_axis=0, concat_axis=0, tiled=True)

    if shard == tok_dev:
        both = to_all(jnp.concatenate([small, picked_low], axis=0))
        small_all, picked_all = both[:, : 16 + expert_count], both[:, 16 + expert_count :]
    else:
        small_all, picked_all = to_all(small), to_all(picked_low)
    small_rows = jnp.swapaxes(small_all, 0, 1).reshape(16 + expert_count, width)
    gains = small_rows[:4].astype(F32)
    full_router = small_rows[16:]
    picked_all = by_piece(picked_all)

    x_all = lax.all_gather(tokens[0], "sp", axis=0, tiled=True)
    w_own = jnp.concatenate([own_columns(w) for w in (w_query, w_key, w_value, w_out)], axis=1)
    cot_own = cotangent[0]
    if n_ep == 8:
        w_pieces = gather_line(w_own)
        w_pieces[6], cot_own = tie(w_pieces[6], cot_own)
        cot_pieces, w_pieces[7] = gather_double(cot_own, w_pieces[7])
    else:
        w_pieces, cot_pieces = gather_whole(w_own), gather_whole(cot_own)

    upper = (
        jnp.arange(tok_dev, dtype=jnp.int32)[:, None] < jnp.arange(tok_dev, dtype=jnp.int32)[None, :]
    ).astype(BF16)
    picked_mine = lax.dynamic_slice_in_dim(picked_all, ep_index * local, local, 1)
    picked_mine = picked_mine.reshape(n_ep * local, tok_dev)
    earlier = product(picked_mine, upper).astype(jnp.int32)
    places = jnp.where((picked_mine > 0) & (earlier < capacity), earlier, -1)
    picked_flat = picked_all.reshape(n_ep * expert_count, tok_dev).astype(F32)

    positions = jnp.arange(total, dtype=jnp.int32)
    lengths = doc_lengths[0]
    doc_ends = jnp.cumsum(lengths)
    starts = jnp.sum(
        jnp.where(doc_ends[None, :] <= positions[:, None], lengths[None, :], 0), axis=1
    )
    half = HEAD_DIM // 2
    frequency = THETA ** (-(2.0 * jnp.arange(half, dtype=F32)) / HEAD_DIM)
    angles = (positions - starts).astype(F32)[:, None] * frequency[None, :]
    cosine = jnp.concatenate([jnp.cos(angles), jnp.cos(angles)], axis=1)
    sine = jnp.concatenate([-jnp.sin(angles), jnp.sin(angles)], axis=1)
    starts = starts[:, None].astype(jnp.int32)

    w_o = [
        jnp.concatenate([piece[:, 3 * head_width :] for piece in half])
        for half in (w_pieces[: n_ep // 2], w_pieces[n_ep // 2 :])
    ]
    w_o_over = [swap_sp(half, 2) for half in w_o]
    q_raw, k_raw, v_low, squares, w_qkv, h_all = qkv_project(
        ids, x_all, gains[0:1], w_pieces, [places, picked_flat]
    )
    scales = lax.rsqrt(sum_sp(squares) / width + EPS)
    gain_q, gain_k = own_columns(gains)[1:2], own_columns(gains)[2:3]
    q_rot, k_rot, mixed = attend(
        q_raw, k_raw, v_low, scales, gain_q, gain_k, cosine, sine, starts,
        [w_o_over[0]] + [cot_pieces[k] for k in ((1, 2, 4) if n_ep == 8 else ())],
    )

    def pair_places(p):
        return places[p * local : (p + 2) * local]

    def cot_rows(g, after):
        d_rows = None
        for at, p in enumerate(range(g, g + group, 2)):
            (d_rows,) = dispatch(
                mine, cot_pieces[p : p + 2], pair_places(p), None, None, local, cap, group, at,
                d_rows, None, after,
            )
        return d_rows

    if n_ep == 8:
        cot_pieces[3], cot_pieces[6], w_o_over[1], mixed = tie(
            cot_pieces[3], cot_pieces[6], w_o_over[1], mixed
        )
    attn_tok = lax.all_to_all(mixed, "sp", split_axis=0, concat_axis=1, tiled=True)
    w_o_parts = (
        w_o + [swap_sp(half, 1) for half in w_o] + w_o_over + [swap_sp(half, 1) for half in w_o_over]
    )
    if n_ep == 8:
        cot_pieces[5], attn_tok = tie(cot_pieces[5], attn_tok)
    x_one, h2_low = out_project(
        ids, n_ep, attn_tok, tokens[0], gains[3:4], w_o_parts
    )
    attn_all = lax.all_gather(attn_tok, "sp", axis=0, tiled=True)

    h2_pieces = gather(h2_low, n_ep)
    cots = [cot_rows(g, [x_one]) for g in range(0, n_ep, group)]
    groups, d_pieces, d_gates, d_sums = [], [], [], []
    home_gates = None

    def rows_of(g, after):
        rows = gates = first_gates = None
        for at, p in enumerate(range(g, g + group, 2)):
            rows, gates, piece_gates = dispatch(
                mine, h2_pieces[p : p + 2], pair_places(p),
                picked_flat[p * expert_count : (p + 2) * expert_count], full_router, local, cap,
                group, at, rows, gates, after,
            )
            first_gates = piece_gates if first_gates is None else first_gates
        return rows, gates, first_gates

    rows, gates, home_gates = rows_of(0, [])
    for g in range(0, n_ep, group):
        d_rows = cots[g // group]
        made = experts(rows, d_rows, gates, w_gate, w_up, w_down, d_pieces[-group:] + cots + h2_pieces[4:7:2])
        groups.append((rows, d_rows, made))
        following = []
        if g + group < n_ep:
            rows, gates, _ = rows_of(g + group, [made[5]])
            following = [rows]
        sums_before = list(d_sums)
        for at in range(group // 2):
            *two, dots = combine(
                pair_places(g + 2 * at), made[5], 2, local, cap, at, made[3],
                sums_before + following,
            )
            d_pieces += two
            d_gates.append(dots)
        if n_ep == 8:
            d_sums += crossed_sums(d_pieces[-group:])

    acts = [made[0] for _, _, made in groups]
    d_gate_rows = [made[1] for _, _, made in groups]
    d_up_rows = [made[2] for _, _, made in groups]
    ins = [rows for rows, _, _ in groups]
    outs = [d_rows for _, d_rows, _ in groups]
    d_gates = by_piece(jnp.concatenate(d_gates, axis=0).reshape(n_ep, local, tok_dev))
    d_gates = lax.all_to_all(d_gates, "ep", split_axis=0, concat_axis=0, tiled=True)
    d_gates = d_gates.reshape(expert_count, tok_dev)
    mix_stacks = combine_stacks(
        places, [made[4] for _, _, made in groups], n_ep, local, cap, group, d_pieces
    )
    grad_down = weight_grad(acts, outs, mix_stacks[:1])
    if n_ep == 8:
        d_sums[2], mix_stacks[2], mix_stacks[3], grad_down = tie(
            d_sums[2], mix_stacks[2], mix_stacks[3], grad_down
        )
        d_h2, d_far = scatter_z(*d_sums)
        d_last = [d_far]
    else:
        d_h2, d_last = scatter(d_pieces, n_ep), []
    grad_gate = weight_grad(ins, d_gate_rows, [grad_down, d_gates, *d_last])
    grad_up = weight_grad(ins, d_up_rows, [grad_gate])

    def over_sp(value):
        return lax.psum_scatter(value, "sp", scatter_dimension=1, tiled=True).astype(F32)


    if n_ep == 8:
        gates_here = home_gates[:expert_count]
    else:
        logits = product_right(full_router, h2_low)
        logits = jnp.where(picked.T, logits, NEG_FILL)
        gates_here = jax.nn.softmax(logits, axis=0)
    d_logits = gates_here * (d_gates - jnp.sum(gates_here * d_gates, axis=0, keepdims=True))
    d_logits = jnp.where(picked.T, d_logits, 0.0).astype(BF16)
    grad_router = product(d_logits, h2_low)
    d_h2 = d_h2 + product_left(d_logits, full_router)
    one_scale = lax.rsqrt(jnp.mean(x_one * x_one, axis=-1, keepdims=True) + EPS)
    one_normed = x_one * one_scale
    grad_ffn = jnp.sum(d_h2 * one_normed, axis=0)
    d_normed = d_h2 * gains[3][None, :]
    d_one = cotangent[0].astype(F32) + one_scale * (
        d_normed - one_normed * jnp.mean(d_normed * one_normed, axis=-1, keepdims=True)
    )
    d_z, grad_up = tie(d_one.astype(BF16), grad_up)
    d_attn = out_back(ids, n_ep, d_z, w_o_parts)
    d_heads = lax.all_to_all(d_attn, "sp", split_axis=1, concat_axis=0, tiled=True)
    d_z_cols = lax.all_to_all(d_z, "sp", split_axis=1, concat_axis=0, tiled=True)
    mix, mix_far = scatter_stacks(mix_stacks, n_ep)
    if n_ep == 8:
        mix, mix_far, d_heads = tie(mix, mix_far, d_heads)
    grad_down, grad_gate, grad_up = over_sp(grad_down), over_sp(grad_gate), over_sp(grad_up)

    d_qn, d_kn, d_v, sums, grad_qg, grad_kg = attend_back(
        q_rot, k_rot, v_low, d_heads, q_raw, k_raw, scales, gain_q, gain_k, cosine, sine, starts
    )
    output = (x_one + last_hop(mix, mix_far)).astype(BF16)
    vo_stacks = vo_grads(ids, n_ep, h_all, d_v, attn_all, d_z_cols)

    grad_vo = last_hop(*scatter_stacks(vo_stacks, n_ep)).astype(BF16)

    def placed(value):
        return lax.dynamic_update_slice_in_dim(
            jnp.zeros((1, width), F32), value, sp_index * head_width, 1
        )

    tiny = jnp.concatenate(
        [placed(grad_qg), placed(grad_kg), grad_ffn[None], grad_router], axis=0
    )
    *qk_stacks, d_qk = qk_back(
        ids, n_ep, h_all, d_qn, d_kn, q_raw, k_raw, scales, sum_sp_swaps(sums), tiny, vo_stacks[:1]
    )
    grad_qk = last_hop(*scatter_stacks(qk_stacks, n_ep)).astype(BF16)

    d_h = d_h_rows(ids, n_ep, n_sp, d_qk, d_v, w_qkv, [])
    output, d_h = tie(output, d_h)
    halves = plus(d_h[:2], swap_sp(d_h[2:], 1))
    d_h = halves[0].astype(F32) + swap_sp(halves[1], 2).astype(F32)
    x_rows = tokens[0].astype(F32)
    x_scale = lax.rsqrt(jnp.mean(x_rows * x_rows, axis=-1, keepdims=True) + EPS)
    x_normed = x_rows * x_scale
    d_normed = d_h * gains[0][None, :]
    input_grad = d_one + x_scale * (
        d_normed - x_normed * jnp.mean(d_normed * x_normed, axis=-1, keepdims=True)
    )

    g_query, g_key, g_value, g_out, tiny, g_attn = finish(
        ids, n_ep, w_query, w_key, w_value, attn_gain.astype(F32)[:, None],
        gather_sp(grad_qk), gather_sp(grad_vo), [grad_down, grad_gate, grad_up],
    )
    per_row = 2 * head_width // shard

    def vector(at):
        col = (at % per_row) * shard
        return tiny[at // per_row, col : col + shard]

    g_router = jnp.stack([vector(3 + i) for i in range(expert_count)], axis=1)
    return (
        output[None], input_grad[None], g_attn[:, 0], g_query, g_key, g_value, vector(0), vector(1),
        g_out, vector(2), g_router, grad_gate, grad_up, grad_down,
    )


def solution(mesh):
    seq = P("ep", "sp", None)
    vec = P("ep")
    mat = P("ep", None)
    expert = P("ep", None, None)
    in_specs = (
        seq, mat, seq, vec, mat, mat, mat, vec, vec, mat, vec, mat, expert, expert, expert, seq,
    )
    out_specs = (
        seq, seq, vec, mat, mat, mat, vec, vec, mat, vec, mat, seq, seq, seq,
    )
    return jax.shard_map(body, mesh=mesh, in_specs=in_specs, out_specs=out_specs, check_vma=False)
```

```python
import functools

import jax
import jax.numpy as jnp
from jax import lax
from jax.experimental import pallas as pl
from jax.experimental.pallas import tpu as pltpu
from jax.sharding import PartitionSpec as P

HEAD_DIM = 128
EPS = 1e-05
THETA = 10000.0
NEG_FILL = -1e30
F32 = jnp.float32
BF16 = jnp.bfloat16
MIB = 1 << 20
COVER = 20


def product(left, right):
    return jnp.dot(left, right, preferred_element_type=F32)


def product_left(left, right):
    return lax.dot_general(left, right, (((0,), (0,)), ((), ())), preferred_element_type=F32)


def product_right(left, right):
    return lax.dot_general(left, right, (((1,), (1,)), ((), ())), preferred_element_type=F32)


def row_sums(values_in):
    sums = jnp.sum(values_in, axis=1, keepdims=True)
    return jnp.transpose(jnp.broadcast_to(sums, (sums.shape[0], HEAD_DIM)))[:8]


def call(kernel, out_shape, args, flops, name, scratch=(), scalars=(), grid=(1,), in_specs=None,
         out_specs=None, aliases=None, vmem=60, after=()):
    single = not isinstance(out_shape, (list, tuple))
    shapes = [out_shape] if single else list(out_shape)
    count = len(grid)

    def fixed(shape):
        rank = len(shape)
        return pl.BlockSpec(tuple(shape), lambda *ids: (0,) * rank)

    in_specs = in_specs or [None] * len(args)
    out_specs = out_specs or [None] * len(shapes)
    in_specs = [s if s is not None else fixed(a.shape) for s, a in zip(in_specs, args)]
    out_specs = [s if s is not None else fixed(o.shape) for s, o in zip(out_specs, shapes)]
    waited = len(after)
    args = [*args, *after]
    in_specs = in_specs + [pl.BlockSpec(memory_space=pl.ANY)] * waited
    if waited:
        inner, first = kernel, len(scalars) + len(args) - waited

        def kernel(*refs):
            inner(*refs[:first], *refs[first + waited :])

    moved = sum(a.size * a.dtype.itemsize for a in args[: len(args) - waited])
    moved += sum(o.size * o.dtype.itemsize for o in shapes)
    result = pl.pallas_call(
        kernel,
        grid_spec=pltpu.PrefetchScalarGridSpec(
            num_scalar_prefetch=len(scalars), grid=grid, in_specs=in_specs, out_specs=out_specs,
            scratch_shapes=list(scratch),
        ),
        out_shape=shapes,
        input_output_aliases={k + len(scalars): v for k, v in (aliases or {}).items()},
        compiler_params=pltpu.CompilerParams(
            vmem_limit_bytes=vmem * MIB, dimension_semantics=("arbitrary",) * count
        ),
        cost_estimate=pl.CostEstimate(flops=int(COVER * flops), bytes_accessed=int(moved), transcendentals=0),
        name=name,
    )(*scalars, *args)
    return result[0] if single else list(result)


def like(shape, dtype):
    return jax.ShapeDtypeStruct(tuple(shape), dtype)


def tie(*values):
    return lax.optimization_barrier(values)


def swap(value, bits):
    return lax.ppermute(value, "ep", [(i, i ^ bits) for i in range(8)])


def swap_sp(value, bits):
    return lax.ppermute(value, "sp", [(i, i ^ bits) for i in range(4)])


def piece_blocks(n_ep, ep_index):
    ids = jnp.arange(n_ep, dtype=jnp.int32)
    return jnp.bitwise_xor(ids, ep_index) if n_ep == 8 else ids


MIDDLE = [(2, 4), (3, 5), (4, 2), (5, 3)]
OUTWARD = [(2, 0), (3, 1), (4, 6), (5, 7)]


def gather_line(value):
    crossed = swap(value, 1)
    near = swap(value, 2)
    inner = lax.ppermute(value, "ep", MIDDLE)
    near_x, outer = swap(near, 1), lax.ppermute(near, "ep", MIDDLE)
    near_x, crossed, outer = tie(near_x, crossed, outer)
    far = outer + lax.ppermute(inner, "ep", OUTWARD)
    farther = inner + lax.ppermute(outer, "ep", OUTWARD)
    return [value, crossed, near, near_x, far, swap(far, 1), farther, swap(farther, 1)]


def gather_double(value, after):
    after, held = tie(after, value)
    crossed = swap(held, 1)
    near, far = swap(value, 2), swap(value, 4)
    farther = swap(far, 2)
    near_x, held = tie(swap(near, 1), far)
    return [
        value, crossed, near, near_x, far, swap(held, 1), farther, swap(farther, 1)
    ], after


def gather_whole(value):
    whole = lax.all_gather(value, "ep", axis=0, tiled=False)
    return [whole[i] for i in range(whole.shape[0])]


def gather(value, n_ep):
    return gather_line(value) if n_ep == 8 else gather_whole(value)


def plus(left, right):
    return (left.astype(F32) + right.astype(F32)).astype(left.dtype)


def crossed_sums(pieces):
    return [plus(pieces[i], swap(pieces[i + 1], 1)) for i in range(0, len(pieces), 2)]


def scatter_z(own, near, far, farther):
    far = plus(far, swap(farther, 2))
    far, near = tie(far, near)
    return own.astype(F32) + swap(near, 2).astype(F32) + swap(far, 4).astype(F32), far


def scatter(pieces, n_ep):
    if n_ep != 8:
        stacked = jnp.stack(pieces)
        return lax.psum_scatter(stacked, "ep", scatter_dimension=0, tiled=False).astype(F32)
    return scatter_z(*crossed_sums(pieces))[0]


def stack_at(piece, n_ep):
    if n_ep != 8:
        return 0, piece
    return 2 * (piece % 2) + (piece // 2) % 2, piece // 4


def stack_shapes(n_ep, shape):
    return [like((2, *shape), BF16)] * 4 if n_ep == 8 else [like((n_ep, *shape), BF16)]


def odd_sums(stacks):
    return plus(stacks[1], swap(stacks[3], 1))


def even_sums(stacks, odd):
    even = stacks[0].astype(F32) + swap(stacks[2], 1).astype(F32) + swap(odd, 2).astype(F32)
    return even[0], even[1].astype(BF16)


def scatter_stacks(stacks, n_ep):
    if n_ep != 8:
        total = lax.psum_scatter(stacks[0], "ep", scatter_dimension=0, tiled=False)
        return total.astype(F32), None
    return even_sums(stacks, odd_sums(stacks))


def last_hop(total, far):
    return total if far is None else total + swap(far, 4).astype(F32)


def gather_sp(value):
    over = swap_sp(value, 2)
    return [value, swap_sp(value, 1), over, swap_sp(over, 1)]


def sum_sp(value):
    n_sp = lax.axis_size("sp")
    value = jnp.broadcast_to(value[None], (n_sp, *value.shape))
    return jnp.sum(lax.all_to_all(value, "sp", split_axis=0, concat_axis=0, tiled=True), axis=0)


def sum_sp_swaps(value):
    return (value + swap_sp(value, 1)) + (swap_sp(value, 2) + swap_sp(value, 3))


def block_at(ids, position, size):
    if size % HEAD_DIM:
        return pl.ds(position * size, size)
    return pl.ds(pl.multiple_of(ids[position] * size, size), size)


def qkv_kernel(count, ids, x_ref, gain_ref, *refs):
    pieces, refs = refs[:count], refs[count:]
    q_ref, k_ref, v_ref, squares_ref, w_ref, h_ref = refs
    shard = pieces[0].shape[0]
    width = q_ref.shape[1]

    @pl.when(pl.program_id(0) == 0)
    def _():
        for k in range(count):
            rows = block_at(ids, k, shard)
            w_ref[rows, :] = pieces[k][:, : 3 * width]

    x_rows = x_ref[...].astype(F32)
    scale = lax.rsqrt(jnp.mean(x_rows * x_rows, axis=1, keepdims=True) + EPS)
    h_ref[...] = (x_rows * scale * gain_ref[...]).astype(BF16)
    for at, ref in enumerate((q_ref, k_ref)):
        part = product(h_ref[...], w_ref[:, at * width : (at + 1) * width])
        ref[...] = part
        squares_ref[8 * at : 8 * at + 8, :] = row_sums(part * part)
    v_ref[...] = product(h_ref[...], w_ref[:, 2 * width :]).astype(BF16)


def qkv_project(ids, x_all, gain, pieces, after):
    total, depth = x_all.shape
    width = pieces[0].shape[1] // 4
    rows = min(256, total)
    block = pl.BlockSpec((rows, width), lambda i, ids: (i, 0))
    wide = pl.BlockSpec((rows, depth), lambda i, ids: (i, 0))
    return call(
        functools.partial(qkv_kernel, len(pieces)),
        [like((total, width), F32)] * 2
        + [like((total, width), BF16), like((16, total), F32), like((depth, 3 * width), BF16)]
        + [like((total, depth), BF16)],
        [x_all, gain, *pieces],
        6 * total * depth * width,
        "qkv_project",
        after=after,
        scalars=(ids,),
        grid=(total // rows,),
        in_specs=[wide] + [None] * (len(pieces) + 1),
        out_specs=[
            block, block, block, pl.BlockSpec((16, rows), lambda i, ids: (0, i)), None, wide,
        ],
    )


def out_kernel(n_ep, n_sp, ids, attn_ref, x_ref, gain_ref, *refs):
    weights, (one_ref, low_ref, turned_ref) = refs[: 2 * n_sp], refs[2 * n_sp :]
    rows, width = weights[0].shape
    shard = 2 * rows // n_ep
    for k in range(n_ep):
        turned_ref[:, k * shard : (k + 1) * shard] = attn_ref[:, block_at(ids, k, shard)]
    for j in range(n_sp):
        cols = block_at(ids, n_ep + j, width)
        one_ref[:, cols] = (
            x_ref[:, cols].astype(F32)
            + product(turned_ref[:, :rows], weights[2 * j][...])
            + product(turned_ref[:, rows:], weights[2 * j + 1][...])
        )
    one = one_ref[...]
    scale = lax.rsqrt(jnp.mean(one * one, axis=1, keepdims=True) + EPS)
    low_ref[...] = (one * scale * gain_ref[...]).astype(BF16)


def out_project(ids, n_ep, attn_tok, tokens, gain, weights):
    return call(
        functools.partial(out_kernel, n_ep, len(weights) // 2),
        [like(tokens.shape, F32), like(tokens.shape, BF16)],
        [attn_tok, tokens, gain, *weights],
        2 * tokens.size * attn_tok.shape[1],
        "out_project",
        scratch=[pltpu.VMEM(attn_tok.shape, BF16)],
        scalars=(ids,),
    )


def out_back_kernel(n_ep, n_sp, ids, d_ref, *refs):
    weights, d_attn_ref = refs[:-1], refs[-1]
    rows, width = weights[0].shape
    shard = 2 * rows // n_ep
    for half in range(2):
        total = None
        for j in range(n_sp):
            part = product_right(
                d_ref[:, block_at(ids, n_ep + j, width)], weights[2 * j + half][...]
            )
            total = part if total is None else total + part
        total = total.astype(BF16)
        for k in range(n_ep // 2):
            block = block_at(ids, half * (n_ep // 2) + k, shard)
            d_attn_ref[:, block] = total[:, k * shard : (k + 1) * shard]


def out_back(ids, n_ep, d_z, weights):
    return call(
        functools.partial(out_back_kernel, n_ep, len(weights) // 2),
        like((d_z.shape[0], 2 * weights[0].shape[0]), BF16),
        [d_z, *weights],
        2 * d_z.size * weights[0].shape[0] * 2,
        "out_back",
        scalars=(ids,),
    )


def vo_grads_kernel(count, shard, ids, h_ref, dv_ref, attn_ref, dz_ref, *stacks):
    width = dv_ref.shape[1]
    for k in range(count):
        block = block_at(ids, k, shard)
        array, place = stack_at(k, count)
        stacks[array][place, :, :width] = product_left(h_ref[:, block], dv_ref[...]).astype(BF16)
        stacks[array][place, :, width:] = product_left(attn_ref[:, block], dz_ref[...]).astype(BF16)


def vo_grads(ids, count, h_all, d_v, attn_all, d_z_cols):
    shard = h_all.shape[1] // count
    width = d_v.shape[1]
    return call(
        functools.partial(vo_grads_kernel, count, shard),
        stack_shapes(count, (shard, 2 * width)),
        [h_all, d_v, attn_all, d_z_cols],
        4 * h_all.size * width,
        "vo_grads",
        scalars=(ids,),
    )


def qk_back_kernel(
    count, shard, ids, h_ref, dqn_ref, dkn_ref, qr_ref, kr_ref, scale_ref, sums_ref, tiny_ref, *refs
):
    stacks, d_ref = refs[:-1], refs[-1]
    width = dqn_ref.shape[1]
    scales = jnp.transpose(scale_ref[...])
    means = jnp.transpose(sums_ref[...]) * (1.0 / h_ref.shape[1])
    for at, (d_normed, raw) in enumerate(((dqn_ref, qr_ref), (dkn_ref, kr_ref))):
        scale, mean = scales[:, 8 * at : 8 * at + 1], means[:, 8 * at : 8 * at + 1]
        d_ref[:, at * width : (at + 1) * width] = (
            scale * (d_normed[...] - raw[...] * scale * mean)
        ).astype(BF16)
    per_row = 2 * width // shard
    extra = stacks[0].shape[1] - shard
    for k in range(count):
        block = block_at(ids, k, shard)
        array, place = stack_at(k, count)
        ref = stacks[array]
        ref[place, :shard, :] = product_left(h_ref[:, block], d_ref[...]).astype(BF16)
        ref[place, shard:, :] = jnp.zeros((extra, 2 * width), BF16)
        for at in range(tiny_ref.shape[0]):
            row, col = shard + at // per_row, (at % per_row) * shard
            ref[place, row : row + 1, col : col + shard] = tiny_ref[at : at + 1, block].astype(BF16)


def qk_back(ids, count, h_all, d_qn, d_kn, q_raw, k_raw, scales, sums, tiny, after):
    total, depth = h_all.shape
    width = d_qn.shape[1]
    shard = depth // count
    extra = -(-tiny.shape[0] // (2 * width // shard))
    extra = -(-extra // 16) * 16
    return call(
        functools.partial(qk_back_kernel, count, shard),
        stack_shapes(count, (shard + extra, 2 * width)) + [like((total, 2 * width), BF16)],
        [h_all, d_qn, d_kn, q_raw, k_raw, scales, sums, tiny],
        2 * h_all.size * 2 * width,
        "qk_back",
        scalars=(ids,),
        after=after,
    )


def d_h_kernel(ids, d_ref, dv_ref, w_ref, out_ref):
    both = d_ref.shape[1]
    out_ref[0] = (
        product_right(d_ref[...], w_ref[:, :both]) + product_right(dv_ref[...], w_ref[:, both:])
    ).astype(BF16)


def d_h_rows(ids, n_ep, n_sp, d_qk, d_v, w_qkv, after):
    total, wide = d_qk.shape
    depth = w_qkv.shape[0]
    rows = total // n_sp

    def partner(j, ids):
        return ids[n_ep + (j % 2) * 2 + j // 2], 0

    return call(
        d_h_kernel,
        like((n_sp, rows, depth), BF16),
        [d_qk, d_v, w_qkv],
        3 * d_qk.size * depth,
        "d_h",
        after=after,
        scalars=(ids,),
        grid=(n_sp,),
        in_specs=[
            pl.BlockSpec((rows, wide), partner), pl.BlockSpec((rows, d_v.shape[1]), partner), None,
        ],
        out_specs=[pl.BlockSpec((1, rows, depth), lambda j, ids: (j, 0, 0))],
    )


def finish_kernel(n_ep, n_sp, ids, wq_ref, wk_ref, wv_ref, gain_ref, *refs):
    firsts, seconds = refs[:n_sp], refs[n_sp : 2 * n_sp]
    gq_ref, gk_ref, gv_ref, go_ref, tiny_ref, attn_ref = refs[2 * n_sp :]
    shard = wq_ref.shape[0]
    width = firsts[0].shape[1] // 2
    dots = jnp.zeros((shard, 1), F32)
    tiny = jnp.zeros(tiny_ref.shape, F32)
    for j in range(n_sp):
        cols = block_at(ids, n_ep + j, width)
        for at, grad, weight in ((0, gq_ref, wq_ref), (1, gk_ref, wk_ref), (2, gv_ref, wv_ref)):
            part = firsts[j][:shard, at * width : (at + 1) * width] if at < 2 else seconds[j][:, :width]
            value = part.astype(F32)
            grad[:, cols] = value
            dots += jnp.sum(value * weight[:, cols].astype(F32), axis=1, keepdims=True)
        go_ref[:, cols] = seconds[j][:, width:].astype(F32)
        tiny += firsts[j][shard:, :].astype(F32)
    tiny_ref[...] = tiny
    attn_ref[...] = dots / gain_ref[...]


def finish(ids, n_ep, w_query, w_key, w_value, gain, firsts, seconds, after):
    shard, depth = w_query.shape
    extra = firsts[0].shape[0] - shard
    return call(
        functools.partial(finish_kernel, n_ep, len(firsts)),
        [like((shard, depth), F32)] * 4 + [like((extra, firsts[0].shape[1]), F32), like((shard, 1), F32)],
        [w_query, w_key, w_value, gain, *firsts, *seconds],
        shard * depth * 6,
        "finish",
        after=after,
        scalars=(ids,),
    )


def turn(values_in):
    return pltpu.roll(values_in, HEAD_DIM // 2, 1)


def masked_probs(q_ref, k_ref, start_ref, block, rows):
    first, last = block * rows, (block + 1) * rows
    scores = product_right(q_ref[first:last, :], k_ref[0:last, :]) * (HEAD_DIM ** (-0.5))
    row_ids = first + lax.broadcasted_iota(jnp.int32, scores.shape, 0)
    places = lax.broadcasted_iota(jnp.int32, scores.shape, 1)
    allowed = (places <= row_ids) & (places >= start_ref[first:last, :])
    scores = jnp.where(allowed, scores, NEG_FILL)
    top = jnp.max(scores, axis=1, keepdims=True)
    weights = jnp.exp(scores - top)
    return weights * (1.0 / jnp.sum(weights, axis=1, keepdims=True))


def attend_kernel(
    rows, qr_ref, kr_ref, v_ref, scale_ref, gq_ref, gk_ref, cos_ref, sin_ref, start_ref,
    q_ref, k_ref, out_ref,
):
    scales = jnp.transpose(scale_ref[...])
    for at, (raw, gain, low) in enumerate(((qr_ref, gq_ref, q_ref), (kr_ref, gk_ref, k_ref))):
        normed = raw[...] * scales[:, 8 * at : 8 * at + 1] * gain[...]
        low[...] = (normed * cos_ref[...] + turn(normed) * sin_ref[...]).astype(BF16)
    for block in range(q_ref.shape[0] // rows):
        probs = masked_probs(q_ref, k_ref, start_ref, block, rows)
        last = (block + 1) * rows
        out_ref[block * rows : last, :] = product(
            probs.astype(BF16), v_ref[0:last, :]
        ).astype(BF16)


def head_spec(rows):
    return pl.BlockSpec((rows, HEAD_DIM), lambda h: (0, h))


def attend(q_raw, k_raw, v_low, scales, q_gain, k_gain, cosine, sine, starts, after):
    total, width = v_low.shape
    heads = width // HEAD_DIM
    head, gain = head_spec(total), head_spec(1)
    return call(
        functools.partial(attend_kernel, min(256, total)),
        [like((total, width), BF16)] * 3,
        [q_raw, k_raw, v_low, scales, q_gain, k_gain, cosine, sine, starts],
        3 * heads * total * total * HEAD_DIM,
        "attend",
        after=after,
        grid=(heads,),
        in_specs=[head, head, head, None, gain, gain, None, None, None],
        out_specs=[head, head, head],
    )


def attend_back_kernel(
    rows, q_ref, k_ref, v_ref, do_ref, qr_ref, kr_ref, scale_ref, gq_ref, gk_ref,
    cos_ref, sin_ref, start_ref,
    dq_ref, dk_ref, dv_ref, sums_ref, dgq_ref, dgk_ref, q_acc, k_acc, v_acc,
):
    k_acc[...] = jnp.zeros_like(k_acc)
    v_acc[...] = jnp.zeros_like(v_acc)
    for block in range(q_ref.shape[0] // rows):
        first, last = block * rows, (block + 1) * rows
        probs = masked_probs(q_ref, k_ref, start_ref, block, rows)
        d_rows = do_ref[first:last, :]
        d_probs = product_right(d_rows, v_ref[0:last, :])
        delta = jnp.sum(probs * d_probs, axis=1, keepdims=True)
        d_scores = (probs * (d_probs - delta) * (HEAD_DIM ** (-0.5))).astype(BF16)
        q_acc[first:last, :] = product(d_scores, k_ref[0:last, :])
        k_acc[0:last, :] += product_left(d_scores, q_ref[first:last, :])
        v_acc[0:last, :] += product_left(probs.astype(BF16), d_rows)
    dv_ref[...] = v_acc[...].astype(BF16)

    @pl.when(pl.program_id(0) == 0)
    def _():
        sums_ref[...] = jnp.zeros_like(sums_ref)

    scales = jnp.transpose(scale_ref[...])
    for at, (acc, raw, gain, d_ref, dg_ref) in enumerate(
        ((q_acc, qr_ref, gq_ref, dq_ref, dgq_ref), (k_acc, kr_ref, gk_ref, dk_ref, dgk_ref))
    ):
        turned = acc[...].astype(BF16).astype(F32)
        back = turned * cos_ref[...] + turn(turned * sin_ref[...])
        normed = raw[...] * scales[:, 8 * at : 8 * at + 1]
        both = back * normed
        dg_ref[...] = jnp.sum(both, axis=0, keepdims=True)
        d_ref[...] = back * gain[...]
        sums_ref[8 * at : 8 * at + 8, :] += row_sums(both * gain[...])


def attend_back(
    q_rot, k_rot, v_low, d_heads, q_raw, k_raw, scales, q_gain, k_gain, cosine, sine, starts
):
    total, width = v_low.shape
    heads = width // HEAD_DIM
    head, gain = head_spec(total), head_spec(1)
    wide, thin = like((total, width), F32), like((1, width), F32)
    return call(
        functools.partial(attend_back_kernel, min(256, total)),
        [wide, wide, like((total, width), BF16), like((16, total), F32), thin, thin],
        [q_rot, k_rot, v_low, d_heads, q_raw, k_raw, scales, q_gain, k_gain, cosine, sine, starts],
        7 * heads * total * total * HEAD_DIM,
        "attend_back",
        scratch=[pltpu.VMEM((total, HEAD_DIM), F32)] * 3,
        grid=(heads,),
        in_specs=[head] * 6 + [None, gain, gain, None, None, None],
        out_specs=[head, head, head, None, gain, gain],
    )


def chooser(places_ref, at, cap):
    row = places_ref[at : at + 1, :]
    slots = lax.broadcasted_iota(jnp.int32, (cap, row.shape[1]), 0)
    return slots == row


def dispatch_kernel(
    pieces_here, local, cap, gated, mine, *refs
):
    pieces, refs = refs[:pieces_here], refs[pieces_here:]
    places_ref, refs = refs[0], refs[1:]
    if gated:
        (picked_ref, router_ref), refs = refs[:2], refs[2:]
        rows_ref, gate_ref, all_ref = refs[-3:]
    else:
        rows_ref = refs[-1]
    for p in range(pieces_here):
        if gated:
            logits = product_right(router_ref[...], pieces[p][...])
            experts = logits.shape[0]
            picked = picked_ref[p * experts : (p + 1) * experts, :] > 0
            logits = jnp.where(picked, logits, NEG_FILL)
            weights = jnp.exp(logits - jnp.max(logits, axis=0, keepdims=True))
            weights = jnp.where(picked, weights, 0.0)
            gates = weights / jnp.sum(weights, axis=0, keepdims=True)
            all_ref[p * experts : (p + 1) * experts, :] = gates
        for e in range(local):
            chosen = chooser(places_ref, p * local + e, cap)
            rows_ref[e, p * cap : (p + 1) * cap, :] = product(
                chosen.astype(BF16), pieces[p][...]
            ).astype(BF16)
            if gated:
                row = all_ref[pl.ds(p * experts + mine[0] * local + e, 1), :]
                gate_ref[e, p * cap : (p + 1) * cap, :] = jnp.sum(
                    jnp.where(chosen, row, 0.0), axis=1, keepdims=True
                )


def dispatch(mine, pieces, places, picked, router, local, cap, group, at, rows, gates, after=()):
    gated = router is not None
    here = len(pieces)
    width = pieces[0].shape[1]
    args = [*pieces, places]
    shapes = [like((local, group * cap, width), BF16)]
    spec = pl.BlockSpec((local, here * cap, width), lambda i, mine: (0, at, 0))
    out_specs = [spec]
    if gated:
        args += [picked, router]
        shapes += [like((local, group * cap, 1), F32), like((picked.shape[0], places.shape[1]), F32)]
        out_specs += [pl.BlockSpec((local, here * cap, 1), lambda i, mine: (0, at, 0)), None]
    in_specs = [None] * len(args)
    aliases = {}
    if rows is not None:
        aliases[len(args)] = 0
        args.append(rows)
        in_specs.append(pl.BlockSpec(memory_space=pl.ANY))
        if gated:
            aliases[len(args)] = 1
            args.append(gates)
            in_specs.append(pl.BlockSpec(memory_space=pl.ANY))
    return call(
        functools.partial(dispatch_kernel, here, local, cap, gated),
        shapes,
        args,
        2 * here * local * cap * places.shape[1] * width,
        "dispatch",
        scalars=(mine,),
        in_specs=in_specs,
        out_specs=out_specs,
        aliases=aliases,
        after=after,
    )


def expert_kernel(
    x_ref, d_ref, gate_ref, wg_ref, wu_ref, wd_ref,
    act_ref, dg_ref, du_ref, dots_ref, mix_ref, back_ref, mix_acc, back_acc,
):
    step = pl.program_id(1)
    last = pl.num_programs(1) - 1
    x_rows, d_rows, gate = x_ref[0], d_ref[0], gate_ref[0]
    pre = product(x_rows, wg_ref[0])
    up = product(x_rows, wu_ref[0])
    pulled = product_right(d_rows, wd_ref[0])
    sigma = jax.nn.sigmoid(pre)
    silu = pre * sigma
    act = silu * up
    dots = jnp.sum(act * pulled, axis=1, keepdims=True)
    act_low = (act * gate).astype(BF16)
    act_ref[0] = act_low
    d_act = pulled * gate
    du_low = (d_act * silu).astype(BF16)
    dg_low = (d_act * up * sigma * (1.0 + pre * (1.0 - sigma))).astype(BF16)
    dg_ref[0] = dg_low
    du_ref[0] = du_low
    mix = product(act_low, wd_ref[0])
    back = product_right(dg_low, wg_ref[0]) + product_right(du_low, wu_ref[0])

    @pl.when(step == 0)
    def _():
        dots_ref[0] = dots
        mix_acc[...] = mix
        back_acc[...] = back

    @pl.when((step > 0) & (step < last))
    def _():
        dots_ref[0] += dots
        mix_acc[...] += mix
        back_acc[...] += back

    @pl.when(step == last)
    def _():
        dots_ref[0] += dots
        mix_ref[0] = (mix_acc[...] + mix).astype(BF16)
        back_ref[0] = (back_acc[...] + back).astype(BF16)


def experts(rows, d_rows, gates, w_gate, w_up, w_down, after=()):
    local, count, width = rows.shape
    hidden = w_gate.shape[2]
    part = hidden // 2
    wide = pl.BlockSpec((1, count, width), lambda e, f: (e, 0, 0))
    column = pl.BlockSpec((1, count, 1), lambda e, f: (e, 0, 0))
    thin = pl.BlockSpec((1, count, part), lambda e, f: (e, 0, f))
    into = pl.BlockSpec((1, width, part), lambda e, f: (e, 0, f))
    outof = pl.BlockSpec((1, part, width), lambda e, f: (e, f, 0))
    return call(
        expert_kernel,
        [like((local, count, hidden), BF16)] * 3
        + [like((local, count, 1), F32)]
        + [like((local, count, width), BF16)] * 2,
        [rows, d_rows, gates, w_gate, w_up, w_down],
        12 * rows.size * hidden,
        "experts",
        after=after,
        scratch=[pltpu.VMEM((count, width), F32)] * 2,
        grid=(local, 2),
        in_specs=[wide, wide, column, into, into, outof],
        out_specs=[thin, thin, thin, column, wide, wide],
    )


def combine_kernel(here, local, cap, dotted, places_ref, rows_ref, *refs):
    pieces = refs[int(dotted) : int(dotted) + here]
    for p in range(here):
        chosen = [chooser(places_ref, p * local + e, cap) for e in range(local)]
        total = None
        for e in range(local):
            part = product_left(chosen[e].astype(BF16), rows_ref[e, p * cap : (p + 1) * cap, :])
            total = part if total is None else total + part
            if dotted:
                refs[-1][p * local + e : p * local + e + 1, :] = jnp.sum(
                    jnp.where(chosen[e], refs[0][e, p * cap : (p + 1) * cap, :], 0.0),
                    axis=0, keepdims=True,
                )
        pieces[p][...] = total.astype(BF16)


def combine(places, rows, here, local, cap, at, dots=None, after=()):
    width = rows.shape[2]
    tokens = places.shape[1]
    dotted = dots is not None
    args = [places, rows] + ([dots] if dotted else [])
    in_specs = [None, pl.BlockSpec((local, here * cap, width), lambda i: (0, at, 0))]
    if dotted:
        in_specs.append(pl.BlockSpec((local, here * cap, 1), lambda i: (0, at, 0)))
    shapes = [like((tokens, width), BF16)] * here
    if dotted:
        shapes.append(like(places.shape, F32))
    return call(
        functools.partial(combine_kernel, here, local, cap, dotted),
        shapes,
        args,
        2 * here * local * cap * tokens * width,
        "combine",
        after=after,
        in_specs=in_specs,
    )


def combine_stacks_kernel(count, local, cap, group, places_ref, *refs):
    groups = count // group
    for k in range(count):
        rows = refs[k // group]
        at = (k % group) * cap
        total = None
        for e in range(local):
            chosen = chooser(places_ref, k * local + e, cap).astype(BF16)
            part = product_left(chosen, rows[e, at : at + cap, :])
            total = part if total is None else total + part
        array, place = stack_at(k, count)
        refs[groups + array][place] = total.astype(BF16)


def combine_stacks(places, rows, count, local, cap, group, after):
    tokens, width = places.shape[1], rows[0].shape[2]
    return call(
        functools.partial(combine_stacks_kernel, count, local, cap, group),
        stack_shapes(count, (tokens, width)),
        [places, *rows],
        2 * count * local * cap * tokens * width,
        "combine_stacks",
        after=after,
    )


def weight_grad_kernel(groups, *refs):
    lefts, rights = refs[:groups], refs[groups : 2 * groups]
    total = None
    for left, right in zip(lefts, rights):
        part = product_left(left[0], right[0])
        total = part if total is None else total + part
    refs[-1][0] = total.astype(BF16)


def weight_grad(lefts, rights, after=()):
    local, count, tall = lefts[0].shape
    wide = rights[0].shape[2]
    part = min(512, tall)
    left = pl.BlockSpec((1, count, part), lambda e, i: (e, 0, i))
    right = pl.BlockSpec((1, count, wide), lambda e, i: (e, 0, 0))
    return call(
        functools.partial(weight_grad_kernel, len(lefts)),
        like((local, tall, wide), BF16),
        [*lefts, *rights],
        2 * len(lefts) * lefts[0].size * wide,
        "weight_grad",
        after=after,
        grid=(local, tall // part),
        in_specs=[left] * len(lefts) + [right] * len(lefts),
        out_specs=[pl.BlockSpec((1, part, wide), lambda e, i: (e, i, 0))],
    )


def body(
    tokens, doc_lengths, routes, attn_gain, w_query, w_key, w_value, q_gain, k_gain, w_out,
    ffn_gain, w_router, w_gate, w_up, w_down, cotangent,
):
    n_sp = lax.axis_size("sp")
    n_ep = lax.axis_size("ep")
    sp_index = lax.axis_index("sp")
    ep_index = lax.axis_index("ep")
    tok_dev, width = tokens.shape[1:]
    total = tok_dev * n_sp
    shard = width // n_ep
    head_width = width // n_sp
    top_count = routes.shape[2]
    local = w_gate.shape[0]
    expert_count = local * n_ep
    capacity = 9 * tok_dev * top_count // (8 * expert_count)
    cap = -(-capacity // 16) * 16
    group = 4
    blocks = piece_blocks(n_ep, ep_index)
    partners = jnp.bitwise_xor(jnp.arange(n_sp, dtype=jnp.int32), sp_index)
    ids = jnp.concatenate([blocks, partners]).astype(jnp.int32)
    mine = ep_index.astype(jnp.int32).reshape(1)

    def own_columns(value):
        return lax.dynamic_slice_in_dim(value, sp_index * head_width, head_width, 1)

    def by_piece(value):
        return jnp.stack(
            [lax.dynamic_index_in_dim(value, blocks[i], 0, keepdims=False) for i in range(n_ep)]
        )

    expert_ids = jnp.arange(expert_count, dtype=jnp.int32)
    picked = jnp.any(routes[0][:, :, None] == expert_ids[None, None, :], axis=1)
    picked_low = picked.T.astype(BF16)
    small = jnp.concatenate(
        [
            jnp.stack([attn_gain, q_gain, k_gain, ffn_gain]),
            jnp.zeros((12, shard), BF16),
            w_router.T,
        ],
        axis=0,
    )

    def to_all(value):
        value = jnp.broadcast_to(value[None], (n_ep, *value.shape))
        return lax.all_to_all(value, "ep", split_axis=0, concat_axis=0, tiled=True)

    if shard == tok_dev:
        both = to_all(jnp.concatenate([small, picked_low], axis=0))
        small_all, picked_all = both[:, : 16 + expert_count], both[:, 16 + expert_count :]
    else:
        small_all, picked_all = to_all(small), to_all(picked_low)
    small_rows = jnp.swapaxes(small_all, 0, 1).reshape(16 + expert_count, width)
    gains = small_rows[:4].astype(F32)
    full_router = small_rows[16:]
    picked_all = by_piece(picked_all)

    x_all = lax.all_gather(tokens[0], "sp", axis=0, tiled=True)
    w_own = jnp.concatenate([own_columns(w) for w in (w_query, w_key, w_value, w_out)], axis=1)
    cot_own = cotangent[0]
    positions = jnp.arange(total, dtype=jnp.int32)
    lengths = doc_lengths[0]
    doc_ends = jnp.cumsum(lengths)
    starts = jnp.sum(
        jnp.where(doc_ends[None, :] <= positions[:, None], lengths[None, :], 0), axis=1
    )
    half = HEAD_DIM // 2
    frequency = THETA ** (-(2.0 * jnp.arange(half, dtype=F32)) / HEAD_DIM)
    angles = (positions - starts).astype(F32)[:, None] * frequency[None, :]
    cosine = jnp.concatenate([jnp.cos(angles), jnp.cos(angles)], axis=1)
    sine = jnp.concatenate([-jnp.sin(angles), jnp.sin(angles)], axis=1)
    starts = starts[:, None].astype(jnp.int32)
    w_own, cosine, sine, starts, ids = tie(w_own, cosine, sine, starts, ids)
    if n_ep == 8:
        w_pieces = gather_line(w_own)
        w_pieces[6], cot_own = tie(w_pieces[6], cot_own)
        cot_pieces, w_pieces[7] = gather_double(cot_own, w_pieces[7])
    else:
        w_pieces, cot_pieces = gather_whole(w_own), gather_whole(cot_own)

    upper = (
        jnp.arange(tok_dev, dtype=jnp.int32)[:, None] < jnp.arange(tok_dev, dtype=jnp.int32)[None, :]
    ).astype(BF16)
    picked_mine = lax.dynamic_slice_in_dim(picked_all, ep_index * local, local, 1)
    picked_mine = picked_mine.reshape(n_ep * local, tok_dev)
    earlier = product(picked_mine, upper).astype(jnp.int32)
    places = jnp.where((picked_mine > 0) & (earlier < capacity), earlier, -1)
    picked_flat = picked_all.reshape(n_ep * expert_count, tok_dev).astype(F32)


    w_o = [
        jnp.concatenate([piece[:, 3 * head_width :] for piece in half])
        for half in (w_pieces[: n_ep // 2], w_pieces[n_ep // 2 :])
    ]
    w_o_over = [swap_sp(half, 2) for half in w_o]
    q_raw, k_raw, v_low, squares, w_qkv, h_all = qkv_project(
        ids, x_all, gains[0:1], w_pieces, [places, picked_flat]
    )
    scales = lax.rsqrt(sum_sp(squares) / width + EPS)
    gain_q, gain_k = own_columns(gains)[1:2], own_columns(gains)[2:3]
    q_rot, k_rot, mixed = attend(
        q_raw, k_raw, v_low, scales, gain_q, gain_k, cosine, sine, starts,
        [w_o_over[0]] + [cot_pieces[k] for k in ((1, 2, 4) if n_ep == 8 else ())],
    )

    def pair_places(p):
        return places[p * local : (p + 2) * local]

    def cot_rows(g, after):
        d_rows = None
        for at, p in enumerate(range(g, g + group, 2)):
            (d_rows,) = dispatch(
                mine, cot_pieces[p : p + 2], pair_places(p), None, None, local, cap, group, at,
                d_rows, None, after,
            )
        return d_rows

    if n_ep == 8:
        cot_pieces[6], w_o_over[1], mixed = tie(cot_pieces[6], w_o_over[1], mixed)
    attn_tok = lax.all_to_all(mixed, "sp", split_axis=0, concat_axis=1, tiled=True)
    w_o_parts = (
        w_o + [swap_sp(half, 1) for half in w_o] + w_o_over + [swap_sp(half, 1) for half in w_o_over]
    )
    if n_ep == 8:
        cot_pieces[3], attn_tok = tie(cot_pieces[3], attn_tok)
    x_one, h2_low = out_project(
        ids, n_ep, attn_tok, tokens[0], gains[3:4], w_o_parts
    )
    attn_all = lax.all_gather(attn_tok, "sp", axis=0, tiled=True)

    h2_pieces = gather(h2_low, n_ep)
    cots = [cot_rows(g, [x_one]) for g in range(0, n_ep, group)]
    groups, d_pieces, d_gates, d_sums = [], [], [], []
    home_gates = None

    def rows_of(g, after):
        rows = gates = first_gates = None
        for at, p in enumerate(range(g, g + group, 2)):
            rows, gates, piece_gates = dispatch(
                mine, h2_pieces[p : p + 2], pair_places(p),
                picked_flat[p * expert_count : (p + 2) * expert_count], full_router, local, cap,
                group, at, rows, gates, after,
            )
            first_gates = piece_gates if first_gates is None else first_gates
        return rows, gates, first_gates

    rows, gates, home_gates = rows_of(0, [])
    for g in range(0, n_ep, group):
        d_rows = cots[g // group]
        made = experts(rows, d_rows, gates, w_gate, w_up, w_down, d_pieces[-group:] + cots + h2_pieces[4:7:2])
        groups.append((rows, d_rows, made))
        following = []
        if g + group < n_ep:
            rows, gates, _ = rows_of(g + group, [made[5]])
            following = [rows]
        sums_before = list(d_sums)
        for at in range(group // 2):
            *two, dots = combine(
                pair_places(g + 2 * at), made[5], 2, local, cap, at, made[3],
                sums_before + following,
            )
            d_pieces += two
            d_gates.append(dots)
        if n_ep == 8:
            d_sums += crossed_sums(d_pieces[-group:])

    acts = [made[0] for _, _, made in groups]
    d_gate_rows = [made[1] for _, _, made in groups]
    d_up_rows = [made[2] for _, _, made in groups]
    ins = [rows for rows, _, _ in groups]
    outs = [d_rows for _, d_rows, _ in groups]
    d_gates = by_piece(jnp.concatenate(d_gates, axis=0).reshape(n_ep, local, tok_dev))
    d_gates = lax.all_to_all(d_gates, "ep", split_axis=0, concat_axis=0, tiled=True)
    d_gates = d_gates.reshape(expert_count, tok_dev)
    mix_stacks = combine_stacks(
        places, [made[4] for _, _, made in groups], n_ep, local, cap, group, d_pieces
    )
    grad_down = weight_grad(acts, outs, mix_stacks[:1])
    if n_ep == 8:
        d_sums[2], mix_stacks[2], mix_stacks[3], grad_down = tie(
            d_sums[2], mix_stacks[2], mix_stacks[3], grad_down
        )
        d_h2, d_far = scatter_z(*d_sums)
        d_last = [d_far]
    else:
        d_h2, d_last = scatter(d_pieces, n_ep), []
    grad_gate = weight_grad(ins, d_gate_rows, [grad_down, d_gates, *d_last])
    grad_up = weight_grad(ins, d_up_rows, [grad_gate])

    def over_sp(value):
        return lax.psum_scatter(value, "sp", scatter_dimension=1, tiled=True).astype(F32)


    if n_ep == 8:
        gates_here = home_gates[:expert_count]
    else:
        logits = product_right(full_router, h2_low)
        logits = jnp.where(picked.T, logits, NEG_FILL)
        gates_here = jax.nn.softmax(logits, axis=0)
    d_logits = gates_here * (d_gates - jnp.sum(gates_here * d_gates, axis=0, keepdims=True))
    d_logits = jnp.where(picked.T, d_logits, 0.0).astype(BF16)
    grad_router = product(d_logits, h2_low)
    d_h2 = d_h2 + product_left(d_logits, full_router)
    one_scale = lax.rsqrt(jnp.mean(x_one * x_one, axis=-1, keepdims=True) + EPS)
    one_normed = x_one * one_scale
    grad_ffn = jnp.sum(d_h2 * one_normed, axis=0)
    d_normed = d_h2 * gains[3][None, :]
    d_one = cotangent[0].astype(F32) + one_scale * (
        d_normed - one_normed * jnp.mean(d_normed * one_normed, axis=-1, keepdims=True)
    )
    d_z, grad_up = tie(d_one.astype(BF16), grad_up)
    d_attn = out_back(ids, n_ep, d_z, w_o_parts)
    d_heads = lax.all_to_all(d_attn, "sp", split_axis=1, concat_axis=0, tiled=True)
    d_z_cols = lax.all_to_all(d_z, "sp", split_axis=1, concat_axis=0, tiled=True)
    mix, mix_far = scatter_stacks(mix_stacks, n_ep)
    if n_ep == 8:
        mix, mix_far, d_heads = tie(mix, mix_far, d_heads)
    grad_down, grad_gate, grad_up = over_sp(grad_down), over_sp(grad_gate), over_sp(grad_up)

    d_qn, d_kn, d_v, sums, grad_qg, grad_kg = attend_back(
        q_rot, k_rot, v_low, d_heads, q_raw, k_raw, scales, gain_q, gain_k, cosine, sine, starts
    )
    output = (x_one + last_hop(mix, mix_far)).astype(BF16)
    vo_stacks = vo_grads(ids, n_ep, h_all, d_v, attn_all, d_z_cols)

    grad_vo = last_hop(*scatter_stacks(vo_stacks, n_ep)).astype(BF16)

    def placed(value):
        return lax.dynamic_update_slice_in_dim(
            jnp.zeros((1, width), F32), value, sp_index * head_width, 1
        )

    tiny = jnp.concatenate(
        [placed(grad_qg), placed(grad_kg), grad_ffn[None], grad_router], axis=0
    )
    *qk_stacks, d_qk = qk_back(
        ids, n_ep, h_all, d_qn, d_kn, q_raw, k_raw, scales, sum_sp_swaps(sums), tiny, vo_stacks[:1]
    )
    grad_qk = last_hop(*scatter_stacks(qk_stacks, n_ep)).astype(BF16)

    d_h = d_h_rows(ids, n_ep, n_sp, d_qk, d_v, w_qkv, [grad_down, grad_gate])
    output, d_h = tie(output, d_h)
    halves = plus(d_h[:2], swap_sp(d_h[2:], 1))
    d_h = halves[0].astype(F32) + swap_sp(halves[1], 2).astype(F32)
    x_rows = tokens[0].astype(F32)
    x_scale = lax.rsqrt(jnp.mean(x_rows * x_rows, axis=-1, keepdims=True) + EPS)
    x_normed = x_rows * x_scale
    d_normed = d_h * gains[0][None, :]
    input_grad = d_one + x_scale * (
        d_normed - x_normed * jnp.mean(d_normed * x_normed, axis=-1, keepdims=True)
    )

    g_query, g_key, g_value, g_out, tiny, g_attn = finish(
        ids, n_ep, w_query, w_key, w_value, attn_gain.astype(F32)[:, None],
        gather_sp(grad_qk), gather_sp(grad_vo), [grad_down, grad_gate, grad_up],
    )
    per_row = 2 * head_width // shard

    def vector(at):
        col = (at % per_row) * shard
        return tiny[at // per_row, col : col + shard]

    g_router = jnp.stack([vector(3 + i) for i in range(expert_count)], axis=1)
    return (
        output[None], input_grad[None], g_attn[:, 0], g_query, g_key, g_value, vector(0), vector(1),
        g_out, vector(2), g_router, grad_gate, grad_up, grad_down,
    )


def solution(mesh):
    seq = P("ep", "sp", None)
    vec = P("ep")
    mat = P("ep", None)
    expert = P("ep", None, None)
    in_specs = (
        seq, mat, seq, vec, mat, mat, mat, vec, vec, mat, vec, mat, expert, expert, expert, seq,
    )
    out_specs = (
        seq, seq, vec, mat, mat, mat, vec, vec, mat, vec, mat, seq, seq, seq,
    )
    return jax.shard_map(body, mesh=mesh, in_specs=in_specs, out_specs=out_specs, check_vma=False)
```

```python
import functools

import jax
import jax.numpy as jnp
from jax import lax
from jax.experimental import pallas as pl
from jax.experimental.pallas import tpu as pltpu
from jax.sharding import PartitionSpec as P

HEAD_DIM = 128
EPS = 1e-05
THETA = 10000.0
NEG_FILL = -1e30
F32 = jnp.float32
BF16 = jnp.bfloat16
MIB = 1 << 20
COVER = 20


def product(left, right):
    return jnp.dot(left, right, preferred_element_type=F32)


def product_left(left, right):
    return lax.dot_general(left, right, (((0,), (0,)), ((), ())), preferred_element_type=F32)


def product_right(left, right):
    return lax.dot_general(left, right, (((1,), (1,)), ((), ())), preferred_element_type=F32)


def row_sums(values_in):
    sums = jnp.sum(values_in, axis=1, keepdims=True)
    return jnp.transpose(jnp.broadcast_to(sums, (sums.shape[0], HEAD_DIM)))[:8]


def call(kernel, out_shape, args, flops, name, scratch=(), scalars=(), grid=(1,), in_specs=None,
         out_specs=None, aliases=None, vmem=60, after=()):
    single = not isinstance(out_shape, (list, tuple))
    shapes = [out_shape] if single else list(out_shape)
    count = len(grid)

    def fixed(shape):
        rank = len(shape)
        return pl.BlockSpec(tuple(shape), lambda *ids: (0,) * rank)

    in_specs = in_specs or [None] * len(args)
    out_specs = out_specs or [None] * len(shapes)
    in_specs = [s if s is not None else fixed(a.shape) for s, a in zip(in_specs, args)]
    out_specs = [s if s is not None else fixed(o.shape) for s, o in zip(out_specs, shapes)]
    waited = len(after)
    args = [*args, *after]
    in_specs = in_specs + [pl.BlockSpec(memory_space=pl.ANY)] * waited
    if waited:
        inner, first = kernel, len(scalars) + len(args) - waited

        def kernel(*refs):
            inner(*refs[:first], *refs[first + waited :])

    moved = sum(a.size * a.dtype.itemsize for a in args[: len(args) - waited])
    moved += sum(o.size * o.dtype.itemsize for o in shapes)
    result = pl.pallas_call(
        kernel,
        grid_spec=pltpu.PrefetchScalarGridSpec(
            num_scalar_prefetch=len(scalars), grid=grid, in_specs=in_specs, out_specs=out_specs,
            scratch_shapes=list(scratch),
        ),
        out_shape=shapes,
        input_output_aliases={k + len(scalars): v for k, v in (aliases or {}).items()},
        compiler_params=pltpu.CompilerParams(
            vmem_limit_bytes=vmem * MIB, dimension_semantics=("arbitrary",) * count
        ),
        cost_estimate=pl.CostEstimate(flops=int(COVER * flops), bytes_accessed=int(moved), transcendentals=0),
        name=name,
    )(*scalars, *args)
    return result[0] if single else list(result)


def like(shape, dtype):
    return jax.ShapeDtypeStruct(tuple(shape), dtype)


def tie(*values):
    return lax.optimization_barrier(values)


def swap(value, bits):
    return lax.ppermute(value, "ep", [(i, i ^ bits) for i in range(8)])


def swap_sp(value, bits):
    return lax.ppermute(value, "sp", [(i, i ^ bits) for i in range(4)])


def piece_blocks(n_ep, ep_index):
    ids = jnp.arange(n_ep, dtype=jnp.int32)
    return jnp.bitwise_xor(ids, ep_index) if n_ep == 8 else ids


MIDDLE = [(2, 4), (3, 5), (4, 2), (5, 3)]
OUTWARD = [(2, 0), (3, 1), (4, 6), (5, 7)]


def gather_line(value):
    crossed = swap(value, 1)
    near = swap(value, 2)
    inner = lax.ppermute(value, "ep", MIDDLE)
    near_x, outer = swap(near, 1), lax.ppermute(near, "ep", MIDDLE)
    near_x, crossed, outer = tie(near_x, crossed, outer)
    far = outer + lax.ppermute(inner, "ep", OUTWARD)
    farther = inner + lax.ppermute(outer, "ep", OUTWARD)
    return [value, crossed, near, near_x, far, swap(far, 1), farther, swap(farther, 1)]


def gather_double(value, after):
    after, held = tie(after, value)
    crossed = swap(held, 1)
    near, far = swap(value, 2), swap(value, 4)
    farther = swap(far, 2)
    near_x, held = tie(swap(near, 1), far)
    return [
        value, crossed, near, near_x, far, swap(held, 1), farther
    ], after


def gather_whole(value):
    whole = lax.all_gather(value, "ep", axis=0, tiled=False)
    return [whole[i] for i in range(whole.shape[0])]


def gather(value, n_ep):
    return gather_line(value) if n_ep == 8 else gather_whole(value)


def plus(left, right):
    return (left.astype(F32) + right.astype(F32)).astype(left.dtype)


def crossed_sums(pieces):
    return [plus(pieces[i], swap(pieces[i + 1], 1)) for i in range(0, len(pieces), 2)]


def scatter_z(own, near, far, farther):
    far = plus(far, swap(farther, 2))
    far, near = tie(far, near)
    return own.astype(F32) + swap(near, 2).astype(F32) + swap(far, 4).astype(F32), far


def scatter(pieces, n_ep):
    if n_ep != 8:
        stacked = jnp.stack(pieces)
        return lax.psum_scatter(stacked, "ep", scatter_dimension=0, tiled=False).astype(F32)
    return scatter_z(*crossed_sums(pieces))[0]


def stack_at(piece, n_ep):
    if n_ep != 8:
        return 0, piece
    return 2 * (piece % 2) + (piece // 2) % 2, piece // 4


def stack_shapes(n_ep, shape):
    return [like((2, *shape), BF16)] * 4 if n_ep == 8 else [like((n_ep, *shape), BF16)]


def odd_sums(stacks):
    return plus(stacks[1], swap(stacks[3], 1))


def even_sums(stacks, odd):
    even = stacks[0].astype(F32) + swap(stacks[2], 1).astype(F32) + swap(odd, 2).astype(F32)
    return even[0], even[1].astype(BF16)


def scatter_stacks(stacks, n_ep):
    if n_ep != 8:
        total = lax.psum_scatter(stacks[0], "ep", scatter_dimension=0, tiled=False)
        return total.astype(F32), None
    return even_sums(stacks, odd_sums(stacks))


def last_hop(total, far):
    return total if far is None else total + swap(far, 4).astype(F32)


def gather_sp(value):
    over = swap_sp(value, 2)
    return [value, swap_sp(value, 1), over, swap_sp(over, 1)]


def sum_sp(value):
    n_sp = lax.axis_size("sp")
    value = jnp.broadcast_to(value[None], (n_sp, *value.shape))
    return jnp.sum(lax.all_to_all(value, "sp", split_axis=0, concat_axis=0, tiled=True), axis=0)


def sum_sp_swaps(value):
    return (value + swap_sp(value, 1)) + (swap_sp(value, 2) + swap_sp(value, 3))


def block_at(ids, position, size):
    if size % HEAD_DIM:
        return pl.ds(position * size, size)
    return pl.ds(pl.multiple_of(ids[position] * size, size), size)


def qkv_kernel(count, ids, x_ref, gain_ref, *refs):
    pieces, refs = refs[:count], refs[count:]
    q_ref, k_ref, v_ref, squares_ref, w_ref, h_ref = refs
    shard = pieces[0].shape[0]
    width = q_ref.shape[1]

    @pl.when(pl.program_id(0) == 0)
    def _():
        for k in range(count):
            rows = block_at(ids, k, shard)
            w_ref[rows, :] = pieces[k][:, : 3 * width]

    x_rows = x_ref[...].astype(F32)
    scale = lax.rsqrt(jnp.mean(x_rows * x_rows, axis=1, keepdims=True) + EPS)
    h_ref[...] = (x_rows * scale * gain_ref[...]).astype(BF16)
    for at, ref in enumerate((q_ref, k_ref)):
        part = product(h_ref[...], w_ref[:, at * width : (at + 1) * width])
        ref[...] = part
        squares_ref[8 * at : 8 * at + 8, :] = row_sums(part * part)
    v_ref[...] = product(h_ref[...], w_ref[:, 2 * width :]).astype(BF16)


def qkv_project(ids, x_all, gain, pieces, after):
    total, depth = x_all.shape
    width = pieces[0].shape[1] // 4
    rows = min(256, total)
    block = pl.BlockSpec((rows, width), lambda i, ids: (i, 0))
    wide = pl.BlockSpec((rows, depth), lambda i, ids: (i, 0))
    return call(
        functools.partial(qkv_kernel, len(pieces)),
        [like((total, width), F32)] * 2
        + [like((total, width), BF16), like((16, total), F32), like((depth, 3 * width), BF16)]
        + [like((total, depth), BF16)],
        [x_all, gain, *pieces],
        6 * total * depth * width,
        "qkv_project",
        after=after,
        scalars=(ids,),
        grid=(total // rows,),
        in_specs=[wide] + [None] * (len(pieces) + 1),
        out_specs=[
            block, block, block, pl.BlockSpec((16, rows), lambda i, ids: (0, i)), None, wide,
        ],
    )


def out_kernel(n_ep, n_sp, ids, attn_ref, x_ref, gain_ref, *refs):
    weights, (one_ref, low_ref, turned_ref) = refs[: 2 * n_sp], refs[2 * n_sp :]
    rows, width = weights[0].shape
    shard = 2 * rows // n_ep
    for k in range(n_ep):
        turned_ref[:, k * shard : (k + 1) * shard] = attn_ref[:, block_at(ids, k, shard)]
    for j in range(n_sp):
        cols = block_at(ids, n_ep + j, width)
        one_ref[:, cols] = (
            x_ref[:, cols].astype(F32)
            + product(turned_ref[:, :rows], weights[2 * j][...])
            + product(turned_ref[:, rows:], weights[2 * j + 1][...])
        )
    one = one_ref[...]
    scale = lax.rsqrt(jnp.mean(one * one, axis=1, keepdims=True) + EPS)
    low_ref[...] = (one * scale * gain_ref[...]).astype(BF16)


def out_project(ids, n_ep, attn_tok, tokens, gain, weights):
    return call(
        functools.partial(out_kernel, n_ep, len(weights) // 2),
        [like(tokens.shape, F32), like(tokens.shape, BF16)],
        [attn_tok, tokens, gain, *weights],
        2 * tokens.size * attn_tok.shape[1],
        "out_project",
        scratch=[pltpu.VMEM(attn_tok.shape, BF16)],
        scalars=(ids,),
    )


def out_back_kernel(n_ep, n_sp, ids, d_ref, *refs):
    weights, d_attn_ref = refs[:-1], refs[-1]
    rows, width = weights[0].shape
    shard = 2 * rows // n_ep
    for half in range(2):
        total = None
        for j in range(n_sp):
            part = product_right(
                d_ref[:, block_at(ids, n_ep + j, width)], weights[2 * j + half][...]
            )
            total = part if total is None else total + part
        total = total.astype(BF16)
        for k in range(n_ep // 2):
            block = block_at(ids, half * (n_ep // 2) + k, shard)
            d_attn_ref[:, block] = total[:, k * shard : (k + 1) * shard]


def out_back(ids, n_ep, d_z, weights):
    return call(
        functools.partial(out_back_kernel, n_ep, len(weights) // 2),
        like((d_z.shape[0], 2 * weights[0].shape[0]), BF16),
        [d_z, *weights],
        2 * d_z.size * weights[0].shape[0] * 2,
        "out_back",
        scalars=(ids,),
    )


def vo_grads_kernel(count, shard, ids, h_ref, dv_ref, attn_ref, dz_ref, *stacks):
    width = dv_ref.shape[1]
    for k in range(count):
        block = block_at(ids, k, shard)
        array, place = stack_at(k, count)
        stacks[array][place, :, :width] = product_left(h_ref[:, block], dv_ref[...]).astype(BF16)
        stacks[array][place, :, width:] = product_left(attn_ref[:, block], dz_ref[...]).astype(BF16)


def vo_grads(ids, count, h_all, d_v, attn_all, d_z_cols):
    shard = h_all.shape[1] // count
    width = d_v.shape[1]
    return call(
        functools.partial(vo_grads_kernel, count, shard),
        stack_shapes(count, (shard, 2 * width)),
        [h_all, d_v, attn_all, d_z_cols],
        4 * h_all.size * width,
        "vo_grads",
        scalars=(ids,),
    )


def qk_back_kernel(
    count, shard, ids, h_ref, dqn_ref, dkn_ref, qr_ref, kr_ref, scale_ref, sums_ref, tiny_ref, *refs
):
    stacks, d_ref = refs[:-1], refs[-1]
    width = dqn_ref.shape[1]
    scales = jnp.transpose(scale_ref[...])
    means = jnp.transpose(sums_ref[...]) * (1.0 / h_ref.shape[1])
    for at, (d_normed, raw) in enumerate(((dqn_ref, qr_ref), (dkn_ref, kr_ref))):
        scale, mean = scales[:, 8 * at : 8 * at + 1], means[:, 8 * at : 8 * at + 1]
        d_ref[:, at * width : (at + 1) * width] = (
            scale * (d_normed[...] - raw[...] * scale * mean)
        ).astype(BF16)
    per_row = 2 * width // shard
    extra = stacks[0].shape[1] - shard
    for k in range(count):
        block = block_at(ids, k, shard)
        array, place = stack_at(k, count)
        ref = stacks[array]
        ref[place, :shard, :] = product_left(h_ref[:, block], d_ref[...]).astype(BF16)
        ref[place, shard:, :] = jnp.zeros((extra, 2 * width), BF16)
        for at in range(tiny_ref.shape[0]):
            row, col = shard + at // per_row, (at % per_row) * shard
            ref[place, row : row + 1, col : col + shard] = tiny_ref[at : at + 1, block].astype(BF16)


def qk_back(ids, count, h_all, d_qn, d_kn, q_raw, k_raw, scales, sums, tiny, after):
    total, depth = h_all.shape
    width = d_qn.shape[1]
    shard = depth // count
    extra = -(-tiny.shape[0] // (2 * width // shard))
    extra = -(-extra // 16) * 16
    return call(
        functools.partial(qk_back_kernel, count, shard),
        stack_shapes(count, (shard + extra, 2 * width)) + [like((total, 2 * width), BF16)],
        [h_all, d_qn, d_kn, q_raw, k_raw, scales, sums, tiny],
        2 * h_all.size * 2 * width,
        "qk_back",
        scalars=(ids,),
        after=after,
    )


def d_h_kernel(ids, d_ref, dv_ref, w_ref, out_ref):
    both = d_ref.shape[1]
    out_ref[0] = (
        product_right(d_ref[...], w_ref[:, :both]) + product_right(dv_ref[...], w_ref[:, both:])
    ).astype(BF16)


def d_h_rows(ids, n_ep, n_sp, d_qk, d_v, w_qkv, after):
    total, wide = d_qk.shape
    depth = w_qkv.shape[0]
    rows = total // n_sp

    def partner(j, ids):
        return ids[n_ep + (j % 2) * 2 + j // 2], 0

    return call(
        d_h_kernel,
        like((n_sp, rows, depth), BF16),
        [d_qk, d_v, w_qkv],
        3 * d_qk.size * depth,
        "d_h",
        after=after,
        scalars=(ids,),
        grid=(n_sp,),
        in_specs=[
            pl.BlockSpec((rows, wide), partner), pl.BlockSpec((rows, d_v.shape[1]), partner), None,
        ],
        out_specs=[pl.BlockSpec((1, rows, depth), lambda j, ids: (j, 0, 0))],
    )


def finish_kernel(n_ep, n_sp, ids, wq_ref, wk_ref, wv_ref, gain_ref, *refs):
    firsts, seconds = refs[:n_sp], refs[n_sp : 2 * n_sp]
    gq_ref, gk_ref, gv_ref, go_ref, tiny_ref, attn_ref = refs[2 * n_sp :]
    shard = wq_ref.shape[0]
    width = firsts[0].shape[1] // 2
    dots = jnp.zeros((shard, 1), F32)
    tiny = jnp.zeros(tiny_ref.shape, F32)
    for j in range(n_sp):
        cols = block_at(ids, n_ep + j, width)
        for at, grad, weight in ((0, gq_ref, wq_ref), (1, gk_ref, wk_ref), (2, gv_ref, wv_ref)):
            part = firsts[j][:shard, at * width : (at + 1) * width] if at < 2 else seconds[j][:, :width]
            value = part.astype(F32)
            grad[:, cols] = value
            dots += jnp.sum(value * weight[:, cols].astype(F32), axis=1, keepdims=True)
        go_ref[:, cols] = seconds[j][:, width:].astype(F32)
        tiny += firsts[j][shard:, :].astype(F32)
    tiny_ref[...] = tiny
    attn_ref[...] = dots / gain_ref[...]


def finish(ids, n_ep, w_query, w_key, w_value, gain, firsts, seconds, after):
    shard, depth = w_query.shape
    extra = firsts[0].shape[0] - shard
    return call(
        functools.partial(finish_kernel, n_ep, len(firsts)),
        [like((shard, depth), F32)] * 4 + [like((extra, firsts[0].shape[1]), F32), like((shard, 1), F32)],
        [w_query, w_key, w_value, gain, *firsts, *seconds],
        shard * depth * 6,
        "finish",
        after=after,
        scalars=(ids,),
    )


def turn(values_in):
    return pltpu.roll(values_in, HEAD_DIM // 2, 1)


def masked_probs(q_ref, k_ref, start_ref, block, rows):
    first, last = block * rows, (block + 1) * rows
    scores = product_right(q_ref[first:last, :], k_ref[0:last, :]) * (HEAD_DIM ** (-0.5))
    row_ids = first + lax.broadcasted_iota(jnp.int32, scores.shape, 0)
    places = lax.broadcasted_iota(jnp.int32, scores.shape, 1)
    allowed = (places <= row_ids) & (places >= start_ref[first:last, :])
    scores = jnp.where(allowed, scores, NEG_FILL)
    top = jnp.max(scores, axis=1, keepdims=True)
    weights = jnp.exp(scores - top)
    return weights * (1.0 / jnp.sum(weights, axis=1, keepdims=True))


def attend_kernel(
    rows, qr_ref, kr_ref, v_ref, scale_ref, gq_ref, gk_ref, cos_ref, sin_ref, start_ref,
    q_ref, k_ref, out_ref,
):
    scales = jnp.transpose(scale_ref[...])
    for at, (raw, gain, low) in enumerate(((qr_ref, gq_ref, q_ref), (kr_ref, gk_ref, k_ref))):
        normed = raw[...] * scales[:, 8 * at : 8 * at + 1] * gain[...]
        low[...] = (normed * cos_ref[...] + turn(normed) * sin_ref[...]).astype(BF16)
    for block in range(q_ref.shape[0] // rows):
        probs = masked_probs(q_ref, k_ref, start_ref, block, rows)
        last = (block + 1) * rows
        out_ref[block * rows : last, :] = product(
            probs.astype(BF16), v_ref[0:last, :]
        ).astype(BF16)


def head_spec(rows):
    return pl.BlockSpec((rows, HEAD_DIM), lambda h: (0, h))


def attend(q_raw, k_raw, v_low, scales, q_gain, k_gain, cosine, sine, starts, after):
    total, width = v_low.shape
    heads = width // HEAD_DIM
    head, gain = head_spec(total), head_spec(1)
    return call(
        functools.partial(attend_kernel, min(256, total)),
        [like((total, width), BF16)] * 3,
        [q_raw, k_raw, v_low, scales, q_gain, k_gain, cosine, sine, starts],
        3 * heads * total * total * HEAD_DIM,
        "attend",
        after=after,
        grid=(heads,),
        in_specs=[head, head, head, None, gain, gain, None, None, None],
        out_specs=[head, head, head],
    )


def attend_back_kernel(
    rows, q_ref, k_ref, v_ref, do_ref, qr_ref, kr_ref, scale_ref, gq_ref, gk_ref,
    cos_ref, sin_ref, start_ref,
    dq_ref, dk_ref, dv_ref, sums_ref, dgq_ref, dgk_ref, q_acc, k_acc, v_acc,
):
    k_acc[...] = jnp.zeros_like(k_acc)
    v_acc[...] = jnp.zeros_like(v_acc)
    for block in range(q_ref.shape[0] // rows):
        first, last = block * rows, (block + 1) * rows
        probs = masked_probs(q_ref, k_ref, start_ref, block, rows)
        d_rows = do_ref[first:last, :]
        d_probs = product_right(d_rows, v_ref[0:last, :])
        delta = jnp.sum(probs * d_probs, axis=1, keepdims=True)
        d_scores = (probs * (d_probs - delta) * (HEAD_DIM ** (-0.5))).astype(BF16)
        q_acc[first:last, :] = product(d_scores, k_ref[0:last, :])
        k_acc[0:last, :] += product_left(d_scores, q_ref[first:last, :])
        v_acc[0:last, :] += product_left(probs.astype(BF16), d_rows)
    dv_ref[...] = v_acc[...].astype(BF16)

    @pl.when(pl.program_id(0) == 0)
    def _():
        sums_ref[...] = jnp.zeros_like(sums_ref)

    scales = jnp.transpose(scale_ref[...])
    for at, (acc, raw, gain, d_ref, dg_ref) in enumerate(
        ((q_acc, qr_ref, gq_ref, dq_ref, dgq_ref), (k_acc, kr_ref, gk_ref, dk_ref, dgk_ref))
    ):
        turned = acc[...].astype(BF16).astype(F32)
        back = turned * cos_ref[...] + turn(turned * sin_ref[...])
        normed = raw[...] * scales[:, 8 * at : 8 * at + 1]
        both = back * normed
        dg_ref[...] = jnp.sum(both, axis=0, keepdims=True)
        d_ref[...] = back * gain[...]
        sums_ref[8 * at : 8 * at + 8, :] += row_sums(both * gain[...])


def attend_back(
    q_rot, k_rot, v_low, d_heads, q_raw, k_raw, scales, q_gain, k_gain, cosine, sine, starts
):
    total, width = v_low.shape
    heads = width // HEAD_DIM
    head, gain = head_spec(total), head_spec(1)
    wide, thin = like((total, width), F32), like((1, width), F32)
    return call(
        functools.partial(attend_back_kernel, min(256, total)),
        [wide, wide, like((total, width), BF16), like((16, total), F32), thin, thin],
        [q_rot, k_rot, v_low, d_heads, q_raw, k_raw, scales, q_gain, k_gain, cosine, sine, starts],
        7 * heads * total * total * HEAD_DIM,
        "attend_back",
        scratch=[pltpu.VMEM((total, HEAD_DIM), F32)] * 3,
        grid=(heads,),
        in_specs=[head] * 6 + [None, gain, gain, None, None, None],
        out_specs=[head, head, head, None, gain, gain],
    )


def chooser(places_ref, at, cap):
    row = places_ref[at : at + 1, :]
    slots = lax.broadcasted_iota(jnp.int32, (cap, row.shape[1]), 0)
    return slots == row


def dispatch_kernel(
    pieces_here, local, cap, gated, mine, *refs
):
    pieces, refs = refs[:pieces_here], refs[pieces_here:]
    places_ref, refs = refs[0], refs[1:]
    if gated:
        (picked_ref, router_ref), refs = refs[:2], refs[2:]
        rows_ref, gate_ref, all_ref = refs[-3:]
    else:
        rows_ref = refs[-1]
    for p in range(pieces_here):
        if gated:
            logits = product_right(router_ref[...], pieces[p][...])
            experts = logits.shape[0]
            picked = picked_ref[p * experts : (p + 1) * experts, :] > 0
            logits = jnp.where(picked, logits, NEG_FILL)
            weights = jnp.exp(logits - jnp.max(logits, axis=0, keepdims=True))
            weights = jnp.where(picked, weights, 0.0)
            gates = weights / jnp.sum(weights, axis=0, keepdims=True)
            all_ref[p * experts : (p + 1) * experts, :] = gates
        for e in range(local):
            chosen = chooser(places_ref, p * local + e, cap)
            rows_ref[e, p * cap : (p + 1) * cap, :] = product(
                chosen.astype(BF16), pieces[p][...]
            ).astype(BF16)
            if gated:
                row = all_ref[pl.ds(p * experts + mine[0] * local + e, 1), :]
                gate_ref[e, p * cap : (p + 1) * cap, :] = jnp.sum(
                    jnp.where(chosen, row, 0.0), axis=1, keepdims=True
                )


def dispatch(mine, pieces, places, picked, router, local, cap, group, at, rows, gates, after=()):
    gated = router is not None
    here = len(pieces)
    width = pieces[0].shape[1]
    args = [*pieces, places]
    shapes = [like((local, group * cap, width), BF16)]
    spec = pl.BlockSpec((local, here * cap, width), lambda i, mine: (0, at, 0))
    out_specs = [spec]
    if gated:
        args += [picked, router]
        shapes += [like((local, group * cap, 1), F32), like((picked.shape[0], places.shape[1]), F32)]
        out_specs += [pl.BlockSpec((local, here * cap, 1), lambda i, mine: (0, at, 0)), None]
    in_specs = [None] * len(args)
    aliases = {}
    if rows is not None:
        aliases[len(args)] = 0
        args.append(rows)
        in_specs.append(pl.BlockSpec(memory_space=pl.ANY))
        if gated:
            aliases[len(args)] = 1
            args.append(gates)
            in_specs.append(pl.BlockSpec(memory_space=pl.ANY))
    return call(
        functools.partial(dispatch_kernel, here, local, cap, gated),
        shapes,
        args,
        2 * here * local * cap * places.shape[1] * width,
        "dispatch",
        scalars=(mine,),
        in_specs=in_specs,
        out_specs=out_specs,
        aliases=aliases,
        after=after,
    )


def expert_kernel(
    x_ref, d_ref, gate_ref, wg_ref, wu_ref, wd_ref,
    act_ref, dg_ref, du_ref, dots_ref, mix_ref, back_ref, mix_acc, back_acc,
):
    step = pl.program_id(1)
    last = pl.num_programs(1) - 1
    x_rows, d_rows, gate = x_ref[0], d_ref[0], gate_ref[0]
    pre = product(x_rows, wg_ref[0])
    up = product(x_rows, wu_ref[0])
    pulled = product_right(d_rows, wd_ref[0])
    sigma = jax.nn.sigmoid(pre)
    silu = pre * sigma
    act = silu * up
    dots = jnp.sum(act * pulled, axis=1, keepdims=True)
    act_low = (act * gate).astype(BF16)
    act_ref[0] = act_low
    d_act = pulled * gate
    du_low = (d_act * silu).astype(BF16)
    dg_low = (d_act * up * sigma * (1.0 + pre * (1.0 - sigma))).astype(BF16)
    dg_ref[0] = dg_low
    du_ref[0] = du_low
    mix = product(act_low, wd_ref[0])
    back = product_right(dg_low, wg_ref[0]) + product_right(du_low, wu_ref[0])

    @pl.when(step == 0)
    def _():
        dots_ref[0] = dots
        mix_acc[...] = mix
        back_acc[...] = back

    @pl.when((step > 0) & (step < last))
    def _():
        dots_ref[0] += dots
        mix_acc[...] += mix
        back_acc[...] += back

    @pl.when(step == last)
    def _():
        dots_ref[0] += dots
        mix_ref[0] = (mix_acc[...] + mix).astype(BF16)
        back_ref[0] = (back_acc[...] + back).astype(BF16)


def experts(rows, d_rows, gates, w_gate, w_up, w_down, after=()):
    local, count, width = rows.shape
    hidden = w_gate.shape[2]
    part = hidden // 2
    wide = pl.BlockSpec((1, count, width), lambda e, f: (e, 0, 0))
    column = pl.BlockSpec((1, count, 1), lambda e, f: (e, 0, 0))
    thin = pl.BlockSpec((1, count, part), lambda e, f: (e, 0, f))
    into = pl.BlockSpec((1, width, part), lambda e, f: (e, 0, f))
    outof = pl.BlockSpec((1, part, width), lambda e, f: (e, f, 0))
    return call(
        expert_kernel,
        [like((local, count, hidden), BF16)] * 3
        + [like((local, count, 1), F32)]
        + [like((local, count, width), BF16)] * 2,
        [rows, d_rows, gates, w_gate, w_up, w_down],
        12 * rows.size * hidden,
        "experts",
        after=after,
        scratch=[pltpu.VMEM((count, width), F32)] * 2,
        grid=(local, 2),
        in_specs=[wide, wide, column, into, into, outof],
        out_specs=[thin, thin, thin, column, wide, wide],
    )


def combine_kernel(here, local, cap, dotted, places_ref, rows_ref, *refs):
    pieces = refs[int(dotted) : int(dotted) + here]
    for p in range(here):
        chosen = [chooser(places_ref, p * local + e, cap) for e in range(local)]
        total = None
        for e in range(local):
            part = product_left(chosen[e].astype(BF16), rows_ref[e, p * cap : (p + 1) * cap, :])
            total = part if total is None else total + part
            if dotted:
                refs[-1][p * local + e : p * local + e + 1, :] = jnp.sum(
                    jnp.where(chosen[e], refs[0][e, p * cap : (p + 1) * cap, :], 0.0),
                    axis=0, keepdims=True,
                )
        pieces[p][...] = total.astype(BF16)


def combine(places, rows, here, local, cap, at, dots=None, after=()):
    width = rows.shape[2]
    tokens = places.shape[1]
    dotted = dots is not None
    args = [places, rows] + ([dots] if dotted else [])
    in_specs = [None, pl.BlockSpec((local, here * cap, width), lambda i: (0, at, 0))]
    if dotted:
        in_specs.append(pl.BlockSpec((local, here * cap, 1), lambda i: (0, at, 0)))
    shapes = [like((tokens, width), BF16)] * here
    if dotted:
        shapes.append(like(places.shape, F32))
    return call(
        functools.partial(combine_kernel, here, local, cap, dotted),
        shapes,
        args,
        2 * here * local * cap * tokens * width,
        "combine",
        after=after,
        in_specs=in_specs,
    )


def combine_stacks_kernel(count, local, cap, group, places_ref, *refs):
    groups = count // group
    for k in range(count):
        rows = refs[k // group]
        at = (k % group) * cap
        total = None
        for e in range(local):
            chosen = chooser(places_ref, k * local + e, cap).astype(BF16)
            part = product_left(chosen, rows[e, at : at + cap, :])
            total = part if total is None else total + part
        array, place = stack_at(k, count)
        refs[groups + array][place] = total.astype(BF16)


def combine_stacks(places, rows, count, local, cap, group, after):
    tokens, width = places.shape[1], rows[0].shape[2]
    return call(
        functools.partial(combine_stacks_kernel, count, local, cap, group),
        stack_shapes(count, (tokens, width)),
        [places, *rows],
        2 * count * local * cap * tokens * width,
        "combine_stacks",
        after=after,
    )


def weight_grad_kernel(groups, *refs):
    lefts, rights = refs[:groups], refs[groups : 2 * groups]
    total = None
    for left, right in zip(lefts, rights):
        part = product_left(left[0], right[0])
        total = part if total is None else total + part
    refs[-1][0] = total.astype(BF16)


def weight_grad(lefts, rights, after=()):
    local, count, tall = lefts[0].shape
    wide = rights[0].shape[2]
    part = min(512, tall)
    left = pl.BlockSpec((1, count, part), lambda e, i: (e, 0, i))
    right = pl.BlockSpec((1, count, wide), lambda e, i: (e, 0, 0))
    return call(
        functools.partial(weight_grad_kernel, len(lefts)),
        like((local, tall, wide), BF16),
        [*lefts, *rights],
        2 * len(lefts) * lefts[0].size * wide,
        "weight_grad",
        after=after,
        grid=(local, tall // part),
        in_specs=[left] * len(lefts) + [right] * len(lefts),
        out_specs=[pl.BlockSpec((1, part, wide), lambda e, i: (e, i, 0))],
    )


def body(
    tokens, doc_lengths, routes, attn_gain, w_query, w_key, w_value, q_gain, k_gain, w_out,
    ffn_gain, w_router, w_gate, w_up, w_down, cotangent,
):
    n_sp = lax.axis_size("sp")
    n_ep = lax.axis_size("ep")
    sp_index = lax.axis_index("sp")
    ep_index = lax.axis_index("ep")
    tok_dev, width = tokens.shape[1:]
    total = tok_dev * n_sp
    shard = width // n_ep
    head_width = width // n_sp
    top_count = routes.shape[2]
    local = w_gate.shape[0]
    expert_count = local * n_ep
    capacity = 9 * tok_dev * top_count // (8 * expert_count)
    cap = -(-capacity // 16) * 16
    group = 4
    blocks = piece_blocks(n_ep, ep_index)
    partners = jnp.bitwise_xor(jnp.arange(n_sp, dtype=jnp.int32), sp_index)
    ids = jnp.concatenate([blocks, partners]).astype(jnp.int32)
    mine = ep_index.astype(jnp.int32).reshape(1)

    def own_columns(value):
        return lax.dynamic_slice_in_dim(value, sp_index * head_width, head_width, 1)

    def by_piece(value):
        return jnp.stack(
            [lax.dynamic_index_in_dim(value, blocks[i], 0, keepdims=False) for i in range(n_ep)]
        )

    expert_ids = jnp.arange(expert_count, dtype=jnp.int32)
    picked = jnp.any(routes[0][:, :, None] == expert_ids[None, None, :], axis=1)
    picked_low = picked.T.astype(BF16)
    small = jnp.concatenate(
        [
            jnp.stack([attn_gain, q_gain, k_gain, ffn_gain]),
            jnp.zeros((12, shard), BF16),
            w_router.T,
        ],
        axis=0,
    )

    def to_all(value):
        value = jnp.broadcast_to(value[None], (n_ep, *value.shape))
        return lax.all_to_all(value, "ep", split_axis=0, concat_axis=0, tiled=True)

    if shard == tok_dev:
        both = to_all(jnp.concatenate([small, picked_low], axis=0))
        small_all, picked_all = both[:, : 16 + expert_count], both[:, 16 + expert_count :]
    else:
        small_all, picked_all = to_all(small), to_all(picked_low)
    small_rows = jnp.swapaxes(small_all, 0, 1).reshape(16 + expert_count, width)
    gains = small_rows[:4].astype(F32)
    full_router = small_rows[16:]
    picked_all = by_piece(picked_all)

    x_all = lax.all_gather(tokens[0], "sp", axis=0, tiled=True)
    w_own = jnp.concatenate([own_columns(w) for w in (w_query, w_key, w_value, w_out)], axis=1)
    cot_own = cotangent[0]
    positions = jnp.arange(total, dtype=jnp.int32)
    lengths = doc_lengths[0]
    doc_ends = jnp.cumsum(lengths)
    starts = jnp.sum(
        jnp.where(doc_ends[None, :] <= positions[:, None], lengths[None, :], 0), axis=1
    )
    half = HEAD_DIM // 2
    frequency = THETA ** (-(2.0 * jnp.arange(half, dtype=F32)) / HEAD_DIM)
    angles = (positions - starts).astype(F32)[:, None] * frequency[None, :]
    cosine = jnp.concatenate([jnp.cos(angles), jnp.cos(angles)], axis=1)
    sine = jnp.concatenate([-jnp.sin(angles), jnp.sin(angles)], axis=1)
    starts = starts[:, None].astype(jnp.int32)
    w_own, cosine, sine, starts, ids = tie(w_own, cosine, sine, starts, ids)
    if n_ep == 8:
        w_pieces = gather_line(w_own)
        w_pieces[6], cot_own = tie(w_pieces[6], cot_own)
        cot_pieces, w_pieces[7] = gather_double(cot_own, w_pieces[7])
    else:
        w_pieces, cot_pieces = gather_whole(w_own), gather_whole(cot_own)

    upper = (
        jnp.arange(tok_dev, dtype=jnp.int32)[:, None] < jnp.arange(tok_dev, dtype=jnp.int32)[None, :]
    ).astype(BF16)
    picked_mine = lax.dynamic_slice_in_dim(picked_all, ep_index * local, local, 1)
    picked_mine = picked_mine.reshape(n_ep * local, tok_dev)
    earlier = product(picked_mine, upper).astype(jnp.int32)
    places = jnp.where((picked_mine > 0) & (earlier < capacity), earlier, -1)
    picked_flat = picked_all.reshape(n_ep * expert_count, tok_dev).astype(F32)


    w_o = [
        jnp.concatenate([piece[:, 3 * head_width :] for piece in half])
        for half in (w_pieces[: n_ep // 2], w_pieces[n_ep // 2 :])
    ]
    w_o_over = [swap_sp(half, 2) for half in w_o]
    q_raw, k_raw, v_low, squares, w_qkv, h_all = qkv_project(
        ids, x_all, gains[0:1], w_pieces, [places, picked_flat]
    )
    scales = lax.rsqrt(sum_sp(squares) / width + EPS)
    gain_q, gain_k = own_columns(gains)[1:2], own_columns(gains)[2:3]
    q_rot, k_rot, mixed = attend(
        q_raw, k_raw, v_low, scales, gain_q, gain_k, cosine, sine, starts,
        [w_o_over[0]] + [cot_pieces[k] for k in ((1, 2, 4) if n_ep == 8 else ())],
    )

    def pair_places(p):
        return places[p * local : (p + 2) * local]

    def cot_rows(g, after):
        d_rows = None
        for at, p in enumerate(range(g, g + group, 2)):
            (d_rows,) = dispatch(
                mine, cot_pieces[p : p + 2], pair_places(p), None, None, local, cap, group, at,
                d_rows, None, after,
            )
        return d_rows

    if n_ep == 8:
        cot_pieces[6], w_o_over[1], mixed = tie(cot_pieces[6], w_o_over[1], mixed)
    attn_tok = lax.all_to_all(mixed, "sp", split_axis=0, concat_axis=1, tiled=True)
    w_o_parts = (
        w_o + [swap_sp(half, 1) for half in w_o] + w_o_over + [swap_sp(half, 1) for half in w_o_over]
    )
    if n_ep == 8:
        cot_pieces[3], attn_tok = tie(cot_pieces[3], attn_tok)
    x_one, h2_low = out_project(
        ids, n_ep, attn_tok, tokens[0], gains[3:4], w_o_parts
    )
    attn_all = lax.all_gather(attn_tok, "sp", axis=0, tiled=True)

    h2_pieces = gather(h2_low, n_ep)
    if n_ep == 8:
        h2_pieces[3], held = tie(h2_pieces[3], cot_pieces[6])
        cot_pieces.append(swap(held, 1))
    cots = [cot_rows(g, [x_one]) for g in range(0, n_ep, group)]
    groups, d_pieces, d_gates, d_sums = [], [], [], []
    home_gates = None

    def rows_of(g, after):
        rows = gates = first_gates = None
        for at, p in enumerate(range(g, g + group, 2)):
            rows, gates, piece_gates = dispatch(
                mine, h2_pieces[p : p + 2], pair_places(p),
                picked_flat[p * expert_count : (p + 2) * expert_count], full_router, local, cap,
                group, at, rows, gates, after,
            )
            first_gates = piece_gates if first_gates is None else first_gates
        return rows, gates, first_gates

    rows, gates, home_gates = rows_of(0, [])
    for g in range(0, n_ep, group):
        d_rows = cots[g // group]
        made = experts(rows, d_rows, gates, w_gate, w_up, w_down, d_pieces[-group:] + h2_pieces[4:7:2])
        groups.append((rows, d_rows, made))
        following = []
        if g + group < n_ep:
            rows, gates, _ = rows_of(g + group, [made[5]])
            following = [rows]
        sums_before = list(d_sums)
        for at in range(group // 2):
            *two, dots = combine(
                pair_places(g + 2 * at), made[5], 2, local, cap, at, made[3],
                sums_before + following,
            )
            d_pieces += two
            d_gates.append(dots)
        if n_ep == 8:
            d_sums += crossed_sums(d_pieces[-group:])

    acts = [made[0] for _, _, made in groups]
    d_gate_rows = [made[1] for _, _, made in groups]
    d_up_rows = [made[2] for _, _, made in groups]
    ins = [rows for rows, _, _ in groups]
    outs = [d_rows for _, d_rows, _ in groups]
    d_gates = by_piece(jnp.concatenate(d_gates, axis=0).reshape(n_ep, local, tok_dev))
    d_gates = lax.all_to_all(d_gates, "ep", split_axis=0, concat_axis=0, tiled=True)
    d_gates = d_gates.reshape(expert_count, tok_dev)
    mix_stacks = combine_stacks(
        places, [made[4] for _, _, made in groups], n_ep, local, cap, group, d_pieces
    )
    grad_down = weight_grad(acts, outs, mix_stacks[:1])
    if n_ep == 8:
        d_sums[2], mix_stacks[2], mix_stacks[3], grad_down = tie(
            d_sums[2], mix_stacks[2], mix_stacks[3], grad_down
        )
        d_h2, d_far = scatter_z(*d_sums)
        d_last = [d_far]
    else:
        d_h2, d_last = scatter(d_pieces, n_ep), []
    grad_gate = weight_grad(ins, d_gate_rows, [grad_down, d_gates, *d_last])
    grad_up = weight_grad(ins, d_up_rows, [grad_gate])

    def over_sp(value):
        return lax.psum_scatter(value, "sp", scatter_dimension=1, tiled=True).astype(F32)


    if n_ep == 8:
        gates_here = home_gates[:expert_count]
    else:
        logits = product_right(full_router, h2_low)
        logits = jnp.where(picked.T, logits, NEG_FILL)
        gates_here = jax.nn.softmax(logits, axis=0)
    d_logits = gates_here * (d_gates - jnp.sum(gates_here * d_gates, axis=0, keepdims=True))
    d_logits = jnp.where(picked.T, d_logits, 0.0).astype(BF16)
    grad_router = product(d_logits, h2_low)
    d_h2 = d_h2 + product_left(d_logits, full_router)
    one_scale = lax.rsqrt(jnp.mean(x_one * x_one, axis=-1, keepdims=True) + EPS)
    one_normed = x_one * one_scale
    grad_ffn = jnp.sum(d_h2 * one_normed, axis=0)
    d_normed = d_h2 * gains[3][None, :]
    d_one = cotangent[0].astype(F32) + one_scale * (
        d_normed - one_normed * jnp.mean(d_normed * one_normed, axis=-1, keepdims=True)
    )
    d_z, grad_up = tie(d_one.astype(BF16), grad_up)
    d_attn = out_back(ids, n_ep, d_z, w_o_parts)
    d_heads = lax.all_to_all(d_attn, "sp", split_axis=1, concat_axis=0, tiled=True)
    d_z_cols = lax.all_to_all(d_z, "sp", split_axis=1, concat_axis=0, tiled=True)
    mix, mix_far = scatter_stacks(mix_stacks, n_ep)
    if n_ep == 8:
        mix, mix_far, d_heads = tie(mix, mix_far, d_heads)
    grad_down, grad_gate, grad_up = over_sp(grad_down), over_sp(grad_gate), over_sp(grad_up)

    d_qn, d_kn, d_v, sums, grad_qg, grad_kg = attend_back(
        q_rot, k_rot, v_low, d_heads, q_raw, k_raw, scales, gain_q, gain_k, cosine, sine, starts
    )
    output = (x_one + last_hop(mix, mix_far)).astype(BF16)
    vo_stacks = vo_grads(ids, n_ep, h_all, d_v, attn_all, d_z_cols)

    grad_vo = last_hop(*scatter_stacks(vo_stacks, n_ep)).astype(BF16)

    def placed(value):
        return lax.dynamic_update_slice_in_dim(
            jnp.zeros((1, width), F32), value, sp_index * head_width, 1
        )

    tiny = jnp.concatenate(
        [placed(grad_qg), placed(grad_kg), grad_ffn[None], grad_router], axis=0
    )
    *qk_stacks, d_qk = qk_back(
        ids, n_ep, h_all, d_qn, d_kn, q_raw, k_raw, scales, sum_sp_swaps(sums), tiny, vo_stacks[:1]
    )
    grad_qk = last_hop(*scatter_stacks(qk_stacks, n_ep)).astype(BF16)

    d_h = d_h_rows(ids, n_ep, n_sp, d_qk, d_v, w_qkv, [])
    halves = plus(d_h[:2], swap_sp(d_h[2:], 1))
    halves, output, grad_down, grad_gate = tie(halves, output, grad_down, grad_gate)
    d_h = halves[0].astype(F32) + swap_sp(halves[1], 2).astype(F32)
    x_rows = tokens[0].astype(F32)
    x_scale = lax.rsqrt(jnp.mean(x_rows * x_rows, axis=-1, keepdims=True) + EPS)
    x_normed = x_rows * x_scale
    d_normed = d_h * gains[0][None, :]
    input_grad = d_one + x_scale * (
        d_normed - x_normed * jnp.mean(d_normed * x_normed, axis=-1, keepdims=True)
    )

    g_query, g_key, g_value, g_out, tiny, g_attn = finish(
        ids, n_ep, w_query, w_key, w_value, attn_gain.astype(F32)[:, None],
        gather_sp(grad_qk), gather_sp(grad_vo), [grad_down, grad_gate, grad_up],
    )
    per_row = 2 * head_width // shard

    def vector(at):
        col = (at % per_row) * shard
        return tiny[at // per_row, col : col + shard]

    g_router = jnp.stack([vector(3 + i) for i in range(expert_count)], axis=1)
    return (
        output[None], input_grad[None], g_attn[:, 0], g_query, g_key, g_value, vector(0), vector(1),
        g_out, vector(2), g_router, grad_gate, grad_up, grad_down,
    )


def solution(mesh):
    seq = P("ep", "sp", None)
    vec = P("ep")
    mat = P("ep", None)
    expert = P("ep", None, None)
    in_specs = (
        seq, mat, seq, vec, mat, mat, mat, vec, vec, mat, vec, mat, expert, expert, expert, seq,
    )
    out_specs = (
        seq, seq, vec, mat, mat, mat, vec, vec, mat, vec, mat, seq, seq, seq,
    )
    return jax.shard_map(body, mesh=mesh, in_specs=in_specs, out_specs=out_specs, check_vma=False)
```

```python
import functools

import jax
import jax.numpy as jnp
from jax import lax
from jax.experimental import pallas as pl
from jax.experimental.pallas import tpu as pltpu
from jax.sharding import PartitionSpec as P

HEAD_DIM = 128
EPS = 1e-05
THETA = 10000.0
NEG_FILL = -1e30
F32 = jnp.float32
BF16 = jnp.bfloat16
MIB = 1 << 20
COVER = 20


def product(left, right):
    return jnp.dot(left, right, preferred_element_type=F32)


def product_left(left, right):
    return lax.dot_general(left, right, (((0,), (0,)), ((), ())), preferred_element_type=F32)


def product_right(left, right):
    return lax.dot_general(left, right, (((1,), (1,)), ((), ())), preferred_element_type=F32)


def row_sums(values_in):
    sums = jnp.sum(values_in, axis=1, keepdims=True)
    return jnp.transpose(jnp.broadcast_to(sums, (sums.shape[0], HEAD_DIM)))[:8]


def call(kernel, out_shape, args, flops, name, scratch=(), scalars=(), grid=(1,), in_specs=None,
         out_specs=None, aliases=None, vmem=60, after=()):
    single = not isinstance(out_shape, (list, tuple))
    shapes = [out_shape] if single else list(out_shape)
    count = len(grid)

    def fixed(shape):
        rank = len(shape)
        return pl.BlockSpec(tuple(shape), lambda *ids: (0,) * rank)

    in_specs = in_specs or [None] * len(args)
    out_specs = out_specs or [None] * len(shapes)
    in_specs = [s if s is not None else fixed(a.shape) for s, a in zip(in_specs, args)]
    out_specs = [s if s is not None else fixed(o.shape) for s, o in zip(out_specs, shapes)]
    waited = len(after)
    args = [*args, *after]
    in_specs = in_specs + [pl.BlockSpec(memory_space=pl.ANY)] * waited
    if waited:
        inner, first = kernel, len(scalars) + len(args) - waited

        def kernel(*refs):
            inner(*refs[:first], *refs[first + waited :])

    moved = sum(a.size * a.dtype.itemsize for a in args[: len(args) - waited])
    moved += sum(o.size * o.dtype.itemsize for o in shapes)
    result = pl.pallas_call(
        kernel,
        grid_spec=pltpu.PrefetchScalarGridSpec(
            num_scalar_prefetch=len(scalars), grid=grid, in_specs=in_specs, out_specs=out_specs,
            scratch_shapes=list(scratch),
        ),
        out_shape=shapes,
        input_output_aliases={k + len(scalars): v for k, v in (aliases or {}).items()},
        compiler_params=pltpu.CompilerParams(
            vmem_limit_bytes=vmem * MIB, dimension_semantics=("arbitrary",) * count
        ),
        cost_estimate=pl.CostEstimate(flops=int(COVER * flops), bytes_accessed=int(moved), transcendentals=0),
        name=name,
    )(*scalars, *args)
    return result[0] if single else list(result)


def like(shape, dtype):
    return jax.ShapeDtypeStruct(tuple(shape), dtype)


def tie(*values):
    return lax.optimization_barrier(values)


def swap(value, bits):
    return lax.ppermute(value, "ep", [(i, i ^ bits) for i in range(8)])


def swap_sp(value, bits):
    return lax.ppermute(value, "sp", [(i, i ^ bits) for i in range(4)])


def piece_blocks(n_ep, ep_index):
    ids = jnp.arange(n_ep, dtype=jnp.int32)
    return jnp.bitwise_xor(ids, ep_index) if n_ep == 8 else ids


MIDDLE = [(2, 4), (3, 5), (4, 2), (5, 3)]
OUTWARD = [(2, 0), (3, 1), (4, 6), (5, 7)]


def gather_line(value):
    crossed = swap(value, 1)
    near = swap(value, 2)
    inner = lax.ppermute(value, "ep", MIDDLE)
    near_x, outer = swap(near, 1), lax.ppermute(near, "ep", MIDDLE)
    near_x, crossed, outer = tie(near_x, crossed, outer)
    far = outer + lax.ppermute(inner, "ep", OUTWARD)
    farther = inner + lax.ppermute(outer, "ep", OUTWARD)
    return [value, crossed, near, near_x, far, swap(far, 1), farther, swap(farther, 1)]


def gather_double(value, after):
    after, held = tie(after, value)
    crossed = swap(held, 1)
    near, far = swap(value, 2), swap(value, 4)
    farther = swap(far, 2)
    near_x, held = tie(swap(near, 1), far)
    return [
        value, crossed, near, near_x, far, swap(held, 1), farther
    ], after


def gather_whole(value):
    whole = lax.all_gather(value, "ep", axis=0, tiled=False)
    return [whole[i] for i in range(whole.shape[0])]


def gather(value, n_ep):
    return gather_line(value) if n_ep == 8 else gather_whole(value)


def plus(left, right):
    return (left.astype(F32) + right.astype(F32)).astype(left.dtype)


def crossed_sums(pieces):
    return [plus(pieces[i], swap(pieces[i + 1], 1)) for i in range(0, len(pieces), 2)]


def scatter_z(own, near, far, farther):
    far = plus(far, swap(farther, 2))
    far, near = tie(far, near)
    return own.astype(F32) + swap(near, 2).astype(F32) + swap(far, 4).astype(F32), far


def scatter(pieces, n_ep):
    if n_ep != 8:
        stacked = jnp.stack(pieces)
        return lax.psum_scatter(stacked, "ep", scatter_dimension=0, tiled=False).astype(F32)
    return scatter_z(*crossed_sums(pieces))[0]


def stack_at(piece, n_ep):
    if n_ep != 8:
        return 0, piece
    return 2 * (piece % 2) + (piece // 2) % 2, piece // 4


def stack_shapes(n_ep, shape):
    return [like((2, *shape), BF16)] * 4 if n_ep == 8 else [like((n_ep, *shape), BF16)]


def odd_sums(stacks):
    return plus(stacks[1], swap(stacks[3], 1))


def even_sums(stacks, odd):
    even = stacks[0].astype(F32) + swap(stacks[2], 1).astype(F32) + swap(odd, 2).astype(F32)
    return even[0], even[1].astype(BF16)


def scatter_stacks(stacks, n_ep):
    if n_ep != 8:
        total = lax.psum_scatter(stacks[0], "ep", scatter_dimension=0, tiled=False)
        return total.astype(F32), None
    return even_sums(stacks, odd_sums(stacks))


def last_hop(total, far):
    return total if far is None else total + swap(far, 4).astype(F32)


def gather_sp(value):
    over = swap_sp(value, 2)
    return [value, swap_sp(value, 1), over, swap_sp(over, 1)]


def sum_sp(value):
    n_sp = lax.axis_size("sp")
    value = jnp.broadcast_to(value[None], (n_sp, *value.shape))
    return jnp.sum(lax.all_to_all(value, "sp", split_axis=0, concat_axis=0, tiled=True), axis=0)


def sum_sp_swaps(value):
    return (value + swap_sp(value, 1)) + (swap_sp(value, 2) + swap_sp(value, 3))


def block_at(ids, position, size):
    if size % HEAD_DIM:
        return pl.ds(position * size, size)
    return pl.ds(pl.multiple_of(ids[position] * size, size), size)


def qkv_kernel(count, ids, x_ref, gain_ref, *refs):
    pieces, refs = refs[:count], refs[count:]
    q_ref, k_ref, v_ref, squares_ref, w_ref, h_ref = refs
    shard = pieces[0].shape[0]
    width = q_ref.shape[1]

    @pl.when(pl.program_id(0) == 0)
    def _():
        for k in range(count):
            rows = block_at(ids, k, shard)
            w_ref[rows, :] = pieces[k][:, : 3 * width]

    x_rows = x_ref[...].astype(F32)
    scale = lax.rsqrt(jnp.mean(x_rows * x_rows, axis=1, keepdims=True) + EPS)
    h_ref[...] = (x_rows * scale * gain_ref[...]).astype(BF16)
    for at, ref in enumerate((q_ref, k_ref)):
        part = product(h_ref[...], w_ref[:, at * width : (at + 1) * width])
        ref[...] = part
        squares_ref[8 * at : 8 * at + 8, :] = row_sums(part * part)
    v_ref[...] = product(h_ref[...], w_ref[:, 2 * width :]).astype(BF16)


def qkv_project(ids, x_all, gain, pieces, after):
    total, depth = x_all.shape
    width = pieces[0].shape[1] // 4
    rows = min(256, total)
    block = pl.BlockSpec((rows, width), lambda i, ids: (i, 0))
    wide = pl.BlockSpec((rows, depth), lambda i, ids: (i, 0))
    return call(
        functools.partial(qkv_kernel, len(pieces)),
        [like((total, width), F32)] * 2
        + [like((total, width), BF16), like((16, total), F32), like((depth, 3 * width), BF16)]
        + [like((total, depth), BF16)],
        [x_all, gain, *pieces],
        6 * total * depth * width,
        "qkv_project",
        after=after,
        scalars=(ids,),
        grid=(total // rows,),
        in_specs=[wide] + [None] * (len(pieces) + 1),
        out_specs=[
            block, block, block, pl.BlockSpec((16, rows), lambda i, ids: (0, i)), None, wide,
        ],
    )


def out_kernel(n_ep, n_sp, ids, attn_ref, x_ref, gain_ref, *refs):
    weights, (one_ref, low_ref, turned_ref) = refs[: 2 * n_sp], refs[2 * n_sp :]
    rows, width = weights[0].shape
    shard = 2 * rows // n_ep
    for k in range(n_ep):
        turned_ref[:, k * shard : (k + 1) * shard] = attn_ref[:, block_at(ids, k, shard)]
    for j in range(n_sp):
        cols = block_at(ids, n_ep + j, width)
        one_ref[:, cols] = (
            x_ref[:, cols].astype(F32)
            + product(turned_ref[:, :rows], weights[2 * j][...])
            + product(turned_ref[:, rows:], weights[2 * j + 1][...])
        )
    one = one_ref[...]
    scale = lax.rsqrt(jnp.mean(one * one, axis=1, keepdims=True) + EPS)
    low_ref[...] = (one * scale * gain_ref[...]).astype(BF16)


def out_project(ids, n_ep, attn_tok, tokens, gain, weights):
    return call(
        functools.partial(out_kernel, n_ep, len(weights) // 2),
        [like(tokens.shape, F32), like(tokens.shape, BF16)],
        [attn_tok, tokens, gain, *weights],
        2 * tokens.size * attn_tok.shape[1],
        "out_project",
        scratch=[pltpu.VMEM(attn_tok.shape, BF16)],
        scalars=(ids,),
    )


def out_back_kernel(n_ep, n_sp, ids, d_ref, *refs):
    weights, d_attn_ref = refs[:-1], refs[-1]
    rows, width = weights[0].shape
    shard = 2 * rows // n_ep
    for half in range(2):
        total = None
        for j in range(n_sp):
            part = product_right(
                d_ref[:, block_at(ids, n_ep + j, width)], weights[2 * j + half][...]
            )
            total = part if total is None else total + part
        total = total.astype(BF16)
        for k in range(n_ep // 2):
            block = block_at(ids, half * (n_ep // 2) + k, shard)
            d_attn_ref[:, block] = total[:, k * shard : (k + 1) * shard]


def out_back(ids, n_ep, d_z, weights):
    return call(
        functools.partial(out_back_kernel, n_ep, len(weights) // 2),
        like((d_z.shape[0], 2 * weights[0].shape[0]), BF16),
        [d_z, *weights],
        2 * d_z.size * weights[0].shape[0] * 2,
        "out_back",
        scalars=(ids,),
    )


def vo_grads_kernel(count, shard, ids, h_ref, dv_ref, attn_ref, dz_ref, *stacks):
    width = dv_ref.shape[1]
    for k in range(count):
        block = block_at(ids, k, shard)
        array, place = stack_at(k, count)
        stacks[array][place, :, :width] = product_left(h_ref[:, block], dv_ref[...]).astype(BF16)
        stacks[array][place, :, width:] = product_left(attn_ref[:, block], dz_ref[...]).astype(BF16)


def vo_grads(ids, count, h_all, d_v, attn_all, d_z_cols):
    shard = h_all.shape[1] // count
    width = d_v.shape[1]
    return call(
        functools.partial(vo_grads_kernel, count, shard),
        stack_shapes(count, (shard, 2 * width)),
        [h_all, d_v, attn_all, d_z_cols],
        4 * h_all.size * width,
        "vo_grads",
        scalars=(ids,),
    )


def qk_back_kernel(
    count, shard, ids, h_ref, dqn_ref, dkn_ref, qr_ref, kr_ref, scale_ref, sums_ref, tiny_ref, *refs
):
    stacks, d_ref = refs[:-1], refs[-1]
    width = dqn_ref.shape[1]
    scales = jnp.transpose(scale_ref[...])
    means = jnp.transpose(sums_ref[...]) * (1.0 / h_ref.shape[1])
    for at, (d_normed, raw) in enumerate(((dqn_ref, qr_ref), (dkn_ref, kr_ref))):
        scale, mean = scales[:, 8 * at : 8 * at + 1], means[:, 8 * at : 8 * at + 1]
        d_ref[:, at * width : (at + 1) * width] = (
            scale * (d_normed[...] - raw[...] * scale * mean)
        ).astype(BF16)
    per_row = 2 * width // shard
    extra = stacks[0].shape[1] - shard
    for k in range(count):
        block = block_at(ids, k, shard)
        array, place = stack_at(k, count)
        ref = stacks[array]
        ref[place, :shard, :] = product_left(h_ref[:, block], d_ref[...]).astype(BF16)
        ref[place, shard:, :] = jnp.zeros((extra, 2 * width), BF16)
        for at in range(tiny_ref.shape[0]):
            row, col = shard + at // per_row, (at % per_row) * shard
            ref[place, row : row + 1, col : col + shard] = tiny_ref[at : at + 1, block].astype(BF16)


def qk_back(ids, count, h_all, d_qn, d_kn, q_raw, k_raw, scales, sums, tiny, after):
    total, depth = h_all.shape
    width = d_qn.shape[1]
    shard = depth // count
    extra = -(-tiny.shape[0] // (2 * width // shard))
    extra = -(-extra // 16) * 16
    return call(
        functools.partial(qk_back_kernel, count, shard),
        stack_shapes(count, (shard + extra, 2 * width)) + [like((total, 2 * width), BF16)],
        [h_all, d_qn, d_kn, q_raw, k_raw, scales, sums, tiny],
        2 * h_all.size * 2 * width,
        "qk_back",
        scalars=(ids,),
        after=after,
    )


def d_h_kernel(ids, d_ref, dv_ref, w_ref, out_ref):
    both = d_ref.shape[1]
    out_ref[0] = (
        product_right(d_ref[...], w_ref[:, :both]) + product_right(dv_ref[...], w_ref[:, both:])
    ).astype(BF16)


def d_h_rows(ids, n_ep, n_sp, d_qk, d_v, w_qkv, after):
    total, wide = d_qk.shape
    depth = w_qkv.shape[0]
    rows = total // n_sp

    def partner(j, ids):
        return ids[n_ep + (j % 2) * 2 + j // 2], 0

    return call(
        d_h_kernel,
        like((n_sp, rows, depth), BF16),
        [d_qk, d_v, w_qkv],
        3 * d_qk.size * depth,
        "d_h",
        after=after,
        scalars=(ids,),
        grid=(n_sp,),
        in_specs=[
            pl.BlockSpec((rows, wide), partner), pl.BlockSpec((rows, d_v.shape[1]), partner), None,
        ],
        out_specs=[pl.BlockSpec((1, rows, depth), lambda j, ids: (j, 0, 0))],
    )


def finish_kernel(n_ep, n_sp, ids, wq_ref, wk_ref, wv_ref, gain_ref, *refs):
    firsts, seconds = refs[:n_sp], refs[n_sp : 2 * n_sp]
    gq_ref, gk_ref, gv_ref, go_ref, tiny_ref, attn_ref = refs[2 * n_sp :]
    shard = wq_ref.shape[0]
    width = firsts[0].shape[1] // 2
    dots = jnp.zeros((shard, 1), F32)
    tiny = jnp.zeros(tiny_ref.shape, F32)
    for j in range(n_sp):
        cols = block_at(ids, n_ep + j, width)
        for at, grad, weight in ((0, gq_ref, wq_ref), (1, gk_ref, wk_ref), (2, gv_ref, wv_ref)):
            part = firsts[j][:shard, at * width : (at + 1) * width] if at < 2 else seconds[j][:, :width]
            value = part.astype(F32)
            grad[:, cols] = value
            dots += jnp.sum(value * weight[:, cols].astype(F32), axis=1, keepdims=True)
        go_ref[:, cols] = seconds[j][:, width:].astype(F32)
        tiny += firsts[j][shard:, :].astype(F32)
    tiny_ref[...] = tiny
    attn_ref[...] = dots / gain_ref[...]


def finish(ids, n_ep, w_query, w_key, w_value, gain, firsts, seconds, after):
    shard, depth = w_query.shape
    extra = firsts[0].shape[0] - shard
    return call(
        functools.partial(finish_kernel, n_ep, len(firsts)),
        [like((shard, depth), F32)] * 4 + [like((extra, firsts[0].shape[1]), F32), like((shard, 1), F32)],
        [w_query, w_key, w_value, gain, *firsts, *seconds],
        shard * depth * 6,
        "finish",
        after=after,
        scalars=(ids,),
    )


def turn(values_in):
    return pltpu.roll(values_in, HEAD_DIM // 2, 1)


def masked_probs(q_ref, k_ref, start_ref, block, rows):
    first, last = block * rows, (block + 1) * rows
    scores = product_right(q_ref[first:last, :], k_ref[0:last, :]) * (HEAD_DIM ** (-0.5))
    row_ids = first + lax.broadcasted_iota(jnp.int32, scores.shape, 0)
    places = lax.broadcasted_iota(jnp.int32, scores.shape, 1)
    allowed = (places <= row_ids) & (places >= start_ref[first:last, :])
    scores = jnp.where(allowed, scores, NEG_FILL)
    top = jnp.max(scores, axis=1, keepdims=True)
    weights = jnp.exp(scores - top)
    return weights * (1.0 / jnp.sum(weights, axis=1, keepdims=True))


def attend_kernel(
    rows, qr_ref, kr_ref, v_ref, scale_ref, gq_ref, gk_ref, cos_ref, sin_ref, start_ref,
    q_ref, k_ref, out_ref,
):
    scales = jnp.transpose(scale_ref[...])
    for at, (raw, gain, low) in enumerate(((qr_ref, gq_ref, q_ref), (kr_ref, gk_ref, k_ref))):
        normed = raw[...] * scales[:, 8 * at : 8 * at + 1] * gain[...]
        low[...] = (normed * cos_ref[...] + turn(normed) * sin_ref[...]).astype(BF16)
    for block in range(q_ref.shape[0] // rows):
        probs = masked_probs(q_ref, k_ref, start_ref, block, rows)
        last = (block + 1) * rows
        out_ref[block * rows : last, :] = product(
            probs.astype(BF16), v_ref[0:last, :]
        ).astype(BF16)


def head_spec(rows):
    return pl.BlockSpec((rows, HEAD_DIM), lambda h: (0, h))


def attend(q_raw, k_raw, v_low, scales, q_gain, k_gain, cosine, sine, starts, after):
    total, width = v_low.shape
    heads = width // HEAD_DIM
    head, gain = head_spec(total), head_spec(1)
    return call(
        functools.partial(attend_kernel, min(256, total)),
        [like((total, width), BF16)] * 3,
        [q_raw, k_raw, v_low, scales, q_gain, k_gain, cosine, sine, starts],
        3 * heads * total * total * HEAD_DIM,
        "attend",
        after=after,
        grid=(heads,),
        in_specs=[head, head, head, None, gain, gain, None, None, None],
        out_specs=[head, head, head],
    )


def attend_back_kernel(
    rows, q_ref, k_ref, v_ref, do_ref, qr_ref, kr_ref, scale_ref, gq_ref, gk_ref,
    cos_ref, sin_ref, start_ref,
    dq_ref, dk_ref, dv_ref, sums_ref, dgq_ref, dgk_ref, q_acc, k_acc, v_acc,
):
    k_acc[...] = jnp.zeros_like(k_acc)
    v_acc[...] = jnp.zeros_like(v_acc)
    for block in range(q_ref.shape[0] // rows):
        first, last = block * rows, (block + 1) * rows
        probs = masked_probs(q_ref, k_ref, start_ref, block, rows)
        d_rows = do_ref[first:last, :]
        d_probs = product_right(d_rows, v_ref[0:last, :])
        delta = jnp.sum(probs * d_probs, axis=1, keepdims=True)
        d_scores = (probs * (d_probs - delta) * (HEAD_DIM ** (-0.5))).astype(BF16)
        q_acc[first:last, :] = product(d_scores, k_ref[0:last, :])
        k_acc[0:last, :] += product_left(d_scores, q_ref[first:last, :])
        v_acc[0:last, :] += product_left(probs.astype(BF16), d_rows)
    dv_ref[...] = v_acc[...].astype(BF16)

    @pl.when(pl.program_id(0) == 0)
    def _():
        sums_ref[...] = jnp.zeros_like(sums_ref)

    scales = jnp.transpose(scale_ref[...])
    for at, (acc, raw, gain, d_ref, dg_ref) in enumerate(
        ((q_acc, qr_ref, gq_ref, dq_ref, dgq_ref), (k_acc, kr_ref, gk_ref, dk_ref, dgk_ref))
    ):
        turned = acc[...].astype(BF16).astype(F32)
        back = turned * cos_ref[...] + turn(turned * sin_ref[...])
        normed = raw[...] * scales[:, 8 * at : 8 * at + 1]
        both = back * normed
        dg_ref[...] = jnp.sum(both, axis=0, keepdims=True)
        d_ref[...] = back * gain[...]
        sums_ref[8 * at : 8 * at + 8, :] += row_sums(both * gain[...])


def attend_back(
    q_rot, k_rot, v_low, d_heads, q_raw, k_raw, scales, q_gain, k_gain, cosine, sine, starts
):
    total, width = v_low.shape
    heads = width // HEAD_DIM
    head, gain = head_spec(total), head_spec(1)
    wide, thin = like((total, width), F32), like((1, width), F32)
    return call(
        functools.partial(attend_back_kernel, min(256, total)),
        [wide, wide, like((total, width), BF16), like((16, total), F32), thin, thin],
        [q_rot, k_rot, v_low, d_heads, q_raw, k_raw, scales, q_gain, k_gain, cosine, sine, starts],
        7 * heads * total * total * HEAD_DIM,
        "attend_back",
        scratch=[pltpu.VMEM((total, HEAD_DIM), F32)] * 3,
        grid=(heads,),
        in_specs=[head] * 6 + [None, gain, gain, None, None, None],
        out_specs=[head, head, head, None, gain, gain],
    )


def chooser(places_ref, at, cap):
    row = places_ref[at : at + 1, :]
    slots = lax.broadcasted_iota(jnp.int32, (cap, row.shape[1]), 0)
    return slots == row


def dispatch_kernel(
    pieces_here, local, cap, gated, mine, *refs
):
    pieces, refs = refs[:pieces_here], refs[pieces_here:]
    places_ref, refs = refs[0], refs[1:]
    if gated:
        (picked_ref, router_ref), refs = refs[:2], refs[2:]
        rows_ref, gate_ref, all_ref = refs[-3:]
    else:
        rows_ref = refs[-1]
    for p in range(pieces_here):
        if gated:
            logits = product_right(router_ref[...], pieces[p][...])
            experts = logits.shape[0]
            picked = picked_ref[p * experts : (p + 1) * experts, :] > 0
            logits = jnp.where(picked, logits, NEG_FILL)
            weights = jnp.exp(logits - jnp.max(logits, axis=0, keepdims=True))
            weights = jnp.where(picked, weights, 0.0)
            gates = weights / jnp.sum(weights, axis=0, keepdims=True)
            all_ref[p * experts : (p + 1) * experts, :] = gates
        for e in range(local):
            chosen = chooser(places_ref, p * local + e, cap)
            rows_ref[e, p * cap : (p + 1) * cap, :] = product(
                chosen.astype(BF16), pieces[p][...]
            ).astype(BF16)
            if gated:
                row = all_ref[pl.ds(p * experts + mine[0] * local + e, 1), :]
                gate_ref[e, p * cap : (p + 1) * cap, :] = jnp.sum(
                    jnp.where(chosen, row, 0.0), axis=1, keepdims=True
                )


def dispatch(mine, pieces, places, picked, router, local, cap, group, at, rows, gates, after=()):
    gated = router is not None
    here = len(pieces)
    width = pieces[0].shape[1]
    args = [*pieces, places]
    shapes = [like((local, group * cap, width), BF16)]
    spec = pl.BlockSpec((local, here * cap, width), lambda i, mine: (0, at, 0))
    out_specs = [spec]
    if gated:
        args += [picked, router]
        shapes += [like((local, group * cap, 1), F32), like((picked.shape[0], places.shape[1]), F32)]
        out_specs += [pl.BlockSpec((local, here * cap, 1), lambda i, mine: (0, at, 0)), None]
    in_specs = [None] * len(args)
    aliases = {}
    if rows is not None:
        aliases[len(args)] = 0
        args.append(rows)
        in_specs.append(pl.BlockSpec(memory_space=pl.ANY))
        if gated:
            aliases[len(args)] = 1
            args.append(gates)
            in_specs.append(pl.BlockSpec(memory_space=pl.ANY))
    return call(
        functools.partial(dispatch_kernel, here, local, cap, gated),
        shapes,
        args,
        2 * here * local * cap * places.shape[1] * width,
        "dispatch",
        scalars=(mine,),
        in_specs=in_specs,
        out_specs=out_specs,
        aliases=aliases,
        after=after,
    )


def expert_kernel(
    x_ref, d_ref, gate_ref, wg_ref, wu_ref, wd_ref,
    act_ref, dg_ref, du_ref, dots_ref, mix_ref, back_ref, mix_acc, back_acc,
):
    step = pl.program_id(1)
    last = pl.num_programs(1) - 1
    x_rows, d_rows, gate = x_ref[0], d_ref[0], gate_ref[0]
    pre = product(x_rows, wg_ref[0])
    up = product(x_rows, wu_ref[0])
    pulled = product_right(d_rows, wd_ref[0])
    sigma = jax.nn.sigmoid(pre)
    silu = pre * sigma
    act = silu * up
    dots = jnp.sum(act * pulled, axis=1, keepdims=True)
    act_low = (act * gate).astype(BF16)
    act_ref[0] = act_low
    d_act = pulled * gate
    du_low = (d_act * silu).astype(BF16)
    dg_low = (d_act * up * sigma * (1.0 + pre * (1.0 - sigma))).astype(BF16)
    dg_ref[0] = dg_low
    du_ref[0] = du_low
    mix = product(act_low, wd_ref[0])
    back = product_right(dg_low, wg_ref[0]) + product_right(du_low, wu_ref[0])

    @pl.when(step == 0)
    def _():
        dots_ref[0] = dots
        mix_acc[...] = mix
        back_acc[...] = back

    @pl.when((step > 0) & (step < last))
    def _():
        dots_ref[0] += dots
        mix_acc[...] += mix
        back_acc[...] += back

    @pl.when(step == last)
    def _():
        dots_ref[0] += dots
        mix_ref[0] = (mix_acc[...] + mix).astype(BF16)
        back_ref[0] = (back_acc[...] + back).astype(BF16)


def experts(rows, d_rows, gates, w_gate, w_up, w_down, after=()):
    local, count, width = rows.shape
    hidden = w_gate.shape[2]
    part = hidden // 2
    wide = pl.BlockSpec((1, count, width), lambda e, f: (e, 0, 0))
    column = pl.BlockSpec((1, count, 1), lambda e, f: (e, 0, 0))
    thin = pl.BlockSpec((1, count, part), lambda e, f: (e, 0, f))
    into = pl.BlockSpec((1, width, part), lambda e, f: (e, 0, f))
    outof = pl.BlockSpec((1, part, width), lambda e, f: (e, f, 0))
    return call(
        expert_kernel,
        [like((local, count, hidden), BF16)] * 3
        + [like((local, count, 1), F32)]
        + [like((local, count, width), BF16)] * 2,
        [rows, d_rows, gates, w_gate, w_up, w_down],
        12 * rows.size * hidden,
        "experts",
        after=after,
        scratch=[pltpu.VMEM((count, width), F32)] * 2,
        grid=(local, 2),
        in_specs=[wide, wide, column, into, into, outof],
        out_specs=[thin, thin, thin, column, wide, wide],
    )


def combine_kernel(here, local, cap, dotted, places_ref, rows_ref, *refs):
    pieces = refs[int(dotted) : int(dotted) + here]
    for p in range(here):
        chosen = [chooser(places_ref, p * local + e, cap) for e in range(local)]
        total = None
        for e in range(local):
            part = product_left(chosen[e].astype(BF16), rows_ref[e, p * cap : (p + 1) * cap, :])
            total = part if total is None else total + part
            if dotted:
                refs[-1][p * local + e : p * local + e + 1, :] = jnp.sum(
                    jnp.where(chosen[e], refs[0][e, p * cap : (p + 1) * cap, :], 0.0),
                    axis=0, keepdims=True,
                )
        pieces[p][...] = total.astype(BF16)


def combine(places, rows, here, local, cap, at, dots=None, after=()):
    width = rows.shape[2]
    tokens = places.shape[1]
    dotted = dots is not None
    args = [places, rows] + ([dots] if dotted else [])
    in_specs = [None, pl.BlockSpec((local, here * cap, width), lambda i: (0, at, 0))]
    if dotted:
        in_specs.append(pl.BlockSpec((local, here * cap, 1), lambda i: (0, at, 0)))
    shapes = [like((tokens, width), BF16)] * here
    if dotted:
        shapes.append(like(places.shape, F32))
    return call(
        functools.partial(combine_kernel, here, local, cap, dotted),
        shapes,
        args,
        2 * here * local * cap * tokens * width,
        "combine",
        after=after,
        in_specs=in_specs,
    )


def combine_stacks_kernel(count, local, cap, group, places_ref, *refs):
    groups = count // group
    for k in range(count):
        rows = refs[k // group]
        at = (k % group) * cap
        total = None
        for e in range(local):
            chosen = chooser(places_ref, k * local + e, cap).astype(BF16)
            part = product_left(chosen, rows[e, at : at + cap, :])
            total = part if total is None else total + part
        array, place = stack_at(k, count)
        refs[groups + array][place] = total.astype(BF16)


def combine_stacks(places, rows, count, local, cap, group, after):
    tokens, width = places.shape[1], rows[0].shape[2]
    return call(
        functools.partial(combine_stacks_kernel, count, local, cap, group),
        stack_shapes(count, (tokens, width)),
        [places, *rows],
        2 * count * local * cap * tokens * width,
        "combine_stacks",
        after=after,
    )


def weight_grad_kernel(groups, *refs):
    lefts, rights = refs[:groups], refs[groups : 2 * groups]
    total = None
    for left, right in zip(lefts, rights):
        part = product_left(left[0], right[0])
        total = part if total is None else total + part
    refs[-1][0] = total.astype(BF16)


def weight_grad(lefts, rights, after=()):
    local, count, tall = lefts[0].shape
    wide = rights[0].shape[2]
    part = min(512, tall)
    left = pl.BlockSpec((1, count, part), lambda e, i: (e, 0, i))
    right = pl.BlockSpec((1, count, wide), lambda e, i: (e, 0, 0))
    return call(
        functools.partial(weight_grad_kernel, len(lefts)),
        like((local, tall, wide), BF16),
        [*lefts, *rights],
        2 * len(lefts) * lefts[0].size * wide,
        "weight_grad",
        after=after,
        grid=(local, tall // part),
        in_specs=[left] * len(lefts) + [right] * len(lefts),
        out_specs=[pl.BlockSpec((1, part, wide), lambda e, i: (e, i, 0))],
    )


def body(
    tokens, doc_lengths, routes, attn_gain, w_query, w_key, w_value, q_gain, k_gain, w_out,
    ffn_gain, w_router, w_gate, w_up, w_down, cotangent,
):
    n_sp = lax.axis_size("sp")
    n_ep = lax.axis_size("ep")
    sp_index = lax.axis_index("sp")
    ep_index = lax.axis_index("ep")
    tok_dev, width = tokens.shape[1:]
    total = tok_dev * n_sp
    shard = width // n_ep
    head_width = width // n_sp
    top_count = routes.shape[2]
    local = w_gate.shape[0]
    expert_count = local * n_ep
    capacity = 9 * tok_dev * top_count // (8 * expert_count)
    cap = -(-capacity // 16) * 16
    group = 4
    blocks = piece_blocks(n_ep, ep_index)
    partners = jnp.bitwise_xor(jnp.arange(n_sp, dtype=jnp.int32), sp_index)
    ids = jnp.concatenate([blocks, partners]).astype(jnp.int32)
    mine = ep_index.astype(jnp.int32).reshape(1)

    def own_columns(value):
        return lax.dynamic_slice_in_dim(value, sp_index * head_width, head_width, 1)

    def by_piece(value):
        return jnp.stack(
            [lax.dynamic_index_in_dim(value, blocks[i], 0, keepdims=False) for i in range(n_ep)]
        )

    expert_ids = jnp.arange(expert_count, dtype=jnp.int32)
    picked = jnp.any(routes[0][:, :, None] == expert_ids[None, None, :], axis=1)
    picked_low = picked.T.astype(BF16)
    small = jnp.concatenate(
        [
            jnp.stack([attn_gain, q_gain, k_gain, ffn_gain]),
            jnp.zeros((12, shard), BF16),
            w_router.T,
        ],
        axis=0,
    )

    def to_all(value):
        value = jnp.broadcast_to(value[None], (n_ep, *value.shape))
        return lax.all_to_all(value, "ep", split_axis=0, concat_axis=0, tiled=True)

    if shard == tok_dev:
        both = to_all(jnp.concatenate([small, picked_low], axis=0))
        small_all, picked_all = both[:, : 16 + expert_count], both[:, 16 + expert_count :]
    else:
        small_all, picked_all = to_all(small), to_all(picked_low)
    small_rows = jnp.swapaxes(small_all, 0, 1).reshape(16 + expert_count, width)
    gains = small_rows[:4].astype(F32)
    full_router = small_rows[16:]
    picked_all = by_piece(picked_all)

    x_all = lax.all_gather(tokens[0], "sp", axis=0, tiled=True)
    w_own = jnp.concatenate([own_columns(w) for w in (w_query, w_key, w_value, w_out)], axis=1)
    cot_own = cotangent[0]
    positions = jnp.arange(total, dtype=jnp.int32)
    lengths = doc_lengths[0]
    doc_ends = jnp.cumsum(lengths)
    starts = jnp.sum(
        jnp.where(doc_ends[None, :] <= positions[:, None], lengths[None, :], 0), axis=1
    )
    half = HEAD_DIM // 2
    frequency = THETA ** (-(2.0 * jnp.arange(half, dtype=F32)) / HEAD_DIM)
    angles = (positions - starts).astype(F32)[:, None] * frequency[None, :]
    cosine = jnp.concatenate([jnp.cos(angles), jnp.cos(angles)], axis=1)
    sine = jnp.concatenate([-jnp.sin(angles), jnp.sin(angles)], axis=1)
    starts = starts[:, None].astype(jnp.int32)
    w_own, cosine, sine, starts, ids = tie(w_own, cosine, sine, starts, ids)
    if n_ep == 8:
        w_pieces = gather_line(w_own)
        w_pieces[6], cot_own = tie(w_pieces[6], cot_own)
        cot_pieces, w_pieces[7] = gather_double(cot_own, w_pieces[7])
    else:
        w_pieces, cot_pieces = gather_whole(w_own), gather_whole(cot_own)

    upper = (
        jnp.arange(tok_dev, dtype=jnp.int32)[:, None] < jnp.arange(tok_dev, dtype=jnp.int32)[None, :]
    ).astype(BF16)
    picked_mine = lax.dynamic_slice_in_dim(picked_all, ep_index * local, local, 1)
    picked_mine = picked_mine.reshape(n_ep * local, tok_dev)
    earlier = product(picked_mine, upper).astype(jnp.int32)
    places = jnp.where((picked_mine > 0) & (earlier < capacity), earlier, -1)
    picked_flat = picked_all.reshape(n_ep * expert_count, tok_dev).astype(F32)


    w_o = [
        jnp.concatenate([piece[:, 3 * head_width :] for piece in half])
        for half in (w_pieces[: n_ep // 2], w_pieces[n_ep // 2 :])
    ]
    w_o_over = [swap_sp(half, 2) for half in w_o]
    q_raw, k_raw, v_low, squares, w_qkv, h_all = qkv_project(
        ids, x_all, gains[0:1], w_pieces, [places, picked_flat]
    )
    scales = lax.rsqrt(sum_sp(squares) / width + EPS)
    gain_q, gain_k = own_columns(gains)[1:2], own_columns(gains)[2:3]
    q_rot, k_rot, mixed = attend(
        q_raw, k_raw, v_low, scales, gain_q, gain_k, cosine, sine, starts,
        [w_o_over[0]] + [cot_pieces[k] for k in ((1, 2, 4) if n_ep == 8 else ())],
    )

    def pair_places(p):
        return places[p * local : (p + 2) * local]

    def cot_rows(g, after):
        d_rows = None
        for at, p in enumerate(range(g, g + group, 2)):
            (d_rows,) = dispatch(
                mine, cot_pieces[p : p + 2], pair_places(p), None, None, local, cap, group, at,
                d_rows, None, after,
            )
        return d_rows

    if n_ep == 8:
        cot_pieces[6], w_o_over[1], mixed = tie(cot_pieces[6], w_o_over[1], mixed)
    attn_tok = lax.all_to_all(mixed, "sp", split_axis=0, concat_axis=1, tiled=True)
    w_o_parts = (
        w_o + [swap_sp(half, 1) for half in w_o] + w_o_over + [swap_sp(half, 1) for half in w_o_over]
    )
    if n_ep == 8:
        cot_pieces[3], attn_tok = tie(cot_pieces[3], attn_tok)
    x_one, h2_low = out_project(
        ids, n_ep, attn_tok, tokens[0], gains[3:4], w_o_parts
    )
    attn_all = lax.all_gather(attn_tok, "sp", axis=0, tiled=True)

    h2_pieces = gather(h2_low, n_ep)
    if n_ep == 8:
        h2_pieces[3], held = tie(h2_pieces[3], cot_pieces[6])
        cot_pieces.append(swap(held, 1))
    cots = [cot_rows(g, [x_one]) for g in range(0, n_ep, group)]
    groups, d_pieces, d_gates, d_sums = [], [], [], []
    home_gates = None

    def rows_of(g, after):
        rows = gates = first_gates = None
        for at, p in enumerate(range(g, g + group, 2)):
            rows, gates, piece_gates = dispatch(
                mine, h2_pieces[p : p + 2], pair_places(p),
                picked_flat[p * expert_count : (p + 2) * expert_count], full_router, local, cap,
                group, at, rows, gates, after,
            )
            first_gates = piece_gates if first_gates is None else first_gates
        return rows, gates, first_gates

    rows, gates, home_gates = rows_of(0, [])
    for g in range(0, n_ep, group):
        d_rows = cots[g // group]
        made = experts(rows, d_rows, gates, w_gate, w_up, w_down, d_pieces[-group:] + h2_pieces[4:7:2])
        groups.append((rows, d_rows, made))
        following = []
        if g + group < n_ep:
            rows, gates, _ = rows_of(g + group, [made[5]])
            following = [rows]
        sums_before = list(d_sums)
        for at in range(group // 2):
            *two, dots = combine(
                pair_places(g + 2 * at), made[5], 2, local, cap, at, made[3],
                sums_before + following,
            )
            d_pieces += two
            d_gates.append(dots)
        if n_ep == 8:
            d_sums += crossed_sums(d_pieces[-group:])

    acts = [made[0] for _, _, made in groups]
    d_gate_rows = [made[1] for _, _, made in groups]
    d_up_rows = [made[2] for _, _, made in groups]
    ins = [rows for rows, _, _ in groups]
    outs = [d_rows for _, d_rows, _ in groups]
    d_gates = by_piece(jnp.concatenate(d_gates, axis=0).reshape(n_ep, local, tok_dev))
    d_gates = lax.all_to_all(d_gates, "ep", split_axis=0, concat_axis=0, tiled=True)
    d_gates = d_gates.reshape(expert_count, tok_dev)
    mix_stacks = combine_stacks(
        places, [made[4] for _, _, made in groups], n_ep, local, cap, group, d_pieces
    )
    grad_down = weight_grad(acts, outs, mix_stacks[:1])
    if n_ep == 8:
        d_sums[2], mix_stacks[2], mix_stacks[3], grad_down = tie(
            d_sums[2], mix_stacks[2], mix_stacks[3], grad_down
        )
        d_h2, d_far = scatter_z(*d_sums)
        d_last = [d_far]
    else:
        d_h2, d_last = scatter(d_pieces, n_ep), []
    grad_gate = weight_grad(ins, d_gate_rows, [grad_down, d_gates, *d_last])
    grad_up = weight_grad(ins, d_up_rows, [grad_gate])

    def over_sp(value):
        return lax.psum_scatter(value, "sp", scatter_dimension=1, tiled=True).astype(F32)


    if n_ep == 8:
        gates_here = home_gates[:expert_count]
    else:
        logits = product_right(full_router, h2_low)
        logits = jnp.where(picked.T, logits, NEG_FILL)
        gates_here = jax.nn.softmax(logits, axis=0)
    d_logits = gates_here * (d_gates - jnp.sum(gates_here * d_gates, axis=0, keepdims=True))
    d_logits = jnp.where(picked.T, d_logits, 0.0).astype(BF16)
    grad_router = product(d_logits, h2_low)
    d_h2 = d_h2 + product_left(d_logits, full_router)
    one_scale = lax.rsqrt(jnp.mean(x_one * x_one, axis=-1, keepdims=True) + EPS)
    one_normed = x_one * one_scale
    grad_ffn = jnp.sum(d_h2 * one_normed, axis=0)
    d_normed = d_h2 * gains[3][None, :]
    d_one = cotangent[0].astype(F32) + one_scale * (
        d_normed - one_normed * jnp.mean(d_normed * one_normed, axis=-1, keepdims=True)
    )
    d_z, grad_up = tie(d_one.astype(BF16), grad_up)
    d_attn = out_back(ids, n_ep, d_z, w_o_parts)
    d_heads = lax.all_to_all(d_attn, "sp", split_axis=1, concat_axis=0, tiled=True)
    d_z_cols = lax.all_to_all(d_z, "sp", split_axis=1, concat_axis=0, tiled=True)
    mix, mix_far = scatter_stacks(mix_stacks, n_ep)
    if n_ep == 8:
        mix, mix_far, d_heads = tie(mix, mix_far, d_heads)
    grad_down, grad_gate, grad_up = over_sp(grad_down), over_sp(grad_gate), over_sp(grad_up)

    d_qn, d_kn, d_v, sums, grad_qg, grad_kg = attend_back(
        q_rot, k_rot, v_low, d_heads, q_raw, k_raw, scales, gain_q, gain_k, cosine, sine, starts
    )
    output = (x_one + last_hop(mix, mix_far)).astype(BF16)
    vo_stacks = vo_grads(ids, n_ep, h_all, d_v, attn_all, d_z_cols)

    grad_vo = last_hop(*scatter_stacks(vo_stacks, n_ep)).astype(BF16)

    def placed(value):
        return lax.dynamic_update_slice_in_dim(
            jnp.zeros((1, width), F32), value, sp_index * head_width, 1
        )

    tiny = jnp.concatenate(
        [placed(grad_qg), placed(grad_kg), grad_ffn[None], grad_router], axis=0
    )
    *qk_stacks, d_qk = qk_back(
        ids, n_ep, h_all, d_qn, d_kn, q_raw, k_raw, scales, sum_sp_swaps(sums), tiny, vo_stacks[:1]
    )
    grad_qk = last_hop(*scatter_stacks(qk_stacks, n_ep)).astype(BF16)

    d_h = d_h_rows(ids, n_ep, n_sp, d_qk, d_v, w_qkv, [grad_down, grad_gate])
    output, d_h = tie(output, d_h)
    halves = plus(d_h[:2], swap_sp(d_h[2:], 1))
    d_h = halves[0].astype(F32) + swap_sp(halves[1], 2).astype(F32)
    x_rows = tokens[0].astype(F32)
    x_scale = lax.rsqrt(jnp.mean(x_rows * x_rows, axis=-1, keepdims=True) + EPS)
    x_normed = x_rows * x_scale
    d_normed = d_h * gains[0][None, :]
    input_grad = d_one + x_scale * (
        d_normed - x_normed * jnp.mean(d_normed * x_normed, axis=-1, keepdims=True)
    )

    g_query, g_key, g_value, g_out, tiny, g_attn = finish(
        ids, n_ep, w_query, w_key, w_value, attn_gain.astype(F32)[:, None],
        gather_sp(grad_qk), gather_sp(grad_vo), [grad_down, grad_gate, grad_up],
    )
    per_row = 2 * head_width // shard

    def vector(at):
        col = (at % per_row) * shard
        return tiny[at // per_row, col : col + shard]

    g_router = jnp.stack([vector(3 + i) for i in range(expert_count)], axis=1)
    return (
        output[None], input_grad[None], g_attn[:, 0], g_query, g_key, g_value, vector(0), vector(1),
        g_out, vector(2), g_router, grad_gate, grad_up, grad_down,
    )


def solution(mesh):
    seq = P("ep", "sp", None)
    vec = P("ep")
    mat = P("ep", None)
    expert = P("ep", None, None)
    in_specs = (
        seq, mat, seq, vec, mat, mat, mat, vec, vec, mat, vec, mat, expert, expert, expert, seq,
    )
    out_specs = (
        seq, seq, vec, mat, mat, mat, vec, vec, mat, vec, mat, seq, seq, seq,
    )
    return jax.shard_map(body, mesh=mesh, in_specs=in_specs, out_specs=out_specs, check_vma=False)
```
